32 devices in a mesh: dp: 8 (over z, y), tensor: 4 (over x, core).
Axes of the slice: x: 2, y: 2, z: 4, core: 2. Of those that a mesh axis runs over, the one named last changes fastest.
Arguments:
- tokens: bfloat16 [8192, 768], P(('dp', 'tensor')), may hold values from -6 to 6
- cotangent: bfloat16 [8192, 768], P(('dp', 'tensor')), may hold values from -6 to 6
- segments: int32 [8192], P('dp'), may hold values from 0 to 95, as said below
- lengths: int32 [32, 2], P('dp'), may hold values from 2 to 197, as said below
- rel_index: int32 [8192, 256], P('dp'), may hold values from 0 to 731, as said below
- w_qkv: bfloat16 [2, 768, 3, 768], P(None, None, None, 'tensor'), may hold values from -0.21875 to 0.21875
- qv_bias: bfloat16 [2, 2, 768], P(None, None, 'tensor'), may hold values from -3 to 3
- w_out: bfloat16 [2, 768, 768], P(None, 'tensor'), may hold values from -0.875 to 0.875
- w_fc1: bfloat16 [2, 768, 3072], P(None, None, 'tensor'), may hold values from -0.21875 to 0.21875
- fc1_bias: bfloat16 [2, 3072], P(None, 'tensor'), may hold values from -3 to 3
- w_fc2: bfloat16 [2, 3072, 768], P(None, 'tensor'), may hold values from -0.109375 to 0.109375
- rel_table: bfloat16 [2, 732, 12], P(None, None, 'tensor'), may hold values from -5 to 5
- ln_gain: float32 [2, 2, 768], replicated, may hold values from 0.25 to 1.75
- ln_bias: float32 [2, 2, 768], replicated, may hold values from -2 to 2
- layer_scale: float32 [2, 2, 768], replicated, may hold values from 0.25 to 1.75
- row_bias: float32 [2, 2, 768], replicated, may hold values from -2 to 2
Outputs:
- result: bfloat16 [8192, 768], P(('dp', 'tensor'))
- d_tokens: float32 [8192, 768], P(('dp', 'tensor'))
- d_w_qkv: float32 [2, 768, 3, 768], P(None, None, None, 'tensor')
- d_qv_bias: float32 [2, 2, 768], P(None, None, 'tensor')
- d_w_out: float32 [2, 768, 768], P(None, 'tensor')
- d_w_fc1: float32 [2, 768, 3072], P(None, None, 'tensor')
- d_fc1_bias: float32 [2, 3072], P(None, 'tensor')
- d_w_fc2: float32 [2, 3072, 768], P(None, 'tensor')
- d_rel_table: float32 [2, 732, 12], P(None, None, 'tensor')
- d_ln_gain: float32 [2, 2, 768], replicated
- d_ln_bias: float32 [2, 2, 768], replicated
- d_layer_scale: float32 [2, 2, 768], replicated
- d_row_bias: float32 [2, 2, 768], replicated
The draws below stay inside these ranges and needn't reach their ends.
Inputs may be any that keep to these rules, and one draw needn't show every extreme that they name: `segments`: rows with equal ids belong to one image, or to the padding that ends one bin of 256 rows. Bin b holds rows of id 3 b (its first image), then 3 b + 1 (its second image), then one or more rows of id 3 b + 2 (padding). `lengths`: the rows of a bin's first and second image, in the order of segments; an image of r by c patches has r c + 1 rows, its class token first, then its patches row by row; a bin's two lengths sum to 255 or less. `rel_index`: for rows i and j of one image: (dr + 13) * 27 + dc + 13 for two patches whose row and column offsets are dr and dc, 729 from the class token to a patch, 730 from a patch to the class token, 731 for the class token with itself. Other entries are arbitrary.
All inputs are finite; a program needn't handle non-finite values.
Results may differ from the reference program's by a relative error of at most 0.023.
Values may be sent and summed in bfloat16 or wider, within the bound.
A program may use at most 128 MiB of HBM per device.

```python
import jax
import jax.numpy as jnp
from jax import lax

HEADS = 12
HEAD_DIM = 64
D = 768
FF = 3072
SIDE = 14
NB = 732
BIN = 256
LAYERS = 2
GROUP = 1024
BINS = 32
TOKENS = 8192
N_DP = 8


def image_shapes(key):
    base_key = jax.random.fold_in(key, 4049)
    subkeys = jax.random.split(base_key, 5)
    lowest_side = max(1, SIDE // 2)
    is_first = jnp.arange(BINS) == 0
    rows_first = jnp.where(is_first, SIDE, jax.random.randint(subkeys[0], (BINS,), lowest_side, SIDE + 1))
    cols_first = jnp.where(is_first, SIDE, jax.random.randint(subkeys[1], (BINS,), lowest_side, SIDE + 1))
    len_first = rows_first * cols_first + 1
    rows_second = jax.random.randint(subkeys[2], (BINS,), 1, SIDE + 1)
    spare_cols = (BIN - len_first - 2) // rows_second
    cols_second = jnp.clip(jax.random.randint(subkeys[3], (BINS,), 1, SIDE + 1), 1, spare_cols)
    return (rows_first, cols_first, rows_second, cols_second, subkeys[4])


def token_layout(key):
    rows_first, cols_first, rows_second, cols_second, fill_key = image_shapes(key)
    len_first = rows_first * cols_first + 1
    len_second = rows_second * cols_second + 1
    position = jnp.arange(TOKENS) % BIN
    bin_of = jnp.arange(TOKENS) // BIN
    end_first = len_first[bin_of]
    end_second = end_first + len_second[bin_of]
    slot_of = jnp.where(position < end_first, 0, jnp.where(position < end_second, 1, 2))
    offset = jnp.where(slot_of == 0, position - 1, position - end_first - 1)
    columns = jnp.where(slot_of == 0, cols_first[bin_of], cols_second[bin_of])
    columns = jnp.where(slot_of == 2, 1, columns)
    patch_row = jnp.where(offset < 0, 0, offset) // columns
    patch_col = jnp.where(offset < 0, 0, offset) % columns
    return (len_first, len_second, bin_of, slot_of, offset, patch_row, patch_col, fill_key)


def draw_lengths(key, part):
    len_first, len_second, bin_of, slot_of, offset, patch_row, patch_col, fill_key = token_layout(key)
    return jnp.stack([len_first, len_second], 1).astype(jnp.int32)


def draw_segments(key, part):
    len_first, len_second, bin_of, slot_of, offset, patch_row, patch_col, fill_key = token_layout(key)
    return (bin_of * 3 + slot_of).astype(jnp.int32)


def draw_rel_index(key, part):
    len_first, len_second, bin_of, slot_of, offset, patch_row, patch_col, fill_key = token_layout(key)
    stride = 2 * SIDE - 1
    base_code = patch_row * stride + patch_col

    def per_bin(values):
        return jnp.repeat(values.reshape(BINS, BIN), BIN, axis=0)
    key_slot = per_bin(slot_of)
    key_code = per_bin(base_code)
    key_class = per_bin(offset < 0)
    query_class = (offset < 0)[:, None]
    same_image = (slot_of[:, None] == key_slot) & (slot_of[:, None] < 2)
    code = base_code[:, None] - key_code + (SIDE - 1) * stride + SIDE - 1
    code = jnp.where(query_class & key_class, NB - 1, jnp.where(query_class, NB - 3, jnp.where(key_class, NB - 2, code)))
    filler = jax.random.randint(fill_key, (TOKENS, BIN), 0, NB)
    return jnp.where(same_image, code, filler).astype(jnp.int32)


def levels(rng, dims, cuts, least, top_value):
    gain, own = 1.0, jax.random.fold_in(rng, 6)
    for axis_at, shards_of in cuts:
        heights = jnp.exp(jax.random.uniform(jax.random.fold_in(own, axis_at), (shards_of,), jnp.float32, least / len(cuts), top_value / len(cuts)))
        gain = gain * jnp.repeat(heights, dims[axis_at] // shards_of).reshape([-1 if axis == axis_at else 1 for axis in range(len(dims))])
    return gain


def scatter_about(rng, shape, spread, reach, shards=(), kind=jnp.bfloat16):
    gain = levels(rng, shape, shards, -0.22, 0.18) if shards else 1.0
    drawn = jax.random.normal(rng, shape, jnp.float32) * spread * gain
    return jnp.minimum(jnp.maximum(drawn, -reach), reach).astype(kind)


def setup_inputs(seed: int = 0) -> dict:
    arg_keys = jax.random.split(jax.random.key(seed), 17)
    return {
        "tokens": scatter_about(arg_keys[0], (TOKENS, D), 1.0, 6.0, ((0, 32),)),
        "cotangent": scatter_about(arg_keys[1], (TOKENS, D), 1.0, 6.0, ((0, 32),)),
        "segments": draw_segments(jax.random.fold_in(arg_keys[16], 71), 0),
        "lengths": draw_lengths(jax.random.fold_in(arg_keys[16], 71), 0),
        "rel_index": draw_rel_index(jax.random.fold_in(arg_keys[16], 71), 0),
        "w_qkv": scatter_about(arg_keys[5], (LAYERS, D, 3, D), D ** -0.5, 0.21875, ((3, 4),)),
        "qv_bias": scatter_about(arg_keys[6], (LAYERS, 2, D), 0.5, 3.0, ((2, 4),)),
        "w_out": scatter_about(arg_keys[7], (LAYERS, D, D), (D // 16) ** -0.5, 0.875, ((1, 4),)),
        "w_fc1": scatter_about(arg_keys[8], (LAYERS, D, FF), D ** -0.5, 0.21875, ((2, 4),)),
        "fc1_bias": scatter_about(arg_keys[9], (LAYERS, FF), 0.5, 3.0, ((1, 4),)),
        "w_fc2": scatter_about(arg_keys[10], (LAYERS, FF, D), FF ** -0.5, 0.109375, ((1, 4),)),
        "rel_table": scatter_about(arg_keys[11], (LAYERS, NB, HEADS), 1.0, 5.0, ((2, 4),)),
        "ln_gain": jnp.clip(1.0 + 0.15 * jax.random.normal(arg_keys[12], (LAYERS, 2, D), jnp.float32), 0.25, 1.75),
        "ln_bias": scatter_about(arg_keys[13], (LAYERS, 2, D), 0.3, 2.0, (), jnp.float32),
        "layer_scale": jnp.clip(1.0 + 0.15 * jax.random.normal(arg_keys[14], (LAYERS, 2, D), jnp.float32), 0.25, 1.75),
        "row_bias": scatter_about(arg_keys[15], (LAYERS, 2, D), 0.3, 2.0, (), jnp.float32),
    }


@jax.custom_vjp
def low(v):
    return lax.optimization_barrier(v.astype(jnp.bfloat16)).astype(jnp.float32)

@jax.custom_vjp
def low_back(v):
    return v

def low_keep(v):
    return (low(v), None)

def low_pass(kept, grad):
    return (grad,)

def back_keep(v):
    return (v, None)

def back_low(kept, grad):
    return (low(grad),)
low.defvjp(low_keep, low_pass)
low_back.defvjp(back_keep, back_low)

def narrow_both(values):
    return low(low_back(values))

def layer_norm(stream, norm_gain, norm_shift):
    center = stream - lax.optimization_barrier(jnp.mean(stream, -1, keepdims=True))
    inverse = lax.rsqrt(lax.optimization_barrier(jnp.mean(center * center, -1, keepdims=True)) + 1e-06)
    return center * inverse * norm_gain + norm_shift

def group_forward(params, stream, seg_group, index_group):
    w_qkv, qv_bias, w_out, w_fc1, fc1_bias, w_fc2, rel_table, ln_gain, ln_bias, layer_scale, row_bias = params
    highest = lax.Precision.HIGHEST
    bin_total = GROUP // BIN
    seg_bins = seg_group.reshape(bin_total, BIN)
    same_image = seg_bins[:, :, None] == seg_bins[:, None, :]
    index_flat = index_group.reshape(GROUP * BIN)
    blocked = (bin_total, BIN, HEADS, HEAD_DIM)
    for layer_at in range(LAYERS):
        normed = low(layer_norm(stream, ln_gain[layer_at, 0], ln_bias[layer_at, 0]))
        mixed_proj = jnp.dot(normed, w_qkv[layer_at].reshape(D, 3 * D), precision=highest).reshape(GROUP, 3, D)
        queries = narrow_both(mixed_proj[:, 0] + qv_bias[layer_at, 0]).reshape(blocked)
        key_rows = narrow_both(mixed_proj[:, 1]).reshape(blocked)
        values = narrow_both(mixed_proj[:, 2] + qv_bias[layer_at, 1]).reshape(blocked)
        position_bias = jnp.take(rel_table[layer_at], index_flat, axis=0).reshape(bin_total, BIN, BIN, HEADS)
        position_bias = jnp.transpose(position_bias, (0, 3, 1, 2))
        scores = jnp.einsum('bqhd,bkhd->bhqk', queries, key_rows, precision=highest) * HEAD_DIM ** (-0.5) + position_bias
        scores = jnp.where(same_image[:, None], low_back(scores), -1000000000.0)
        highest_score = lax.optimization_barrier(jnp.max(scores, -1, keepdims=True))
        powers = jnp.exp(scores - highest_score)
        weights = low(powers / lax.optimization_barrier(jnp.sum(powers, -1, keepdims=True)))
        mixture = jnp.einsum('bhqk,bkhd->bqhd', weights, values, precision=highest).reshape(GROUP, D)
        mixture = narrow_both(mixture)
        branch = low_back(jnp.dot(mixture, w_out[layer_at], precision=highest)) + row_bias[layer_at, 0]
        stream = stream + layer_scale[layer_at, 0] * branch
        normed = low(layer_norm(stream, ln_gain[layer_at, 1], ln_bias[layer_at, 1]))
        hidden = low_back(jnp.dot(normed, w_fc1[layer_at], precision=highest) + fc1_bias[layer_at])
        active = low(jax.nn.gelu(hidden, approximate=False))
        branch = low_back(jnp.dot(active, w_fc2[layer_at], precision=highest)) + row_bias[layer_at, 1]
        stream = stream + layer_scale[layer_at, 1] * branch
    return stream

def reference(tokens, cotangent, segments, lengths, rel_index, w_qkv, qv_bias, w_out, w_fc1, fc1_bias, w_fc2, rel_table, ln_gain, ln_bias, layer_scale, row_bias):
    params = tuple((member.astype(jnp.float32) for member in (w_qkv, qv_bias, w_out, w_fc1, fc1_bias, w_fc2, rel_table, ln_gain, ln_bias, layer_scale, row_bias)))
    inside = jnp.arange(TOKENS) % BIN < jnp.repeat(lax.optimization_barrier(jnp.sum(lengths, 1)), BIN)
    valid = inside[:, None]
    seg_groups = segments.reshape(N_DP, GROUP)
    index_groups = rel_index.reshape(N_DP, GROUP, BIN)
    stepper = jax.checkpoint(group_forward)

    def forward(params_in, begin):

        def one_group(carried, element):
            return (carried, stepper(params_in, element[0], element[1], element[2]))
        unused_carry, outcome = lax.scan(one_group, None, (begin.reshape(N_DP, GROUP, D), seg_groups, index_groups))
        return jnp.where(valid, outcome.reshape(TOKENS, D), 0.0)
    begin = tokens.astype(jnp.float32)
    outcome, pullback = jax.vjp(forward, params, begin)
    grads, grad_begin = pullback(cotangent.astype(jnp.float32))
    return (outcome.astype(jnp.bfloat16), grad_begin, grads[0], grads[1], grads[2], grads[3], grads[4], grads[5], grads[6], grads[7], grads[8], grads[9], grads[10])
```

```python
import math

import jax
import jax.numpy as jnp
from jax import lax
from jax.sharding import PartitionSpec as P

HEAD_DIM = 64


def norm_rows(stream, norm_gain, norm_shift):
    center = stream - jnp.mean(stream, -1, keepdims=True)
    inverse = lax.rsqrt(jnp.mean(center * center, -1, keepdims=True) + 1e-06)
    normal = center * inverse
    return (normal * norm_gain + norm_shift, normal, inverse)


def norm_back(gradient, normal, inverse, norm_gain):
    scaled = gradient * norm_gain
    centered = (
        scaled
        - jnp.mean(scaled, -1, keepdims=True)
        - normal * jnp.mean(scaled * normal, -1, keepdims=True)
    )
    return (inverse * centered, jnp.sum(gradient * normal, 0), jnp.sum(gradient, 0))


def gelu_slope(values):
    return (
        0.5 * (1.0 + lax.erf(values * 0.7071067811865476))
        + values * jnp.exp(-0.5 * values * values) * 0.3989422804014327
    )


def contract_rows(left_side, right_side):
    return lax.dot_general(
        left_side, right_side, (((0,), (0,)), ((), ())), preferred_element_type=jnp.float32
    )


def times_transposed(left_side, right_side):
    return lax.dot_general(
        left_side, right_side, (((1,), (1,)), ((), ())), preferred_element_type=jnp.float32
    )


SIDE = 14
STRIDE = 2 * SIDE - 1
CELLS = SIDE * SIDE


def place_rows(index_rows, lengths, bin_rows):
    bin_total = lengths.shape[0]
    index_bins = index_rows.reshape(bin_total, bin_rows, bin_rows)
    first, both = lengths[:, 0:1], lengths[:, 0:1] + lengths[:, 1:2]
    code_first = index_bins[:, 1]
    code_second = jax.vmap(lambda rows, at: lax.dynamic_index_in_dim(rows, at, 0, False))(
        index_bins, lengths[:, 0] + 1
    )
    at = jnp.arange(bin_rows)[None]
    code = (SIDE - 1) * (STRIDE + 1) - jnp.where(at < first, code_first, code_second)
    cell = (code // STRIDE) * SIDE + code % STRIDE
    cell = jnp.where((at == 0) | (at == first), CELLS, cell)
    cell = jnp.where(at < both, cell, bin_rows - 1)
    return (cell[:, :, None] == jnp.arange(bin_rows)[None, None]).astype(jnp.bfloat16)


def grid_table(table_used, bin_rows):
    layer_count, entries, head_count = table_used.shape
    columns = jnp.transpose(table_used, (0, 2, 1)).reshape(layer_count * head_count, entries)
    turned = columns[:, STRIDE * STRIDE - 1 :: -1].reshape(-1, STRIDE, STRIDE)
    by_col = jnp.stack([turned[:, :, SIDE - 1 - c : STRIDE - c] for c in range(SIDE)], 1)
    by_row = jnp.stack([by_col[:, :, SIDE - 1 - r : STRIDE - r] for r in range(SIDE)], 1)
    grid = by_row.reshape(-1, CELLS, CELLS)
    grid = jnp.pad(grid, ((0, 0), (0, bin_rows - CELLS), (0, bin_rows - CELLS)))
    row = lax.broadcasted_iota(jnp.int32, (1, bin_rows, bin_rows), 1)
    col = lax.broadcasted_iota(jnp.int32, (1, bin_rows, bin_rows), 2)
    last = columns[:, STRIDE * STRIDE :, None, None]
    grid = jnp.where((row == CELLS) & (col < CELLS), last[:, 0], grid)
    grid = jnp.where((col == CELLS) & (row < CELLS), last[:, 1], grid)
    grid = jnp.where((row == CELLS) & (col == CELLS), last[:, 2], grid)
    return grid.reshape(layer_count, head_count, bin_rows, bin_rows)


def look_up(spots, grid):
    half = jnp.einsum("bip,lhpq->lbhiq", spots, grid)
    return jnp.einsum("lbhiq,bjq->lbhij", half, spots)


def skew(values):
    flipped = values[..., ::-1, :]
    padded = jnp.pad(flipped, [(0, 0)] * (values.ndim - 1) + [(0, SIDE)])
    flat = padded.reshape(padded.shape[:-2] + (SIDE * 2 * SIDE,))[..., : SIDE * STRIDE]
    return jnp.sum(flat.reshape(padded.shape[:-2] + (SIDE, STRIDE)), -2)


def table_grad(spots, score_grads, entries):
    half = jnp.einsum("bip,lbhij->lbhpj", spots, score_grads)
    total = jnp.einsum("lbhpj,bjq->lhpq", half, spots, preferred_element_type=jnp.float32)
    layer_count, head_count = total.shape[:2]
    cells = total[:, :, :CELLS, :CELLS].reshape(-1, SIDE, SIDE, SIDE, SIDE)
    by_col = skew(jnp.transpose(cells, (0, 1, 3, 2, 4)))
    by_both = skew(jnp.transpose(by_col, (0, 3, 1, 2)))
    offsets = jnp.transpose(by_both, (0, 2, 1)).reshape(-1, STRIDE * STRIDE)[:, ::-1]
    offsets = offsets.reshape(layer_count, head_count, -1)
    tail = jnp.stack(
        [
            jnp.sum(total[:, :, CELLS, :CELLS], -1),
            jnp.sum(total[:, :, :CELLS, CELLS], -1),
            total[:, :, CELLS, CELLS],
        ],
        -1,
    )
    return jnp.transpose(jnp.concatenate([offsets, tail], -1), (0, 2, 1))


def attend_scores(queries, key_rows, position_bias, same_image, head_count, score_scale):
    local_width = queries.shape[1]
    blocked = (same_image.shape[0], same_image.shape[1], head_count, local_width // head_count)
    products = jnp.einsum(
        "bqhd,bkhd->bhqk",
        queries.reshape(blocked),
        key_rows.reshape(blocked),
        preferred_element_type=jnp.float32,
    )
    return jnp.where(
        same_image[:, None],
        products * score_scale + position_bias.astype(jnp.float32),
        -1000000000.0,
    )


def attend(queries, key_rows, values, position_bias, same_image, head_count, score_scale):
    scores = attend_scores(queries, key_rows, position_bias, same_image, head_count, score_scale)
    highest = jnp.max(scores, -1, keepdims=True)
    powers = jnp.exp(scores - highest)
    totals = jnp.sum(powers, -1, keepdims=True)
    weights = (powers / totals).astype(jnp.bfloat16)
    local_width = queries.shape[1]
    blocked = (same_image.shape[0], same_image.shape[1], head_count, local_width // head_count)
    mixture = jnp.einsum(
        "bhqk,bkhd->bqhd", weights, values.reshape(blocked), preferred_element_type=jnp.float32
    )
    return (mixture.reshape(queries.shape).astype(jnp.bfloat16), highest + jnp.log(totals))


def attend_back(
    queries,
    key_rows,
    values,
    position_bias,
    same_image,
    log_totals,
    grad_mix,
    head_count,
    score_scale,
):
    scores = attend_scores(queries, key_rows, position_bias, same_image, head_count, score_scale)
    weights = jnp.exp(scores - log_totals)
    local_width = queries.shape[1]
    blocked = (same_image.shape[0], same_image.shape[1], head_count, local_width // head_count)
    grad_blocked = grad_mix.reshape(blocked)
    grad_weights = jnp.einsum(
        "bqhd,bkhd->bhqk", grad_blocked, values.reshape(blocked), preferred_element_type=jnp.float32
    )
    grad_values = jnp.einsum(
        "bhqk,bqhd->bkhd",
        weights.astype(jnp.bfloat16),
        grad_blocked,
        preferred_element_type=jnp.float32,
    )
    centered = jnp.sum(weights * grad_weights, -1, keepdims=True)
    grad_scores = (weights * (grad_weights - centered)).astype(jnp.bfloat16)
    grad_query = (
        jnp.einsum(
            "bhqk,bkhd->bqhd",
            grad_scores,
            key_rows.reshape(blocked),
            preferred_element_type=jnp.float32,
        )
        * score_scale
    )
    grad_key = (
        jnp.einsum(
            "bhqk,bqhd->bkhd",
            grad_scores,
            queries.reshape(blocked),
            preferred_element_type=jnp.float32,
        )
        * score_scale
    )
    flat_shape = queries.shape
    return (
        grad_query.reshape(flat_shape).astype(jnp.bfloat16),
        grad_key.reshape(flat_shape).astype(jnp.bfloat16),
        grad_values.reshape(flat_shape).astype(jnp.bfloat16),
        grad_scores,
    )


def per_device(
    tokens,
    cotangent,
    segments,
    lengths,
    rel_index,
    w_qkv,
    qv_bias,
    w_out,
    w_fc1,
    fc1_bias,
    w_fc2,
    rel_table,
    ln_gain,
    ln_bias,
    layer_scale,
    row_bias,
):
    own_rows, width = tokens.shape
    group_rows, bin_rows = rel_index.shape
    layer_count = w_qkv.shape[0]
    entries = rel_table.shape[1]
    place = lax.axis_index("tensor")
    score_scale = float(HEAD_DIM) ** (-0.5)
    totals = jnp.sum(lengths, 1)
    inside = jnp.arange(group_rows) % bin_rows < jnp.repeat(totals, bin_rows)
    valid = lax.dynamic_slice_in_dim(inside, place * own_rows, own_rows)[:, None]
    proj_qkv, proj_bias, proj_out, proj_up, up_bias, proj_down, table_used = (
        w_qkv,
        qv_bias,
        w_out,
        w_fc1,
        fc1_bias,
        w_fc2,
        rel_table,
    )
    head_count = table_used.shape[2]
    local_width = proj_qkv.shape[3]
    bin_total = rel_index.shape[0] // bin_rows
    seg_bins = segments.reshape(bin_total, bin_rows)
    same_image = seg_bins[:, :, None] == seg_bins[:, None, :]
    spots = place_rows(rel_index, lengths, bin_rows)
    position_bias = look_up(spots, grid_table(table_used, bin_rows))

    def spread_rows(values):
        return lax.all_gather(values, "tensor", axis=0, tiled=True)

    def spread_grads(values):
        return lax.all_gather(values, "tensor", axis=0, tiled=True)

    def project_rows(left_side, right_side):
        return lax.psum_scatter(
            jnp.dot(left_side, right_side, preferred_element_type=jnp.float32).astype(jnp.bfloat16),
            "tensor",
            scatter_dimension=0,
            tiled=True,
        ).astype(jnp.float32)

    def project_grads(left_side, right_side):
        return lax.psum_scatter(
            times_transposed(left_side, right_side).astype(jnp.bfloat16),
            "tensor",
            scatter_dimension=0,
            tiled=True,
        ).astype(jnp.float32)

    stream = tokens.astype(jnp.float32)
    kept_state = []
    for layer_at in range(layer_count):
        layer_qkv = proj_qkv[layer_at].reshape(width, 3 * local_width)
        normed, normal_a, inverse_a = norm_rows(stream, ln_gain[layer_at, 0], ln_bias[layer_at, 0])
        spread_a = spread_rows(normed.astype(jnp.bfloat16))
        mixed_proj = jnp.dot(spread_a, layer_qkv, preferred_element_type=jnp.float32).reshape(
            -1, 3, local_width
        )
        biases = proj_bias[layer_at].astype(jnp.float32)
        queries = (mixed_proj[:, 0] + biases[0]).astype(jnp.bfloat16)
        key_rows = mixed_proj[:, 1].astype(jnp.bfloat16)
        values = (mixed_proj[:, 2] + biases[1]).astype(jnp.bfloat16)
        mixture, log_totals = attend(
            queries, key_rows, values, position_bias[layer_at], same_image, head_count, score_scale
        )
        branch_a = project_rows(mixture, proj_out[layer_at]) + row_bias[layer_at, 0]
        middle = stream + layer_scale[layer_at, 0] * branch_a
        normed_b, normal_b, inverse_b = norm_rows(
            middle, ln_gain[layer_at, 1], ln_bias[layer_at, 1]
        )
        spread_b = spread_rows(normed_b.astype(jnp.bfloat16))
        hidden = jnp.dot(spread_b, proj_up[layer_at], preferred_element_type=jnp.float32) + up_bias[
            layer_at
        ].astype(jnp.float32)
        active = jax.nn.gelu(hidden, approximate=False).astype(jnp.bfloat16)
        branch_b = project_rows(active, proj_down[layer_at]) + row_bias[layer_at, 1]
        kept_state.append(
            (
                normal_a,
                inverse_a,
                spread_a,
                queries,
                key_rows,
                values,
                mixture,
                log_totals,
                branch_a,
                normal_b,
                inverse_b,
                spread_b,
                hidden,
                active,
                branch_b,
            )
        )
        stream = middle + layer_scale[layer_at, 1] * branch_b
    result = jnp.where(valid, stream, 0.0).astype(jnp.bfloat16)
    gradient = jnp.where(valid, cotangent.astype(jnp.float32), 0.0)
    list_qkv = [None] * layer_count
    list_qvb = [None] * layer_count
    list_out = [None] * layer_count
    list_up = [None] * layer_count
    list_upb = [None] * layer_count
    list_down = [None] * layer_count
    list_scores = [None] * layer_count
    list_gain = [None] * layer_count
    list_shift = [None] * layer_count
    list_scale = [None] * layer_count
    list_rowb = [None] * layer_count
    for layer_at in reversed(range(layer_count)):
        (
            normal_a,
            inverse_a,
            spread_a,
            queries,
            key_rows,
            values,
            mixture,
            log_totals,
            branch_a,
            normal_b,
            inverse_b,
            spread_b,
            hidden,
            active,
            branch_b,
        ) = kept_state[layer_at]
        scale_b = jnp.sum(gradient * branch_b, 0)
        rowb_b = layer_scale[layer_at, 1] * jnp.sum(gradient, 0)
        spread_down = spread_grads((gradient * layer_scale[layer_at, 1]).astype(jnp.bfloat16))
        list_down[layer_at] = contract_rows(active, spread_down)
        grad_active = times_transposed(spread_down, proj_down[layer_at])
        grad_hidden = (grad_active * gelu_slope(hidden)).astype(jnp.bfloat16)
        list_upb[layer_at] = jnp.sum(grad_hidden.astype(jnp.float32), 0)
        list_up[layer_at] = contract_rows(spread_b, grad_hidden)
        back_b, gain_b, shift_b = norm_back(
            project_grads(grad_hidden, proj_up[layer_at]), normal_b, inverse_b, ln_gain[layer_at, 1]
        )
        gradient = gradient + back_b
        scale_a = jnp.sum(gradient * branch_a, 0)
        rowb_a = layer_scale[layer_at, 0] * jnp.sum(gradient, 0)
        spread_attn = spread_grads((gradient * layer_scale[layer_at, 0]).astype(jnp.bfloat16))
        list_out[layer_at] = contract_rows(mixture, spread_attn)
        grad_mix = times_transposed(spread_attn, proj_out[layer_at]).astype(jnp.bfloat16)
        grad_query, grad_key, grad_value, grad_scores = attend_back(
            queries,
            key_rows,
            values,
            position_bias[layer_at],
            same_image,
            log_totals,
            grad_mix,
            head_count,
            score_scale,
        )
        list_scores[layer_at] = grad_scores
        list_qvb[layer_at] = jnp.stack(
            [jnp.sum(grad_query.astype(jnp.float32), 0), jnp.sum(grad_value.astype(jnp.float32), 0)]
        )
        grad_proj = jnp.stack([grad_query, grad_key, grad_value], 1).reshape(-1, 3 * local_width)
        list_qkv[layer_at] = contract_rows(spread_a, grad_proj).reshape(width, 3, local_width)
        back_a, gain_a, shift_a = norm_back(
            project_grads(grad_proj, proj_qkv[layer_at].reshape(width, 3 * local_width)),
            normal_a,
            inverse_a,
            ln_gain[layer_at, 0],
        )
        gradient = gradient + back_a
        list_gain[layer_at] = jnp.stack([gain_a, gain_b])
        list_shift[layer_at] = jnp.stack([shift_a, shift_b])
        list_scale[layer_at] = jnp.stack([scale_a, scale_b])
        list_rowb[layer_at] = jnp.stack([rowb_a, rowb_b])
    qkv_all = jnp.stack(list_qkv)
    qvb_all = jnp.stack(list_qvb)
    out_all = jnp.stack(list_out)
    up_all = jnp.stack(list_up)
    upb_all = jnp.stack(list_upb)
    down_all = jnp.stack(list_down)
    table_all = table_grad(spots, jnp.stack(list_scores), entries)
    qvb_all, upb_all, table_all = lax.psum((qvb_all, upb_all, table_all), "dp")
    qkv_all, out_all, up_all, down_all = [
        total.astype(jnp.float32)
        for total in lax.psum(
            tuple(part.astype(jnp.bfloat16) for part in (qkv_all, out_all, up_all, down_all)), "dp"
        )
    ]
    gain_all, shift_all, scale_all, rowb_all = lax.psum(
        (jnp.stack(list_gain), jnp.stack(list_shift), jnp.stack(list_scale), jnp.stack(list_rowb)),
        ("dp", "tensor"),
    )
    return (
        result,
        gradient,
        qkv_all,
        qvb_all,
        out_all,
        up_all,
        upb_all,
        down_all,
        table_all,
        gain_all,
        shift_all,
        scale_all,
        rowb_all,
    )


def solution(mesh):
    in_specs = (
        P(("dp", "tensor"), None),
        P(("dp", "tensor"), None),
        P("dp"),
        P("dp", None),
        P("dp", None),
        P(None, None, None, "tensor"),
        P(None, None, "tensor"),
        P(None, "tensor", None),
        P(None, None, "tensor"),
        P(None, "tensor"),
        P(None, "tensor", None),
        P(None, None, "tensor"),
        P(),
        P(),
        P(),
        P(),
    )
    out_specs = (
        P(("dp", "tensor"), None),
        P(("dp", "tensor"), None),
        P(None, None, None, "tensor"),
        P(None, None, "tensor"),
        P(None, "tensor", None),
        P(None, None, "tensor"),
        P(None, "tensor"),
        P(None, "tensor", None),
        P(None, None, "tensor"),
        P(),
        P(),
        P(),
        P(),
    )
    return jax.shard_map(
        per_device, mesh=mesh, in_specs=in_specs, out_specs=out_specs, check_vma=False
    )
```

```python
import functools

import jax
import jax.numpy as jnp
from jax import lax
from jax.experimental import pallas as pl
from jax.experimental.pallas import tpu as pltpu
from jax.sharding import PartitionSpec as P

HEAD_DIM = 64
SIDE = 14
STRIDE = 2 * SIDE - 1
CELLS = SIDE * SIDE
PARTS = 2
CHUNK = 32
MESH = pl.DeviceIdType.MESH
BF16 = jnp.bfloat16
F32 = jnp.float32


def dot(left_side, right_side, left_axis=1, right_axis=0):
    return lax.dot_general(
        left_side,
        right_side,
        (((left_axis,), (right_axis,)), ((), ())),
        preferred_element_type=F32,
    )


class Group:
    def __init__(self, send_sems, recv_sems):
        own = lax.axis_index("tensor")
        self.near = own + 1 - 2 * (own % 2)
        self.far = (own + 2) % 4
        self.sems = (send_sems, recv_sems)

    def meet(self):
        barrier = pltpu.get_barrier_semaphore()
        for other in (self.near, self.far):
            pl.semaphore_signal(
                barrier, inc=1, device_id={"tensor": other}, device_id_type=MESH
            )
        pl.semaphore_wait(barrier, 2)

    def copy(self, at, source, target, other):
        return pltpu.make_async_remote_copy(
            src_ref=source,
            dst_ref=target,
            send_sem=self.sems[0].at[at],
            recv_sem=self.sems[1].at[at],
            device_id={"tensor": other},
            device_id_type=MESH,
        )


class Exchange:
    COPIES = 2 + 4 * PARTS

    def __init__(self, group, base, gath, part, got, summed):
        rows = gath.shape[1] // PARTS
        near, far = group.near, group.far
        self.rows = rows

        def piece(ref, slot, at):
            return ref.at[slot, pl.ds(at * rows, rows)]

        self.to_near = group.copy(base, gath.at[0], gath.at[1], near)
        self.to_far = [
            group.copy(base + 2 + at, piece(gath, 0, at), piece(gath, 2, at), far)
            for at in range(PARTS)
        ]
        self.relay = [
            group.copy(base + 2 + PARTS + at, piece(gath, 2, at), piece(gath, 3, at), near)
            for at in range(PARTS)
        ]
        self.sum_near = group.copy(base + 1, part.at[1], got.at[0], near)
        self.sum_pair = [
            group.copy(base + 2 + 2 * PARTS + at, piece(part, 3, at), piece(got, 1, at), near)
            for at in range(PARTS)
        ]
        self.sum_far = [
            group.copy(
                base + 2 + 3 * PARTS + at,
                summed.at[pl.ds(at * rows, rows)],
                piece(got, 2, at),
                far,
            )
            for at in range(PARTS)
        ]
        self.part, self.got, self.summed = part, got, summed

    def start(self):
        self.to_near.start()
        for step in self.to_far:
            step.start()

    def pass_on(self, at):
        self.to_far[at].wait_recv()
        self.relay[at].start()

    def send_sum(self, at):
        self.sum_pair[at].wait_recv()
        rows = self.rows
        span = pl.ds(at * rows, rows)
        self.summed[span] = (
            self.part[2, span].astype(F32) + self.got[1, span].astype(F32)
        ).astype(BF16)
        self.sum_far[at].start()

    def finish(self):
        self.sum_near.wait_recv()
        for step in self.sum_far:
            step.wait_recv()

    def drain(self):
        self.to_near.wait_send()
        self.sum_near.wait_send()
        for steps in (self.to_far, self.relay, self.sum_pair, self.sum_far):
            for step in steps:
                step.wait_send()


def by_chunk(total_rows, body, size=CHUNK):
    def step(at, carry):
        return body(pl.ds(pl.multiple_of(at * size, size), size), carry)

    return step, total_rows // size


def norm_chunk(values, gain, shift):
    center = values - jnp.mean(values, -1, keepdims=True)
    inverse = lax.rsqrt(jnp.mean(center * center, -1, keepdims=True) + 1e-06)
    normal = center * inverse
    return (normal * gain + shift).astype(BF16), normal, inverse


def gelu_parts(values):
    share = 0.5 * (1.0 + lax.erf(values * 0.7071067811865476))
    slope = share + values * (jnp.exp(-0.5 * values * values) * 0.3989422804014327)
    return values * share, slope


def attend_rows(qkv, weights_kept, mixture, bias, at, slot, first, head_count):
    rows = qkv.shape[2] // PARTS
    wide = qkv.shape[3] // 3
    span = pl.ds(first, rows)
    heads = []
    for head in range(head_count):
        lanes = slice(head * HEAD_DIM, (head + 1) * HEAD_DIM)
        queries = qkv[at, slot, span, 0:wide][:, lanes]
        keys = qkv[at, slot, :, wide : 2 * wide][:, lanes]
        values = qkv[at, slot, :, 2 * wide : 3 * wide][:, lanes]
        scores = dot(queries, keys, 1, 1) + bias[at, slot, head, span].astype(F32)
        powers = jnp.exp(scores - jnp.max(scores, -1, keepdims=True))
        weights = (powers / jnp.sum(powers, -1, keepdims=True)).astype(BF16)
        weights_kept[at, slot, head, span] = weights
        heads.append(dot(weights, values).astype(BF16))
    heads.append(jnp.zeros((rows, wide - head_count * HEAD_DIM), BF16))
    mixture[at, slot, span] = jnp.concatenate(heads, -1)


def forward_body(
    layer_count,
    head_count,
    tokens,
    w_qkv,
    qkv_bias,
    w_out,
    w_up,
    up_bias,
    w_down,
    bias,
    ln_gain,
    ln_bias,
    layer_scale,
    row_bias,
    gath_a_out,
    qkv_out,
    weights_out,
    mixture_out,
    gath_b_out,
    slope_out,
    active_out,
    normal_a,
    normal_b,
    inverse,
    branch_a,
    branch_b,
    stream,
    gath_a,
    qkv,
    weights_kept,
    mixture,
    gath_b,
    slope,
    active,
    hidden,
    part,
    got,
    summed,
    own,
    send_sems,
    recv_sems,
    out_sems,
):
    rows, width = stream.shape
    half = rows // PARTS
    group = Group(send_sems, recv_sems)
    group.meet()

    def each_chunk(body):
        step, count = by_chunk(rows, lambda span, carry: (body(span), carry)[1])
        lax.fori_loop(0, count, step, 0)

    def load(span):
        stream[span] = tokens[span].astype(F32)

    each_chunk(load)

    kept = (
        (gath_a, gath_a_out),
        (qkv, qkv_out),
        (weights_kept, weights_out),
        (mixture, mixture_out),
        (gath_b, gath_b_out),
        (slope, slope_out),
        (active, active_out),
    )

    def keep(number, at):
        source, target = kept[number]
        return pltpu.make_async_copy(source.at[at], target.at[at], out_sems.at[number, at])

    def layer(at, carry):
        trade = Exchange(group, 0, gath_a.at[at], part, got, summed)

        def enter(span):
            low, normal, inv = norm_chunk(
                stream[span], ln_gain[at, 0:1], ln_bias[at, 0:1]
            )
            gath_a[at, 0, span] = low
            normal_a[at, span] = normal
            inverse[at, 0, span] = jnp.broadcast_to(inv, (CHUNK, 128))

        each_chunk(enter)
        trade.start()
        scale = jnp.concatenate(
            [
                jnp.full((1, width // 3), HEAD_DIM**-0.5, F32),
                jnp.full((1, 2 * width // 3), 1.0, F32),
            ],
            -1,
        )

        def project(slot, first, count):
            span = pl.ds(first, count)
            mixed = dot(gath_a[at, slot, span], w_qkv[at])
            mixed = (mixed + qkv_bias[at]).astype(BF16).astype(F32) * scale
            qkv[at, slot, span] = mixed.astype(BF16)

        def attend(slot, first):
            attend_rows(qkv, weights_kept, mixture, bias, at, slot, first, head_count)

        def leave(slot, first):
            return dot(mixture[at, slot, pl.ds(first, half)], w_out[at])

        def whole(slot):
            project(slot, 0, rows)

            def one(place, carry):
                first = pl.multiple_of(place * half, half)
                attend(slot, first)
                result = leave(slot, first)
                if slot == 0:
                    own[pl.ds(first, half)] = result
                else:
                    part[slot, pl.ds(first, half)] = result.astype(BF16)
                return carry

            lax.fori_loop(0, PARTS, one, 0)

        whole(0)
        trade.to_near.wait_recv()
        whole(1)
        trade.sum_near.start()
        for place in range(PARTS):
            trade.pass_on(place)
            project(2, place * half, half)
        for place in range(PARTS):
            trade.relay[place].wait_recv()
            project(3, place * half, half)
        keep(0, at).start()
        keep(1, at).start()
        for place in range(PARTS):
            first = place * half
            attend(3, first)
            part[3, pl.ds(first, half)] = leave(3, first).astype(BF16)
            trade.sum_pair[place].start()
            attend(2, first)
            part[2, pl.ds(first, half)] = leave(2, first).astype(BF16)
            trade.send_sum(place)
        keep(2, at).start()
        keep(3, at).start()
        trade.finish()

        trade_b = Exchange(group, Exchange.COPIES, gath_b.at[at], part, got, summed)

        def between(span):
            total = own[span] + got[0, span].astype(F32) + got[2, span].astype(F32)
            branch = total + row_bias[at, 0:1]
            branch_a[at, span] = branch
            middle = stream[span] + layer_scale[at, 0:1] * branch
            stream[span] = middle
            low, normal, inv = norm_chunk(middle, ln_gain[at, 1:2], ln_bias[at, 1:2])
            gath_b[at, 0, span] = low
            normal_b[at, span] = normal
            inverse[at, 1, span] = jnp.broadcast_to(inv, (CHUNK, 128))

        each_chunk(between)
        trade.drain()

        trade_b.start()

        def raise_rows(values, count, put):
            hidden[pl.ds(0, count)] = dot(values, w_up[at]) + up_bias[at]

            def act(place, carry):
                span = pl.ds(pl.multiple_of(place * 16, 16), 16)
                high, incline = gelu_parts(hidden[span])
                put(place * 16, high.astype(BF16), incline.astype(BF16))
                return carry

            lax.fori_loop(0, count // 16, act, 0)

        def to_slot(slot, start):
            def put(first, high, incline):
                span = pl.ds(pl.multiple_of(start + first, 16), 16)
                active[at, slot, span] = high
                slope[at, slot, span] = incline

            return put

        raise_rows(gath_b[at, 0], rows, to_slot(0, 0))
        own[...] = dot(active[at, 0], w_down[at])
        trade_b.to_near.wait_recv()
        raise_rows(gath_b[at, 1], rows, to_slot(1, 0))
        part[1] = dot(active[at, 1], w_down[at]).astype(BF16)
        trade_b.sum_near.start()
        for place in range(PARTS):
            trade_b.pass_on(place)
            span = pl.ds(place * half, half)
            raise_rows(gath_b[at, 2, span], half, to_slot(2, place * half))
            trade_b.relay[place].wait_recv()
            raise_rows(gath_b[at, 3, span], half, to_slot(3, place * half))
            part[3, span] = dot(active[at, 3, span], w_down[at]).astype(BF16)
            trade_b.sum_pair[place].start()
            part[2, span] = dot(active[at, 2, span], w_down[at]).astype(BF16)
            trade_b.send_sum(place)
        for number in (4, 5, 6):
            keep(number, at).start()
        trade_b.finish()

        def after(span):
            total = own[span] + got[0, span].astype(F32) + got[2, span].astype(F32)
            branch = total + row_bias[at, 1:2]
            branch_b[at, span] = branch
            stream[span] = stream[span] + layer_scale[at, 1:2] * branch

        each_chunk(after)
        trade_b.drain()
        return carry

    lax.fori_loop(0, layer_count, layer, 0)
    for at in range(layer_count):
        for number in range(len(kept)):
            keep(number, at).wait()


def run_forward(tokens, weights, bias, norms, head_count):
    rows, width = tokens.shape
    w_qkv, qkv_bias, w_out, w_up, up_bias, w_down = weights
    layers = w_qkv.shape[0]
    wide = w_qkv.shape[2] // 3
    inner = w_up.shape[2]
    in_vmem = pl.BlockSpec(memory_space=pltpu.VMEM)
    in_hbm = pl.BlockSpec(memory_space=pl.ANY)
    kept = [
        jax.ShapeDtypeStruct((layers, 4) + tail, BF16)
        for tail in (
            (rows, width),
            (rows, 3 * wide),
            (head_count, rows, rows),
            (rows, wide),
            (rows, width),
            (rows, inner),
            (rows, inner),
        )
    ]
    near = [
        jax.ShapeDtypeStruct(shape, F32)
        for shape in (
            (layers, rows, width),
            (layers, rows, width),
            (layers, 2, rows, 128),
            (layers, rows, width),
            (layers, rows, width),
            (rows, width),
        )
    ]
    return pl.pallas_call(
        functools.partial(forward_body, layers, head_count),
        name="forward",
        out_shape=kept + near,
        in_specs=[in_vmem] * 12,
        out_specs=[in_hbm] * len(kept) + [in_vmem] * len(near),
        scratch_shapes=[pltpu.VMEM(leaf.shape, leaf.dtype) for leaf in kept]
        + [
            pltpu.VMEM((rows, inner), F32),
            pltpu.VMEM((4, rows, width), BF16),
            pltpu.VMEM((3, rows, width), BF16),
            pltpu.VMEM((rows, width), BF16),
            pltpu.VMEM((rows, width), F32),
            pltpu.SemaphoreType.DMA((2 * Exchange.COPIES,)),
            pltpu.SemaphoreType.DMA((2 * Exchange.COPIES,)),
            pltpu.SemaphoreType.DMA((len(kept), layers)),
        ],
        compiler_params=pltpu.CompilerParams(
            collective_id=0, has_side_effects=True, vmem_limit_bytes=64 * 1024 * 1000
        ),
    )(tokens, w_qkv, qkv_bias, w_out, w_up, up_bias, w_down, bias, *norms)


def fold(values):
    return jnp.sum(values.reshape(-1, 8, values.shape[-1]), 0)


def enter_back(grad, branch, scale, gath, sums):
    rows, width = grad.shape

    def body(span, carry):
        values = grad[span]
        gath[0, span] = (values * scale).astype(BF16)
        return carry[0] + fold(values * branch[span]), carry[1] + fold(values)

    step, count = by_chunk(rows, body)
    zero = jnp.zeros((8, width), F32)
    by_branch, alone = lax.fori_loop(0, count, step, (zero, zero))
    sums[2:3] = jnp.sum(by_branch, 0, keepdims=True)
    sums[3:4] = jnp.sum(alone, 0, keepdims=True) * scale


def leave_back(grad, own, got, normal, inverse, gain, grad_out, sums):
    rows, width = grad.shape

    def body(span, carry):
        total = own[span] + got[0, span].astype(F32) + got[2, span].astype(F32)
        unit = normal[span]
        scaled = total * gain
        centered = (
            scaled
            - jnp.mean(scaled, -1, keepdims=True)
            - unit * jnp.mean(scaled * unit, -1, keepdims=True)
        )
        grad_out[span] = grad[span] + inverse[span, 0:1] * centered
        return carry[0] + fold(total * unit), carry[1] + fold(total)

    step, count = by_chunk(rows, body)
    zero = jnp.zeros((8, width), F32)
    by_unit, alone = lax.fori_loop(0, count, step, (zero, zero))
    sums[0:1] = jnp.sum(by_unit, 0, keepdims=True)
    sums[1:2] = jnp.sum(alone, 0, keepdims=True)


def weight_grad(left, right, out):
    block = 256

    def step(place, carry):
        span = pl.ds(pl.multiple_of(place * block, block), block)
        total = None
        for slot in range(4):
            term = dot(left[slot, :, span], right[slot], 0, 0)
            total = term if total is None else total + term
        out[span] = total.astype(out.dtype)
        return carry

    lax.fori_loop(0, out.shape[0] // block, step, 0)


class Loads:
    def __init__(self, sems):
        self.sems = sems
        self.steps = []

    def add(self, source, target):
        step = pltpu.make_async_copy(source, target, self.sems.at[len(self.steps)])
        step.start()
        self.steps.append(step)
        return len(self.steps) - 1

    def ready(self, *numbers):
        for number in numbers:
            self.steps[number].wait()


def back_mlp_body(
    at,
    grad,
    branch_all,
    normal_all,
    inverse_all,
    active_all,
    slope_all,
    gath_b_all,
    w_up_all,
    w_down_all,
    ln_gain,
    layer_scale,
    grad_out,
    d_up,
    d_down,
    sums,
    d_up_bias,
    branch,
    normal,
    inverse,
    active,
    slope,
    gath_b,
    w_up,
    w_down,
    gath,
    d_hidden,
    hidden,
    part,
    got,
    summed,
    own,
    send_sems,
    recv_sems,
    load_sems,
):
    rows = grad.shape[0]
    half = rows // PARTS
    loads = Loads(load_sems)
    loads.add(branch_all.at[at], branch)
    loads.add(w_down_all.at[at], w_down)
    loads.add(slope_all.at[at], slope)
    loads.add(w_up_all.at[at], w_up)
    loads.add(normal_all.at[at], normal)
    loads.add(inverse_all.at[at, 1], inverse)
    loads.add(active_all.at[at], active)
    loads.add(gath_b_all.at[at], gath_b)
    group = Group(send_sems, recv_sems)
    group.meet()
    trade = Exchange(group, 0, gath, part, got, summed)
    loads.ready(0)
    enter_back(grad, branch, layer_scale[at, 1:2], gath, sums)
    trade.start()
    loads.ready(1, 2, 3)

    def down(slot, first, count, total):
        span = pl.ds(first, count)
        hidden[pl.ds(0, count)] = dot(gath[slot, span], w_down[...], 1, 1)

        def body(place, carry):
            inside = pl.ds(pl.multiple_of(place * CHUNK, CHUNK), CHUNK)
            there = pl.ds(pl.multiple_of(first + place * CHUNK, CHUNK), CHUNK)
            low = (hidden[inside] * slope[slot, there].astype(F32)).astype(BF16)
            d_hidden[slot, there] = low
            return carry + fold(low.astype(F32))

        return lax.fori_loop(0, count // CHUNK, body, total)

    def back(slot, first, count):
        return dot(d_hidden[slot, pl.ds(first, count)], w_up[...], 1, 1)

    total = jnp.zeros((8, d_up_bias.shape[1]), F32)
    total = down(0, 0, rows, total)
    own[...] = back(0, 0, rows)
    trade.to_near.wait_recv()
    total = down(1, 0, rows, total)
    part[1] = back(1, 0, rows).astype(BF16)
    trade.sum_near.start()
    for place in range(PARTS):
        trade.pass_on(place)
        first = place * half
        span = pl.ds(first, half)
        total = down(2, first, half, total)
        trade.relay[place].wait_recv()
        total = down(3, first, half, total)
        part[3, span] = back(3, first, half).astype(BF16)
        trade.sum_pair[place].start()
        part[2, span] = back(2, first, half).astype(BF16)
        trade.send_sum(place)
    d_up_bias[...] = jnp.sum(total, 0, keepdims=True)
    loads.ready(4, 5, 6, 7)
    weight_grad(active, gath, d_down)
    weight_grad(gath_b, d_hidden, d_up)
    trade.finish()
    leave_back(grad, own, got, normal, inverse, ln_gain[at, 1:2], grad_out, sums)
    trade.drain()


def run_back_mlp(at, grad, kept, weights, norms):
    rows, width = grad.shape
    branch, normal, inverse, active, slope, gath_b = kept
    w_up, w_down = weights
    inner = w_up.shape[2]
    in_vmem = pl.BlockSpec(memory_space=pltpu.VMEM)
    in_hbm = pl.BlockSpec(memory_space=pl.ANY)
    own_rows = pltpu.VMEM((rows, width), F32)
    four = pltpu.VMEM((4, rows, width), BF16)
    four_inner = pltpu.VMEM((4, rows, inner), BF16)
    return pl.pallas_call(
        functools.partial(back_mlp_body, at),
        name="back_mlp",
        out_shape=[
            jax.ShapeDtypeStruct((rows, width), F32),
            jax.ShapeDtypeStruct((width, inner), BF16),
            jax.ShapeDtypeStruct((inner, width), BF16),
            jax.ShapeDtypeStruct((8, width), F32),
            jax.ShapeDtypeStruct((1, inner), F32),
        ],
        in_specs=[in_vmem] + [in_hbm] * 8 + [in_vmem] * 2,
        out_specs=[in_vmem] * 5,
        scratch_shapes=[
            own_rows,
            own_rows,
            pltpu.VMEM((rows, 128), F32),
            four_inner,
            four_inner,
            four,
            pltpu.VMEM((width, inner), BF16),
            pltpu.VMEM((inner, width), BF16),
            four,
            four_inner,
            pltpu.VMEM((rows, inner), F32),
            four,
            pltpu.VMEM((3, rows, width), BF16),
            pltpu.VMEM((rows, width), BF16),
            own_rows,
            pltpu.SemaphoreType.DMA((Exchange.COPIES,)),
            pltpu.SemaphoreType.DMA((Exchange.COPIES,)),
            pltpu.SemaphoreType.DMA((8,)),
        ],
        compiler_params=pltpu.CompilerParams(
            collective_id=1 + 2 * at, has_side_effects=True, vmem_limit_bytes=48 * 1024 * 1000
        ),
    )(grad, branch, normal, inverse, active, slope, gath_b, w_up, w_down, norms[0], norms[2])


def back_attend_body(
    at,
    head_count,
    grad,
    branch_all,
    normal_all,
    inverse_all,
    mixture_all,
    qkv_all,
    weights_all,
    gath_a_all,
    w_out_all,
    w_qkv_all,
    spots,
    ln_gain,
    layer_scale,
    grad_out,
    d_qkv,
    d_out,
    sums,
    d_qkv_bias,
    d_grid,
    branch,
    normal,
    inverse,
    mixture,
    qkv,
    weights,
    gath_a,
    w_out,
    w_qkv,
    gath,
    d_mixed,
    d_scores,
    part,
    got,
    summed,
    own,
    send_sems,
    recv_sems,
    load_sems,
):
    rows = grad.shape[0]
    half = rows // PARTS
    wide = mixture.shape[2]
    loads = Loads(load_sems)
    loads.add(branch_all.at[at], branch)
    loads.add(w_out_all.at[at], w_out)
    loads.add(qkv_all.at[at], qkv)
    loads.add(weights_all.at[at], weights)
    loads.add(w_qkv_all.at[at], w_qkv)
    loads.add(normal_all.at[at], normal)
    loads.add(inverse_all.at[at, 0], inverse)
    loads.add(mixture_all.at[at], mixture)
    loads.add(gath_a_all.at[at], gath_a)
    group = Group(send_sems, recv_sems)
    group.meet()
    trade = Exchange(group, 0, gath, part, got, summed)
    loads.ready(0)
    enter_back(grad, branch, layer_scale[at, 0:1], gath, sums)
    trade.start()
    loads.ready(1, 2, 3, 4)
    spare = jnp.zeros((rows, wide - head_count * HEAD_DIM), BF16)

    def attend(slot):
        d_mix = dot(gath[slot], w_out[...], 1, 1).astype(BF16)
        pieces = ([], [], [])
        for head in range(head_count):
            lanes = slice(head * HEAD_DIM, (head + 1) * HEAD_DIM)
            queries = qkv[slot, :, 0:wide][:, lanes]
            keys = qkv[slot, :, wide : 2 * wide][:, lanes]
            values = qkv[slot, :, 2 * wide : 3 * wide][:, lanes]
            share = weights[slot, head]
            d_head = d_mix[:, lanes]
            wide_share = share.astype(F32)
            d_share = dot(d_head, values, 1, 1)
            middle = jnp.sum(wide_share * d_share, -1, keepdims=True)
            d_score = (wide_share * (d_share - middle)).astype(BF16)
            d_scores[slot, head] = d_score
            pieces[0].append((dot(d_score, keys) * HEAD_DIM**-0.5).astype(BF16))
            pieces[1].append(dot(d_score, queries, 0, 0).astype(BF16))
            pieces[2].append(dot(share, d_head, 0, 0).astype(BF16))
        for place in range(3):
            d_mixed[slot, :, place * wide : (place + 1) * wide] = jnp.concatenate(
                pieces[place] + [spare], -1
            )

    def back(slot, first, count):
        return dot(d_mixed[slot, pl.ds(first, count)], w_qkv[...], 1, 1)

    attend(0)
    own[...] = back(0, 0, rows)
    trade.to_near.wait_recv()
    attend(1)
    part[1] = back(1, 0, rows).astype(BF16)
    trade.sum_near.start()
    for place in range(PARTS):
        trade.pass_on(place)
    for place in range(PARTS):
        trade.relay[place].wait_recv()
    attend(3)
    part[3] = back(3, 0, rows).astype(BF16)
    for place in range(PARTS):
        trade.sum_pair[place].start()
    attend(2)
    for place in range(PARTS):
        first = place * half
        part[2, pl.ds(first, half)] = back(2, first, half).astype(BF16)
        trade.send_sum(place)
    loads.ready(5, 6, 7, 8)

    def add(slot, total):
        def body(span, carry):
            return carry + fold(d_mixed[slot, span].astype(F32))

        step, count = by_chunk(rows, body)
        return lax.fori_loop(0, count, step, total)

    total = jnp.zeros((8, 3 * wide), F32)
    for slot in range(4):
        total = add(slot, total)
    d_qkv_bias[...] = jnp.sum(total, 0, keepdims=True)
    weight_grad(gath_a, d_mixed, d_qkv)
    weight_grad(mixture, gath, d_out)
    for head in range(head_count):
        total = None
        for slot in range(4):
            placed = dot(spots[slot], d_scores[slot, head], 0, 0).astype(BF16)
            term = dot(placed, spots[slot])
            total = term if total is None else total + term
        d_grid[head] = total
    trade.finish()
    leave_back(grad, own, got, normal, inverse, ln_gain[at, 0:1], grad_out, sums)
    trade.drain()


def run_back_attend(at, grad, kept, weights, spots, norms):
    rows, width = grad.shape
    branch, normal, inverse, mixture, qkv, shares, gath_a = kept
    w_out, w_qkv = weights
    wide = w_out.shape[1]
    head_count = shares.shape[2]
    in_vmem = pl.BlockSpec(memory_space=pltpu.VMEM)
    in_hbm = pl.BlockSpec(memory_space=pl.ANY)
    own_rows = pltpu.VMEM((rows, width), F32)
    four = pltpu.VMEM((4, rows, width), BF16)
    mixed = pltpu.VMEM((4, rows, 3 * wide), BF16)
    square = pltpu.VMEM((4, head_count, rows, rows), BF16)
    return pl.pallas_call(
        functools.partial(back_attend_body, at, head_count),
        name="back_attend",
        out_shape=[
            jax.ShapeDtypeStruct((rows, width), F32),
            jax.ShapeDtypeStruct((width, 3 * wide), BF16),
            jax.ShapeDtypeStruct((wide, width), BF16),
            jax.ShapeDtypeStruct((8, width), F32),
            jax.ShapeDtypeStruct((1, 3 * wide), F32),
            jax.ShapeDtypeStruct((head_count, rows, rows), F32),
        ],
        in_specs=[in_vmem] + [in_hbm] * 9 + [in_vmem] * 3,
        out_specs=[in_vmem] * 6,
        scratch_shapes=[
            own_rows,
            own_rows,
            pltpu.VMEM((rows, 128), F32),
            pltpu.VMEM((4, rows, wide), BF16),
            mixed,
            square,
            four,
            pltpu.VMEM((wide, width), BF16),
            pltpu.VMEM((width, 3 * wide), BF16),
            four,
            mixed,
            square,
            four,
            pltpu.VMEM((3, rows, width), BF16),
            pltpu.VMEM((rows, width), BF16),
            own_rows,
            pltpu.SemaphoreType.DMA((Exchange.COPIES,)),
            pltpu.SemaphoreType.DMA((Exchange.COPIES,)),
            pltpu.SemaphoreType.DMA((9,)),
        ],
        compiler_params=pltpu.CompilerParams(
            collective_id=2 + 2 * at, has_side_effects=True, vmem_limit_bytes=48 * 1024 * 1000
        ),
    )(
        grad,
        branch,
        normal,
        inverse,
        mixture,
        qkv,
        shares,
        gath_a,
        w_out,
        w_qkv,
        spots,
        norms[0],
        norms[2],
    )


def place_rows(index_rows, lengths, bin_rows):
    bin_total = lengths.shape[0]
    index_bins = index_rows.reshape(bin_total, bin_rows, bin_rows)
    first, both = lengths[:, 0:1], lengths[:, 0:1] + lengths[:, 1:2]
    code_first = index_bins[:, 1]
    code_second = jnp.concatenate(
        [
            lax.dynamic_slice(index_bins, (at, lengths[at, 0] + 1, 0), (1, 1, bin_rows))[0]
            for at in range(bin_total)
        ]
    )
    at = jnp.arange(bin_rows)[None]
    code = (SIDE - 1) * (STRIDE + 1) - jnp.where(at < first, code_first, code_second)
    cell = (code // STRIDE) * SIDE + code % STRIDE
    cell = jnp.where((at == 0) | (at == first), CELLS, cell)
    cell = jnp.where(at < both, cell, bin_rows - 1)
    return (cell[:, :, None] == jnp.arange(bin_rows)[None, None]).astype(BF16)


def grid_table(table_used, bin_rows):
    layer_count, entries, head_count = table_used.shape
    columns = jnp.transpose(table_used, (0, 2, 1)).reshape(layer_count * head_count, entries)
    turned = columns[:, STRIDE * STRIDE - 1 :: -1].reshape(-1, STRIDE, STRIDE)
    by_col = jnp.stack([turned[:, :, SIDE - 1 - c : STRIDE - c] for c in range(SIDE)], 1)
    by_row = jnp.stack([by_col[:, :, SIDE - 1 - r : STRIDE - r] for r in range(SIDE)], 1)
    grid = by_row.reshape(-1, CELLS, CELLS)
    grid = jnp.pad(grid, ((0, 0), (0, bin_rows - CELLS), (0, bin_rows - CELLS)))
    row = lax.broadcasted_iota(jnp.int32, (1, bin_rows, bin_rows), 1)
    col = lax.broadcasted_iota(jnp.int32, (1, bin_rows, bin_rows), 2)
    last = columns[:, STRIDE * STRIDE :, None, None]
    grid = jnp.where((row == CELLS) & (col < CELLS), last[:, 0], grid)
    grid = jnp.where((col == CELLS) & (row < CELLS), last[:, 1], grid)
    grid = jnp.where((row == CELLS) & (col == CELLS), last[:, 2], grid)
    return grid.reshape(layer_count, head_count, bin_rows, bin_rows)


def look_up(spots, grid, same_image):
    half = jnp.einsum("bip,lhpq->lbhiq", spots, grid)
    looked = jnp.einsum("lbhiq,bjq->lbhij", half, spots)
    return jnp.where(same_image[None, :, None], looked, jnp.asarray(-1000000000.0, BF16))


def skew(values):
    flipped = values[..., ::-1, :]
    padded = jnp.pad(flipped, [(0, 0)] * (values.ndim - 1) + [(0, SIDE)])
    flat = padded.reshape(padded.shape[:-2] + (SIDE * 2 * SIDE,))[..., : SIDE * STRIDE]
    return jnp.sum(flat.reshape(padded.shape[:-2] + (SIDE, STRIDE)), -2)


def table_grad(total):
    layer_count, head_count = total.shape[:2]
    cells = total[:, :, :CELLS, :CELLS].reshape(-1, SIDE, SIDE, SIDE, SIDE)
    by_col = skew(jnp.transpose(cells, (0, 1, 3, 2, 4)))
    by_both = skew(jnp.transpose(by_col, (0, 3, 1, 2)))
    offsets = jnp.transpose(by_both, (0, 2, 1)).reshape(-1, STRIDE * STRIDE)[:, ::-1]
    offsets = offsets.reshape(layer_count, head_count, -1)
    tail = jnp.stack(
        [
            jnp.sum(total[:, :, CELLS, :CELLS], -1),
            jnp.sum(total[:, :, :CELLS, CELLS], -1),
            total[:, :, CELLS, CELLS],
        ],
        -1,
    )
    return jnp.transpose(jnp.concatenate([offsets, tail], -1), (0, 2, 1))


def per_device(
    tokens,
    cotangent,
    segments,
    lengths,
    rel_index,
    w_qkv,
    qv_bias,
    w_out,
    w_fc1,
    fc1_bias,
    w_fc2,
    rel_table,
    ln_gain,
    ln_bias,
    layer_scale,
    row_bias,
):
    own_rows, width = tokens.shape
    group_rows, bin_rows = rel_index.shape
    layer_count = w_qkv.shape[0]
    head_count = rel_table.shape[2]
    local_width = w_qkv.shape[3]
    wide = -(-local_width // 256) * 256
    bin_total = group_rows // bin_rows
    place = lax.axis_index("tensor")
    assert own_rows == bin_rows and bin_total == 4

    order = jnp.stack([place, place + 1 - 2 * (place % 2), (place + 2) % 4, 3 - place])
    own_length = jnp.sum(lax.dynamic_slice_in_dim(lengths, place, 1))
    valid = (jnp.arange(own_rows) < own_length)[:, None]
    seg_bins = jnp.take(segments.reshape(bin_total, bin_rows), order, axis=0)
    same_image = seg_bins[:, :, None] == seg_bins[:, None, :]
    spots = jnp.take(place_rows(rel_index, lengths, bin_rows), order, axis=0)
    bias = look_up(spots, grid_table(rel_table, bin_rows), same_image)

    extra = wide - local_width
    qkv_used = jnp.pad(w_qkv, ((0, 0), (0, 0), (0, 0), (0, extra))).reshape(
        layer_count, width, 3 * wide
    )
    out_used = jnp.pad(w_out, ((0, 0), (0, extra), (0, 0)))
    zero_bias = jnp.zeros((layer_count, wide), F32)
    qv = jnp.pad(qv_bias.astype(F32), ((0, 0), (0, 0), (0, extra)))
    qkv_bias = jnp.concatenate([qv[:, 0], zero_bias, qv[:, 1]], -1)[:, None]
    up_bias = fc1_bias.astype(F32)[:, None]
    norms = (ln_gain, ln_bias, layer_scale, row_bias)

    (
        gath_a,
        qkv,
        shares,
        mixture,
        gath_b,
        slope,
        active,
        normal_a,
        normal_b,
        inverse,
        branch_a,
        branch_b,
        stream,
    ) = run_forward(
        tokens, (qkv_used, qkv_bias, out_used, w_fc1, up_bias, w_fc2), bias, norms, head_count
    )
    result = jnp.where(valid, stream, 0.0).astype(BF16)
    gradient = jnp.where(valid, cotangent.astype(F32), 0.0)

    weight_parts = [None] * layer_count
    row_parts = [None] * layer_count
    up_biases = [None] * layer_count
    qkv_biases = [None] * layer_count
    grids = [None] * layer_count
    for at in reversed(range(layer_count)):
        gradient, d_up, d_down, sums_b, up_biases[at] = run_back_mlp(
            at, gradient, (branch_b, normal_b, inverse, active, slope, gath_b), (w_fc1, w_fc2), norms
        )
        d_up, d_down = lax.psum((d_up, d_down), "dp")
        gradient, d_qkv, d_out, sums_a, qkv_biases[at], grids[at] = run_back_attend(
            at,
            gradient,
            (branch_a, normal_a, inverse, mixture, qkv, shares, gath_a),
            (out_used, qkv_used),
            spots,
            norms,
        )
        d_qkv, d_out = lax.psum((d_qkv, d_out), "dp")
        weight_parts[at] = (d_qkv, d_out, d_up, d_down)
        row_parts[at] = jnp.stack([sums_a[:4], sums_b[:4]], 1)
    d_qkv, d_out, d_up, d_down = [
        jnp.stack(parts).astype(F32) for parts in zip(*weight_parts)
    ]
    d_qkv = d_qkv.reshape(layer_count, width, 3, wide)[..., :local_width]
    d_out = d_out[:, :local_width]
    d_bias = jnp.concatenate(qkv_biases).reshape(layer_count, 3, wide)[:, ::2, :local_width]
    d_table = table_grad(jnp.stack(grids))
    d_bias, d_up_bias, d_table = lax.psum((d_bias, jnp.concatenate(up_biases), d_table), "dp")
    rows_all = lax.psum(jnp.stack(row_parts, 1), ("dp", "tensor"))
    return (
        result,
        gradient,
        d_qkv,
        d_bias,
        d_out,
        d_up,
        d_up_bias,
        d_down,
        d_table,
        rows_all[0],
        rows_all[1],
        rows_all[2],
        rows_all[3],
    )


def solution(mesh):
    in_specs = (
        P(("dp", "tensor"), None),
        P(("dp", "tensor"), None),
        P("dp"),
        P("dp", None),
        P("dp", None),
        P(None, None, None, "tensor"),
        P(None, None, "tensor"),
        P(None, "tensor", None),
        P(None, None, "tensor"),
        P(None, "tensor"),
        P(None, "tensor", None),
        P(None, None, "tensor"),
        P(),
        P(),
        P(),
        P(),
    )
    out_specs = (
        P(("dp", "tensor"), None),
        P(("dp", "tensor"), None),
        P(None, None, None, "tensor"),
        P(None, None, "tensor"),
        P(None, "tensor", None),
        P(None, None, "tensor"),
        P(None, "tensor"),
        P(None, "tensor", None),
        P(None, None, "tensor"),
        P(),
        P(),
        P(),
        P(),
    )
    return jax.shard_map(
        per_device, mesh=mesh, in_specs=in_specs, out_specs=out_specs, check_vma=False
    )
```

```python
import functools

import jax
import jax.numpy as jnp
from jax import lax
from jax.experimental import pallas as pl
from jax.experimental.pallas import tpu as pltpu
from jax.sharding import PartitionSpec as P

HEAD_DIM = 64
SIDE = 14
STRIDE = 2 * SIDE - 1
CELLS = SIDE * SIDE
PARTS = 2
CHUNK = 32
MESH = pl.DeviceIdType.MESH
BF16 = jnp.bfloat16
F32 = jnp.float32


def dot(left_side, right_side, left_axis=1, right_axis=0):
    return lax.dot_general(
        left_side,
        right_side,
        (((left_axis,), (right_axis,)), ((), ())),
        preferred_element_type=F32,
    )


class Group:
    def __init__(self, send_sems, recv_sems):
        own = lax.axis_index("tensor")
        self.near = own + 1 - 2 * (own % 2)
        self.far = (own + 2) % 4
        self.sems = (send_sems, recv_sems)

    def meet(self):
        barrier = pltpu.get_barrier_semaphore()
        for other in (self.near, self.far):
            pl.semaphore_signal(
                barrier, inc=1, device_id={"tensor": other}, device_id_type=MESH
            )
        pl.semaphore_wait(barrier, 2)

    def copy(self, at, source, target, other):
        return pltpu.make_async_remote_copy(
            src_ref=source,
            dst_ref=target,
            send_sem=self.sems[0].at[at],
            recv_sem=self.sems[1].at[at],
            device_id={"tensor": other},
            device_id_type=MESH,
        )


class Exchange:
    COPIES = 2 + 4 * PARTS

    def __init__(self, group, base, gath, part, got, summed):
        rows = gath.shape[1] // PARTS
        near, far = group.near, group.far
        self.rows = rows

        def piece(ref, slot, at):
            return ref.at[slot, pl.ds(at * rows, rows)]

        self.to_near = group.copy(base, gath.at[0], gath.at[1], near)
        self.to_far = [
            group.copy(base + 2 + at, piece(gath, 0, at), piece(gath, 2, at), far)
            for at in range(PARTS)
        ]
        self.relay = [
            group.copy(base + 2 + PARTS + at, piece(gath, 2, at), piece(gath, 3, at), near)
            for at in range(PARTS)
        ]
        self.sum_near = group.copy(base + 1, part.at[1], got.at[0], near)
        self.sum_pair = [
            group.copy(base + 2 + 2 * PARTS + at, piece(part, 3, at), piece(got, 1, at), near)
            for at in range(PARTS)
        ]
        self.sum_far = [
            group.copy(
                base + 2 + 3 * PARTS + at,
                summed.at[pl.ds(at * rows, rows)],
                piece(got, 2, at),
                far,
            )
            for at in range(PARTS)
        ]
        self.part, self.got, self.summed = part, got, summed

    def start(self):
        self.to_near.start()
        for step in self.to_far:
            step.start()

    def pass_on(self, at):
        self.to_far[at].wait_recv()
        self.relay[at].start()

    def send_sum(self, at):
        self.sum_pair[at].wait_recv()
        rows = self.rows
        span = pl.ds(at * rows, rows)
        self.summed[span] = (
            self.part[2, span].astype(F32) + self.got[1, span].astype(F32)
        ).astype(BF16)
        self.sum_far[at].start()

    def finish(self):
        self.sum_near.wait_recv()
        for step in self.sum_far:
            step.wait_recv()

    def drain(self):
        self.to_near.wait_send()
        self.sum_near.wait_send()
        for steps in (self.to_far, self.relay, self.sum_pair, self.sum_far):
            for step in steps:
                step.wait_send()


def by_chunk(total_rows, body, size=CHUNK):
    def step(at, carry):
        return body(pl.ds(pl.multiple_of(at * size, size), size), carry)

    return step, total_rows // size


def norm_chunk(values, gain, shift):
    center = values - jnp.mean(values, -1, keepdims=True)
    inverse = lax.rsqrt(jnp.mean(center * center, -1, keepdims=True) + 1e-06)
    normal = center * inverse
    return (normal * gain + shift).astype(BF16), normal, inverse


def gelu_parts(values):
    share = 0.5 * (1.0 + lax.erf(values * 0.7071067811865476))
    slope = share + values * (jnp.exp(-0.5 * values * values) * 0.3989422804014327)
    return values * share, slope


SPAN = 384
LAST = (SIDE - 1) * (STRIDE + 1)
CLASS = LAST + 1
TABLE_WIDTH = 2 * SPAN


def prepare_body(
    head_count, lengths, index_rows, table, bias, spots, turned, windows, same, load_sems
):
    rows = bias.shape[3]
    own = lax.axis_index("tensor")
    order = (own, own + 1 - 2 * (own % 2), (own + 2) % 4, 3 - own)

    loads = []
    for slot in range(4):
        for image in range(2):
            row = order[slot] * rows + 1 + (lengths[order[slot], 0] if image else 0)
            load = pltpu.make_async_copy(
                index_rows.at[pl.ds(pl.multiple_of(row // 8 * 8, 8), 8)],
                windows.at[slot, image],
                load_sems.at[slot, image],
            )
            load.start()
            loads.append(load)
    for load in loads:
        load.wait()

    ones = []
    for slot in range(4):
        first = lengths[order[slot], 0]
        both = first + lengths[order[slot], 1]
        in_window = lax.broadcasted_iota(jnp.int32, (8, rows), 0)

        def pick(image):
            row = 1 + (first if image else 0)
            return jnp.sum(
                jnp.where(in_window == row % 8, windows[slot, image], 0), 0, keepdims=True
            )

        at = lax.broadcasted_iota(jnp.int32, (1, rows), 1)
        code = LAST - jnp.where(at < first, pick(0), pick(1))
        code = jnp.where((at == 0) | (at == first), CLASS, code)
        code = jnp.where(at < both, code, -1)
        upright = lax.broadcasted_iota(jnp.int32, (SPAN, rows), 0)
        spots[slot] = (upright == code).astype(F32).astype(BF16)
        column = jnp.transpose(jnp.broadcast_to(code.astype(F32), (128, rows)))
        column = jnp.concatenate([column] * (SPAN // 128), -1)
        flat = lax.broadcasted_iota(jnp.int32, (rows, SPAN), 1).astype(F32)
        ones.append((flat == column).astype(F32).astype(BF16))
        mirrored = jnp.where(column < CLASS, LAST - column, column)
        mirrored = jnp.where(column < 0, -1.0, mirrored)
        turned[slot] = (flat == mirrored).astype(F32).astype(BF16)

        def image_of(values):
            return (values >= first).astype(jnp.int32) + (values >= both).astype(jnp.int32)

        by_row = image_of(lax.broadcasted_iota(jnp.int32, (rows, rows), 0))
        by_col = image_of(lax.broadcasted_iota(jnp.int32, (rows, rows), 1))
        same[slot] = (by_row == by_col).astype(F32)

    key_at = lax.broadcasted_iota(jnp.int32, (SPAN, SPAN), 0)
    query_at = lax.broadcasted_iota(jnp.int32, (SPAN, SPAN), 1)
    shift = SPAN - LAST

    def each(at, carry):
        row = table[pl.ds(at, 1), :]
        rolled = pltpu.roll(
            jnp.broadcast_to(row, (SPAN, TABLE_WIDTH)), 0, 1, stride=1, stride_axis=0
        )
        pairs = rolled[:, SPAN:]
        tail = shift + STRIDE * STRIDE
        pairs = jnp.where(query_at == CLASS, row[:, tail : tail + 1], pairs)
        pairs = jnp.where(key_at == CLASS, row[:, tail + 1 : tail + 2], pairs)
        pairs = jnp.where(
            (query_at == CLASS) & (key_at == CLASS), row[:, tail + 2 : tail + 3], pairs
        ).astype(BF16)
        for slot in range(4):
            half = dot(ones[slot], pairs, 1, 1).astype(BF16)
            looked = dot(half, spots[slot])
            bias[at // head_count, slot, at % head_count] = jnp.where(
                same[slot] > 0.5, looked, -1000000000.0
            ).astype(BF16)
        return carry

    lax.fori_loop(0, table.shape[0], each, 0)


def run_prepare(lengths, index_rows, rel_table):
    bin_rows = index_rows.shape[1]
    layers, entries, head_count = rel_table.shape
    shift = SPAN - LAST
    table = jnp.transpose(rel_table, (0, 2, 1)).reshape(layers * head_count, entries).astype(F32)
    table = jnp.pad(table, ((0, 0), (shift, TABLE_WIDTH - shift - entries)))
    in_vmem = pl.BlockSpec(memory_space=pltpu.VMEM)
    return pl.pallas_call(
        functools.partial(prepare_body, head_count),
        name="prepare",
        out_shape=[
            jax.ShapeDtypeStruct((layers, 4, head_count, bin_rows, bin_rows), BF16),
            jax.ShapeDtypeStruct((4, SPAN, bin_rows), BF16),
            jax.ShapeDtypeStruct((4, bin_rows, SPAN), BF16),
        ],
        in_specs=[
            pl.BlockSpec(memory_space=pltpu.SMEM),
            pl.BlockSpec(memory_space=pl.ANY),
            in_vmem,
        ],
        out_specs=[in_vmem] * 3,
        scratch_shapes=[
            pltpu.VMEM((4, 2, 8, bin_rows), jnp.int32),
            pltpu.VMEM((4, bin_rows, bin_rows), F32),
            pltpu.SemaphoreType.DMA((4, 2)),
        ],
        compiler_params=pltpu.CompilerParams(vmem_limit_bytes=32 * 1024 * 1000),
    )(lengths, index_rows, table)


def table_row(pairs):
    query_at = lax.broadcasted_iota(jnp.int32, (SPAN, SPAN), 0)
    key_at = lax.broadcasted_iota(jnp.int32, (SPAN, SPAN), 1)
    zero = jnp.zeros((SPAN, SPAN), F32)
    patches = jnp.where((query_at <= LAST) & (key_at <= LAST), pairs, zero)
    rolled = pltpu.roll(
        jnp.concatenate([patches, zero], -1), 0, 1, stride=1, stride_axis=0
    )
    row = jnp.sum(rolled, 0, keepdims=True)
    at = lax.broadcasted_iota(jnp.int32, (1, TABLE_WIDTH), 1)
    tails = (
        (query_at == CLASS) & (key_at <= LAST),
        (query_at <= LAST) & (key_at == CLASS),
        (query_at == CLASS) & (key_at == CLASS),
    )
    for number, mask in enumerate(tails):
        row = jnp.where(at == STRIDE * STRIDE + number, jnp.sum(jnp.where(mask, pairs, zero)), row)
    return row


def attend_rows(qkv, weights_kept, mixture, bias, at, slot, first, head_count):
    rows = qkv.shape[2] // PARTS
    wide = qkv.shape[3] // 3
    span = pl.ds(first, rows)
    heads = []
    for head in range(head_count):
        lanes = slice(head * HEAD_DIM, (head + 1) * HEAD_DIM)
        queries = qkv[at, slot, span, 0:wide][:, lanes]
        keys = qkv[at, slot, :, wide : 2 * wide][:, lanes]
        values = qkv[at, slot, :, 2 * wide : 3 * wide][:, lanes]
        scores = dot(queries, keys, 1, 1) + bias[at, slot, head, span].astype(F32)
        powers = jnp.exp(scores - jnp.max(scores, -1, keepdims=True))
        weights = (powers / jnp.sum(powers, -1, keepdims=True)).astype(BF16)
        weights_kept[at, slot, head, span] = weights
        heads.append(dot(weights, values).astype(BF16))
    heads.append(jnp.zeros((rows, wide - head_count * HEAD_DIM), BF16))
    mixture[at, slot, span] = jnp.concatenate(heads, -1)


def forward_body(
    layer_count,
    head_count,
    tokens,
    w_qkv,
    qkv_bias,
    w_out,
    w_up,
    up_bias,
    w_down,
    bias,
    ln_gain,
    ln_bias,
    layer_scale,
    row_bias,
    gath_a_out,
    qkv_out,
    weights_out,
    mixture_out,
    gath_b_out,
    slope_out,
    active_out,
    normal_a,
    normal_b,
    inverse,
    branch_a,
    branch_b,
    stream,
    gath_a,
    qkv,
    weights_kept,
    mixture,
    gath_b,
    slope,
    active,
    hidden,
    part,
    got,
    summed,
    own,
    send_sems,
    recv_sems,
    out_sems,
):
    rows, width = stream.shape
    half = rows // PARTS
    group = Group(send_sems, recv_sems)
    group.meet()

    def each_chunk(body):
        step, count = by_chunk(rows, lambda span, carry: (body(span), carry)[1])
        lax.fori_loop(0, count, step, 0)

    def load(span):
        stream[span] = tokens[span].astype(F32)

    each_chunk(load)

    kept = (
        (gath_a, gath_a_out),
        (qkv, qkv_out),
        (weights_kept, weights_out),
        (mixture, mixture_out),
        (gath_b, gath_b_out),
        (slope, slope_out),
        (active, active_out),
    )

    def keep(number, at):
        source, target = kept[number]
        return pltpu.make_async_copy(source.at[at], target.at[at], out_sems.at[number, at])

    def layer(at, carry):
        trade = Exchange(group, 0, gath_a.at[at], part, got, summed)

        def enter(span):
            low, normal, inv = norm_chunk(
                stream[span], ln_gain[at, 0:1], ln_bias[at, 0:1]
            )
            gath_a[at, 0, span] = low
            normal_a[at, span] = normal
            inverse[at, 0, span] = jnp.broadcast_to(inv, (CHUNK, 128))

        each_chunk(enter)
        trade.start()
        scale = jnp.concatenate(
            [
                jnp.full((1, width // 3), HEAD_DIM**-0.5, F32),
                jnp.full((1, 2 * width // 3), 1.0, F32),
            ],
            -1,
        )

        def project(slot, first, count):
            span = pl.ds(first, count)
            mixed = dot(gath_a[at, slot, span], w_qkv[at])
            mixed = (mixed + qkv_bias[at]).astype(BF16).astype(F32) * scale
            qkv[at, slot, span] = mixed.astype(BF16)

        def attend(slot, first):
            attend_rows(qkv, weights_kept, mixture, bias, at, slot, first, head_count)

        def leave(slot, first):
            return dot(mixture[at, slot, pl.ds(first, half)], w_out[at])

        def whole(slot):
            project(slot, 0, rows)

            def one(place, carry):
                first = pl.multiple_of(place * half, half)
                attend(slot, first)
                result = leave(slot, first)
                if slot == 0:
                    own[pl.ds(first, half)] = result
                else:
                    part[slot, pl.ds(first, half)] = result.astype(BF16)
                return carry

            lax.fori_loop(0, PARTS, one, 0)

        whole(0)
        trade.to_near.wait_recv()
        whole(1)
        trade.sum_near.start()
        for place in range(PARTS):
            trade.pass_on(place)
            project(2, place * half, half)
        for place in range(PARTS):
            trade.relay[place].wait_recv()
            project(3, place * half, half)
        keep(0, at).start()
        keep(1, at).start()
        for place in range(PARTS):
            first = place * half
            attend(3, first)
            part[3, pl.ds(first, half)] = leave(3, first).astype(BF16)
            trade.sum_pair[place].start()
            attend(2, first)
            part[2, pl.ds(first, half)] = leave(2, first).astype(BF16)
            trade.send_sum(place)
        keep(2, at).start()
        keep(3, at).start()
        trade.finish()

        trade_b = Exchange(group, Exchange.COPIES, gath_b.at[at], part, got, summed)

        def between(span):
            total = own[span] + got[0, span].astype(F32) + got[2, span].astype(F32)
            branch = total + row_bias[at, 0:1]
            branch_a[at, span] = branch
            middle = stream[span] + layer_scale[at, 0:1] * branch
            stream[span] = middle
            low, normal, inv = norm_chunk(middle, ln_gain[at, 1:2], ln_bias[at, 1:2])
            gath_b[at, 0, span] = low
            normal_b[at, span] = normal
            inverse[at, 1, span] = jnp.broadcast_to(inv, (CHUNK, 128))

        each_chunk(between)
        trade.drain()

        trade_b.start()

        def raise_rows(values, count, put):
            hidden[pl.ds(0, count)] = dot(values, w_up[at]) + up_bias[at]

            def act(place, carry):
                span = pl.ds(pl.multiple_of(place * 16, 16), 16)
                high, incline = gelu_parts(hidden[span])
                put(place * 16, high.astype(BF16), incline.astype(BF16))
                return carry

            lax.fori_loop(0, count // 16, act, 0)

        def to_slot(slot, start):
            def put(first, high, incline):
                span = pl.ds(pl.multiple_of(start + first, 16), 16)
                active[at, slot, span] = high
                slope[at, slot, span] = incline

            return put

        raise_rows(gath_b[at, 0], rows, to_slot(0, 0))
        own[...] = dot(active[at, 0], w_down[at])
        trade_b.to_near.wait_recv()
        raise_rows(gath_b[at, 1], rows, to_slot(1, 0))
        part[1] = dot(active[at, 1], w_down[at]).astype(BF16)
        trade_b.sum_near.start()
        for place in range(PARTS):
            trade_b.pass_on(place)
            span = pl.ds(place * half, half)
            raise_rows(gath_b[at, 2, span], half, to_slot(2, place * half))
            trade_b.relay[place].wait_recv()
            raise_rows(gath_b[at, 3, span], half, to_slot(3, place * half))
            part[3, span] = dot(active[at, 3, span], w_down[at]).astype(BF16)
            trade_b.sum_pair[place].start()
            part[2, span] = dot(active[at, 2, span], w_down[at]).astype(BF16)
            trade_b.send_sum(place)
        for number in (4, 5, 6):
            keep(number, at).start()
        trade_b.finish()

        def after(span):
            total = own[span] + got[0, span].astype(F32) + got[2, span].astype(F32)
            branch = total + row_bias[at, 1:2]
            branch_b[at, span] = branch
            stream[span] = stream[span] + layer_scale[at, 1:2] * branch

        each_chunk(after)
        trade_b.drain()
        return carry

    lax.fori_loop(0, layer_count, layer, 0)
    for at in range(layer_count):
        for number in range(len(kept)):
            keep(number, at).wait()


def run_forward(tokens, weights, bias, norms, head_count):
    rows, width = tokens.shape
    w_qkv, qkv_bias, w_out, w_up, up_bias, w_down = weights
    layers = w_qkv.shape[0]
    wide = w_qkv.shape[2] // 3
    inner = w_up.shape[2]
    in_vmem = pl.BlockSpec(memory_space=pltpu.VMEM)
    in_hbm = pl.BlockSpec(memory_space=pl.ANY)
    kept = [
        jax.ShapeDtypeStruct((layers, 4) + tail, BF16)
        for tail in (
            (rows, width),
            (rows, 3 * wide),
            (head_count, rows, rows),
            (rows, wide),
            (rows, width),
            (rows, inner),
            (rows, inner),
        )
    ]
    near = [
        jax.ShapeDtypeStruct(shape, F32)
        for shape in (
            (layers, rows, width),
            (layers, rows, width),
            (layers, 2, rows, 128),
            (layers, rows, width),
            (layers, rows, width),
            (rows, width),
        )
    ]
    return pl.pallas_call(
        functools.partial(forward_body, layers, head_count),
        name="forward",
        out_shape=kept + near,
        in_specs=[in_vmem] * 12,
        out_specs=[in_hbm] * len(kept) + [in_vmem] * len(near),
        scratch_shapes=[pltpu.VMEM(leaf.shape, leaf.dtype) for leaf in kept]
        + [
            pltpu.VMEM((rows, inner), F32),
            pltpu.VMEM((4, rows, width), BF16),
            pltpu.VMEM((3, rows, width), BF16),
            pltpu.VMEM((rows, width), BF16),
            pltpu.VMEM((rows, width), F32),
            pltpu.SemaphoreType.DMA((2 * Exchange.COPIES,)),
            pltpu.SemaphoreType.DMA((2 * Exchange.COPIES,)),
            pltpu.SemaphoreType.DMA((len(kept), layers)),
        ],
        compiler_params=pltpu.CompilerParams(
            collective_id=0, has_side_effects=True, vmem_limit_bytes=64 * 1024 * 1000
        ),
    )(tokens, w_qkv, qkv_bias, w_out, w_up, up_bias, w_down, bias, *norms)


def fold(values):
    return jnp.sum(values.reshape(-1, 8, values.shape[-1]), 0)


def enter_back(grad, branch, scale, gath, sums):
    rows, width = grad.shape

    def body(span, carry):
        values = grad[span]
        gath[0, span] = (values * scale).astype(BF16)
        return carry[0] + fold(values * branch[span]), carry[1] + fold(values)

    step, count = by_chunk(rows, body)
    zero = jnp.zeros((8, width), F32)
    by_branch, alone = lax.fori_loop(0, count, step, (zero, zero))
    sums[2:3] = jnp.sum(by_branch, 0, keepdims=True)
    sums[3:4] = jnp.sum(alone, 0, keepdims=True) * scale


def leave_back(grad, own, got, normal, inverse, gain, sums):
    rows, width = grad.shape

    def body(span, carry):
        total = own[span] + got[0, span].astype(F32) + got[2, span].astype(F32)
        unit = normal[span]
        scaled = total * gain
        centered = (
            scaled
            - jnp.mean(scaled, -1, keepdims=True)
            - unit * jnp.mean(scaled * unit, -1, keepdims=True)
        )
        grad[span] = grad[span] + inverse[span, 0:1] * centered
        return carry[0] + fold(total * unit), carry[1] + fold(total)

    step, count = by_chunk(rows, body)
    zero = jnp.zeros((8, width), F32)
    by_unit, alone = lax.fori_loop(0, count, step, (zero, zero))
    sums[0:1] = jnp.sum(by_unit, 0, keepdims=True)
    sums[1:2] = jnp.sum(alone, 0, keepdims=True)


def weight_grad(left, right, out, start, count):
    block = 256
    used = count * block // left.shape[2]

    def step(place, carry):
        span = pl.ds(pl.multiple_of(place * block, block), block)
        total = None
        for slot in range(4):
            term = dot(left[slot, :, span], right[slot], 0, 0)
            total = term if total is None else total + term
        there = pl.ds(pl.multiple_of(start + place * used, 16), used)
        out[there] = total[:used].astype(out.dtype)
        return carry

    lax.fori_loop(0, left.shape[2] // block, step, 0)


class Names:
    def __init__(self, names, refs):
        for name, ref in zip(names, refs, strict=True):
            setattr(self, name, ref)


class Ticker:
    def __init__(self, ring):
        self.ring = ring
        self.under_way = []

    def add(self, streams):
        self.ring.start(streams)
        self.under_way.append([streams, 0])

    def tick(self):
        if not self.under_way:
            return
        ring = self.ring
        streams, step = self.under_way.pop(0)
        turn = ring.count - 1
        for stream in streams:
            if step < turn:
                ring.add(stream, step)
                ring.copy(stream, step, False).wait_send()
            else:
                ring.copy(stream, step, True).wait_recv()
            if step + 1 < ring.steps:
                ring.copy(stream, step + 1, step + 1 >= turn).start()
        if step + 1 < ring.steps:
            self.under_way.append([streams, step + 1])
        else:
            ring.drain(streams)

    def finish(self):
        while self.under_way:
            self.tick()


def load_all(number, at, pairs, sems):
    steps = []
    for place, (source, target) in enumerate(pairs):
        step = pltpu.make_async_copy(source, target, sems.at[at, number, place])
        step.start()
        steps.append(step)
    return steps


def mlp_loads(refs, at):
    return load_all(
        0,
        at,
        (
            (refs.branch_b_all.at[at], refs.branch_b),
            (refs.w_down_all.at[at], refs.w_down),
            (refs.slope_all.at[at], refs.slope),
            (refs.w_up_all.at[at], refs.w_up),
            (refs.normal_b_all.at[at], refs.normal_b),
            (refs.inverse_all.at[at, 1], refs.inverse_b),
            (refs.active_all.at[at], refs.active),
            (refs.gath_b_all.at[at], refs.gath_b),
        ),
        refs.load_sems,
    )


def attend_loads(refs, at):
    return load_all(
        1,
        at,
        (
            (refs.branch_a_all.at[at], refs.branch_a),
            (refs.w_out_all.at[at], refs.w_out),
            (refs.qkv_all.at[at], refs.qkv),
            (refs.weights_all.at[at], refs.weights),
            (refs.w_qkv_all.at[at], refs.w_qkv),
            (refs.normal_a_all.at[at], refs.normal_a),
            (refs.inverse_all.at[at, 0], refs.inverse_a),
            (refs.mixture_all.at[at], refs.mixture),
            (refs.gath_a_all.at[at], refs.gath_a),
        ),
        refs.load_sems,
    )


def back_mlp(refs, group, base, at, loads, tick, data, begin_ring):
    rows = refs.grad.shape[0]
    half = rows // PARTS
    gath, part, hidden, d_hidden = refs.gath_m, refs.part, refs.hidden, refs.d_hidden
    trade = Exchange(group, base, gath, part, refs.got, refs.summed)
    sums = refs.sums.at[2 * at + 1]
    loads[0].wait()
    enter_back(refs.grad, refs.branch_b, refs.layer_scale[at, 1:2], gath, sums)
    trade.start()
    tick()
    for load in loads[1:4]:
        load.wait()

    def down(slot, first, count, total):
        span = pl.ds(first, count)
        hidden[pl.ds(0, count)] = dot(gath[slot, span], refs.w_down[...], 1, 1)

        def body(place, carry):
            inside = pl.ds(pl.multiple_of(place * CHUNK, CHUNK), CHUNK)
            there = pl.ds(pl.multiple_of(first + place * CHUNK, CHUNK), CHUNK)
            low = (hidden[inside] * refs.slope[slot, there].astype(F32)).astype(BF16)
            d_hidden[slot, there] = low
            return carry + fold(low.astype(F32))

        return lax.fori_loop(0, count // CHUNK, body, total)

    def back(slot, first, count):
        return dot(d_hidden[slot, pl.ds(first, count)], refs.w_up[...], 1, 1)

    total = jnp.zeros((8, hidden.shape[1]), F32)
    total = down(0, 0, rows, total)
    refs.own[...] = back(0, 0, rows)
    tick()
    trade.to_near.wait_recv()
    total = down(1, 0, rows, total)
    part[1] = back(1, 0, rows).astype(BF16)
    trade.sum_near.start()
    tick()
    for place in range(PARTS):
        trade.pass_on(place)
        first = place * half
        span = pl.ds(first, half)
        total = down(2, first, half, total)
        trade.relay[place].wait_recv()
        total = down(3, first, half, total)
        part[3, span] = back(3, first, half).astype(BF16)
        trade.sum_pair[place].start()
        part[2, span] = back(2, first, half).astype(BF16)
        trade.send_sum(place)
        tick()
    refs.up_sums[at : at + 1] = jnp.sum(total, 0, keepdims=True)
    for load in loads[4:]:
        load.wait()
    inner = hidden.shape[1]
    weight_grad(refs.active, gath, data, 0, inner)
    tick()
    weight_grad(refs.gath_b, d_hidden, data, inner, refs.grad.shape[1])
    begin_ring()
    tick()
    trade.finish()
    leave_back(
        refs.grad,
        refs.own,
        refs.got,
        refs.normal_b,
        refs.inverse_b,
        refs.ln_gain[at, 1:2],
        sums,
    )
    trade.drain()
    tick()


def back_attend(refs, group, base, at, head_count, loads, tick, data, begin_ring):
    rows = refs.grad.shape[0]
    half = rows // PARTS
    wide = refs.mixture.shape[2]
    gath, part, d_mixed, d_scores = refs.gath_t, refs.part, refs.d_mixed, refs.d_scores
    qkv = refs.qkv
    trade = Exchange(group, base, gath, part, refs.got, refs.summed)
    sums = refs.sums.at[2 * at]
    loads[0].wait()
    enter_back(refs.grad, refs.branch_a, refs.layer_scale[at, 0:1], gath, sums)
    trade.start()
    tick()
    for load in loads[1:5]:
        load.wait()
    spare = jnp.zeros((rows, wide - head_count * HEAD_DIM), BF16)

    def attend(slot):
        d_mix = dot(gath[slot], refs.w_out[...], 1, 1).astype(BF16)
        pieces = ([], [], [])
        for head in range(head_count):
            lanes = slice(head * HEAD_DIM, (head + 1) * HEAD_DIM)
            queries = qkv[slot, :, 0:wide][:, lanes]
            keys = qkv[slot, :, wide : 2 * wide][:, lanes]
            values = qkv[slot, :, 2 * wide : 3 * wide][:, lanes]
            share = refs.weights[slot, head]
            d_head = d_mix[:, lanes]
            wide_share = share.astype(F32)
            d_share = dot(d_head, values, 1, 1)
            middle = jnp.sum(wide_share * d_share, -1, keepdims=True)
            d_score = (wide_share * (d_share - middle)).astype(BF16)
            d_scores[slot, head] = d_score
            pieces[0].append((dot(d_score, keys) * HEAD_DIM**-0.5).astype(BF16))
            pieces[1].append(dot(d_score, queries, 0, 0).astype(BF16))
            pieces[2].append(dot(share, d_head, 0, 0).astype(BF16))
        for place in range(3):
            d_mixed[slot, :, place * wide : (place + 1) * wide] = jnp.concatenate(
                pieces[place] + [spare], -1
            )

    def back(slot, first, count):
        return dot(d_mixed[slot, pl.ds(first, count)], refs.w_qkv[...], 1, 1)

    attend(0)
    tick()
    refs.own[...] = back(0, 0, rows)
    trade.to_near.wait_recv()
    attend(1)
    part[1] = back(1, 0, rows).astype(BF16)
    trade.sum_near.start()
    tick()
    for place in range(PARTS):
        trade.pass_on(place)
    for place in range(PARTS):
        trade.relay[place].wait_recv()
    attend(3)
    part[3] = back(3, 0, rows).astype(BF16)
    for place in range(PARTS):
        trade.sum_pair[place].start()
    tick()
    attend(2)
    for place in range(PARTS):
        first = place * half
        part[2, pl.ds(first, half)] = back(2, first, half).astype(BF16)
        trade.send_sum(place)
    tick()
    for load in loads[5:]:
        load.wait()

    def add(slot, total):
        def body(span, carry):
            return carry + fold(d_mixed[slot, span].astype(F32))

        step, count = by_chunk(rows, body)
        return lax.fori_loop(0, count, step, total)

    total = jnp.zeros((8, 3 * wide), F32)
    for slot in range(4):
        total = add(slot, total)
    refs.qkv_sums[at : at + 1] = jnp.sum(total, 0, keepdims=True)
    used = 3 * head_count * HEAD_DIM
    weight_grad(d_mixed, refs.gath_a, data, 0, used)
    tick()
    weight_grad(refs.mixture, gath, data, used, used // 3)
    begin_ring()
    tick()
    for head in range(head_count):
        total = None
        for slot in range(4):
            placed = dot(refs.spots[slot], d_scores[slot, head]).astype(BF16)
            term = dot(placed, refs.turned[slot])
            total = term if total is None else total + term
        row = at * head_count + head
        refs.table_sums[row : row + 1] = table_row(total)
    trade.finish()
    leave_back(
        refs.grad,
        refs.own,
        refs.got,
        refs.normal_a,
        refs.inverse_a,
        refs.ln_gain[at, 0:1],
        sums,
    )
    trade.drain()
    tick()


BACK_INPUTS = (
    "grad_in",
    "branch_a_all",
    "branch_b_all",
    "normal_a_all",
    "normal_b_all",
    "inverse_all",
    "mixture_all",
    "qkv_all",
    "weights_all",
    "gath_a_all",
    "active_all",
    "slope_all",
    "gath_b_all",
    "w_qkv_all",
    "w_out_all",
    "w_up_all",
    "w_down_all",
    "spots",
    "turned",
    "ln_gain",
    "layer_scale",
)
BACK_OUTPUTS = (
    "grad",
    "d_qkv",
    "d_out",
    "d_up",
    "d_down",
    "small_out",
)
BACK_SCRATCH = (
    "branch_a",
    "branch_b",
    "normal_a",
    "normal_b",
    "inverse_a",
    "inverse_b",
    "mixture",
    "qkv",
    "weights",
    "gath_a",
    "active",
    "slope",
    "gath_b",
    "w_qkv",
    "w_out",
    "w_up",
    "w_down",
    "gath_m",
    "gath_t",
    "d_hidden",
    "hidden",
    "d_mixed",
    "d_scores",
    "part",
    "got",
    "summed",
    "own",
    "sums",
    "up_sums",
    "qkv_sums",
    "table_sums",
    "lines",
    "near_got",
    "pair_sum",
    "far_got",
    "data_m",
    "data_t",
    "got_m",
    "got_t",
    "small",
    "got_small",
    "send_sems",
    "recv_sems",
    "load_sems",
    "ring_send_m",
    "ring_recv_m",
    "ring_send_t",
    "ring_recv_t",
    "ring_send_s",
    "ring_recv_s",
    "out_sems",
)


def backward_body(layers, head_count, count, *all_refs):
    refs = Names((*BACK_INPUTS, *BACK_OUTPUTS, *BACK_SCRATCH), all_refs)
    rows, width = refs.grad.shape
    group = Group(refs.send_sems, refs.recv_sems)
    loads_m = mlp_loads(refs, layers - 1)
    loads_t = attend_loads(refs, layers - 1)
    barrier = pltpu.get_barrier_semaphore()
    for other in (group.near, group.far):
        pl.semaphore_signal(barrier, inc=1, device_id={"tensor": other}, device_id_type=MESH)
    ring = Ring(count) if count else None
    if ring:
        for other in ring.sides:
            pl.semaphore_signal(barrier, inc=1, device_id={"dp": other}, device_id_type=MESH)
    refs.grad[...] = refs.grad_in[...]
    pl.semaphore_wait(barrier, 4 if ring else 2)

    ticker = Ticker(ring)
    ring_sets = []
    for at in range(layers if ring else 0):
        ring_sets.append(
            (
                ring.streams(
                    (
                        refs.data_m.at[at],
                        refs.got_m.at[at],
                        refs.ring_send_m.at[at],
                        refs.ring_recv_m.at[at],
                    )
                ),
                ring.streams(
                    (
                        refs.data_t.at[at],
                        refs.got_t.at[at],
                        refs.ring_send_t.at[at],
                        refs.ring_recv_t.at[at],
                    )
                ),
            )
        )

    def begin(at, kind):
        if ring:
            ticker.add(ring_sets[at][kind])

    for at in reversed(range(layers)):
        base = at * 2 * Exchange.COPIES
        back_mlp(
            refs,
            group,
            base,
            at,
            loads_m,
            ticker.tick,
            refs.data_m.at[at],
            lambda: begin(at, 0),
        )
        if at:
            loads_m = mlp_loads(refs, at - 1)
        back_attend(
            refs,
            group,
            base + Exchange.COPIES,
            at,
            head_count,
            loads_t,
            ticker.tick,
            refs.data_t.at[at],
            lambda: begin(at, 1),
        )
        if at:
            loads_t = attend_loads(refs, at - 1)

    shared = 8 * layers
    lines = refs.lines
    lines[...] = jnp.zeros_like(lines)
    for kind in range(4):
        for at in range(2 * layers):
            row = kind * 2 * layers + at
            lines[row : row + 1] = refs.sums[at, kind : kind + 1]
    base = layers * 2 * Exchange.COPIES
    first = group.copy(base, lines.at[pl.ds(0, shared)], refs.near_got, group.near)
    first.start()
    ticker.tick()
    first.wait_recv()
    refs.pair_sum[...] = lines[0:shared] + refs.near_got[...]
    second = group.copy(base + 1, refs.pair_sum, refs.far_got, group.far)
    second.start()
    ticker.tick()
    second.wait_recv()
    first.wait_send()
    lines[0:shared] = refs.pair_sum[...] + refs.far_got[...]
    row = shared
    for leaf, height in (
        (refs.qkv_sums, layers),
        (refs.up_sums, layers),
        (refs.table_sums, layers * head_count),
    ):
        lines[row : row + height] = leaf[0:height]
        row += height
    cuts = [
        (slice(at * SMALL_ROWS, (at + 1) * SMALL_ROWS), slice(at * 128, (at + 1) * 128))
        for at in range(width // 128)
    ]
    if ring:
        small = refs.small
        small[...] = jnp.zeros_like(small)
        for rows_at, lanes in cuts:
            small[rows_at] = lines[:, lanes]
        ticker.add(
            ring.streams((small, refs.got_small, refs.ring_send_s, refs.ring_recv_s))
        )
        ticker.finish()
    second.wait_send()
    used = refs.d_qkv.shape[1]
    inner = refs.d_down.shape[1]
    leaves = []
    for at in range(layers):
        for source, first, target in (
            (refs.data_t, 0, refs.d_qkv),
            (refs.data_t, used, refs.d_out),
            (refs.data_m, 0, refs.d_down),
            (refs.data_m, inner, refs.d_up),
        ):
            leave = pltpu.make_async_copy(
                source.at[at, pl.ds(first, target.shape[1])],
                target.at[at],
                refs.out_sems.at[len(leaves)],
            )
            leave.start()
            leaves.append(leave)
    if ring:
        for rows_at, lanes in cuts:
            refs.small_out[:, lanes] = small[rows_at]
    else:
        refs.small_out[...] = lines[...]
    for leave in leaves:
        leave.wait()


def run_backward(count, inputs, head_count):
    grad, gath_b, w_qkv, w_out, w_up = inputs[0], inputs[12], inputs[13], inputs[14], inputs[15]
    rows, width = grad.shape
    layers, wide = w_out.shape[:2]
    inner = w_up.shape[2]
    used = head_count * HEAD_DIM
    ring_count = count or 2
    steps = 2 * (ring_count - 1)
    in_vmem = pl.BlockSpec(memory_space=pltpu.VMEM)
    in_hbm = pl.BlockSpec(memory_space=pl.ANY)
    assert inner == width == 3 * wide

    def wide_rows(*shape):
        return pltpu.VMEM(shape, F32)

    def low(*shape):
        return pltpu.VMEM(shape, BF16)

    def sems(*shape):
        return pltpu.SemaphoreType.DMA(shape)

    own = wide_rows(rows, width)
    four = low(4, rows, width)
    four_inner = low(4, rows, inner)
    mixed = low(4, rows, 3 * wide)
    square = low(4, head_count, rows, rows)
    data_m = (layers, inner + width, width)
    data_t = (layers, 4 * used, width)
    lines = wide_rows(8 * layers, width)
    small_rows = -(-SMALL_ROWS * (width // 128) // (16 * ring_count)) * 16 * ring_count

    def ring_got(data, subs):
        return low(layers, 2, subs, ring_count - 1, data[1] // (2 * ring_count * subs), width)

    scratch = (
        [own] * 4
        + [wide_rows(rows, 128)] * 2
        + [low(4, rows, wide), mixed, square, four, four_inner, four_inner, four]
        + [low(width, 3 * wide), low(wide, width), low(width, inner), low(inner, width)]
        + [four, four, four_inner, wide_rows(rows, inner), mixed, square, four]
        + [low(3, rows, width), low(rows, width), own]
        + [wide_rows(2 * layers, 8, width), wide_rows(8, inner), wide_rows(8, 3 * wide)]
        + [wide_rows(8, TABLE_WIDTH), wide_rows(SMALL_ROWS, width), lines, lines, lines]
        + [low(*data_m), low(*data_t), ring_got(data_m, SUBS), ring_got(data_t, 1)]
        + [wide_rows(small_rows, 128)]
        + [wide_rows(2, 1, ring_count - 1, small_rows // (2 * ring_count), 128)]
        + [sems(2 * layers * Exchange.COPIES + 2)] * 2
        + [sems(layers, 2, 9)]
        + [sems(layers, 2, SUBS, steps)] * 2
        + [sems(layers, 2, 1, steps)] * 2
        + [sems(2, 1, steps)] * 2
        + [sems(4 * layers)]
    )
    return pl.pallas_call(
        functools.partial(backward_body, layers, head_count, count),
        name="backward",
        out_shape=[
            jax.ShapeDtypeStruct((rows, width), F32),
            jax.ShapeDtypeStruct((layers, 3 * used, width), BF16),
            jax.ShapeDtypeStruct((layers, used, width), BF16),
            jax.ShapeDtypeStruct((layers, width, inner), BF16),
            jax.ShapeDtypeStruct((layers, inner, width), BF16),
            jax.ShapeDtypeStruct((SMALL_ROWS, width), F32),
        ],
        in_specs=[in_vmem] + [in_hbm] * 16 + [in_vmem] * 4,
        out_specs=[in_vmem] + [in_hbm] * 4 + [in_vmem],
        scratch_shapes=scratch,
        compiler_params=pltpu.CompilerParams(
            collective_id=1, has_side_effects=True, vmem_limit_bytes=65400 * 1024
        ),
    )(*inputs)


SUBS = 2
SMALL_ROWS = 32


class Ring:
    def __init__(self, count):
        self.count = count
        self.steps = 2 * (count - 1)
        self.place = self.place_of(lax.axis_index("dp"))
        self.sides = (
            self.number_of((self.place + 1) % count),
            self.number_of((self.place + count - 1) % count),
        )

    def place_of(self, number):
        row, side = number // 2, number % 2
        return row + side * (self.count - 1 - 2 * row)

    def number_of(self, place):
        side = place // (self.count // 2)
        return 2 * (place + side * (self.count - 1 - 2 * place)) + side

    def streams(self, *sets):
        return [
            (leaf, way, sub)
            for leaf in sets
            for sub in range(leaf[1].shape[1])
            for way in range(2)
        ]

    def rows(self, stream, step):
        (data, got, _, _), way, sub = stream
        subs, piece = got.shape[1], got.shape[3]
        if way == 0:
            chunk = (self.place + 3 * self.count - step) % self.count
        else:
            chunk = (self.place + step) % self.count
        first = ((way * self.count + chunk) * subs + sub) * piece
        return pl.ds(pl.multiple_of(first, piece), piece)

    def copy(self, stream, step, gather):
        (data, got, send_sems, recv_sems), way, sub = stream
        rows = self.rows(stream, step)
        return pltpu.make_async_remote_copy(
            src_ref=data.at[rows],
            dst_ref=data.at[rows] if gather else got.at[way, sub, step],
            send_sem=send_sems.at[way, sub, step],
            recv_sem=recv_sems.at[way, sub, step],
            device_id={"dp": self.sides[way]},
            device_id_type=MESH,
        )

    def start(self, streams):
        for stream in streams:
            self.copy(stream, 0, False).start()

    def add(self, stream, step):
        (data, got, _, _), way, sub = stream
        self.copy(stream, step, False).wait_recv()
        rows = self.rows(stream, step + 1)
        total = data[rows].astype(F32) + got[way, sub, step].astype(F32)
        data[rows] = total.astype(data.dtype)

    def drain(self, streams):
        for step in range(self.count - 1, self.steps):
            for stream in streams:
                self.copy(stream, step, True).wait_send()


def ring_fits(count, rows):
    return count == 8 and rows % (2 * count * 16) == 0


def per_device(
    tokens,
    cotangent,
    segments,
    lengths,
    rel_index,
    w_qkv,
    qv_bias,
    w_out,
    w_fc1,
    fc1_bias,
    w_fc2,
    rel_table,
    ln_gain,
    ln_bias,
    layer_scale,
    row_bias,
):
    own_rows, width = tokens.shape
    group_rows, bin_rows = rel_index.shape
    layer_count = w_qkv.shape[0]
    head_count = rel_table.shape[2]
    local_width = w_qkv.shape[3]
    wide = -(-local_width // 256) * 256
    bin_total = group_rows // bin_rows
    place = lax.axis_index("tensor")
    assert own_rows == bin_rows and bin_total == 4

    own_length = jnp.sum(lax.dynamic_slice_in_dim(lengths, place, 1))
    valid = (jnp.arange(own_rows) < own_length)[:, None]
    bias, *spots = run_prepare(lengths, rel_index, rel_table)

    extra = wide - local_width
    qkv_used = jnp.pad(w_qkv, ((0, 0), (0, 0), (0, 0), (0, extra))).reshape(
        layer_count, width, 3 * wide
    )
    out_used = jnp.pad(w_out, ((0, 0), (0, extra), (0, 0)))
    zero_bias = jnp.zeros((layer_count, wide), F32)
    qv = jnp.pad(qv_bias.astype(F32), ((0, 0), (0, 0), (0, extra)))
    qkv_bias = jnp.concatenate([qv[:, 0], zero_bias, qv[:, 1]], -1)[:, None]
    up_bias = fc1_bias.astype(F32)[:, None]
    norms = (ln_gain, ln_bias, layer_scale, row_bias)

    (
        gath_a,
        qkv,
        shares,
        mixture,
        gath_b,
        slope,
        active,
        normal_a,
        normal_b,
        inverse,
        branch_a,
        branch_b,
        stream,
    ) = run_forward(
        tokens, (qkv_used, qkv_bias, out_used, w_fc1, up_bias, w_fc2), bias, norms, head_count
    )
    result = jnp.where(valid, stream, 0.0).astype(BF16)
    gradient = jnp.where(valid, cotangent.astype(F32), 0.0)

    dp_count = lax.axis_size("dp")
    with_ring = ring_fits(dp_count, width + w_fc1.shape[2]) and ring_fits(
        dp_count, 4 * local_width
    )
    gradient, *sums = run_backward(
        dp_count if with_ring else None,
        (
            gradient,
            branch_a,
            branch_b,
            normal_a,
            normal_b,
            inverse,
            mixture,
            qkv,
            shares,
            gath_a,
            active,
            slope,
            gath_b,
            qkv_used,
            out_used,
            w_fc1,
            w_fc2,
            *spots,
            ln_gain,
            layer_scale,
        ),
        head_count,
    )
    if not with_ring:
        sums = lax.psum(sums, "dp")
    *weight_sums, small = sums
    d_qkv, d_out, d_up, d_down = [leaf.astype(F32) for leaf in weight_sums]
    d_qkv = jnp.transpose(d_qkv.reshape(layer_count, 3, local_width, width), (0, 3, 1, 2))
    kinds = small[: 8 * layer_count].reshape(4, layer_count, 2, width)
    first = 8 * layer_count
    d_bias = small[first : first + layer_count].reshape(layer_count, 3, wide)
    d_bias = d_bias[:, ::2, :local_width]
    first += layer_count
    d_up_bias = small[first : first + layer_count]
    first += layer_count
    d_table = small[first : first + layer_count * head_count, : rel_table.shape[1]]
    d_table = jnp.transpose(d_table.reshape(layer_count, head_count, -1), (0, 2, 1))
    return (
        result,
        gradient,
        d_qkv,
        d_bias,
        d_out,
        d_up,
        d_up_bias,
        d_down,
        d_table,
        *kinds,
    )


def solution(mesh):
    in_specs = (
        P(("dp", "tensor"), None),
        P(("dp", "tensor"), None),
        P("dp"),
        P("dp", None),
        P("dp", None),
        P(None, None, None, "tensor"),
        P(None, None, "tensor"),
        P(None, "tensor", None),
        P(None, None, "tensor"),
        P(None, "tensor"),
        P(None, "tensor", None),
        P(None, None, "tensor"),
        P(),
        P(),
        P(),
        P(),
    )
    out_specs = (
        P(("dp", "tensor"), None),
        P(("dp", "tensor"), None),
        P(None, None, None, "tensor"),
        P(None, None, "tensor"),
        P(None, "tensor", None),
        P(None, None, "tensor"),
        P(None, "tensor"),
        P(None, "tensor", None),
        P(None, None, "tensor"),
        P(),
        P(),
        P(),
        P(),
    )
    return jax.shard_map(
        per_device, mesh=mesh, in_specs=in_specs, out_specs=out_specs, check_vma=False
    )
```

```python
import functools
from typing import NamedTuple

import jax
import jax.numpy as jnp
from jax import lax
from jax.experimental import pallas as pl
from jax.experimental.pallas import tpu as pltpu
from jax.sharding import PartitionSpec as P

HEAD_DIM = 64
SIDE = 14
STRIDE = 2 * SIDE - 1
CELLS = SIDE * SIDE
CHUNK = 32
MESH = pl.DeviceIdType.MESH
BF16 = jnp.bfloat16
F32 = jnp.float32


def dot(left_side, right_side, left_axis=1, right_axis=0):
    return lax.dot_general(
        left_side,
        right_side,
        (((left_axis,), (right_axis,)), ((), ())),
        preferred_element_type=F32,
    )


class Group:
    def __init__(self, send_sems, recv_sems):
        own = lax.axis_index("tensor")
        self.core = own % 2
        self.near = own + 1 - 2 * self.core
        self.far = (own + 2) % 4
        self.far_chip = 1 - own // 2
        self.sems = (send_sems, recv_sems)

    def greet(self, barrier):
        for other in (self.near, self.far, self.far + 1 - 2 * self.core):
            pl.semaphore_signal(
                barrier, inc=1, device_id={"tensor": other}, device_id_type=MESH
            )
        return 3

    def copy(self, sent, arrived, source, target, other):
        return pltpu.make_async_remote_copy(
            src_ref=source,
            dst_ref=target,
            send_sem=self.sems[0].at[sent],
            recv_sem=self.sems[1].at[arrived],
            device_id={"tensor": other},
            device_id_type=MESH,
        )


class Exchange:
    COPIES = 10

    def __init__(self, group, base, gath, part, got, summed):
        self.group, self.base = group, base
        self.gath, self.part, self.got, self.summed = gath, part, got, summed
        self.rows = (part if gath is None else gath).shape[1] // 2
        self.keep = group.core * self.rows
        self.give = (1 - group.core) * self.rows

    def slot(self, stage):
        core = self.group.core
        return 2 + core + stage * (1 - 2 * core)

    def span(self, first):
        return pl.ds(pl.multiple_of(first, self.rows), self.rows)

    def symmetric(self, number, source, target, other):
        at = self.base + number
        return self.group.copy(at, at, source, target, other)

    def to_near(self):
        return self.symmetric(0, self.gath.at[0], self.gath.at[1], self.group.near)

    def across(self, stage):
        core, rows = self.group.core, self.span(self.keep)
        source = core + stage * (1 - 2 * core)
        return self.symmetric(
            2 + stage,
            self.gath.at[source, rows],
            self.gath.at[self.slot(stage), rows],
            self.group.far,
        )

    def relay(self, stage):
        rows = self.span(self.keep)
        return self.symmetric(
            4 + stage,
            self.gath.at[self.slot(stage), rows],
            self.gath.at[self.slot(1 - stage), rows],
            self.group.near,
        )

    def sum_near(self):
        return self.symmetric(1, self.part.at[1], self.got.at[0], self.group.near)

    def pair(self, stage):
        return self.symmetric(
            6 + stage,
            self.part.at[self.slot(stage), self.span(self.give)],
            self.got.at[1, self.span(stage * self.rows)],
            self.group.near,
        )

    def home(self, stage, sender):
        return self.group.copy(
            self.base + 8 + stage,
            self.base + 8 + sender,
            self.summed.at[self.span(stage * self.rows)],
            self.got.at[2, self.span(sender * self.rows)],
            self.group.far_chip * 2 + stage,
        )

    def start(self):
        self.to_near().start()

        @pl.when(self.group.core == 0)
        def _():
            self.across(0).start()

    def spread(self):
        self.to_near().wait_recv()

        @pl.when(self.group.core == 1)
        def _():
            self.across(0).start()

        self.across(1).start()

    def pass_on(self, stage):
        self.across(stage).wait_recv()
        self.relay(stage).start()

    def arrived(self, stage):
        self.relay(stage).wait_recv()

    def send_sum(self, stage):
        self.pair(stage).wait_recv()
        rows = self.span(stage * self.rows)
        self.summed[rows] = self.part[self.slot(stage), self.span(self.keep)] + self.got[1, rows]
        self.home(stage, self.group.core).start()

    def finish(self):
        self.sum_near().wait_recv()
        for sender in range(2):
            self.home(0, sender).wait_recv()

    def drain_gather(self):
        self.to_near().wait_send()
        for stage in range(2):
            self.across(stage).wait_send()
            self.relay(stage).wait_send()

    def drain_sum(self):
        self.sum_near().wait_send()
        for stage in range(2):
            self.pair(stage).wait_send()
            self.home(stage, self.group.core).wait_send()


def by_chunk(total_rows, body, size=CHUNK):
    def step(at, carry):
        return body(pl.ds(pl.multiple_of(at * size, size), size), carry)

    return step, total_rows // size


def norm_chunk(values, gain, shift):
    center = values - jnp.mean(values, -1, keepdims=True)
    inverse = lax.rsqrt(jnp.mean(center * center, -1, keepdims=True) + 1e-06)
    normal = center * inverse
    return (normal * gain + shift).astype(BF16), normal, inverse


def gelu_parts(values):
    share = 0.5 * (1.0 + lax.erf(values * 0.7071067811865476))
    slope = share + values * (jnp.exp(-0.5 * values * values) * 0.3989422804014327)
    return values * share, slope


SPAN = 384
LAST = (SIDE - 1) * (STRIDE + 1)
CLASS = LAST + 1
TABLE_WIDTH = 2 * SPAN


def prepare(head_count, lengths, index_rows, table, bias, spots, turned, same):
    rows = bias.shape[3]
    own = lax.axis_index("tensor")
    order = (own, own + 1 - 2 * (own % 2), (own + 2) % 4, 3 - own)

    ones = []
    for slot in range(4):
        first = lengths[order[slot], 0]
        both = first + lengths[order[slot], 1]

        def pick(row):
            return index_rows[pl.ds(order[slot] * rows + row, 1), :]

        at = lax.broadcasted_iota(jnp.int32, (1, rows), 1)
        code = LAST - jnp.where(at < first, pick(1), pick(first + 1))
        code = jnp.where((at == 0) | (at == first), CLASS, code)
        code = jnp.where(at < both, code, -1)
        upright = lax.broadcasted_iota(jnp.int32, (SPAN, rows), 0)
        spots[slot] = (upright == code).astype(F32).astype(BF16)
        column = jnp.transpose(jnp.broadcast_to(code.astype(F32), (128, rows)))
        column = jnp.concatenate([column] * (SPAN // 128), -1)
        flat = lax.broadcasted_iota(jnp.int32, (rows, SPAN), 1).astype(F32)
        ones.append((flat == column).astype(F32).astype(BF16))
        mirrored = jnp.where(column < CLASS, LAST - column, column)
        mirrored = jnp.where(column < 0, -1.0, mirrored)
        turned[slot] = (flat == mirrored).astype(F32).astype(BF16)

        def image_of(values):
            return (values >= first).astype(jnp.int32) + (values >= both).astype(jnp.int32)

        by_row = image_of(lax.broadcasted_iota(jnp.int32, (rows, rows), 0))
        by_col = image_of(lax.broadcasted_iota(jnp.int32, (rows, rows), 1))
        same[slot] = (by_row == by_col).astype(F32)

    key_at = lax.broadcasted_iota(jnp.int32, (SPAN, SPAN), 0)
    query_at = lax.broadcasted_iota(jnp.int32, (SPAN, SPAN), 1)
    shift = SPAN - LAST

    def each(at, carry):
        row = table[pl.ds(at, 1), :]
        rolled = pltpu.roll(
            jnp.broadcast_to(row, (SPAN, TABLE_WIDTH)), 0, 1, stride=1, stride_axis=0
        )
        pairs = rolled[:, SPAN:]
        tail = shift + STRIDE * STRIDE
        pairs = jnp.where(query_at == CLASS, row[:, tail : tail + 1], pairs)
        pairs = jnp.where(key_at == CLASS, row[:, tail + 1 : tail + 2], pairs)
        pairs = jnp.where(
            (query_at == CLASS) & (key_at == CLASS), row[:, tail + 2 : tail + 3], pairs
        ).astype(BF16)
        for slot in range(4):
            half = dot(ones[slot], pairs, 1, 1).astype(BF16)
            looked = dot(half, spots[slot])
            bias[at // head_count, slot, at % head_count] = jnp.where(
                same[slot] > 0.5, looked, -1000000000.0
            ).astype(BF16)
        return carry

    lax.fori_loop(0, table.shape[0], each, 0)


def shifted_table(rel_table):
    layers, entries, head_count = rel_table.shape
    shift = SPAN - LAST
    table = jnp.transpose(rel_table, (0, 2, 1)).reshape(layers * head_count, entries).astype(F32)
    return jnp.pad(table, ((0, 0), (shift, TABLE_WIDTH - shift - entries)))


def table_row(pairs):
    query_at = lax.broadcasted_iota(jnp.int32, (SPAN, SPAN), 0)
    key_at = lax.broadcasted_iota(jnp.int32, (SPAN, SPAN), 1)
    zero = jnp.zeros((SPAN, SPAN), F32)
    patches = jnp.where((query_at <= LAST) & (key_at <= LAST), pairs, zero)
    rolled = pltpu.roll(
        jnp.concatenate([patches, zero], -1), 0, 1, stride=1, stride_axis=0
    )
    row = jnp.sum(rolled, 0, keepdims=True)
    at = lax.broadcasted_iota(jnp.int32, (1, TABLE_WIDTH), 1)
    tails = (
        (query_at == CLASS) & (key_at <= LAST),
        (query_at <= LAST) & (key_at == CLASS),
        (query_at == CLASS) & (key_at == CLASS),
    )
    for number, mask in enumerate(tails):
        row = jnp.where(at == STRIDE * STRIDE + number, jnp.sum(jnp.where(mask, pairs, zero)), row)
    return row


class Names:
    def __init__(self, names, refs):
        for name, ref in zip(names, refs, strict=True):
            setattr(self, name, ref)


def load_all(pairs, sems):
    steps = []
    for place, (source, target) in enumerate(pairs):
        step = pltpu.make_async_copy(source, target, sems.at[place])
        step.start()
        steps.append(step)
    return steps


def each_chunk(rows, body):
    def step(at, carry):
        body(pl.ds(pl.multiple_of(at * CHUNK, CHUNK), CHUNK))
        return carry

    lax.fori_loop(0, rows // CHUNK, step, 0)


def attend_rows(refs, at, slot, first, head_count):
    qkv = refs.qkv
    rows = qkv.shape[2] // 2
    wide = qkv.shape[3] // 3
    span = pl.ds(first, rows)
    heads = []
    for head in range(head_count):
        lanes = slice(head * HEAD_DIM, (head + 1) * HEAD_DIM)
        queries = qkv[at, slot, span, 0:wide][:, lanes]
        keys = qkv[at, slot, :, wide : 2 * wide][:, lanes]
        values = qkv[at, slot, :, 2 * wide : 3 * wide][:, lanes]
        scores = dot(queries, keys, 1, 1) + refs.bias[at, slot, head, span].astype(F32)
        powers = jnp.exp(scores - jnp.max(scores, -1, keepdims=True))
        weights = (powers / jnp.sum(powers, -1, keepdims=True)).astype(BF16)
        refs.weights[at, slot, head, span] = weights
        heads.append(dot(weights, values).astype(BF16))
    heads.append(jnp.zeros((rows, wide - head_count * HEAD_DIM), BF16))
    refs.mixture[at, slot, span] = jnp.concatenate(heads, -1)


class ForwardInputs(NamedTuple):
    lengths: object
    tokens: object
    cotangent: object
    qv_bias: object
    fc1_bias: object
    table: object
    ln_gain: object
    ln_bias: object
    layer_scale: object
    row_bias: object
    index_in: object
    w_qkv_in: object
    w_out_in: object
    w_up_in: object
    w_down_in: object


class ForwardKept(NamedTuple):
    gath_a: object
    qkv: object
    weights: object
    mixture: object
    gath_b: object
    slope: object
    active: object


class ForwardOutputs(NamedTuple):
    gath_z_out: object
    spots: object
    turned: object
    grad: object
    normal_a: object
    normal_b: object
    inverse: object
    branch_a: object
    branch_b: object
    stream: object


class ForwardScratch(NamedTuple):
    gath_z: object
    bias: object
    same: object
    index_rows: object
    w_qkv: object
    w_out: object
    w_up: object
    w_down: object
    qkv_bias: object
    up_bias: object
    hidden: object
    part: object
    got: object
    summed: object
    own: object
    send_sems: object
    recv_sems: object
    load_sems: object
    out_sems: object


def forward_body(layers, head_count, *all_refs):
    kept_outs = tuple(name + "_kept" for name in ForwardKept._fields)
    refs = Names(
        (*ForwardInputs._fields, *kept_outs, *ForwardOutputs._fields, *ForwardKept._fields, *ForwardScratch._fields), all_refs
    )
    stream, own, got, part = refs.stream, refs.own, refs.got, refs.part
    rows, width = stream.shape
    half = rows // 2
    last = layers - 1
    used = refs.w_out_in.shape[1]
    wide = refs.w_out.shape[1]
    loads = load_all(
        (
            (refs.index_in, refs.index_rows),
            (refs.w_qkv_in, refs.w_qkv),
            *(
                (refs.w_out_in.at[at], refs.w_out.at[at, pl.ds(0, used)])
                for at in range(layers)
            ),
            (refs.w_up_in, refs.w_up),
            (refs.w_down_in, refs.w_down),
        ),
        refs.load_sems,
    )
    group = Group(refs.send_sems, refs.recv_sems)
    barrier = pltpu.get_barrier_semaphore()
    greeted = group.greet(barrier)
    pl.semaphore_wait(barrier, greeted)
    early = Exchange(group, 2 * Exchange.COPIES, refs.gath_z, None, None, None)

    def load(span):
        stream[span] = refs.tokens[span].astype(F32)

    each_chunk(rows, load)
    refs.qkv_bias[...] = jnp.zeros_like(refs.qkv_bias)
    for at in range(layers):
        refs.w_out[at, used:] = jnp.zeros_like(refs.w_out[at, used:])
        refs.up_bias[at] = refs.fc1_bias[at : at + 1].astype(F32)
        for half_at in range(2):
            first = 2 * half_at * wide
            refs.qkv_bias[at, :, first : first + used] = refs.qv_bias[
                at, half_at : half_at + 1
            ].astype(F32)

    def keep(number, at):
        source = getattr(refs, ForwardKept._fields[number])
        target = getattr(refs, kept_outs[number])
        return pltpu.make_async_copy(source.at[at], target.at[at], refs.out_sems.at[number, at])

    def layer(at, carry):
        trade = Exchange(group, 0, refs.gath_a.at[at], part, got, refs.summed)

        def enter(span):
            low, normal, inv = norm_chunk(
                stream[span], refs.ln_gain[at, 0:1], refs.ln_bias[at, 0:1]
            )
            refs.gath_a[at, 0, span] = low
            refs.normal_a[at, span] = normal
            refs.inverse[at, 0, span] = jnp.broadcast_to(inv, (CHUNK, 128))

        each_chunk(rows, enter)
        trade.start()

        @pl.when(at == 0)
        def _():
            place = lax.axis_index("tensor")
            length = refs.lengths[place, 0] + refs.lengths[place, 1]

            def mask(number, carry):
                span = pl.ds(pl.multiple_of(number * CHUNK, CHUNK), CHUNK)
                row = number * CHUNK + lax.broadcasted_iota(jnp.int32, (CHUNK, width), 0)
                values = jnp.where(row < length, refs.cotangent[span].astype(F32), 0.0)
                refs.grad[span] = values
                refs.gath_z[0, span] = (values * refs.layer_scale[last, 1:2]).astype(BF16)
                return carry

            lax.fori_loop(0, rows // CHUNK, mask, 0)

        trade.spread()

        @pl.when(at == 0)
        def _():
            early.start()
            early.spread()
            loads[0].wait()
            prepare(
                head_count,
                refs.lengths,
                refs.index_rows,
                refs.table,
                refs.bias,
                refs.spots,
                refs.turned,
                refs.same,
            )
            for step in loads[1:]:
                step.wait()

        scale = jnp.concatenate(
            [
                jnp.full((1, refs.qkv.shape[3] // 3), HEAD_DIM**-0.5, F32),
                jnp.full((1, 2 * refs.qkv.shape[3] // 3), 1.0, F32),
            ],
            -1,
        )

        def project(slot):
            mixed = dot(refs.gath_a[at, slot], refs.w_qkv[at])
            mixed = (mixed + refs.qkv_bias[at]).astype(BF16).astype(F32) * scale
            refs.qkv[at, slot] = mixed.astype(BF16)

        def attend(slot, first):
            attend_rows(refs, at, slot, first, head_count)
            return dot(refs.mixture[at, slot, pl.ds(first, half)], refs.w_out[at])

        def chip_slot(slot, carry):
            project(slot)

            def one(place, carry):
                first = pl.multiple_of(place * half, half)
                result = attend(slot, first)

                @pl.when(slot == 0)
                def _():
                    own[pl.ds(first, half)] = result

                @pl.when(slot == 1)
                def _():
                    part[1, pl.ds(first, half)] = result.astype(BF16)

                return carry

            lax.fori_loop(0, 2, one, 0)
            return carry

        lax.fori_loop(0, 2, chip_slot, 0)
        trade.sum_near().start()
        trade.pass_on(0)

        def far_slot(stage, carry):
            slot = trade.slot(stage)
            trade.arrived(stage)
            project(slot)

            def one(place, carry):
                first = pl.multiple_of(
                    place * trade.keep + (1 - place) * trade.give, half
                )
                part[slot, pl.ds(first, half)] = attend(slot, first).astype(BF16)

                @pl.when(place == 0)
                def _():
                    trade.pair(stage).start()

                return carry

            lax.fori_loop(0, 2, one, 0)
            trade.send_sum(stage)

            @pl.when(stage == 0)
            def _():
                trade.pass_on(1)

            return carry

        lax.fori_loop(0, 2, far_slot, 0)
        for number in range(4):
            keep(number, at).start()

        @pl.when(at == 0)
        def _():
            for stage in range(2):
                early.pass_on(stage)

        trade.finish()

        def between(span):
            total = own[span] + got[0, span].astype(F32) + got[2, span].astype(F32)
            branch = total + refs.row_bias[at, 0:1]
            refs.branch_a[at, span] = branch
            middle = stream[span] + refs.layer_scale[at, 0:1] * branch
            stream[span] = middle
            low, normal, inv = norm_chunk(middle, refs.ln_gain[at, 1:2], refs.ln_bias[at, 1:2])
            refs.gath_b[at, 0, span] = low
            refs.normal_b[at, span] = normal
            refs.inverse[at, 1, span] = jnp.broadcast_to(inv, (CHUNK, 128))

        each_chunk(rows, between)

        @pl.when(at < last)
        def _():
            trade_b = Exchange(
                group, Exchange.COPIES, refs.gath_b.at[at], part, got, refs.summed
            )
            trade_b.start()
            trade.drain_gather()
            trade.drain_sum()
            trade_b.spread()

            def raise_rows(slot):
                refs.hidden[...] = dot(refs.gath_b[at, slot], refs.w_up[at]) + refs.up_bias[at]

                def act(place, carry):
                    span = pl.ds(pl.multiple_of(place * 16, 16), 16)
                    high, incline = gelu_parts(refs.hidden[span])
                    refs.active[at, slot, span] = high.astype(BF16)
                    refs.slope[at, slot, span] = incline.astype(BF16)
                    return carry

                lax.fori_loop(0, rows // 16, act, 0)

            def lower(slot, first, count):
                return dot(refs.active[at, slot, pl.ds(first, count)], refs.w_down[at])

            def chip_slot(slot, carry):
                raise_rows(slot)
                result = lower(slot, 0, rows)

                @pl.when(slot == 0)
                def _():
                    own[...] = result

                @pl.when(slot == 1)
                def _():
                    part[1] = result.astype(BF16)

                return carry

            lax.fori_loop(0, 2, chip_slot, 0)
            trade_b.sum_near().start()
            trade_b.pass_on(0)

            def far_slot(stage, carry):
                slot = trade_b.slot(stage)
                trade_b.arrived(stage)
                raise_rows(slot)

                def one(place, carry):
                    first = pl.multiple_of(
                        place * trade_b.keep + (1 - place) * trade_b.give, half
                    )
                    part[slot, pl.ds(first, half)] = lower(slot, first, half).astype(BF16)

                    @pl.when(place == 0)
                    def _():
                        trade_b.pair(stage).start()

                    return carry

                lax.fori_loop(0, 2, one, 0)
                trade_b.send_sum(stage)

                @pl.when(stage == 0)
                def _():
                    trade_b.pass_on(1)

                return carry

            lax.fori_loop(0, 2, far_slot, 0)
            for number in (4, 5, 6):
                keep(number, at).start()
            trade_b.finish()

            def after(span):
                total = own[span] + got[0, span].astype(F32) + got[2, span].astype(F32)
                branch = total + refs.row_bias[at, 1:2]
                refs.branch_b[at, span] = branch
                stream[span] = stream[span] + refs.layer_scale[at, 1:2] * branch

            each_chunk(rows, after)
            trade_b.drain_gather()
            trade_b.drain_sum()

        @pl.when(at == last)
        def _():
            pltpu.make_async_copy(
                refs.gath_b.at[at, 0], refs.gath_b_kept.at[at, 0], refs.out_sems.at[4, at]
            ).start()
            trade.drain_gather()
            trade.drain_sum()

        return carry

    lax.fori_loop(0, layers, layer, 0)
    for stage in range(2):
        early.arrived(stage)
    early.drain_gather()
    leave = pltpu.make_async_copy(refs.gath_z, refs.gath_z_out, refs.load_sems.at[0])
    leave.start()
    pltpu.make_async_copy(
        refs.gath_b.at[last, 0], refs.gath_b_kept.at[last, 0], refs.out_sems.at[4, last]
    ).wait()
    for at in range(layers):
        for number in range(len(ForwardKept._fields)):
            if at < last or number < 4:
                keep(number, at).wait()
    leave.wait()


def run_forward(lengths, index_rows, rel_table, rows_in, weights, norms):
    tokens, cotangent = rows_in
    rows, width = tokens.shape
    w_qkv, qv_bias, w_out, w_up, fc1_bias, w_down = weights
    layers, _, head_count = rel_table.shape
    wide = w_qkv.shape[2] // 3
    inner = w_up.shape[2]
    in_vmem = pl.BlockSpec(memory_space=pltpu.VMEM)
    in_hbm = pl.BlockSpec(memory_space=pl.ANY)

    def low(*shape):
        return jax.ShapeDtypeStruct(shape, BF16)

    def full(*shape):
        return jax.ShapeDtypeStruct(shape, F32)

    kept = [
        low(layers, 4, *tail)
        for tail in (
            (rows, width),
            (rows, 3 * wide),
            (head_count, rows, rows),
            (rows, wide),
            (rows, width),
            (rows, inner),
            (rows, inner),
        )
    ]
    own = full(rows, width)
    by_layer = full(layers, rows, width)
    near = [low(4, SPAN, rows), low(4, rows, SPAN), own, by_layer, by_layer]
    near += [full(layers, 2, rows, 128), by_layer, by_layer, own]
    scratch = [
        *kept,
        low(4, rows, width),
        low(layers, 4, head_count, rows, rows),
        full(4, rows, rows),
        jax.ShapeDtypeStruct(index_rows.shape, index_rows.dtype),
        low(*w_qkv.shape),
        low(layers, wide, width),
        low(*w_up.shape),
        low(*w_down.shape),
        full(layers, 1, 3 * wide),
        full(layers, 1, inner),
        full(rows, inner),
        low(4, rows, width),
        low(3, rows, width),
        low(rows, width),
        own,
    ]
    copies = 3 * Exchange.COPIES
    return pl.pallas_call(
        functools.partial(forward_body, layers, head_count),
        name="forward",
        out_shape=[*kept, low(4, rows, width), *near],
        in_specs=[pl.BlockSpec(memory_space=pltpu.SMEM)] + [in_vmem] * 9 + [in_hbm] * 5,
        out_specs=[in_hbm] * (len(kept) + 1) + [in_vmem] * len(near),
        scratch_shapes=[
            *[pltpu.VMEM(leaf.shape, leaf.dtype) for leaf in scratch],
            pltpu.SemaphoreType.DMA((copies,)),
            pltpu.SemaphoreType.DMA((copies,)),
            pltpu.SemaphoreType.DMA((4 + layers,)),
            pltpu.SemaphoreType.DMA((len(kept), layers)),
        ],
        compiler_params=pltpu.CompilerParams(
            collective_id=0, has_side_effects=True, vmem_limit_bytes=65400 * 1024
        ),
    )(
        lengths,
        tokens,
        cotangent,
        qv_bias,
        fc1_bias,
        shifted_table(rel_table),
        *norms,
        index_rows,
        w_qkv,
        w_out,
        w_up,
        w_down,
    )


def fold(values):
    return jnp.sum(values.reshape(-1, 8, values.shape[-1]), 0)


def enter_back(grad, branch, scale, gath, sums):
    rows, width = grad.shape

    def body(span, carry):
        values = grad[span]
        gath[0, span] = (values * scale).astype(BF16)
        return carry[0] + fold(values * branch[span]), carry[1] + fold(values)

    step, count = by_chunk(rows, body)
    zero = jnp.zeros((8, width), F32)
    by_branch, alone = lax.fori_loop(0, count, step, (zero, zero))
    sums[2:3] = jnp.sum(by_branch, 0, keepdims=True)
    sums[3:4] = jnp.sum(alone, 0, keepdims=True) * scale


def leave_back(grad, own, got, normal, inverse, gain, sums):
    rows, width = grad.shape

    def body(span, carry):
        total = own[span] + got[0, span].astype(F32) + got[2, span].astype(F32)
        unit = normal[span]
        scaled = total * gain
        centered = (
            scaled
            - jnp.mean(scaled, -1, keepdims=True)
            - unit * jnp.mean(scaled * unit, -1, keepdims=True)
        )
        grad[span] = grad[span] + inverse[span, 0:1] * centered
        return carry[0] + fold(total * unit), carry[1] + fold(total)

    step, count = by_chunk(rows, body)
    zero = jnp.zeros((8, width), F32)
    by_unit, alone = lax.fori_loop(0, count, step, (zero, zero))
    sums[0:1] = jnp.sum(by_unit, 0, keepdims=True)
    sums[1:2] = jnp.sum(alone, 0, keepdims=True)


def weight_grad(left, right, out, start, count, tick=None):
    block = 256
    used = count * block // left.shape[2]

    def step(place, carry):
        span = pl.ds(pl.multiple_of(place * block, block), block)
        total = None
        for slot in range(4):
            term = dot(left[slot, :, span], right[slot], 0, 0)
            total = term if total is None else total + term
        there = pl.ds(pl.multiple_of(start + place * used, 16), used)
        out[there] = total[:used].astype(out.dtype)
        return carry

    if tick is None:
        lax.fori_loop(0, left.shape[2] // block, step, 0)
    else:
        for place in range(left.shape[2] // block):
            step(place, 0)
            tick()


PIECES = 2


class Ticker:
    def __init__(self, ring):
        self.ring = ring
        self.under_way = []

    def add(self, streams):
        self.ring.start(streams)
        self.under_way.append([streams, 0])

    def tick(self):
        if self.under_way:
            self.one()

    def one(self):
        ring = self.ring
        streams, step = self.under_way.pop(0)
        turn = ring.count - 1
        for stream in streams:
            if step < turn:
                ring.add(stream, step)
                ring.copy(stream, step, False).wait_send()
            else:
                ring.copy(stream, step, True).wait_recv()
            if step + 1 < ring.steps:
                ring.copy(stream, step + 1, step + 1 >= turn).start()
        if step + 1 < ring.steps:
            self.under_way.append([streams, step + 1])
        else:
            ring.drain(streams)

    def alike(self, step):
        turn = self.ring.count - 1
        return turn - 1 - step if step < turn else self.ring.steps - 1 - step

    def finish(self):
        ring = self.ring
        turn = ring.count - 1
        while self.under_way:
            run = min(self.alike(step) for _, step in self.under_way)
            if run < 2:
                for _ in range(len(self.under_way)):
                    self.one()
                continue
            rings = list(self.under_way)

            def body(number, carry):
                for streams, start in rings:
                    step = start + number
                    for stream in streams:
                        if start < turn:
                            ring.add(stream, step)
                            ring.copy(stream, step, False).wait_send()
                        else:
                            ring.copy(stream, step, True).wait_recv()
                        ring.copy(stream, step + 1, start >= turn).start()
                return carry

            lax.fori_loop(0, run, body, 0)
            for leaf in self.under_way:
                leaf[1] += run


def mlp_loads(refs, at):
    return load_all(
        (
            (refs.branch_b_all.at[at], refs.branch_b),
            (refs.w_down_all.at[at], refs.w_down),
            (refs.slope_all.at[at], refs.slope),
            (refs.w_up_all.at[at], refs.w_up),
            (refs.normal_b_all.at[at], refs.normal_b),
            (refs.inverse_all.at[at, 1], refs.inverse_b),
            (refs.active_all.at[at], refs.active),
            (refs.gath_b_all.at[at], refs.gath_b),
        ),
        refs.load_sems.at[1 + 2 * at],
    )


def attend_loads(refs, at):
    return load_all(
        (
            (refs.branch_a_all.at[at], refs.branch_a),
            (refs.w_out_all.at[at], refs.w_out.at[pl.ds(0, refs.w_out_all.shape[1])]),
            (refs.qkv_all.at[at], refs.qkv),
            (refs.weights_all.at[at], refs.weights),
            (refs.w_qkv_all.at[at], refs.w_qkv),
            (refs.normal_a_all.at[at], refs.normal_a),
            (refs.inverse_all.at[at, 0], refs.inverse_a),
            (refs.mixture_all.at[at], refs.mixture),
            (refs.gath_a_all.at[at], refs.gath_a),
        ),
        refs.load_sems.at[2 + 2 * at],
    )


def front(refs, group, at, tick, begin):
    rows = refs.grad.shape[0]
    half = rows // 2
    ahead = Exchange(
        group, Exchange.COPIES, refs.gath_b, refs.part_f, refs.got_f, refs.summed_f
    )
    trade = Exchange(group, 0, None, refs.part, refs.got, refs.summed)
    loads = load_all(
        (
            (refs.gath_b_all.at[at, 0], refs.gath_b.at[0]),
            (refs.w_up_all.at[at], refs.w_up),
            (refs.w_down_all.at[at], refs.w_down),
            (refs.gath_z, refs.gath_m),
            (refs.normal_b_all.at[at], refs.normal_b),
            (refs.inverse_all.at[at, 1], refs.inverse_b),
        ),
        refs.load_sems.at[0],
    )
    loads[0].wait()
    ahead.start()
    ahead.spread()
    for load in loads[1:4]:
        load.wait()

    def work(slot):
        refs.hidden[...] = dot(refs.gath_b[slot], refs.w_up[...]) + refs.up_bias[at : at + 1].astype(F32)
        refs.hidden_f[...] = dot(refs.gath_m[slot], refs.w_down[...], 1, 1)

        def act(place, carry):
            span = pl.ds(pl.multiple_of(place * 16, 16), 16)
            high, incline = gelu_parts(refs.hidden[span])
            refs.active[slot, span] = high.astype(BF16)
            back = (refs.hidden_f[span] * incline).astype(BF16)
            refs.d_hidden[slot, span] = back
            refs.up_total[...] += fold(back.astype(F32))
            return carry

        lax.fori_loop(0, rows // 16, act, 0)

    refs.up_total[...] = jnp.zeros_like(refs.up_total)

    def chip_slot(slot, carry):
        work(slot)
        result = dot(refs.d_hidden[slot], refs.w_up[...], 1, 1)
        result_f = dot(refs.active[slot], refs.w_down[...])

        @pl.when(slot == 0)
        def _():
            refs.own[...] = result
            refs.own_f[...] = result_f

        @pl.when(slot == 1)
        def _():
            refs.part[1] = result.astype(BF16)
            refs.part_f[1] = result_f.astype(BF16)

        return carry

    lax.fori_loop(0, 2, chip_slot, 0)
    trade.sum_near().start()
    ahead.sum_near().start()
    ahead.pass_on(0)

    def far_slot(stage, carry):
        slot = ahead.slot(stage)
        ahead.arrived(stage)
        work(slot)

        def one(place, carry):
            first = pl.multiple_of(place * ahead.keep + (1 - place) * ahead.give, half)
            span = pl.ds(first, half)
            refs.part[slot, span] = dot(
                refs.d_hidden[slot, span], refs.w_up[...], 1, 1
            ).astype(BF16)

            @pl.when(place == 0)
            def _():
                trade.pair(stage).start()

            refs.part_f[slot, span] = dot(refs.active[slot, span], refs.w_down[...]).astype(BF16)

            @pl.when(place == 0)
            def _():
                ahead.pair(stage).start()

            return carry

        lax.fori_loop(0, 2, one, 0)
        trade.send_sum(stage)
        ahead.send_sum(stage)

        @pl.when(stage == 0)
        def _():
            ahead.pass_on(1)

        return carry

    lax.fori_loop(0, 2, far_slot, 0)
    data, inner = refs.data_m.at[at], refs.w_down.shape[0]
    weight_grad(refs.active, refs.gath_m, data, 0, inner)
    weight_grad(refs.gath_b, refs.d_hidden, data, inner, refs.w_up.shape[0])
    begin(at, 0)
    refs.up_sums[at : at + 1] = jnp.sum(refs.up_total[...], 0, keepdims=True)
    for load in loads[4:]:
        load.wait()
    trade.finish()
    tick()
    leave_back(
        refs.grad,
        refs.own,
        refs.got,
        refs.normal_b,
        refs.inverse_b,
        refs.ln_gain[at, 1:2],
        refs.sums.at[2 * at + 1],
    )
    ahead.drain_gather()
    trade.drain_sum()

    def end():
        ahead.finish()
        sums = refs.sums.at[2 * at + 1]
        scale = refs.layer_scale[at, 1:2]
        width = refs.grad.shape[1]

        def body(span, carry):
            branch = (
                refs.own_f[span]
                + refs.got_f[0, span].astype(F32)
                + refs.got_f[2, span].astype(F32)
                + refs.row_bias[at, 1:2]
            )
            refs.stream[span] = refs.middle[span] + scale * branch
            values = refs.grad_in[span]
            return carry[0] + fold(values * branch), carry[1] + fold(values)

        step, count = by_chunk(rows, body)
        zero = jnp.zeros((8, width), F32)
        by_branch, alone = lax.fori_loop(0, count, step, (zero, zero))
        sums[2:3] = jnp.sum(by_branch, 0, keepdims=True)
        sums[3:4] = jnp.sum(alone, 0, keepdims=True) * scale
        ahead.drain_sum()

    return end


def back_mlp(refs, group, base, at, loads, tick, begin):
    rows = refs.grad.shape[0]
    half = rows // 2
    gath, part, hidden, d_hidden = refs.gath_m, refs.part, refs.hidden, refs.d_hidden
    trade = Exchange(group, base, gath, part, refs.got, refs.summed)
    sums = refs.sums.at[2 * at + 1]
    loads[0].wait()
    enter_back(refs.grad, refs.branch_b, refs.layer_scale[at, 1:2], gath, sums)
    trade.start()
    tick()
    trade.spread()
    for load in loads[1:4]:
        load.wait()

    refs.up_total[...] = jnp.zeros_like(refs.up_total)

    def down(slot):
        hidden[...] = dot(gath[slot], refs.w_down[...], 1, 1)

        def body(place, carry):
            span = pl.ds(pl.multiple_of(place * CHUNK, CHUNK), CHUNK)
            low = (hidden[span] * refs.slope[slot, span].astype(F32)).astype(BF16)
            d_hidden[slot, span] = low
            return carry + fold(low.astype(F32))

        zero = jnp.zeros((8, hidden.shape[1]), F32)
        refs.up_total[...] += lax.fori_loop(0, rows // CHUNK, body, zero)

    def back(slot, first, count):
        return dot(d_hidden[slot, pl.ds(first, count)], refs.w_up[...], 1, 1)

    down(0)
    tick()
    refs.own[...] = back(0, 0, rows)
    tick()
    down(1)
    part[1] = back(1, 0, rows).astype(BF16)
    trade.sum_near().start()
    tick()
    trade.pass_on(0)
    for stage in range(2):
        slot = trade.slot(stage)
        trade.arrived(stage)
        down(slot)
        tick()

        def one(place, carry):
            first = pl.multiple_of(place * trade.keep + (1 - place) * trade.give, half)
            part[slot, pl.ds(first, half)] = back(slot, first, half).astype(BF16)

            @pl.when(place == 0)
            def _():
                trade.pair(stage).start()

            return carry

        lax.fori_loop(0, 2, one, 0)
        trade.send_sum(stage)
        if stage == 0:
            trade.pass_on(1)
        tick()
    refs.up_sums[at : at + 1] = jnp.sum(refs.up_total[...], 0, keepdims=True)
    for load in loads[4:]:
        load.wait()
    data, inner = refs.data_m.at[at], refs.w_down.shape[0]
    weight_grad(refs.active, gath, data, 0, inner)
    tick()
    weight_grad(refs.gath_b, d_hidden, data, inner, refs.w_up.shape[0])
    begin(at, 0)
    tick()
    trade.finish()
    leave_back(
        refs.grad,
        refs.own,
        refs.got,
        refs.normal_b,
        refs.inverse_b,
        refs.ln_gain[at, 1:2],
        sums,
    )
    trade.drain_gather()
    trade.drain_sum()
    tick()


def back_attend(refs, group, base, at, head_count, loads, tick, begin, meanwhile):
    rows = refs.grad.shape[0]
    half = rows // 2
    data = refs.data_t.at[at]
    wide = refs.mixture.shape[2]
    gath, part, d_mixed, d_scores = refs.gath_t, refs.part, refs.d_mixed, refs.d_scores
    qkv = refs.qkv
    trade = Exchange(group, base, gath, part, refs.got, refs.summed)
    sums = refs.sums.at[2 * at]
    loads[0].wait()
    enter_back(refs.grad, refs.branch_a, refs.layer_scale[at, 0:1], gath, sums)
    trade.start()
    tick()
    trade.spread()
    if meanwhile is not None:
        meanwhile()
        tick()
    for load in loads[1:5]:
        load.wait()
    spare = jnp.zeros((rows, wide - head_count * HEAD_DIM), BF16)

    def attend(slot):
        d_mix = dot(gath[slot], refs.w_out[...], 1, 1).astype(BF16)
        pieces = ([], [], [])
        for head in range(head_count):
            lanes = slice(head * HEAD_DIM, (head + 1) * HEAD_DIM)
            queries = qkv[slot, :, 0:wide][:, lanes]
            keys = qkv[slot, :, wide : 2 * wide][:, lanes]
            values = qkv[slot, :, 2 * wide : 3 * wide][:, lanes]
            share = refs.weights[slot, head]
            d_head = d_mix[:, lanes]
            wide_share = share.astype(F32)
            d_share = dot(d_head, values, 1, 1)
            middle = jnp.sum(wide_share * d_share, -1, keepdims=True)
            d_score = (wide_share * (d_share - middle)).astype(BF16)
            d_scores[slot, head] = d_score
            pieces[0].append((dot(d_score, keys) * HEAD_DIM**-0.5).astype(BF16))
            pieces[1].append(dot(d_score, queries, 0, 0).astype(BF16))
            pieces[2].append(dot(share, d_head, 0, 0).astype(BF16))
        for place in range(3):
            d_mixed[slot, :, place * wide : (place + 1) * wide] = jnp.concatenate(
                pieces[place] + [spare], -1
            )

    def back(slot, first, count):
        return dot(d_mixed[slot, pl.ds(first, count)], refs.w_qkv[...], 1, 1)

    attend(0)
    tick()
    refs.own[...] = back(0, 0, rows)
    attend(1)
    tick()
    part[1] = back(1, 0, rows).astype(BF16)
    trade.sum_near().start()
    trade.pass_on(0)
    for stage in range(2):
        slot = trade.slot(stage)
        trade.arrived(stage)
        attend(slot)
        tick()

        def one(place, carry):
            first = pl.multiple_of(place * trade.keep + (1 - place) * trade.give, half)
            part[slot, pl.ds(first, half)] = back(slot, first, half).astype(BF16)

            @pl.when(place == 0)
            def _():
                trade.pair(stage).start()

            return carry

        lax.fori_loop(0, 2, one, 0)
        trade.send_sum(stage)
        if stage == 0:
            trade.pass_on(1)
        tick()
    for load in loads[5:]:
        load.wait()

    def add(slot, total):
        def body(span, carry):
            return carry + fold(d_mixed[slot, span].astype(F32))

        step, count = by_chunk(rows, body)
        return lax.fori_loop(0, count, step, total)

    total = jnp.zeros((8, 3 * wide), F32)
    for slot in range(4):
        total = add(slot, total)
    refs.qkv_sums[at : at + 1] = jnp.sum(total, 0, keepdims=True)
    used = 3 * head_count * HEAD_DIM
    weight_grad(d_mixed, refs.gath_a, data, 0, used)
    tick()
    weight_grad(refs.mixture, gath, data, used, used // 3)
    begin(at, 1)
    tick()
    for head in range(head_count):
        total = None
        for slot in range(4):
            placed = dot(refs.spots[slot], d_scores[slot, head]).astype(BF16)
            term = dot(placed, refs.turned[slot])
            total = term if total is None else total + term
        row = at * head_count + head
        refs.table_sums[row : row + 1] = table_row(total)
    trade.finish()
    leave_back(
        refs.grad,
        refs.own,
        refs.got,
        refs.normal_a,
        refs.inverse_a,
        refs.ln_gain[at, 0:1],
        sums,
    )
    trade.drain_gather()
    trade.drain_sum()
    tick()


class BackInputs(NamedTuple):
    grad_in: object
    middle: object
    branch_a_all: object
    branch_b_all: object
    normal_a_all: object
    normal_b_all: object
    inverse_all: object
    mixture_all: object
    qkv_all: object
    weights_all: object
    gath_a_all: object
    active_all: object
    slope_all: object
    gath_b_all: object
    gath_z: object
    w_qkv_all: object
    w_out_all: object
    w_up_all: object
    w_down_all: object
    spots: object
    turned: object
    up_bias: object
    ln_gain: object
    layer_scale: object
    row_bias: object


class BackOutputs(NamedTuple):
    grad: object
    stream: object
    d_qkv: object
    d_out: object
    d_up: object
    d_down: object
    small_out: object


class BackScratch(NamedTuple):
    branch_a: object
    branch_b: object
    normal_a: object
    normal_b: object
    own: object
    own_f: object
    inverse_a: object
    inverse_b: object
    mixture: object
    qkv: object
    weights: object
    gath_a: object
    active: object
    slope: object
    gath_b: object
    gath_m: object
    gath_t: object
    w_qkv: object
    w_out: object
    w_up: object
    w_down: object
    d_hidden: object
    hidden: object
    hidden_f: object
    d_mixed: object
    d_scores: object
    part: object
    part_f: object
    got: object
    got_f: object
    summed: object
    summed_f: object
    sums: object
    up_total: object
    up_sums: object
    qkv_sums: object
    table_sums: object
    lines: object
    near_got: object
    pair_sum: object
    far_got: object
    data_m: object
    data_t: object
    got_m: object
    got_t: object
    small: object
    got_small: object
    send_sems: object
    recv_sems: object
    load_sems: object
    ring_send_m: object
    ring_recv_m: object
    ring_send_t: object
    ring_recv_t: object
    ring_send_s: object
    ring_recv_s: object
    out_sems: object


def backward_body(layers, head_count, count, *all_refs):
    refs = Names((*BackInputs._fields, *BackOutputs._fields, *BackScratch._fields), all_refs)
    rows, width = refs.grad.shape
    last = layers - 1
    group = Group(refs.send_sems, refs.recv_sems)
    barrier = pltpu.get_barrier_semaphore()
    greeted = group.greet(barrier)
    ring = Ring(count) if count else None
    if ring:
        for other in ring.sides:
            pl.semaphore_signal(barrier, inc=1, device_id={"dp": other}, device_id_type=MESH)
        greeted += 2
    pl.semaphore_wait(barrier, greeted)
    ticker = Ticker(ring)

    def begin(at, kind):
        if not ring:
            return
        leaf = (
            (refs.data_m, refs.got_m, refs.ring_send_m, refs.ring_recv_m),
            (refs.data_t, refs.got_t, refs.ring_send_t, refs.ring_recv_t),
        )[kind]
        streams = ring.streams(tuple(ref.at[at] for ref in leaf))
        for first in range(0, len(streams), 2):
            ticker.add(streams[first : first + 2])

    refs.grad[...] = refs.grad_in[...]
    refs.w_out[refs.w_out_all.shape[1] :] = jnp.zeros_like(refs.w_out[refs.w_out_all.shape[1] :])
    end = front(refs, group, last, ticker.tick, begin)
    loads_m = None
    for at in reversed(range(layers)):
        base = (2 + 2 * at) * Exchange.COPIES
        if at < last:
            back_mlp(refs, group, base, at, loads_m, ticker.tick, begin)
        loads_t = attend_loads(refs, at)
        if at:
            loads_m = mlp_loads(refs, at - 1)
        back_attend(
            refs,
            group,
            base + Exchange.COPIES,
            at,
            head_count,
            loads_t,
            ticker.tick,
            begin,
            end if at == last else None,
        )

    shared = 8 * layers
    lines = refs.lines
    lines[...] = jnp.zeros_like(lines)
    for kind in range(4):
        for at in range(2 * layers):
            row = kind * 2 * layers + at
            lines[row : row + 1] = refs.sums[at, kind : kind + 1]
    base = (2 + 2 * layers) * Exchange.COPIES
    first = group.copy(base, base, lines.at[pl.ds(0, shared)], refs.near_got, group.near)
    first.start()
    ticker.tick()
    first.wait_recv()
    refs.pair_sum[...] = lines[0:shared] + refs.near_got[...]
    second = group.copy(base + 1, base + 1, refs.pair_sum, refs.far_got, group.far)
    second.start()
    ticker.tick()
    second.wait_recv()
    first.wait_send()
    lines[0:shared] = refs.pair_sum[...] + refs.far_got[...]
    row = shared
    for leaf, height in (
        (refs.qkv_sums, layers),
        (refs.up_sums, layers),
        (refs.table_sums, layers * head_count),
    ):
        lines[row : row + height] = leaf[0:height]
        row += height
    cuts = [
        (slice(at * SMALL_ROWS, (at + 1) * SMALL_ROWS), slice(at * 128, (at + 1) * 128))
        for at in range(width // 128)
    ]
    used = refs.d_qkv.shape[1]
    leaves = []

    def leave(at):
        for source, first, target in (
            (refs.data_m, 0, refs.d_down),
            (refs.data_m, refs.d_down.shape[1], refs.d_up),
            (refs.data_t, 0, refs.d_qkv),
            (refs.data_t, used, refs.d_out),
        ):
            step = pltpu.make_async_copy(
                source.at[at, pl.ds(first, target.shape[1])],
                target.at[at],
                refs.out_sems.at[len(leaves)],
            )
            step.start()
            leaves.append(step)

    if ring:
        small = refs.small
        small[...] = jnp.zeros_like(small)
        for rows_at, lanes in cuts:
            small[rows_at] = lines[:, lanes]
        ticker.add(
            ring.streams((small, refs.got_small, refs.ring_send_s, refs.ring_recv_s))
        )
        ticker.finish()
    for at in reversed(range(layers)):
        leave(at)
    second.wait_send()
    if ring:
        for rows_at, lanes in cuts:
            refs.small_out[:, lanes] = small[rows_at]
    else:
        refs.small_out[...] = lines[...]
    for step in leaves:
        step.wait()


def run_backward(count, inputs, head_count):
    grad, w_out, w_up = inputs[0], inputs[16], inputs[17]
    rows, width = grad.shape
    layers, wide = w_out.shape[0], inputs[15].shape[2] // 3
    inner = w_up.shape[2]
    used = head_count * HEAD_DIM
    ring_count = count or 2
    steps = 2 * (ring_count - 1)
    in_vmem = pl.BlockSpec(memory_space=pltpu.VMEM)
    in_hbm = pl.BlockSpec(memory_space=pl.ANY)
    assert inner == width == 3 * wide == 4 * used and layers == 2

    def wide_rows(*shape):
        return pltpu.VMEM(shape, F32)

    def low(*shape):
        return pltpu.VMEM(shape, BF16)

    def sems(*shape):
        return pltpu.SemaphoreType.DMA(shape)

    def ring_got(total, pieces):
        piece = total // (2 * ring_count * pieces)
        return low(layers, 2, pieces, ring_count - 1, piece, width)

    own = wide_rows(rows, width)
    four = low(4, rows, width)
    square = low(4, head_count, rows, rows)
    lines = wide_rows(8 * layers, width)
    small_rows = -(-SMALL_ROWS * (width // 128) // (16 * ring_count)) * 16 * ring_count
    exchanges = (2 + 2 * layers) * Exchange.COPIES + 2
    scratch = (
        [own] * 6
        + [wide_rows(rows, 128)] * 2
        + [low(4, rows, wide), four, square, four, four, four, four, four, four]
        + [low(width, 3 * wide), low(wide, width), low(width, inner), low(inner, width)]
        + [four, own, own, four, square, four, four]
        + [low(3, rows, width)] * 2
        + [low(rows, width)] * 2
        + [wide_rows(2 * layers, 8, width)]
        + [wide_rows(8, width)] * 4
        + [wide_rows(SMALL_ROWS, width), lines, lines, lines]
        + [low(layers, 2 * width, width), low(layers, width, width)]
        + [ring_got(2 * width, PIECES), ring_got(width, 1)]
        + [wide_rows(small_rows, 128)]
        + [wide_rows(2, 1, ring_count - 1, small_rows // (2 * ring_count), 128)]
        + [sems(exchanges)] * 2
        + [sems(1 + 2 * layers, 9)]
        + [sems(layers, 2, PIECES, steps)] * 2
        + [sems(layers, 2, 1, steps)] * 2
        + [sems(2, 1, steps)] * 2
        + [sems(4 * layers)]
    )
    return pl.pallas_call(
        functools.partial(backward_body, layers, head_count, count),
        name="backward",
        out_shape=[
            jax.ShapeDtypeStruct((rows, width), F32),
            jax.ShapeDtypeStruct((rows, width), F32),
            jax.ShapeDtypeStruct((layers, 3 * used, width), BF16),
            jax.ShapeDtypeStruct((layers, used, width), BF16),
            jax.ShapeDtypeStruct((layers, width, inner), BF16),
            jax.ShapeDtypeStruct((layers, inner, width), BF16),
            jax.ShapeDtypeStruct((SMALL_ROWS, width), F32),
        ],
        in_specs=[in_vmem] * 2 + [in_hbm] * 17 + [in_vmem] * 6,
        out_specs=[in_vmem] * 2 + [in_hbm] * 4 + [in_vmem],
        scratch_shapes=scratch,
        compiler_params=pltpu.CompilerParams(
            collective_id=1, has_side_effects=True, vmem_limit_bytes=65400 * 1024
        ),
    )(*inputs)


SMALL_ROWS = 32


class Ring:
    def __init__(self, count):
        self.count = count
        self.steps = 2 * (count - 1)
        self.place = self.place_of(lax.axis_index("dp"))
        self.sides = (
            self.number_of((self.place + 1) % count),
            self.number_of((self.place + count - 1) % count),
        )

    def place_of(self, number):
        row, side = number // 2, number % 2
        return row + side * (self.count - 1 - 2 * row)

    def number_of(self, place):
        side = place // (self.count // 2)
        return 2 * (place + side * (self.count - 1 - 2 * place)) + side

    def streams(self, *sets):
        return [
            (leaf, way, sub)
            for leaf in sets
            for sub in range(leaf[1].shape[1])
            for way in range(2)
        ]

    def rows(self, stream, step):
        (data, got, _, _), way, sub = stream
        subs, piece = got.shape[1], got.shape[3]
        if way == 0:
            chunk = (self.place + 3 * self.count - step) % self.count
        else:
            chunk = (self.place + step) % self.count
        first = ((way * self.count + chunk) * subs + sub) * piece
        return pl.ds(pl.multiple_of(first, piece), piece)

    def copy(self, stream, step, gather):
        (data, got, send_sems, recv_sems), way, sub = stream
        rows = self.rows(stream, step)
        return pltpu.make_async_remote_copy(
            src_ref=data.at[rows],
            dst_ref=data.at[rows] if gather else got.at[way, sub, step],
            send_sem=send_sems.at[way, sub, step],
            recv_sem=recv_sems.at[way, sub, step],
            device_id={"dp": self.sides[way]},
            device_id_type=MESH,
        )

    def start(self, streams):
        for stream in streams:
            self.copy(stream, 0, False).start()

    def add(self, stream, step):
        (data, got, _, _), way, sub = stream
        self.copy(stream, step, False).wait_recv()
        rows = self.rows(stream, step + 1)
        data[rows] = data[rows] + got[way, sub, step]

    def drain(self, streams):
        for step in range(self.count - 1, self.steps):
            for stream in streams:
                self.copy(stream, step, True).wait_send()


def ring_fits(count, rows):
    return count == 8 and rows % (2 * count * 16) == 0


def widen_body(
    wide,
    lengths,
    stream,
    gradient,
    out_in,
    up_in,
    down_in,
    small,
    result,
    d_tokens,
    d_out,
    d_up,
    d_down,
    d_bias,
    d_up_bias,
    *kinds,
):
    number = pl.program_id(0)
    rows, width = stream.shape
    layers, _, used = d_bias.shape
    place = lax.axis_index("tensor")
    length = lengths[place, 0] + lengths[place, 1]
    row = number * rows + lax.broadcasted_iota(jnp.int32, (rows, width), 0)
    result[...] = jnp.where(row < length, stream[...], 0.0).astype(BF16)
    d_tokens[...] = gradient[...]
    d_out[...] = out_in[...].astype(F32)
    d_up[...] = up_in[...].astype(F32)
    d_down[...] = down_in[...].astype(F32)

    @pl.when(number == 0)
    def _():
        for kind, leaf in enumerate(kinds):
            for at in range(layers):
                first = 2 * (kind * layers + at)
                leaf[at] = small[first : first + 2]
        first = 8 * layers
        for at in range(layers):
            for half in range(2):
                start = 2 * half * wide
                d_bias[at, half : half + 1] = small[
                    first + at : first + at + 1, start : start + used
                ]
        first += layers
        d_up_bias[...] = small[first : first + layers]


def run_widen(lengths, stream, gradient, d_out, d_up, d_down, small, wide, used):
    rows, width = stream.shape
    layers = d_out.shape[0]
    parts = 4
    steps = layers * parts

    def rows_of(total):
        return pl.BlockSpec((total // steps, width), lambda at: (at, 0))

    def block(leaf):
        return pl.BlockSpec(
            (1, leaf.shape[1] // parts, width), lambda at: (at // parts, at % parts, 0)
        )

    def whole(*shape):
        return pl.BlockSpec(shape, lambda at: (0,) * len(shape))

    def full(*shape):
        return jax.ShapeDtypeStruct(shape, F32)

    return pl.pallas_call(
        functools.partial(widen_body, wide),
        name="widen",
        grid=(steps,),
        out_shape=[
            jax.ShapeDtypeStruct((rows, width), BF16),
            full(rows, width),
            full(*d_out.shape),
            full(*d_up.shape),
            full(*d_down.shape),
            full(layers, 2, used),
            full(layers, width),
            *[full(layers, 2, width)] * 4,
        ],
        in_specs=[
            pl.BlockSpec(memory_space=pltpu.SMEM),
            rows_of(rows),
            rows_of(rows),
            block(d_out),
            block(d_up),
            block(d_down),
            whole(*small.shape),
        ],
        out_specs=[
            rows_of(rows),
            rows_of(rows),
            block(d_out),
            block(d_up),
            block(d_down),
            whole(layers, 2, used),
            whole(layers, width),
            *[whole(layers, 2, width)] * 4,
        ],
    )(lengths, stream, gradient, d_out, d_up, d_down, small)


def per_device(
    tokens,
    cotangent,
    segments,
    lengths,
    rel_index,
    w_qkv,
    qv_bias,
    w_out,
    w_fc1,
    fc1_bias,
    w_fc2,
    rel_table,
    ln_gain,
    ln_bias,
    layer_scale,
    row_bias,
):
    own_rows, width = tokens.shape
    group_rows, bin_rows = rel_index.shape
    layer_count = w_qkv.shape[0]
    head_count = rel_table.shape[2]
    local_width = w_qkv.shape[3]
    wide = -(-local_width // 256) * 256
    bin_total = group_rows // bin_rows
    place = lax.axis_index("tensor")
    assert own_rows == bin_rows and bin_total == 4

    extra = wide - local_width
    qkv_used = jnp.pad(w_qkv, ((0, 0), (0, 0), (0, 0), (0, extra))).reshape(
        layer_count, width, 3 * wide
    )
    norms = (ln_gain, ln_bias, layer_scale, row_bias)

    (
        gath_a,
        qkv,
        shares,
        mixture,
        gath_b,
        slope,
        active,
        gath_z,
        spots,
        turned,
        gradient,
        normal_a,
        normal_b,
        inverse,
        branch_a,
        branch_b,
        middle,
    ) = run_forward(
        lengths,
        rel_index,
        rel_table,
        (tokens, cotangent),
        (qkv_used, qv_bias, w_out, w_fc1, fc1_bias, w_fc2),
        norms,
    )
    dp_count = lax.axis_size("dp")
    with_ring = ring_fits(dp_count, width)
    gradient, stream, *sums = run_backward(
        dp_count if with_ring else None,
        (
            gradient,
            middle,
            branch_a,
            branch_b,
            normal_a,
            normal_b,
            inverse,
            mixture,
            qkv,
            shares,
            gath_a,
            active,
            slope,
            gath_b,
            gath_z,
            qkv_used,
            w_out,
            w_fc1,
            w_fc2,
            spots,
            turned,
            fc1_bias,
            ln_gain,
            layer_scale,
            row_bias,
        ),
        head_count,
    )
    if not with_ring:
        sums = lax.psum(sums, "dp")
    *weight_sums, small = sums
    d_qkv, d_out, d_up, d_down = weight_sums
    result, d_tokens, d_out, d_up, d_down, d_bias, d_up_bias, *kinds = run_widen(
        lengths, stream, gradient, d_out, d_up, d_down, small, wide, local_width
    )
    d_qkv = jnp.transpose(
        d_qkv.astype(F32).reshape(layer_count, 3, local_width, width), (0, 3, 1, 2)
    )
    first = 8 * layer_count + 2 * layer_count
    d_table = small[first : first + layer_count * head_count, : rel_table.shape[1]]
    d_table = jnp.transpose(d_table.reshape(layer_count, head_count, -1), (0, 2, 1))
    return (
        result,
        d_tokens,
        d_qkv,
        d_bias,
        d_out,
        d_up,
        d_up_bias,
        d_down,
        d_table,
        *kinds,
    )


def solution(mesh):
    in_specs = (
        P(("dp", "tensor"), None),
        P(("dp", "tensor"), None),
        P("dp"),
        P("dp", None),
        P("dp", None),
        P(None, None, None, "tensor"),
        P(None, None, "tensor"),
        P(None, "tensor", None),
        P(None, None, "tensor"),
        P(None, "tensor"),
        P(None, "tensor", None),
        P(None, None, "tensor"),
        P(),
        P(),
        P(),
        P(),
    )
    out_specs = (
        P(("dp", "tensor"), None),
        P(("dp", "tensor"), None),
        P(None, None, None, "tensor"),
        P(None, None, "tensor"),
        P(None, "tensor", None),
        P(None, None, "tensor"),
        P(None, "tensor"),
        P(None, "tensor", None),
        P(None, None, "tensor"),
        P(),
        P(),
        P(),
        P(),
    )
    return jax.shard_map(
        per_device, mesh=mesh, in_specs=in_specs, out_specs=out_specs, check_vma=False
    )
```

```python
import functools
from typing import NamedTuple

import jax
import jax.numpy as jnp
from jax import lax
from jax.experimental import pallas as pl
from jax.experimental.pallas import tpu as pltpu
from jax.sharding import PartitionSpec as P

HEAD_DIM = 64
SIDE = 14
STRIDE = 2 * SIDE - 1
CELLS = SIDE * SIDE
CHUNK = 32
MESH = pl.DeviceIdType.MESH
BF16 = jnp.bfloat16
F32 = jnp.float32


def dot(left_side, right_side, left_axis=1, right_axis=0):
    return lax.dot_general(
        left_side,
        right_side,
        (((left_axis,), (right_axis,)), ((), ())),
        preferred_element_type=F32,
    )


class Group:
    def __init__(self, send_sems, recv_sems):
        own = lax.axis_index("tensor")
        self.core = own % 2
        self.near = own + 1 - 2 * self.core
        self.far = (own + 2) % 4
        self.far_chip = 1 - own // 2
        self.sems = (send_sems, recv_sems)

    def greet(self, barrier):
        for other in (self.near, self.far, self.far + 1 - 2 * self.core):
            pl.semaphore_signal(
                barrier, inc=1, device_id={"tensor": other}, device_id_type=MESH
            )
        return 3

    def copy(self, sent, arrived, source, target, other):
        return pltpu.make_async_remote_copy(
            src_ref=source,
            dst_ref=target,
            send_sem=self.sems[0].at[sent],
            recv_sem=self.sems[1].at[arrived],
            device_id={"tensor": other},
            device_id_type=MESH,
        )


class Exchange:
    COPIES = 10

    def __init__(self, group, base, gath, part, got, summed):
        self.group, self.base = group, base
        self.gath, self.part, self.got, self.summed = gath, part, got, summed
        self.rows = (part if gath is None else gath).shape[1] // 2
        self.keep = group.core * self.rows
        self.give = (1 - group.core) * self.rows

    def slot(self, stage):
        core = self.group.core
        return 2 + core + stage * (1 - 2 * core)

    def span(self, first):
        return pl.ds(pl.multiple_of(first, self.rows), self.rows)

    def symmetric(self, number, source, target, other):
        at = self.base + number
        return self.group.copy(at, at, source, target, other)

    def to_near(self):
        return self.symmetric(0, self.gath.at[0], self.gath.at[1], self.group.near)

    def across(self, stage):
        core, rows = self.group.core, self.span(self.keep)
        source = core + stage * (1 - 2 * core)
        return self.symmetric(
            2 + stage,
            self.gath.at[source, rows],
            self.gath.at[self.slot(stage), rows],
            self.group.far,
        )

    def relay(self, stage):
        rows = self.span(self.keep)
        return self.symmetric(
            4 + stage,
            self.gath.at[self.slot(stage), rows],
            self.gath.at[self.slot(1 - stage), rows],
            self.group.near,
        )

    def sum_near(self):
        return self.symmetric(1, self.part.at[1], self.got.at[0], self.group.near)

    def pair(self, stage):
        return self.symmetric(
            6 + stage,
            self.part.at[self.slot(stage), self.span(self.give)],
            self.got.at[1, self.span(stage * self.rows)],
            self.group.near,
        )

    def home(self, stage, sender):
        return self.group.copy(
            self.base + 8 + stage,
            self.base + 8 + sender,
            self.summed.at[self.span(stage * self.rows)],
            self.got.at[2, self.span(sender * self.rows)],
            self.group.far_chip * 2 + stage,
        )

    def start(self):
        self.to_near().start()

        @pl.when(self.group.core == 0)
        def _():
            self.across(0).start()

    def spread(self):
        self.to_near().wait_recv()

        @pl.when(self.group.core == 1)
        def _():
            self.across(0).start()

        self.across(1).start()

    def pass_on(self, stage):
        self.across(stage).wait_recv()
        self.relay(stage).start()

    def arrived(self, stage):
        self.relay(stage).wait_recv()

    def send_sum(self, stage):
        self.pair(stage).wait_recv()
        rows = self.span(stage * self.rows)
        self.summed[rows] = self.part[self.slot(stage), self.span(self.keep)] + self.got[1, rows]
        self.home(stage, self.group.core).start()

    def finish(self):
        self.sum_near().wait_recv()
        for sender in range(2):
            self.home(0, sender).wait_recv()

    def drain_gather(self):
        self.to_near().wait_send()
        for stage in range(2):
            self.across(stage).wait_send()
            self.relay(stage).wait_send()

    def drain_sum(self):
        self.sum_near().wait_send()
        for stage in range(2):
            self.pair(stage).wait_send()
            self.home(stage, self.group.core).wait_send()


def by_chunk(total_rows, body, size=CHUNK):
    def step(at, carry):
        return body(pl.ds(pl.multiple_of(at * size, size), size), carry)

    return step, total_rows // size


def norm_chunk(values, gain, shift):
    center = values - jnp.mean(values, -1, keepdims=True)
    inverse = lax.rsqrt(jnp.mean(center * center, -1, keepdims=True) + 1e-06)
    normal = center * inverse
    return (normal * gain + shift).astype(BF16), normal, inverse


def gelu_parts(values):
    share = 0.5 * (1.0 + lax.erf(values * 0.7071067811865476))
    slope = share + values * (jnp.exp(-0.5 * values * values) * 0.3989422804014327)
    return values * share, slope


SPAN = 384
LAST = (SIDE - 1) * (STRIDE + 1)
CLASS = LAST + 1
TABLE_WIDTH = 2 * SPAN


def prepare(head_count, lengths, index_rows, table, bias, spots, turned, same):
    rows = bias.shape[3]
    own = lax.axis_index("tensor")
    order = (own, own + 1 - 2 * (own % 2), (own + 2) % 4, 3 - own)

    ones = []
    for slot in range(4):
        first = lengths[order[slot], 0]
        both = first + lengths[order[slot], 1]

        def pick(row):
            return index_rows[pl.ds(order[slot] * rows + row, 1), :]

        at = lax.broadcasted_iota(jnp.int32, (1, rows), 1)
        code = LAST - jnp.where(at < first, pick(1), pick(first + 1))
        code = jnp.where((at == 0) | (at == first), CLASS, code)
        code = jnp.where(at < both, code, -1)
        upright = lax.broadcasted_iota(jnp.int32, (SPAN, rows), 0)
        spots[slot] = (upright == code).astype(F32).astype(BF16)
        column = jnp.transpose(jnp.broadcast_to(code.astype(F32), (128, rows)))
        column = jnp.concatenate([column] * (SPAN // 128), -1)
        flat = lax.broadcasted_iota(jnp.int32, (rows, SPAN), 1).astype(F32)
        ones.append((flat == column).astype(F32).astype(BF16))
        mirrored = jnp.where(column < CLASS, LAST - column, column)
        mirrored = jnp.where(column < 0, -1.0, mirrored)
        turned[slot] = (flat == mirrored).astype(F32).astype(BF16)

        def image_of(values):
            return (values >= first).astype(jnp.int32) + (values >= both).astype(jnp.int32)

        by_row = image_of(lax.broadcasted_iota(jnp.int32, (rows, rows), 0))
        by_col = image_of(lax.broadcasted_iota(jnp.int32, (rows, rows), 1))
        same[slot] = (by_row == by_col).astype(F32)

    key_at = lax.broadcasted_iota(jnp.int32, (SPAN, SPAN), 0)
    query_at = lax.broadcasted_iota(jnp.int32, (SPAN, SPAN), 1)
    shift = SPAN - LAST

    def each(at, carry):
        row = table[pl.ds(at, 1), :]
        rolled = pltpu.roll(
            jnp.broadcast_to(row, (SPAN, TABLE_WIDTH)), 0, 1, stride=1, stride_axis=0
        )
        pairs = rolled[:, SPAN:]
        tail = shift + STRIDE * STRIDE
        pairs = jnp.where(query_at == CLASS, row[:, tail : tail + 1], pairs)
        pairs = jnp.where(key_at == CLASS, row[:, tail + 1 : tail + 2], pairs)
        pairs = jnp.where(
            (query_at == CLASS) & (key_at == CLASS), row[:, tail + 2 : tail + 3], pairs
        ).astype(BF16)
        for slot in range(4):
            half = dot(ones[slot], pairs, 1, 1).astype(BF16)
            looked = dot(half, spots[slot])
            bias[at // head_count, slot, at % head_count] = jnp.where(
                same[slot] > 0.5, looked, -1000000000.0
            ).astype(BF16)
        return carry

    lax.fori_loop(0, table.shape[0], each, 0)


def shifted_table(rel_table):
    layers, entries, head_count = rel_table.shape
    shift = SPAN - LAST
    table = jnp.transpose(rel_table, (0, 2, 1)).reshape(layers * head_count, entries).astype(F32)
    return jnp.pad(table, ((0, 0), (shift, TABLE_WIDTH - shift - entries)))


def table_row(pairs):
    query_at = lax.broadcasted_iota(jnp.int32, (SPAN, SPAN), 0)
    key_at = lax.broadcasted_iota(jnp.int32, (SPAN, SPAN), 1)
    zero = jnp.zeros((SPAN, SPAN), F32)
    patches = jnp.where((query_at <= LAST) & (key_at <= LAST), pairs, zero)
    rolled = pltpu.roll(
        jnp.concatenate([patches, zero], -1), 0, 1, stride=1, stride_axis=0
    )
    row = jnp.sum(rolled, 0, keepdims=True)
    at = lax.broadcasted_iota(jnp.int32, (1, TABLE_WIDTH), 1)
    tails = (
        (query_at == CLASS) & (key_at <= LAST),
        (query_at <= LAST) & (key_at == CLASS),
        (query_at == CLASS) & (key_at == CLASS),
    )
    for number, mask in enumerate(tails):
        row = jnp.where(at == STRIDE * STRIDE + number, jnp.sum(jnp.where(mask, pairs, zero)), row)
    return row


class Names:
    def __init__(self, names, refs):
        for name, ref in zip(names, refs, strict=True):
            setattr(self, name, ref)


def load_all(pairs, sems):
    steps = []
    for place, (source, target) in enumerate(pairs):
        step = pltpu.make_async_copy(source, target, sems.at[place])
        step.start()
        steps.append(step)
    return steps


def each_chunk(rows, body):
    def step(at, carry):
        body(pl.ds(pl.multiple_of(at * CHUNK, CHUNK), CHUNK))
        return carry

    lax.fori_loop(0, rows // CHUNK, step, 0)


def attend_rows(refs, at, slot, first, head_count):
    qkv = refs.qkv
    rows = qkv.shape[2] // 2
    wide = qkv.shape[3] // 3
    span = pl.ds(first, rows)
    heads = []
    for head in range(head_count):
        lanes = slice(head * HEAD_DIM, (head + 1) * HEAD_DIM)
        queries = qkv[at, slot, span, 0:wide][:, lanes]
        keys = qkv[at, slot, :, wide : 2 * wide][:, lanes]
        values = qkv[at, slot, :, 2 * wide : 3 * wide][:, lanes]
        scores = dot(queries, keys, 1, 1) + refs.bias[at, slot, head, span].astype(F32)
        powers = jnp.exp(scores - jnp.max(scores, -1, keepdims=True))
        weights = (powers / jnp.sum(powers, -1, keepdims=True)).astype(BF16)
        refs.weights[at, slot, head, span] = weights
        heads.append(dot(weights, values).astype(BF16))
    heads.append(jnp.zeros((rows, wide - head_count * HEAD_DIM), BF16))
    refs.mixture[at, slot, span] = jnp.concatenate(heads, -1)


class ForwardInputs(NamedTuple):
    lengths: object
    tokens: object
    cotangent: object
    qv_bias: object
    fc1_bias: object
    table: object
    ln_gain: object
    ln_bias: object
    layer_scale: object
    row_bias: object
    index_in: object
    w_qkv_in: object
    w_out_in: object
    w_up_in: object
    w_down_in: object


class ForwardKept(NamedTuple):
    gath_a: object
    qkv: object
    weights: object
    mixture: object
    gath_b: object
    slope: object
    active: object


class ForwardOutputs(NamedTuple):
    gath_z_out: object
    spots: object
    turned: object
    grad: object
    normal_a: object
    normal_b: object
    inverse: object
    branch_a: object
    branch_b: object
    stream: object


class ForwardScratch(NamedTuple):
    gath_z: object
    bias: object
    same: object
    index_rows: object
    w_qkv: object
    w_out: object
    w_up: object
    w_down: object
    qkv_bias: object
    up_bias: object
    hidden: object
    part: object
    got: object
    summed: object
    own: object
    send_sems: object
    recv_sems: object
    load_sems: object
    out_sems: object


def forward_body(layers, head_count, *all_refs):
    kept_outs = tuple(name + "_kept" for name in ForwardKept._fields)
    refs = Names(
        (*ForwardInputs._fields, *kept_outs, *ForwardOutputs._fields, *ForwardKept._fields, *ForwardScratch._fields), all_refs
    )
    stream, own, got, part = refs.stream, refs.own, refs.got, refs.part
    rows, width = stream.shape
    half = rows // 2
    last = layers - 1
    used = refs.w_out_in.shape[1]
    wide = refs.w_out.shape[1]
    loads = load_all(
        (
            (refs.index_in, refs.index_rows),
            (refs.w_qkv_in, refs.w_qkv),
            *(
                (refs.w_out_in.at[at], refs.w_out.at[at, pl.ds(0, used)])
                for at in range(layers)
            ),
            (refs.w_up_in, refs.w_up),
            (refs.w_down_in, refs.w_down),
        ),
        refs.load_sems,
    )
    group = Group(refs.send_sems, refs.recv_sems)
    barrier = pltpu.get_barrier_semaphore()
    greeted = group.greet(barrier)
    pl.semaphore_wait(barrier, greeted)
    early = Exchange(group, 2 * Exchange.COPIES, refs.gath_z, None, None, None)

    def load(span):
        stream[span] = refs.tokens[span].astype(F32)

    each_chunk(rows, load)
    refs.qkv_bias[...] = jnp.zeros_like(refs.qkv_bias)
    for at in range(layers):
        refs.w_out[at, used:] = jnp.zeros_like(refs.w_out[at, used:])
        refs.up_bias[at] = refs.fc1_bias[at : at + 1].astype(F32)
        for half_at in range(2):
            first = 2 * half_at * wide
            refs.qkv_bias[at, :, first : first + used] = refs.qv_bias[
                at, half_at : half_at + 1
            ].astype(F32)

    def keep(number, at):
        source = getattr(refs, ForwardKept._fields[number])
        target = getattr(refs, kept_outs[number])
        return pltpu.make_async_copy(source.at[at], target.at[at], refs.out_sems.at[number, at])

    def layer(at, carry):
        trade = Exchange(group, 0, refs.gath_a.at[at], part, got, refs.summed)

        def enter(span):
            low, normal, inv = norm_chunk(
                stream[span], refs.ln_gain[at, 0:1], refs.ln_bias[at, 0:1]
            )
            refs.gath_a[at, 0, span] = low
            refs.normal_a[at, span] = normal
            refs.inverse[at, 0, span] = jnp.broadcast_to(inv, (CHUNK, 128))

        each_chunk(rows, enter)
        trade.start()

        @pl.when(at == 0)
        def _():
            place = lax.axis_index("tensor")
            length = refs.lengths[place, 0] + refs.lengths[place, 1]

            def mask(number, carry):
                span = pl.ds(pl.multiple_of(number * CHUNK, CHUNK), CHUNK)
                row = number * CHUNK + lax.broadcasted_iota(jnp.int32, (CHUNK, width), 0)
                values = jnp.where(row < length, refs.cotangent[span].astype(F32), 0.0)
                refs.grad[span] = values
                refs.gath_z[0, span] = (values * refs.layer_scale[last, 1:2]).astype(BF16)
                return carry

            lax.fori_loop(0, rows // CHUNK, mask, 0)

        trade.spread()

        @pl.when(at == 0)
        def _():
            early.start()
            early.spread()
            loads[0].wait()
            prepare(
                head_count,
                refs.lengths,
                refs.index_rows,
                refs.table,
                refs.bias,
                refs.spots,
                refs.turned,
                refs.same,
            )
            for step in loads[1:]:
                step.wait()

        scale = jnp.concatenate(
            [
                jnp.full((1, refs.qkv.shape[3] // 3), HEAD_DIM**-0.5, F32),
                jnp.full((1, 2 * refs.qkv.shape[3] // 3), 1.0, F32),
            ],
            -1,
        )

        def project(slot):
            mixed = dot(refs.gath_a[at, slot], refs.w_qkv[at])
            mixed = (mixed + refs.qkv_bias[at]).astype(BF16).astype(F32) * scale
            refs.qkv[at, slot] = mixed.astype(BF16)

        def attend(slot, first):
            attend_rows(refs, at, slot, first, head_count)
            return dot(refs.mixture[at, slot, pl.ds(first, half)], refs.w_out[at])

        turn = 2 * (at == 0).astype(jnp.int32)

        @pl.when(at == 0)
        def _():
            trade.pass_on(0)
            trade.pass_on(1)

        def one_slot(number, carry):
            role = (number + turn) % 4
            stage = role % 2
            away = role >= 2
            slot = jnp.where(away, trade.slot(stage), role)

            @pl.when(away)
            def _():
                trade.arrived(stage)

            project(slot)

            def one(place, carry):
                first = pl.multiple_of(
                    place * trade.keep + (1 - place) * trade.give, half
                )
                result = attend(slot, first)

                @pl.when(role == 0)
                def _():
                    own[pl.ds(first, half)] = result

                @pl.when(role > 0)
                def _():
                    part[slot, pl.ds(first, half)] = result.astype(BF16)

                @pl.when(away & (place == 0))
                def _():
                    trade.pair(stage).start()

                return carry

            lax.fori_loop(0, 2, one, 0)

            @pl.when(away)
            def _():
                trade.send_sum(stage)

            @pl.when(role == 1)
            def _():
                trade.sum_near().start()

            @pl.when((at > 0) & (role == 1))
            def _():
                trade.pass_on(0)

            @pl.when((at > 0) & (role == 2))
            def _():
                trade.pass_on(1)

            return carry

        lax.fori_loop(0, 4, one_slot, 0)
        for number in range(4):
            keep(number, at).start()

        @pl.when(at == 0)
        def _():
            for stage in range(2):
                early.pass_on(stage)

        trade.finish()

        def between(span):
            total = own[span] + got[0, span].astype(F32) + got[2, span].astype(F32)
            branch = total + refs.row_bias[at, 0:1]
            refs.branch_a[at, span] = branch
            middle = stream[span] + refs.layer_scale[at, 0:1] * branch
            stream[span] = middle
            low, normal, inv = norm_chunk(middle, refs.ln_gain[at, 1:2], refs.ln_bias[at, 1:2])
            refs.gath_b[at, 0, span] = low
            refs.normal_b[at, span] = normal
            refs.inverse[at, 1, span] = jnp.broadcast_to(inv, (CHUNK, 128))

        each_chunk(rows, between)

        @pl.when(at < last)
        def _():
            trade_b = Exchange(
                group, Exchange.COPIES, refs.gath_b.at[at], part, got, refs.summed
            )
            trade_b.start()
            trade.drain_gather()
            trade.drain_sum()
            trade_b.spread()

            def raise_rows(slot):
                refs.hidden[...] = dot(refs.gath_b[at, slot], refs.w_up[at]) + refs.up_bias[at]

                def act(place, carry):
                    span = pl.ds(pl.multiple_of(place * 16, 16), 16)
                    high, incline = gelu_parts(refs.hidden[span])
                    refs.active[at, slot, span] = high.astype(BF16)
                    refs.slope[at, slot, span] = incline.astype(BF16)
                    return carry

                lax.fori_loop(0, rows // 16, act, 0)

            def lower(slot, first, count):
                return dot(refs.active[at, slot, pl.ds(first, count)], refs.w_down[at])

            def one_slot(role, carry):
                stage = role % 2
                away = role >= 2
                slot = jnp.where(away, trade_b.slot(stage), role)

                @pl.when(away)
                def _():
                    trade_b.arrived(stage)

                raise_rows(slot)

                def one(place, carry):
                    first = pl.multiple_of(
                        place * trade_b.keep + (1 - place) * trade_b.give, half
                    )
                    result = lower(slot, first, half)

                    @pl.when(role == 0)
                    def _():
                        own[pl.ds(first, half)] = result

                    @pl.when(role > 0)
                    def _():
                        part[slot, pl.ds(first, half)] = result.astype(BF16)

                    @pl.when(away & (place == 0))
                    def _():
                        trade_b.pair(stage).start()

                    return carry

                lax.fori_loop(0, 2, one, 0)

                @pl.when(away)
                def _():
                    trade_b.send_sum(stage)

                @pl.when(role == 1)
                def _():
                    trade_b.sum_near().start()
                    trade_b.pass_on(0)

                @pl.when(role == 2)
                def _():
                    trade_b.pass_on(1)

                return carry

            lax.fori_loop(0, 4, one_slot, 0)
            for number in (4, 5, 6):
                keep(number, at).start()
            trade_b.finish()

            def after(span):
                total = own[span] + got[0, span].astype(F32) + got[2, span].astype(F32)
                branch = total + refs.row_bias[at, 1:2]
                refs.branch_b[at, span] = branch
                stream[span] = stream[span] + refs.layer_scale[at, 1:2] * branch

            each_chunk(rows, after)
            trade_b.drain_gather()
            trade_b.drain_sum()

        @pl.when(at == last)
        def _():
            pltpu.make_async_copy(
                refs.gath_b.at[at, 0], refs.gath_b_kept.at[at, 0], refs.out_sems.at[4, at]
            ).start()
            trade.drain_gather()
            trade.drain_sum()

        return carry

    lax.fori_loop(0, layers, layer, 0)
    for stage in range(2):
        early.arrived(stage)
    early.drain_gather()
    leave = pltpu.make_async_copy(refs.gath_z, refs.gath_z_out, refs.load_sems.at[0])
    leave.start()
    pltpu.make_async_copy(
        refs.gath_b.at[last, 0], refs.gath_b_kept.at[last, 0], refs.out_sems.at[4, last]
    ).wait()
    for at in range(layers):
        for number in range(len(ForwardKept._fields)):
            if at < last or number < 4:
                keep(number, at).wait()
    leave.wait()


def run_forward(lengths, index_rows, rel_table, rows_in, weights, norms):
    tokens, cotangent = rows_in
    rows, width = tokens.shape
    w_qkv, qv_bias, w_out, w_up, fc1_bias, w_down = weights
    layers, _, head_count = rel_table.shape
    wide = w_qkv.shape[2] // 3
    inner = w_up.shape[2]
    in_vmem = pl.BlockSpec(memory_space=pltpu.VMEM)
    in_hbm = pl.BlockSpec(memory_space=pl.ANY)

    def low(*shape):
        return jax.ShapeDtypeStruct(shape, BF16)

    def full(*shape):
        return jax.ShapeDtypeStruct(shape, F32)

    kept = [
        low(layers, 4, *tail)
        for tail in (
            (rows, width),
            (rows, 3 * wide),
            (head_count, rows, rows),
            (rows, wide),
            (rows, width),
            (rows, inner),
            (rows, inner),
        )
    ]
    own = full(rows, width)
    by_layer = full(layers, rows, width)
    near = [low(4, SPAN, rows), low(4, rows, SPAN), own, by_layer, by_layer]
    near += [full(layers, 2, rows, 128), by_layer, by_layer, own]
    scratch = [
        *kept,
        low(4, rows, width),
        low(layers, 4, head_count, rows, rows),
        full(4, rows, rows),
        jax.ShapeDtypeStruct(index_rows.shape, index_rows.dtype),
        low(*w_qkv.shape),
        low(layers, wide, width),
        low(*w_up.shape),
        low(*w_down.shape),
        full(layers, 1, 3 * wide),
        full(layers, 1, inner),
        full(rows, inner),
        low(4, rows, width),
        low(3, rows, width),
        low(rows, width),
        own,
    ]
    copies = 3 * Exchange.COPIES
    return pl.pallas_call(
        functools.partial(forward_body, layers, head_count),
        name="forward",
        out_shape=[*kept, low(4, rows, width), *near],
        in_specs=[pl.BlockSpec(memory_space=pltpu.SMEM)] + [in_vmem] * 9 + [in_hbm] * 5,
        out_specs=[in_hbm] * (len(kept) + 1) + [in_vmem] * len(near),
        scratch_shapes=[
            *[pltpu.VMEM(leaf.shape, leaf.dtype) for leaf in scratch],
            pltpu.SemaphoreType.DMA((copies,)),
            pltpu.SemaphoreType.DMA((copies,)),
            pltpu.SemaphoreType.DMA((4 + layers,)),
            pltpu.SemaphoreType.DMA((len(kept), layers)),
        ],
        compiler_params=pltpu.CompilerParams(
            collective_id=0, has_side_effects=True, vmem_limit_bytes=65400 * 1024
        ),
    )(
        lengths,
        tokens,
        cotangent,
        qv_bias,
        fc1_bias,
        shifted_table(rel_table),
        *norms,
        index_rows,
        w_qkv,
        w_out,
        w_up,
        w_down,
    )


def fold(values):
    return jnp.sum(values.reshape(-1, 8, values.shape[-1]), 0)


def enter_back(grad, branch, scale, gath, sums):
    rows, width = grad.shape

    def body(span, carry):
        values = grad[span]
        gath[0, span] = (values * scale).astype(BF16)
        return carry[0] + fold(values * branch[span]), carry[1] + fold(values)

    step, count = by_chunk(rows, body)
    zero = jnp.zeros((8, width), F32)
    by_branch, alone = lax.fori_loop(0, count, step, (zero, zero))
    sums[2:3] = jnp.sum(by_branch, 0, keepdims=True)
    sums[3:4] = jnp.sum(alone, 0, keepdims=True) * scale


def leave_back(grad, own, got, normal, inverse, gain, sums):
    rows, width = grad.shape

    def body(span, carry):
        total = own[span] + got[0, span].astype(F32) + got[2, span].astype(F32)
        unit = normal[span]
        scaled = total * gain
        centered = (
            scaled
            - jnp.mean(scaled, -1, keepdims=True)
            - unit * jnp.mean(scaled * unit, -1, keepdims=True)
        )
        grad[span] = grad[span] + inverse[span, 0:1] * centered
        return carry[0] + fold(total * unit), carry[1] + fold(total)

    step, count = by_chunk(rows, body)
    zero = jnp.zeros((8, width), F32)
    by_unit, alone = lax.fori_loop(0, count, step, (zero, zero))
    sums[0:1] = jnp.sum(by_unit, 0, keepdims=True)
    sums[1:2] = jnp.sum(alone, 0, keepdims=True)


def weight_grad(left, right, out, start, count, tick=None):
    block = 256
    used = count * block // left.shape[2]

    def step(place, carry):
        span = pl.ds(pl.multiple_of(place * block, block), block)
        total = None
        for slot in range(4):
            term = dot(left[slot, :, span], right[slot], 0, 0)
            total = term if total is None else total + term
        there = pl.ds(pl.multiple_of(start + place * used, 16), used)
        out[there] = total[:used].astype(out.dtype)
        return carry

    if tick is None:
        lax.fori_loop(0, left.shape[2] // block, step, 0)
    else:
        for place in range(left.shape[2] // block):
            step(place, 0)
            tick()


PIECES = 2


class Ticker:
    def __init__(self, ring):
        self.ring = ring
        self.under_way = []

    def add(self, streams):
        self.ring.start(streams)
        self.under_way.append([streams, 0])

    def tick(self):
        if self.under_way:
            self.one()

    def one(self):
        ring = self.ring
        streams, step = self.under_way.pop(0)
        turn = ring.count - 1
        for stream in streams:
            if step < turn:
                ring.add(stream, step)
                ring.copy(stream, step, False).wait_send()
            else:
                ring.copy(stream, step, True).wait_recv()
            if step + 1 < ring.steps:
                ring.copy(stream, step + 1, step + 1 >= turn).start()
        if step + 1 < ring.steps:
            self.under_way.append([streams, step + 1])
        else:
            ring.drain(streams)

    def alike(self, step):
        turn = self.ring.count - 1
        return turn - 1 - step if step < turn else self.ring.steps - 1 - step

    def finish(self):
        ring = self.ring
        turn = ring.count - 1
        while self.under_way:
            run = min(self.alike(step) for _, step in self.under_way)
            if run < 2:
                for _ in range(len(self.under_way)):
                    self.one()
                continue
            rings = list(self.under_way)

            def body(number, carry):
                for streams, start in rings:
                    step = start + number
                    for stream in streams:
                        if start < turn:
                            ring.add(stream, step)
                            ring.copy(stream, step, False).wait_send()
                        else:
                            ring.copy(stream, step, True).wait_recv()
                        ring.copy(stream, step + 1, start >= turn).start()
                return carry

            lax.fori_loop(0, run, body, 0)
            for leaf in self.under_way:
                leaf[1] += run


def mlp_loads(refs, at):
    return load_all(
        (
            (refs.branch_b_all.at[at], refs.branch_b),
            (refs.w_down_all.at[at], refs.w_down),
            (refs.slope_all.at[at], refs.slope),
            (refs.w_up_all.at[at], refs.w_up),
            (refs.normal_b_all.at[at], refs.normal_b),
            (refs.inverse_all.at[at, 1], refs.inverse_b),
            (refs.active_all.at[at], refs.active),
            (refs.gath_b_all.at[at], refs.gath_b),
        ),
        refs.load_sems.at[1 + 2 * at],
    )


def attend_loads(refs, at):
    return load_all(
        (
            (refs.branch_a_all.at[at], refs.branch_a),
            (refs.w_out_all.at[at], refs.w_out.at[pl.ds(0, refs.w_out_all.shape[1])]),
            (refs.qkv_all.at[at], refs.qkv),
            (refs.weights_all.at[at], refs.weights),
            (refs.w_qkv_all.at[at], refs.w_qkv),
            (refs.normal_a_all.at[at], refs.normal_a),
            (refs.inverse_all.at[at, 0], refs.inverse_a),
            (refs.mixture_all.at[at], refs.mixture),
            (refs.gath_a_all.at[at], refs.gath_a),
        ),
        refs.load_sems.at[2 + 2 * at],
    )


def front(refs, group, at, tick, begin):
    rows = refs.grad.shape[0]
    half = rows // 2
    ahead = Exchange(
        group, Exchange.COPIES, refs.gath_b, refs.part_f, refs.got_f, refs.summed_f
    )
    trade = Exchange(group, 0, None, refs.part, refs.got, refs.summed)
    loads = load_all(
        (
            (refs.gath_b_all.at[at, 0], refs.gath_b.at[0]),
            (refs.w_up_all.at[at], refs.w_up),
            (refs.w_down_all.at[at], refs.w_down),
            (refs.gath_z, refs.gath_m),
            (refs.normal_b_all.at[at], refs.normal_b),
            (refs.inverse_all.at[at, 1], refs.inverse_b),
        ),
        refs.load_sems.at[0],
    )
    loads[0].wait()
    ahead.start()
    ahead.spread()
    for load in loads[1:4]:
        load.wait()

    def work(slot):
        refs.hidden[...] = dot(refs.gath_b[slot], refs.w_up[...]) + refs.up_bias[at : at + 1].astype(F32)
        refs.hidden_f[...] = dot(refs.gath_m[slot], refs.w_down[...], 1, 1)

        def act(place, carry):
            span = pl.ds(pl.multiple_of(place * 16, 16), 16)
            high, incline = gelu_parts(refs.hidden[span])
            refs.active[slot, span] = high.astype(BF16)
            back = (refs.hidden_f[span] * incline).astype(BF16)
            refs.d_hidden[slot, span] = back
            refs.up_total[...] += fold(back.astype(F32))
            return carry

        lax.fori_loop(0, rows // 16, act, 0)

    refs.up_total[...] = jnp.zeros_like(refs.up_total)

    def chip_slot(slot, carry):
        work(slot)
        result = dot(refs.d_hidden[slot], refs.w_up[...], 1, 1)
        result_f = dot(refs.active[slot], refs.w_down[...])

        @pl.when(slot == 0)
        def _():
            refs.own[...] = result
            refs.own_f[...] = result_f

        @pl.when(slot == 1)
        def _():
            refs.part[1] = result.astype(BF16)
            refs.part_f[1] = result_f.astype(BF16)

        return carry

    lax.fori_loop(0, 2, chip_slot, 0)
    trade.sum_near().start()
    ahead.sum_near().start()
    ahead.pass_on(0)

    def far_slot(stage, carry):
        slot = ahead.slot(stage)
        ahead.arrived(stage)
        work(slot)

        def one(place, carry):
            first = pl.multiple_of(place * ahead.keep + (1 - place) * ahead.give, half)
            span = pl.ds(first, half)
            refs.part[slot, span] = dot(
                refs.d_hidden[slot, span], refs.w_up[...], 1, 1
            ).astype(BF16)

            @pl.when(place == 0)
            def _():
                trade.pair(stage).start()

            refs.part_f[slot, span] = dot(refs.active[slot, span], refs.w_down[...]).astype(BF16)

            @pl.when(place == 0)
            def _():
                ahead.pair(stage).start()

            return carry

        lax.fori_loop(0, 2, one, 0)
        trade.send_sum(stage)
        ahead.send_sum(stage)

        @pl.when(stage == 0)
        def _():
            ahead.pass_on(1)

        return carry

    lax.fori_loop(0, 2, far_slot, 0)
    data, inner = refs.data_m.at[at], refs.w_down.shape[0]
    weight_grad(refs.active, refs.gath_m, data, 0, inner)
    begin(at, 0, 0)
    weight_grad(refs.gath_b, refs.d_hidden, data, inner, refs.w_up.shape[0])
    begin(at, 0, 1)
    refs.up_sums[at : at + 1] = jnp.sum(refs.up_total[...], 0, keepdims=True)
    for load in loads[4:]:
        load.wait()
    trade.finish()
    tick()
    leave_back(
        refs.grad,
        refs.own,
        refs.got,
        refs.normal_b,
        refs.inverse_b,
        refs.ln_gain[at, 1:2],
        refs.sums.at[2 * at + 1],
    )
    ahead.drain_gather()
    trade.drain_sum()

    def end():
        ahead.finish()
        sums = refs.sums.at[2 * at + 1]
        scale = refs.layer_scale[at, 1:2]
        width = refs.grad.shape[1]

        def body(span, carry):
            branch = (
                refs.own_f[span]
                + refs.got_f[0, span].astype(F32)
                + refs.got_f[2, span].astype(F32)
                + refs.row_bias[at, 1:2]
            )
            refs.stream[span] = refs.middle[span] + scale * branch
            values = refs.grad_in[span]
            return carry[0] + fold(values * branch), carry[1] + fold(values)

        step, count = by_chunk(rows, body)
        zero = jnp.zeros((8, width), F32)
        by_branch, alone = lax.fori_loop(0, count, step, (zero, zero))
        sums[2:3] = jnp.sum(by_branch, 0, keepdims=True)
        sums[3:4] = jnp.sum(alone, 0, keepdims=True) * scale
        ahead.drain_sum()

    return end


def back_mlp(refs, group, base, at, loads, tick, begin):
    rows = refs.grad.shape[0]
    half = rows // 2
    gath, part, hidden, d_hidden = refs.gath_m, refs.part, refs.hidden, refs.d_hidden
    trade = Exchange(group, base, gath, part, refs.got, refs.summed)
    sums = refs.sums.at[2 * at + 1]
    loads[0].wait()
    enter_back(refs.grad, refs.branch_b, refs.layer_scale[at, 1:2], gath, sums)
    trade.start()
    tick()
    trade.spread()
    for load in loads[1:4]:
        load.wait()

    refs.up_total[...] = jnp.zeros_like(refs.up_total)

    def down(slot):
        hidden[...] = dot(gath[slot], refs.w_down[...], 1, 1)

        def body(place, carry):
            span = pl.ds(pl.multiple_of(place * CHUNK, CHUNK), CHUNK)
            low = (hidden[span] * refs.slope[slot, span].astype(F32)).astype(BF16)
            d_hidden[slot, span] = low
            return carry + fold(low.astype(F32))

        zero = jnp.zeros((8, hidden.shape[1]), F32)
        refs.up_total[...] += lax.fori_loop(0, rows // CHUNK, body, zero)

    def back(slot, first, count):
        return dot(d_hidden[slot, pl.ds(first, count)], refs.w_up[...], 1, 1)

    down(0)
    tick()
    refs.own[...] = back(0, 0, rows)
    tick()
    down(1)
    part[1] = back(1, 0, rows).astype(BF16)
    trade.sum_near().start()
    tick()
    trade.pass_on(0)
    for stage in range(2):
        slot = trade.slot(stage)
        trade.arrived(stage)
        down(slot)
        tick()

        def one(place, carry):
            first = pl.multiple_of(place * trade.keep + (1 - place) * trade.give, half)
            part[slot, pl.ds(first, half)] = back(slot, first, half).astype(BF16)

            @pl.when(place == 0)
            def _():
                trade.pair(stage).start()

            return carry

        lax.fori_loop(0, 2, one, 0)
        trade.send_sum(stage)
        if stage == 0:
            trade.pass_on(1)
        tick()
    refs.up_sums[at : at + 1] = jnp.sum(refs.up_total[...], 0, keepdims=True)
    for load in loads[4:]:
        load.wait()
    data, inner = refs.data_m.at[at], refs.w_down.shape[0]
    weight_grad(refs.active, gath, data, 0, inner)
    begin(at, 0, 0)
    tick()
    weight_grad(refs.gath_b, d_hidden, data, inner, refs.w_up.shape[0])
    begin(at, 0, 1)
    tick()
    trade.finish()
    leave_back(
        refs.grad,
        refs.own,
        refs.got,
        refs.normal_b,
        refs.inverse_b,
        refs.ln_gain[at, 1:2],
        sums,
    )
    trade.drain_gather()
    trade.drain_sum()
    tick()


def back_attend(refs, group, base, at, head_count, loads, tick, begin, meanwhile):
    rows = refs.grad.shape[0]
    half = rows // 2
    data = refs.data_t.at[at]
    wide = refs.mixture.shape[2]
    gath, part, d_mixed, d_scores = refs.gath_t, refs.part, refs.d_mixed, refs.d_scores
    qkv = refs.qkv
    trade = Exchange(group, base, gath, part, refs.got, refs.summed)
    sums = refs.sums.at[2 * at]
    loads[0].wait()
    enter_back(refs.grad, refs.branch_a, refs.layer_scale[at, 0:1], gath, sums)
    trade.start()
    tick()
    trade.spread()
    if meanwhile is not None:
        meanwhile()
        tick()
    for load in loads[1:5]:
        load.wait()
    spare = jnp.zeros((rows, wide - head_count * HEAD_DIM), BF16)

    def attend(slot):
        d_mix = dot(gath[slot], refs.w_out[...], 1, 1).astype(BF16)
        pieces = ([], [], [])
        for head in range(head_count):
            lanes = slice(head * HEAD_DIM, (head + 1) * HEAD_DIM)
            queries = qkv[slot, :, 0:wide][:, lanes]
            keys = qkv[slot, :, wide : 2 * wide][:, lanes]
            values = qkv[slot, :, 2 * wide : 3 * wide][:, lanes]
            share = refs.weights[slot, head]
            d_head = d_mix[:, lanes]
            wide_share = share.astype(F32)
            d_share = dot(d_head, values, 1, 1)
            middle = jnp.sum(wide_share * d_share, -1, keepdims=True)
            d_score = (wide_share * (d_share - middle)).astype(BF16)
            d_scores[slot, head] = d_score
            pieces[0].append((dot(d_score, keys) * HEAD_DIM**-0.5).astype(BF16))
            pieces[1].append(dot(d_score, queries, 0, 0).astype(BF16))
            pieces[2].append(dot(share, d_head, 0, 0).astype(BF16))
        for place in range(3):
            d_mixed[slot, :, place * wide : (place + 1) * wide] = jnp.concatenate(
                pieces[place] + [spare], -1
            )

    def back(slot, first, count):
        return dot(d_mixed[slot, pl.ds(first, count)], refs.w_qkv[...], 1, 1)

    attend(0)
    tick()
    refs.own[...] = back(0, 0, rows)
    attend(1)
    tick()
    part[1] = back(1, 0, rows).astype(BF16)
    trade.sum_near().start()
    trade.pass_on(0)
    for stage in range(2):
        slot = trade.slot(stage)
        trade.arrived(stage)
        attend(slot)
        tick()

        def one(place, carry):
            first = pl.multiple_of(place * trade.keep + (1 - place) * trade.give, half)
            part[slot, pl.ds(first, half)] = back(slot, first, half).astype(BF16)

            @pl.when(place == 0)
            def _():
                trade.pair(stage).start()

            return carry

        lax.fori_loop(0, 2, one, 0)
        trade.send_sum(stage)
        if stage == 0:
            trade.pass_on(1)
        tick()
    for load in loads[5:]:
        load.wait()

    def add(slot, total):
        def body(span, carry):
            return carry + fold(d_mixed[slot, span].astype(F32))

        step, count = by_chunk(rows, body)
        return lax.fori_loop(0, count, step, total)

    total = jnp.zeros((8, 3 * wide), F32)
    for slot in range(4):
        total = add(slot, total)
    refs.qkv_sums[at : at + 1] = jnp.sum(total, 0, keepdims=True)
    used = 3 * head_count * HEAD_DIM
    weight_grad(d_mixed, refs.gath_a, data, 0, used)
    tick()
    weight_grad(refs.mixture, gath, data, used, used // 3)
    begin(at, 1, 0)
    tick()
    for head in range(head_count):
        total = None
        for slot in range(4):
            placed = dot(refs.spots[slot], d_scores[slot, head]).astype(BF16)
            term = dot(placed, refs.turned[slot])
            total = term if total is None else total + term
        row = at * head_count + head
        refs.table_sums[row : row + 1] = table_row(total)
    trade.finish()
    leave_back(
        refs.grad,
        refs.own,
        refs.got,
        refs.normal_a,
        refs.inverse_a,
        refs.ln_gain[at, 0:1],
        sums,
    )
    trade.drain_gather()
    trade.drain_sum()
    tick()


class BackInputs(NamedTuple):
    grad_in: object
    middle: object
    branch_a_all: object
    branch_b_all: object
    normal_a_all: object
    normal_b_all: object
    inverse_all: object
    mixture_all: object
    qkv_all: object
    weights_all: object
    gath_a_all: object
    active_all: object
    slope_all: object
    gath_b_all: object
    gath_z: object
    w_qkv_all: object
    w_out_all: object
    w_up_all: object
    w_down_all: object
    spots: object
    turned: object
    up_bias: object
    ln_gain: object
    layer_scale: object
    row_bias: object


class BackOutputs(NamedTuple):
    grad: object
    stream: object
    d_qkv: object
    d_out: object
    d_up: object
    d_down: object
    small_out: object


class BackScratch(NamedTuple):
    branch_a: object
    branch_b: object
    normal_a: object
    normal_b: object
    own: object
    own_f: object
    inverse_a: object
    inverse_b: object
    mixture: object
    qkv: object
    weights: object
    gath_a: object
    active: object
    slope: object
    gath_b: object
    gath_m: object
    gath_t: object
    w_qkv: object
    w_out: object
    w_up: object
    w_down: object
    d_hidden: object
    hidden: object
    hidden_f: object
    d_mixed: object
    d_scores: object
    part: object
    part_f: object
    got: object
    got_f: object
    summed: object
    summed_f: object
    sums: object
    up_total: object
    up_sums: object
    qkv_sums: object
    table_sums: object
    lines: object
    near_got: object
    pair_sum: object
    far_got: object
    data_m: object
    data_t: object
    got_m: object
    got_t: object
    small: object
    got_small: object
    send_sems: object
    recv_sems: object
    load_sems: object
    ring_send_m: object
    ring_recv_m: object
    ring_send_t: object
    ring_recv_t: object
    ring_send_s: object
    ring_recv_s: object
    out_sems: object


def backward_body(layers, head_count, count, *all_refs):
    refs = Names((*BackInputs._fields, *BackOutputs._fields, *BackScratch._fields), all_refs)
    rows, width = refs.grad.shape
    last = layers - 1
    group = Group(refs.send_sems, refs.recv_sems)
    barrier = pltpu.get_barrier_semaphore()
    greeted = group.greet(barrier)
    ring = Ring(count) if count else None
    if ring:
        for other in ring.sides:
            pl.semaphore_signal(barrier, inc=1, device_id={"dp": other}, device_id_type=MESH)
        greeted += 2
    pl.semaphore_wait(barrier, greeted)
    ticker = Ticker(ring)

    def begin(at, kind, sub):
        if not ring:
            return
        leaf = (
            (refs.data_m, refs.got_m, refs.ring_send_m, refs.ring_recv_m),
            (refs.data_t, refs.got_t, refs.ring_send_t, refs.ring_recv_t),
        )[kind]
        streams = ring.streams(tuple(ref.at[at] for ref in leaf))
        ticker.add(streams[2 * sub : 2 * sub + 2])

    refs.grad[...] = refs.grad_in[...]
    refs.w_out[refs.w_out_all.shape[1] :] = jnp.zeros_like(refs.w_out[refs.w_out_all.shape[1] :])
    end = front(refs, group, last, ticker.tick, begin)
    loads_m = None
    for at in reversed(range(layers)):
        base = (2 + 2 * at) * Exchange.COPIES
        if at < last:
            back_mlp(refs, group, base, at, loads_m, ticker.tick, begin)
        loads_t = attend_loads(refs, at)
        if at:
            loads_m = mlp_loads(refs, at - 1)
        back_attend(
            refs,
            group,
            base + Exchange.COPIES,
            at,
            head_count,
            loads_t,
            ticker.tick,
            begin,
            end if at == last else None,
        )

    shared = 8 * layers
    lines = refs.lines
    lines[...] = jnp.zeros_like(lines)
    for kind in range(4):
        for at in range(2 * layers):
            row = kind * 2 * layers + at
            lines[row : row + 1] = refs.sums[at, kind : kind + 1]
    base = (2 + 2 * layers) * Exchange.COPIES
    first = group.copy(base, base, lines.at[pl.ds(0, shared)], refs.near_got, group.near)
    first.start()
    ticker.tick()
    first.wait_recv()
    refs.pair_sum[...] = lines[0:shared] + refs.near_got[...]
    second = group.copy(base + 1, base + 1, refs.pair_sum, refs.far_got, group.far)
    second.start()
    ticker.tick()
    second.wait_recv()
    first.wait_send()
    lines[0:shared] = refs.pair_sum[...] + refs.far_got[...]
    row = shared
    for leaf, height in (
        (refs.qkv_sums, layers),
        (refs.up_sums, layers),
        (refs.table_sums, layers * head_count),
    ):
        lines[row : row + height] = leaf[0:height]
        row += height
    cuts = [
        (slice(at * SMALL_ROWS, (at + 1) * SMALL_ROWS), slice(at * 128, (at + 1) * 128))
        for at in range(width // 128)
    ]
    used = refs.d_qkv.shape[1]
    leaves = []

    def leave(at):
        for source, first, target in (
            (refs.data_m, 0, refs.d_down),
            (refs.data_m, refs.d_down.shape[1], refs.d_up),
            (refs.data_t, 0, refs.d_qkv),
            (refs.data_t, used, refs.d_out),
        ):
            step = pltpu.make_async_copy(
                source.at[at, pl.ds(first, target.shape[1])],
                target.at[at],
                refs.out_sems.at[len(leaves)],
            )
            step.start()
            leaves.append(step)

    if ring:
        small = refs.small
        small[...] = jnp.zeros_like(small)
        for rows_at, lanes in cuts:
            small[rows_at] = lines[:, lanes]
        ticker.add(
            ring.streams((small, refs.got_small, refs.ring_send_s, refs.ring_recv_s))
        )
        ticker.finish()
    for at in reversed(range(layers)):
        leave(at)
    second.wait_send()
    if ring:
        for rows_at, lanes in cuts:
            refs.small_out[:, lanes] = small[rows_at]
    else:
        refs.small_out[...] = lines[...]
    for step in leaves:
        step.wait()


def run_backward(count, inputs, head_count):
    grad, w_out, w_up = inputs[0], inputs[16], inputs[17]
    rows, width = grad.shape
    layers, wide = w_out.shape[0], inputs[15].shape[2] // 3
    inner = w_up.shape[2]
    used = head_count * HEAD_DIM
    ring_count = count or 2
    steps = 2 * (ring_count - 1)
    in_vmem = pl.BlockSpec(memory_space=pltpu.VMEM)
    in_hbm = pl.BlockSpec(memory_space=pl.ANY)
    assert inner == width == 3 * wide == 4 * used and layers == 2

    def wide_rows(*shape):
        return pltpu.VMEM(shape, F32)

    def low(*shape):
        return pltpu.VMEM(shape, BF16)

    def sems(*shape):
        return pltpu.SemaphoreType.DMA(shape)

    def ring_got(total, pieces):
        piece = total // (2 * ring_count * pieces)
        return low(layers, 2, pieces, ring_count - 1, piece, width)

    own = wide_rows(rows, width)
    four = low(4, rows, width)
    square = low(4, head_count, rows, rows)
    lines = wide_rows(8 * layers, width)
    small_rows = -(-SMALL_ROWS * (width // 128) // (16 * ring_count)) * 16 * ring_count
    exchanges = (2 + 2 * layers) * Exchange.COPIES + 2
    scratch = (
        [own] * 6
        + [wide_rows(rows, 128)] * 2
        + [low(4, rows, wide), four, square, four, four, four, four, four, four]
        + [low(width, 3 * wide), low(wide, width), low(width, inner), low(inner, width)]
        + [four, own, own, four, square, four, four]
        + [low(3, rows, width)] * 2
        + [low(rows, width)] * 2
        + [wide_rows(2 * layers, 8, width)]
        + [wide_rows(8, width)] * 4
        + [wide_rows(SMALL_ROWS, width), lines, lines, lines]
        + [low(layers, 2 * width, width), low(layers, width, width)]
        + [ring_got(2 * width, PIECES), ring_got(width, 1)]
        + [wide_rows(small_rows, 128)]
        + [wide_rows(2, 1, ring_count - 1, small_rows // (2 * ring_count), 128)]
        + [sems(exchanges)] * 2
        + [sems(1 + 2 * layers, 9)]
        + [sems(layers, 2, PIECES, steps)] * 2
        + [sems(layers, 2, 1, steps)] * 2
        + [sems(2, 1, steps)] * 2
        + [sems(4 * layers)]
    )
    return pl.pallas_call(
        functools.partial(backward_body, layers, head_count, count),
        name="backward",
        out_shape=[
            jax.ShapeDtypeStruct((rows, width), F32),
            jax.ShapeDtypeStruct((rows, width), F32),
            jax.ShapeDtypeStruct((layers, 3 * used, width), BF16),
            jax.ShapeDtypeStruct((layers, used, width), BF16),
            jax.ShapeDtypeStruct((layers, width, inner), BF16),
            jax.ShapeDtypeStruct((layers, inner, width), BF16),
            jax.ShapeDtypeStruct((SMALL_ROWS, width), F32),
        ],
        in_specs=[in_vmem] * 2 + [in_hbm] * 17 + [in_vmem] * 6,
        out_specs=[in_vmem] * 2 + [in_hbm] * 4 + [in_vmem],
        scratch_shapes=scratch,
        compiler_params=pltpu.CompilerParams(
            collective_id=1, has_side_effects=True, vmem_limit_bytes=65400 * 1024
        ),
    )(*inputs)


SMALL_ROWS = 32


class Ring:
    def __init__(self, count):
        self.count = count
        self.steps = 2 * (count - 1)
        self.place = self.place_of(lax.axis_index("dp"))
        self.sides = (
            self.number_of((self.place + 1) % count),
            self.number_of((self.place + count - 1) % count),
        )

    def place_of(self, number):
        row, side = number // 2, number % 2
        return row + side * (self.count - 1 - 2 * row)

    def number_of(self, place):
        side = place // (self.count // 2)
        return 2 * (place + side * (self.count - 1 - 2 * place)) + side

    def streams(self, *sets):
        return [
            (leaf, way, sub)
            for leaf in sets
            for sub in range(leaf[1].shape[1])
            for way in range(2)
        ]

    def rows(self, stream, step):
        (data, got, _, _), way, sub = stream
        piece = got.shape[3]
        if way == 0:
            chunk = (self.place + 3 * self.count - step) % self.count
        else:
            chunk = (self.place + step) % self.count
        first = ((sub * 2 + way) * self.count + chunk) * piece
        return pl.ds(pl.multiple_of(first, piece), piece)

    def copy(self, stream, step, gather):
        (data, got, send_sems, recv_sems), way, sub = stream
        rows = self.rows(stream, step)
        return pltpu.make_async_remote_copy(
            src_ref=data.at[rows],
            dst_ref=data.at[rows] if gather else got.at[way, sub, step],
            send_sem=send_sems.at[way, sub, step],
            recv_sem=recv_sems.at[way, sub, step],
            device_id={"dp": self.sides[way]},
            device_id_type=MESH,
        )

    def start(self, streams):
        for stream in streams:
            self.copy(stream, 0, False).start()

    def add(self, stream, step):
        (data, got, _, _), way, sub = stream
        self.copy(stream, step, False).wait_recv()
        rows = self.rows(stream, step + 1)
        data[rows] = data[rows] + got[way, sub, step]

    def drain(self, streams):
        for step in range(self.count - 1, self.steps):
            for stream in streams:
                self.copy(stream, step, True).wait_send()


def ring_fits(count, rows):
    return count == 8 and rows % (2 * count * 16) == 0


def widen_body(
    wide,
    lengths,
    stream,
    gradient,
    out_in,
    up_in,
    down_in,
    small,
    result,
    d_tokens,
    d_out,
    d_up,
    d_down,
    d_bias,
    d_up_bias,
    *kinds,
):
    number = pl.program_id(0)
    rows, width = stream.shape
    layers, _, used = d_bias.shape
    place = lax.axis_index("tensor")
    length = lengths[place, 0] + lengths[place, 1]
    row = number * rows + lax.broadcasted_iota(jnp.int32, (rows, width), 0)
    result[...] = jnp.where(row < length, stream[...], 0.0).astype(BF16)
    d_tokens[...] = gradient[...]
    d_out[...] = out_in[...].astype(F32)
    d_up[...] = up_in[...].astype(F32)
    d_down[...] = down_in[...].astype(F32)

    @pl.when(number == 0)
    def _():
        for kind, leaf in enumerate(kinds):
            for at in range(layers):
                first = 2 * (kind * layers + at)
                leaf[at] = small[first : first + 2]
        first = 8 * layers
        for at in range(layers):
            for half in range(2):
                start = 2 * half * wide
                d_bias[at, half : half + 1] = small[
                    first + at : first + at + 1, start : start + used
                ]
        first += layers
        d_up_bias[...] = small[first : first + layers]


def run_widen(lengths, stream, gradient, d_out, d_up, d_down, small, wide, used):
    rows, width = stream.shape
    layers = d_out.shape[0]
    parts = 4
    steps = layers * parts

    def rows_of(total):
        return pl.BlockSpec((total // steps, width), lambda at: (at, 0))

    def block(leaf):
        return pl.BlockSpec(
            (1, leaf.shape[1] // parts, width), lambda at: (at // parts, at % parts, 0)
        )

    def whole(*shape):
        return pl.BlockSpec(shape, lambda at: (0,) * len(shape))

    def full(*shape):
        return jax.ShapeDtypeStruct(shape, F32)

    return pl.pallas_call(
        functools.partial(widen_body, wide),
        name="widen",
        grid=(steps,),
        out_shape=[
            jax.ShapeDtypeStruct((rows, width), BF16),
            full(rows, width),
            full(*d_out.shape),
            full(*d_up.shape),
            full(*d_down.shape),
            full(layers, 2, used),
            full(layers, width),
            *[full(layers, 2, width)] * 4,
        ],
        in_specs=[
            pl.BlockSpec(memory_space=pltpu.SMEM),
            rows_of(rows),
            rows_of(rows),
            block(d_out),
            block(d_up),
            block(d_down),
            whole(*small.shape),
        ],
        out_specs=[
            rows_of(rows),
            rows_of(rows),
            block(d_out),
            block(d_up),
            block(d_down),
            whole(layers, 2, used),
            whole(layers, width),
            *[whole(layers, 2, width)] * 4,
        ],
    )(lengths, stream, gradient, d_out, d_up, d_down, small)


def per_device(
    tokens,
    cotangent,
    segments,
    lengths,
    rel_index,
    w_qkv,
    qv_bias,
    w_out,
    w_fc1,
    fc1_bias,
    w_fc2,
    rel_table,
    ln_gain,
    ln_bias,
    layer_scale,
    row_bias,
):
    own_rows, width = tokens.shape
    group_rows, bin_rows = rel_index.shape
    layer_count = w_qkv.shape[0]
    head_count = rel_table.shape[2]
    local_width = w_qkv.shape[3]
    wide = -(-local_width // 256) * 256
    bin_total = group_rows // bin_rows
    place = lax.axis_index("tensor")
    assert own_rows == bin_rows and bin_total == 4

    extra = wide - local_width
    qkv_used = jnp.pad(w_qkv, ((0, 0), (0, 0), (0, 0), (0, extra))).reshape(
        layer_count, width, 3 * wide
    )
    norms = (ln_gain, ln_bias, layer_scale, row_bias)

    (
        gath_a,
        qkv,
        shares,
        mixture,
        gath_b,
        slope,
        active,
        gath_z,
        spots,
        turned,
        gradient,
        normal_a,
        normal_b,
        inverse,
        branch_a,
        branch_b,
        middle,
    ) = run_forward(
        lengths,
        rel_index,
        rel_table,
        (tokens, cotangent),
        (qkv_used, qv_bias, w_out, w_fc1, fc1_bias, w_fc2),
        norms,
    )
    dp_count = lax.axis_size("dp")
    with_ring = ring_fits(dp_count, width)
    gradient, stream, *sums = run_backward(
        dp_count if with_ring else None,
        (
            gradient,
            middle,
            branch_a,
            branch_b,
            normal_a,
            normal_b,
            inverse,
            mixture,
            qkv,
            shares,
            gath_a,
            active,
            slope,
            gath_b,
            gath_z,
            qkv_used,
            w_out,
            w_fc1,
            w_fc2,
            spots,
            turned,
            fc1_bias,
            ln_gain,
            layer_scale,
            row_bias,
        ),
        head_count,
    )
    if not with_ring:
        sums = lax.psum(sums, "dp")
    *weight_sums, small = sums
    d_qkv, d_out, d_up, d_down = weight_sums
    result, d_tokens, d_out, d_up, d_down, d_bias, d_up_bias, *kinds = run_widen(
        lengths, stream, gradient, d_out, d_up, d_down, small, wide, local_width
    )
    d_qkv = jnp.transpose(
        d_qkv.astype(F32).reshape(layer_count, 3, local_width, width), (0, 3, 1, 2)
    )
    first = 8 * layer_count + 2 * layer_count
    d_table = small[first : first + layer_count * head_count, : rel_table.shape[1]]
    d_table = jnp.transpose(d_table.reshape(layer_count, head_count, -1), (0, 2, 1))
    return (
        result,
        d_tokens,
        d_qkv,
        d_bias,
        d_out,
        d_up,
        d_up_bias,
        d_down,
        d_table,
        *kinds,
    )


def solution(mesh):
    in_specs = (
        P(("dp", "tensor"), None),
        P(("dp", "tensor"), None),
        P("dp"),
        P("dp", None),
        P("dp", None),
        P(None, None, None, "tensor"),
        P(None, None, "tensor"),
        P(None, "tensor", None),
        P(None, None, "tensor"),
        P(None, "tensor"),
        P(None, "tensor", None),
        P(None, None, "tensor"),
        P(),
        P(),
        P(),
        P(),
    )
    out_specs = (
        P(("dp", "tensor"), None),
        P(("dp", "tensor"), None),
        P(None, None, None, "tensor"),
        P(None, None, "tensor"),
        P(None, "tensor", None),
        P(None, None, "tensor"),
        P(None, "tensor"),
        P(None, "tensor", None),
        P(None, None, "tensor"),
        P(),
        P(),
        P(),
        P(),
    )
    return jax.shard_map(
        per_device, mesh=mesh, in_specs=in_specs, out_specs=out_specs, check_vma=False
    )
```

```python
import functools
from typing import NamedTuple

import jax
import jax.numpy as jnp
from jax import lax
from jax.experimental import pallas as pl
from jax.experimental.pallas import tpu as pltpu
from jax.sharding import PartitionSpec as P

HEAD_DIM = 64
SIDE = 14
STRIDE = 2 * SIDE - 1
CELLS = SIDE * SIDE
CHUNK = 32
MESH = pl.DeviceIdType.MESH
BF16 = jnp.bfloat16
F32 = jnp.float32


def dot(left_side, right_side, left_axis=1, right_axis=0):
    return lax.dot_general(
        left_side,
        right_side,
        (((left_axis,), (right_axis,)), ((), ())),
        preferred_element_type=F32,
    )


class Group:
    def __init__(self, send_sems, recv_sems):
        own = lax.axis_index("tensor")
        self.core = own % 2
        self.near = own + 1 - 2 * self.core
        self.far = (own + 2) % 4
        self.far_chip = 1 - own // 2
        self.sems = (send_sems, recv_sems)

    def greet(self, barrier):
        for other in (self.near, self.far, self.far + 1 - 2 * self.core):
            pl.semaphore_signal(
                barrier, inc=1, device_id={"tensor": other}, device_id_type=MESH
            )
        return 3

    def copy(self, sent, arrived, source, target, other):
        return pltpu.make_async_remote_copy(
            src_ref=source,
            dst_ref=target,
            send_sem=self.sems[0].at[sent],
            recv_sem=self.sems[1].at[arrived],
            device_id={"tensor": other},
            device_id_type=MESH,
        )


class Exchange:
    COPIES = 10

    def __init__(self, group, base, gath, part, got, summed):
        self.group, self.base = group, base
        self.gath, self.part, self.got, self.summed = gath, part, got, summed
        self.rows = (part if gath is None else gath).shape[1] // 2
        self.keep = group.core * self.rows
        self.give = (1 - group.core) * self.rows

    def slot(self, stage):
        core = self.group.core
        return 2 + core + stage * (1 - 2 * core)

    def span(self, first):
        return pl.ds(pl.multiple_of(first, self.rows), self.rows)

    def symmetric(self, number, source, target, other):
        at = self.base + number
        return self.group.copy(at, at, source, target, other)

    def to_near(self):
        return self.symmetric(0, self.gath.at[0], self.gath.at[1], self.group.near)

    def across(self, stage):
        core, rows = self.group.core, self.span(self.keep)
        source = core + stage * (1 - 2 * core)
        return self.symmetric(
            2 + stage,
            self.gath.at[source, rows],
            self.gath.at[self.slot(stage), rows],
            self.group.far,
        )

    def relay(self, stage):
        rows = self.span(self.keep)
        return self.symmetric(
            4 + stage,
            self.gath.at[self.slot(stage), rows],
            self.gath.at[self.slot(1 - stage), rows],
            self.group.near,
        )

    def sum_near(self):
        return self.symmetric(1, self.part.at[1], self.got.at[0], self.group.near)

    def pair(self, stage):
        return self.symmetric(
            6 + stage,
            self.part.at[self.slot(stage), self.span(self.give)],
            self.got.at[1, self.span(stage * self.rows)],
            self.group.near,
        )

    def home(self, stage, sender):
        return self.group.copy(
            self.base + 8 + stage,
            self.base + 8 + sender,
            self.summed.at[self.span(stage * self.rows)],
            self.got.at[2, self.span(sender * self.rows)],
            self.group.far_chip * 2 + stage,
        )

    def start(self):
        self.to_near().start()

        @pl.when(self.group.core == 0)
        def _():
            self.across(0).start()

    def spread(self):
        self.to_near().wait_recv()

        @pl.when(self.group.core == 1)
        def _():
            self.across(0).start()

        self.across(1).start()

    def pass_on(self, stage):
        self.across(stage).wait_recv()
        self.relay(stage).start()

    def arrived(self, stage):
        self.relay(stage).wait_recv()

    def send_sum(self, stage):
        self.pair(stage).wait_recv()
        rows = self.span(stage * self.rows)
        self.summed[rows] = self.part[self.slot(stage), self.span(self.keep)] + self.got[1, rows]
        self.home(stage, self.group.core).start()

    def finish(self):
        self.sum_near().wait_recv()
        for sender in range(2):
            self.home(0, sender).wait_recv()

    def drain_gather(self):
        self.to_near().wait_send()
        for stage in range(2):
            self.across(stage).wait_send()
            self.relay(stage).wait_send()

    def drain_sum(self):
        self.sum_near().wait_send()
        for stage in range(2):
            self.pair(stage).wait_send()
            self.home(stage, self.group.core).wait_send()


def by_chunk(total_rows, body, size=CHUNK):
    def step(at, carry):
        return body(pl.ds(pl.multiple_of(at * size, size), size), carry)

    return step, total_rows // size


def norm_chunk(values, gain, shift):
    center = values - jnp.mean(values, -1, keepdims=True)
    inverse = lax.rsqrt(jnp.mean(center * center, -1, keepdims=True) + 1e-06)
    normal = center * inverse
    return (normal * gain + shift).astype(BF16), normal, inverse


def gelu_parts(values):
    share = 0.5 * (1.0 + lax.erf(values * 0.7071067811865476))
    slope = share + values * (jnp.exp(-0.5 * values * values) * 0.3989422804014327)
    return values * share, slope


SPAN = 384
LAST = (SIDE - 1) * (STRIDE + 1)
CLASS = LAST + 1
TABLE_WIDTH = 2 * SPAN


def prepare(head_count, lengths, index_rows, table, bias, spots, turned, same):
    rows = bias.shape[3]
    own = lax.axis_index("tensor")
    order = (own, own + 1 - 2 * (own % 2), (own + 2) % 4, 3 - own)

    ones = []
    for slot in range(4):
        first = lengths[order[slot], 0]
        both = first + lengths[order[slot], 1]

        def pick(row):
            return index_rows[pl.ds(order[slot] * rows + row, 1), :]

        at = lax.broadcasted_iota(jnp.int32, (1, rows), 1)
        code = LAST - jnp.where(at < first, pick(1), pick(first + 1))
        code = jnp.where((at == 0) | (at == first), CLASS, code)
        code = jnp.where(at < both, code, -1)
        upright = lax.broadcasted_iota(jnp.int32, (SPAN, rows), 0)
        spots[slot] = (upright == code).astype(F32).astype(BF16)
        column = jnp.transpose(jnp.broadcast_to(code.astype(F32), (128, rows)))
        column = jnp.concatenate([column] * (SPAN // 128), -1)
        flat = lax.broadcasted_iota(jnp.int32, (rows, SPAN), 1).astype(F32)
        ones.append((flat == column).astype(F32).astype(BF16))
        mirrored = jnp.where(column < CLASS, LAST - column, column)
        mirrored = jnp.where(column < 0, -1.0, mirrored)
        turned[slot] = (flat == mirrored).astype(F32).astype(BF16)

        def image_of(values):
            return (values >= first).astype(jnp.int32) + (values >= both).astype(jnp.int32)

        by_row = image_of(lax.broadcasted_iota(jnp.int32, (rows, rows), 0))
        by_col = image_of(lax.broadcasted_iota(jnp.int32, (rows, rows), 1))
        same[slot] = (by_row == by_col).astype(F32)

    key_at = lax.broadcasted_iota(jnp.int32, (SPAN, SPAN), 0)
    query_at = lax.broadcasted_iota(jnp.int32, (SPAN, SPAN), 1)
    shift = SPAN - LAST

    def each(at, carry):
        row = table[pl.ds(at, 1), :]
        rolled = pltpu.roll(
            jnp.broadcast_to(row, (SPAN, TABLE_WIDTH)), 0, 1, stride=1, stride_axis=0
        )
        pairs = rolled[:, SPAN:]
        tail = shift + STRIDE * STRIDE
        pairs = jnp.where(query_at == CLASS, row[:, tail : tail + 1], pairs)
        pairs = jnp.where(key_at == CLASS, row[:, tail + 1 : tail + 2], pairs)
        pairs = jnp.where(
            (query_at == CLASS) & (key_at == CLASS), row[:, tail + 2 : tail + 3], pairs
        ).astype(BF16)
        for slot in range(4):
            half = dot(ones[slot], pairs, 1, 1).astype(BF16)
            looked = dot(half, spots[slot])
            bias[at // head_count, slot, at % head_count] = jnp.where(
                same[slot] > 0.5, looked, -1000000000.0
            ).astype(BF16)
        return carry

    lax.fori_loop(0, table.shape[0], each, 0)


def shifted_table(rel_table):
    layers, entries, head_count = rel_table.shape
    shift = SPAN - LAST
    table = jnp.transpose(rel_table, (0, 2, 1)).reshape(layers * head_count, entries).astype(F32)
    return jnp.pad(table, ((0, 0), (shift, TABLE_WIDTH - shift - entries)))


def table_row(pairs):
    query_at = lax.broadcasted_iota(jnp.int32, (SPAN, SPAN), 0)
    key_at = lax.broadcasted_iota(jnp.int32, (SPAN, SPAN), 1)
    zero = jnp.zeros((SPAN, SPAN), F32)
    patches = jnp.where((query_at <= LAST) & (key_at <= LAST), pairs, zero)
    rolled = pltpu.roll(
        jnp.concatenate([patches, zero], -1), 0, 1, stride=1, stride_axis=0
    )
    row = jnp.sum(rolled, 0, keepdims=True)
    at = lax.broadcasted_iota(jnp.int32, (1, TABLE_WIDTH), 1)
    tails = (
        (query_at == CLASS) & (key_at <= LAST),
        (query_at <= LAST) & (key_at == CLASS),
        (query_at == CLASS) & (key_at == CLASS),
    )
    for number, mask in enumerate(tails):
        row = jnp.where(at == STRIDE * STRIDE + number, jnp.sum(jnp.where(mask, pairs, zero)), row)
    return row


class Names:
    def __init__(self, names, refs):
        for name, ref in zip(names, refs, strict=True):
            setattr(self, name, ref)


def load_all(pairs, sems):
    steps = []
    for place, (source, target) in enumerate(pairs):
        step = pltpu.make_async_copy(source, target, sems.at[place])
        step.start()
        steps.append(step)
    return steps


def each_chunk(rows, body):
    def step(at, carry):
        body(pl.ds(pl.multiple_of(at * CHUNK, CHUNK), CHUNK))
        return carry

    lax.fori_loop(0, rows // CHUNK, step, 0)


def attend_rows(refs, at, slot, first, head_count):
    qkv = refs.qkv
    rows = qkv.shape[2] // 2
    wide = qkv.shape[3] // 3
    span = pl.ds(first, rows)
    heads = []
    for head in range(head_count):
        lanes = slice(head * HEAD_DIM, (head + 1) * HEAD_DIM)
        queries = qkv[at, slot, span, 0:wide][:, lanes]
        keys = qkv[at, slot, :, wide : 2 * wide][:, lanes]
        values = qkv[at, slot, :, 2 * wide : 3 * wide][:, lanes]
        scores = dot(queries, keys, 1, 1) + refs.bias[at, slot, head, span].astype(F32)
        powers = jnp.exp(scores - jnp.max(scores, -1, keepdims=True))
        weights = (powers / jnp.sum(powers, -1, keepdims=True)).astype(BF16)
        refs.weights[at, slot, head, span] = weights
        heads.append(dot(weights, values).astype(BF16))
    heads.append(jnp.zeros((rows, wide - head_count * HEAD_DIM), BF16))
    refs.mixture[at, slot, span] = jnp.concatenate(heads, -1)


class ForwardInputs(NamedTuple):
    lengths: object
    tokens: object
    cotangent: object
    qv_bias: object
    fc1_bias: object
    table: object
    ln_gain: object
    ln_bias: object
    layer_scale: object
    row_bias: object
    index_in: object
    w_qkv_in: object
    w_out_in: object
    w_up_in: object
    w_down_in: object


class ForwardKept(NamedTuple):
    gath_a: object
    qkv: object
    weights: object
    mixture: object
    gath_b: object
    slope: object
    active: object
    normal_a: object
    branch_a: object
    normal_b: object
    branch_b: object
    inverse: object
    spots: object
    turned: object


class ForwardOutputs(NamedTuple):
    gath_z_out: object
    grad: object
    stream: object


class ForwardScratch(NamedTuple):
    gath_z: object
    bias: object
    same: object
    index_rows: object
    w_qkv: object
    w_out: object
    w_up: object
    w_down: object
    qkv_bias: object
    up_bias: object
    hidden: object
    part: object
    got: object
    summed: object
    own: object
    send_sems: object
    recv_sems: object
    load_sems: object
    out_sems: object


def forward_body(layers, head_count, *all_refs):
    kept_outs = tuple(name + "_kept" for name in ForwardKept._fields)
    refs = Names(
        (*ForwardInputs._fields, *kept_outs, *ForwardOutputs._fields, *ForwardKept._fields, *ForwardScratch._fields), all_refs
    )
    stream, own, got, part = refs.stream, refs.own, refs.got, refs.part
    rows, width = stream.shape
    half = rows // 2
    last = layers - 1
    used = refs.w_out_in.shape[1]
    wide = refs.w_out.shape[1]
    loads = load_all(
        (
            (refs.index_in, refs.index_rows),
            (refs.w_qkv_in, refs.w_qkv),
            *(
                (refs.w_out_in.at[at], refs.w_out.at[at, pl.ds(0, used)])
                for at in range(layers)
            ),
            (refs.w_up_in, refs.w_up),
            (refs.w_down_in, refs.w_down),
        ),
        refs.load_sems,
    )
    group = Group(refs.send_sems, refs.recv_sems)
    barrier = pltpu.get_barrier_semaphore()
    greeted = group.greet(barrier)
    pl.semaphore_wait(barrier, greeted)
    early = Exchange(group, 2 * Exchange.COPIES, refs.gath_z, None, None, None)

    def load(span):
        stream[span] = refs.tokens[span].astype(F32)

    each_chunk(rows, load)
    refs.qkv_bias[...] = jnp.zeros_like(refs.qkv_bias)
    for at in range(layers):
        refs.w_out[at, used:] = jnp.zeros_like(refs.w_out[at, used:])
        refs.up_bias[at] = refs.fc1_bias[at : at + 1].astype(F32)
        for half_at in range(2):
            first = 2 * half_at * wide
            refs.qkv_bias[at, :, first : first + used] = refs.qv_bias[
                at, half_at : half_at + 1
            ].astype(F32)

    def keep(number, at):
        source = getattr(refs, ForwardKept._fields[number])
        target = getattr(refs, kept_outs[number])
        if number < 12:
            source, target = source.at[at], target.at[at]
        return pltpu.make_async_copy(source, target, refs.out_sems.at[number, at])

    def layer(at, carry):
        trade = Exchange(group, 0, refs.gath_a.at[at], part, got, refs.summed)

        def enter(span):
            low, normal, inv = norm_chunk(
                stream[span], refs.ln_gain[at, 0:1], refs.ln_bias[at, 0:1]
            )
            refs.gath_a[at, 0, span] = low
            refs.normal_a[at, span] = normal
            refs.inverse[at, 0, span] = jnp.broadcast_to(inv, (CHUNK, 128))

        each_chunk(rows, enter)
        trade.start()

        @pl.when(at == 0)
        def _():
            place = lax.axis_index("tensor")
            length = refs.lengths[place, 0] + refs.lengths[place, 1]

            def mask(number, carry):
                span = pl.ds(pl.multiple_of(number * CHUNK, CHUNK), CHUNK)
                row = number * CHUNK + lax.broadcasted_iota(jnp.int32, (CHUNK, width), 0)
                values = jnp.where(row < length, refs.cotangent[span].astype(F32), 0.0)
                refs.grad[span] = values
                refs.gath_z[0, span] = (values * refs.layer_scale[last, 1:2]).astype(BF16)
                return carry

            lax.fori_loop(0, rows // CHUNK, mask, 0)

        trade.spread()

        @pl.when(at == 0)
        def _():
            early.start()
            early.spread()
            loads[0].wait()
            prepare(
                head_count,
                refs.lengths,
                refs.index_rows,
                refs.table,
                refs.bias,
                refs.spots,
                refs.turned,
                refs.same,
            )
            keep(12, 0).start()
            keep(13, 0).start()
            for step in loads[1:]:
                step.wait()

        scale = jnp.concatenate(
            [
                jnp.full((1, refs.qkv.shape[3] // 3), HEAD_DIM**-0.5, F32),
                jnp.full((1, 2 * refs.qkv.shape[3] // 3), 1.0, F32),
            ],
            -1,
        )

        def project(slot):
            mixed = dot(refs.gath_a[at, slot], refs.w_qkv[at])
            mixed = (mixed + refs.qkv_bias[at]).astype(BF16).astype(F32) * scale
            refs.qkv[at, slot] = mixed.astype(BF16)

        def attend(slot, first):
            attend_rows(refs, at, slot, first, head_count)
            return dot(refs.mixture[at, slot, pl.ds(first, half)], refs.w_out[at])

        turn = 2 * (at == 0).astype(jnp.int32)

        @pl.when(at == 0)
        def _():
            trade.pass_on(0)
            trade.pass_on(1)

        def one_slot(number, carry):
            role = (number + turn) % 4
            stage = role % 2
            away = role >= 2
            slot = jnp.where(away, trade.slot(stage), role)

            @pl.when(away)
            def _():
                trade.arrived(stage)

            project(slot)

            def one(place, carry):
                first = pl.multiple_of(
                    place * trade.keep + (1 - place) * trade.give, half
                )
                result = attend(slot, first)

                @pl.when(role == 0)
                def _():
                    own[pl.ds(first, half)] = result

                @pl.when(role > 0)
                def _():
                    part[slot, pl.ds(first, half)] = result.astype(BF16)

                @pl.when(away & (place == 0))
                def _():
                    trade.pair(stage).start()

                return carry

            lax.fori_loop(0, 2, one, 0)

            @pl.when(away)
            def _():
                trade.send_sum(stage)

            @pl.when(role == 1)
            def _():
                trade.sum_near().start()

            @pl.when((at > 0) & (role == 1))
            def _():
                trade.pass_on(0)

            @pl.when((at > 0) & (role == 2))
            def _():
                trade.pass_on(1)

            return carry

        lax.fori_loop(0, 4, one_slot, 0)
        for number in range(4):
            keep(number, at).start()

        @pl.when(at == 0)
        def _():
            for stage in range(2):
                early.pass_on(stage)

        trade.finish()

        def between(span):
            total = own[span] + got[0, span].astype(F32) + got[2, span].astype(F32)
            branch = total + refs.row_bias[at, 0:1]
            refs.branch_a[at, span] = branch
            middle = stream[span] + refs.layer_scale[at, 0:1] * branch
            stream[span] = middle
            low, normal, inv = norm_chunk(middle, refs.ln_gain[at, 1:2], refs.ln_bias[at, 1:2])
            refs.gath_b[at, 0, span] = low
            refs.normal_b[at, span] = normal
            refs.inverse[at, 1, span] = jnp.broadcast_to(inv, (CHUNK, 128))

        each_chunk(rows, between)
        for number in (7, 8, 9, 11):
            keep(number, at).start()

        @pl.when(at < last)
        def _():
            trade_b = Exchange(
                group, Exchange.COPIES, refs.gath_b.at[at], part, got, refs.summed
            )
            trade_b.start()
            trade.drain_gather()
            trade.drain_sum()
            trade_b.spread()

            def raise_rows(slot):
                refs.hidden[...] = dot(refs.gath_b[at, slot], refs.w_up[at]) + refs.up_bias[at]

                def act(place, carry):
                    span = pl.ds(pl.multiple_of(place * 16, 16), 16)
                    high, incline = gelu_parts(refs.hidden[span])
                    refs.active[at, slot, span] = high.astype(BF16)
                    refs.slope[at, slot, span] = incline.astype(BF16)
                    return carry

                lax.fori_loop(0, rows // 16, act, 0)

            def lower(slot, first, count):
                return dot(refs.active[at, slot, pl.ds(first, count)], refs.w_down[at])

            def one_slot(role, carry):
                stage = role % 2
                away = role >= 2
                slot = jnp.where(away, trade_b.slot(stage), role)

                @pl.when(away)
                def _():
                    trade_b.arrived(stage)

                raise_rows(slot)

                def one(place, carry):
                    first = pl.multiple_of(
                        place * trade_b.keep + (1 - place) * trade_b.give, half
                    )
                    result = lower(slot, first, half)

                    @pl.when(role == 0)
                    def _():
                        own[pl.ds(first, half)] = result

                    @pl.when(role > 0)
                    def _():
                        part[slot, pl.ds(first, half)] = result.astype(BF16)

                    @pl.when(away & (place == 0))
                    def _():
                        trade_b.pair(stage).start()

                    return carry

                lax.fori_loop(0, 2, one, 0)

                @pl.when(away)
                def _():
                    trade_b.send_sum(stage)

                @pl.when(role == 1)
                def _():
                    trade_b.sum_near().start()
                    trade_b.pass_on(0)

                @pl.when(role == 2)
                def _():
                    trade_b.pass_on(1)

                return carry

            lax.fori_loop(0, 4, one_slot, 0)
            for number in (4, 5, 6):
                keep(number, at).start()
            trade_b.finish()

            def after(span):
                total = own[span] + got[0, span].astype(F32) + got[2, span].astype(F32)
                branch = total + refs.row_bias[at, 1:2]
                refs.branch_b[at, span] = branch
                stream[span] = stream[span] + refs.layer_scale[at, 1:2] * branch

            each_chunk(rows, after)
            keep(10, at).start()
            trade_b.drain_gather()
            trade_b.drain_sum()

        @pl.when(at == last)
        def _():
            pltpu.make_async_copy(
                refs.gath_b.at[at, 0], refs.gath_b_kept.at[at, 0], refs.out_sems.at[4, at]
            ).start()
            trade.drain_gather()
            trade.drain_sum()

        return carry

    lax.fori_loop(0, layers, layer, 0)
    for stage in range(2):
        early.arrived(stage)
    early.drain_gather()
    leave = pltpu.make_async_copy(refs.gath_z, refs.gath_z_out, refs.load_sems.at[0])
    leave.start()
    pltpu.make_async_copy(
        refs.gath_b.at[last, 0], refs.gath_b_kept.at[last, 0], refs.out_sems.at[4, last]
    ).wait()
    for at in range(layers):
        for number in range(12):
            if at < last or number not in (4, 5, 6, 10):
                keep(number, at).wait()
    keep(12, 0).wait()
    keep(13, 0).wait()
    leave.wait()


def run_forward(lengths, index_rows, rel_table, rows_in, weights, norms):
    tokens, cotangent = rows_in
    rows, width = tokens.shape
    w_qkv, qv_bias, w_out, w_up, fc1_bias, w_down = weights
    layers, _, head_count = rel_table.shape
    wide = w_qkv.shape[2] // 3
    inner = w_up.shape[2]
    in_vmem = pl.BlockSpec(memory_space=pltpu.VMEM)
    in_hbm = pl.BlockSpec(memory_space=pl.ANY)

    def low(*shape):
        return jax.ShapeDtypeStruct(shape, BF16)

    def full(*shape):
        return jax.ShapeDtypeStruct(shape, F32)

    kept = [
        low(layers, 4, *tail)
        for tail in (
            (rows, width),
            (rows, 3 * wide),
            (head_count, rows, rows),
            (rows, wide),
            (rows, width),
            (rows, inner),
            (rows, inner),
        )
    ]
    own = full(rows, width)
    kept += [full(layers, rows, width)] * 4 + [full(layers, 2, rows, 128)]
    kept += [low(4, SPAN, rows), low(4, rows, SPAN)]
    near = [own, own]
    scratch = [
        *kept,
        low(4, rows, width),
        low(layers, 4, head_count, rows, rows),
        full(4, rows, rows),
        jax.ShapeDtypeStruct(index_rows.shape, index_rows.dtype),
        low(*w_qkv.shape),
        low(layers, wide, width),
        low(*w_up.shape),
        low(*w_down.shape),
        full(layers, 1, 3 * wide),
        full(layers, 1, inner),
        full(rows, inner),
        low(4, rows, width),
        low(3, rows, width),
        low(rows, width),
        own,
    ]
    copies = 3 * Exchange.COPIES
    return pl.pallas_call(
        functools.partial(forward_body, layers, head_count),
        name="forward",
        out_shape=[*kept, low(4, rows, width), *near],
        in_specs=[pl.BlockSpec(memory_space=pltpu.SMEM)] + [in_vmem] * 9 + [in_hbm] * 5,
        out_specs=[in_hbm] * (len(kept) + 1) + [in_vmem] * len(near),
        scratch_shapes=[
            *[pltpu.VMEM(leaf.shape, leaf.dtype) for leaf in scratch],
            pltpu.SemaphoreType.DMA((copies,)),
            pltpu.SemaphoreType.DMA((copies,)),
            pltpu.SemaphoreType.DMA((4 + layers,)),
            pltpu.SemaphoreType.DMA((len(kept), layers)),
        ],
        compiler_params=pltpu.CompilerParams(
            collective_id=0, has_side_effects=True, vmem_limit_bytes=65400 * 1024
        ),
    )(
        lengths,
        tokens,
        cotangent,
        qv_bias,
        fc1_bias,
        shifted_table(rel_table),
        *norms,
        index_rows,
        w_qkv,
        w_out,
        w_up,
        w_down,
    )


def fold(values):
    return jnp.sum(values.reshape(-1, 8, values.shape[-1]), 0)


def enter_back(grad, branch, scale, gath, sums):
    rows, width = grad.shape

    def body(span, carry):
        values = grad[span]
        gath[0, span] = (values * scale).astype(BF16)
        return carry[0] + fold(values * branch[span]), carry[1] + fold(values)

    step, count = by_chunk(rows, body)
    zero = jnp.zeros((8, width), F32)
    by_branch, alone = lax.fori_loop(0, count, step, (zero, zero))
    sums[2:3] = jnp.sum(by_branch, 0, keepdims=True)
    sums[3:4] = jnp.sum(alone, 0, keepdims=True) * scale


def leave_back(grad, own, got, normal, inverse, gain, sums):
    rows, width = grad.shape

    def body(span, carry):
        total = own[span] + got[0, span].astype(F32) + got[2, span].astype(F32)
        unit = normal[span]
        scaled = total * gain
        centered = (
            scaled
            - jnp.mean(scaled, -1, keepdims=True)
            - unit * jnp.mean(scaled * unit, -1, keepdims=True)
        )
        grad[span] = grad[span] + inverse[span, 0:1] * centered
        return carry[0] + fold(total * unit), carry[1] + fold(total)

    step, count = by_chunk(rows, body)
    zero = jnp.zeros((8, width), F32)
    by_unit, alone = lax.fori_loop(0, count, step, (zero, zero))
    sums[0:1] = jnp.sum(by_unit, 0, keepdims=True)
    sums[1:2] = jnp.sum(alone, 0, keepdims=True)


def weight_grad(left, right, out, start, count, tick=None):
    block = 256
    used = count * block // left.shape[2]

    def step(place, carry):
        span = pl.ds(pl.multiple_of(place * block, block), block)
        total = None
        for slot in range(4):
            term = dot(left[slot, :, span], right[slot], 0, 0)
            total = term if total is None else total + term
        there = pl.ds(pl.multiple_of(start + place * used, 16), used)
        out[there] = total[:used].astype(out.dtype)
        return carry

    if tick is None:
        lax.fori_loop(0, left.shape[2] // block, step, 0)
    else:
        for place in range(left.shape[2] // block):
            step(place, 0)
            tick()


PIECES = 2


class Ticker:
    def __init__(self, ring):
        self.ring = ring
        self.under_way = []

    def add(self, streams, done):
        self.ring.start(streams)
        self.under_way.append([streams, 0, done])

    def tick(self):
        if self.under_way:
            self.one()

    def one(self):
        ring = self.ring
        streams, step, done = self.under_way.pop(0)
        turn = ring.count - 1
        for stream in streams:
            if step < turn:
                ring.add(stream, step)
                ring.copy(stream, step, False).wait_send()
            else:
                ring.copy(stream, step, True).wait_recv()
            if step + 1 < ring.steps:
                ring.copy(stream, step + 1, step + 1 >= turn).start()
        if step + 1 < ring.steps:
            self.under_way.append([streams, step + 1, done])
        else:
            ring.drain(streams)
            done()

    def alike(self, step):
        turn = self.ring.count - 1
        return turn - 1 - step if step < turn else self.ring.steps - 1 - step

    def finish(self):
        ring = self.ring
        turn = ring.count - 1
        while self.under_way:
            run = min(self.alike(step) for _, step, _ in self.under_way)
            if run < 2:
                for _ in range(len(self.under_way)):
                    self.one()
                continue
            rings = [tuple(leaf) for leaf in self.under_way]

            def body(number, carry):
                for streams, start, _ in rings:
                    step = start + number
                    for stream in streams:
                        if start < turn:
                            ring.add(stream, step)
                            ring.copy(stream, step, False).wait_send()
                        else:
                            ring.copy(stream, step, True).wait_recv()
                        ring.copy(stream, step + 1, start >= turn).start()
                return carry

            lax.fori_loop(0, run, body, 0)
            for leaf in self.under_way:
                leaf[1] += run


def mlp_loads(refs, at):
    return load_all(
        (
            (refs.branch_b_all.at[at], refs.branch_b),
            (refs.w_down_all.at[at], refs.w_down),
            (refs.slope_all.at[at], refs.slope),
            (refs.w_up_all.at[at], refs.w_up),
            (refs.normal_b_all.at[at], refs.normal_b),
            (refs.inverse_all.at[at, 1], refs.inverse_b),
            (refs.active_all.at[at], refs.active),
            (refs.gath_b_all.at[at], refs.gath_b),
        ),
        refs.load_sems.at[1 + 2 * at],
    )


def attend_loads(refs, at):
    return load_all(
        (
            (refs.branch_a_all.at[at], refs.branch_a),
            (refs.w_out_all.at[at], refs.w_out.at[pl.ds(0, refs.w_out_all.shape[1])]),
            (refs.qkv_all.at[at], refs.qkv),
            (refs.weights_all.at[at], refs.weights),
            (refs.w_qkv_all.at[at], refs.w_qkv),
            (refs.normal_a_all.at[at], refs.normal_a),
            (refs.inverse_all.at[at, 0], refs.inverse_a),
            (refs.mixture_all.at[at], refs.mixture),
            (refs.gath_a_all.at[at], refs.gath_a),
        ),
        refs.load_sems.at[2 + 2 * at],
    )


def front(refs, group, at, tick, begin):
    rows = refs.grad.shape[0]
    half = rows // 2
    ahead = Exchange(
        group, Exchange.COPIES, refs.gath_b, refs.part_f, refs.got_f, refs.summed_f
    )
    trade = Exchange(group, 0, None, refs.part, refs.got, refs.summed)
    loads = load_all(
        (
            (refs.gath_b_all.at[at, 0], refs.gath_b.at[0]),
            (refs.w_up_all.at[at], refs.w_up),
            (refs.w_down_all.at[at], refs.w_down),
            (refs.gath_z, refs.gath_m),
            (refs.normal_b_all.at[at], refs.normal_b),
            (refs.inverse_all.at[at, 1], refs.inverse_b),
            (refs.spots_all, refs.spots),
            (refs.turned_all, refs.turned),
        ),
        refs.load_sems.at[0],
    )
    loads[0].wait()
    ahead.start()
    ahead.spread()
    for load in loads[1:4]:
        load.wait()

    def work(slot):
        refs.hidden[...] = dot(refs.gath_b[slot], refs.w_up[...]) + refs.up_bias[at : at + 1].astype(F32)
        refs.hidden_f[...] = dot(refs.gath_m[slot], refs.w_down[...], 1, 1)

        def act(place, carry):
            span = pl.ds(pl.multiple_of(place * 16, 16), 16)
            high, incline = gelu_parts(refs.hidden[span])
            refs.active[slot, span] = high.astype(BF16)
            back = (refs.hidden_f[span] * incline).astype(BF16)
            refs.d_hidden[slot, span] = back
            refs.up_total[...] += fold(back.astype(F32))
            return carry

        lax.fori_loop(0, rows // 16, act, 0)

    refs.up_total[...] = jnp.zeros_like(refs.up_total)

    def chip_slot(slot, carry):
        work(slot)
        result = dot(refs.d_hidden[slot], refs.w_up[...], 1, 1)
        result_f = dot(refs.active[slot], refs.w_down[...])

        @pl.when(slot == 0)
        def _():
            refs.own[...] = result
            refs.own_f[...] = result_f

        @pl.when(slot == 1)
        def _():
            refs.part[1] = result.astype(BF16)
            refs.part_f[1] = result_f.astype(BF16)

        return carry

    lax.fori_loop(0, 2, chip_slot, 0)
    trade.sum_near().start()
    ahead.sum_near().start()
    ahead.pass_on(0)

    def far_slot(stage, carry):
        slot = ahead.slot(stage)
        ahead.arrived(stage)
        work(slot)

        def one(place, carry):
            first = pl.multiple_of(place * ahead.keep + (1 - place) * ahead.give, half)
            span = pl.ds(first, half)
            refs.part[slot, span] = dot(
                refs.d_hidden[slot, span], refs.w_up[...], 1, 1
            ).astype(BF16)

            @pl.when(place == 0)
            def _():
                trade.pair(stage).start()

            refs.part_f[slot, span] = dot(refs.active[slot, span], refs.w_down[...]).astype(BF16)

            @pl.when(place == 0)
            def _():
                ahead.pair(stage).start()

            return carry

        lax.fori_loop(0, 2, one, 0)
        trade.send_sum(stage)
        ahead.send_sum(stage)

        @pl.when(stage == 0)
        def _():
            ahead.pass_on(1)

        return carry

    lax.fori_loop(0, 2, far_slot, 0)
    data, inner = refs.data_m.at[at], refs.w_down.shape[0]
    weight_grad(refs.active, refs.gath_m, data, 0, inner)
    begin(at, 0, 0)
    weight_grad(refs.gath_b, refs.d_hidden, data, inner, refs.w_up.shape[0])
    begin(at, 0, 1)
    refs.up_sums[at : at + 1] = jnp.sum(refs.up_total[...], 0, keepdims=True)
    for load in loads[4:]:
        load.wait()
    trade.finish()
    tick()
    leave_back(
        refs.grad,
        refs.own,
        refs.got,
        refs.normal_b,
        refs.inverse_b,
        refs.ln_gain[at, 1:2],
        refs.sums.at[2 * at + 1],
    )
    ahead.drain_gather()
    trade.drain_sum()

    def end():
        ahead.finish()
        sums = refs.sums.at[2 * at + 1]
        scale = refs.layer_scale[at, 1:2]
        width = refs.grad.shape[1]

        def body(span, carry):
            branch = (
                refs.own_f[span]
                + refs.got_f[0, span].astype(F32)
                + refs.got_f[2, span].astype(F32)
                + refs.row_bias[at, 1:2]
            )
            refs.stream[span] = refs.middle[span] + scale * branch
            values = refs.grad_in[span]
            return carry[0] + fold(values * branch), carry[1] + fold(values)

        step, count = by_chunk(rows, body)
        zero = jnp.zeros((8, width), F32)
        by_branch, alone = lax.fori_loop(0, count, step, (zero, zero))
        sums[2:3] = jnp.sum(by_branch, 0, keepdims=True)
        sums[3:4] = jnp.sum(alone, 0, keepdims=True) * scale
        ahead.drain_sum()

    return end


def back_mlp(refs, group, base, at, loads, tick, begin):
    rows = refs.grad.shape[0]
    half = rows // 2
    gath, part, hidden, d_hidden = refs.gath_m, refs.part, refs.hidden, refs.d_hidden
    trade = Exchange(group, base, gath, part, refs.got, refs.summed)
    sums = refs.sums.at[2 * at + 1]
    loads[0].wait()
    enter_back(refs.grad, refs.branch_b, refs.layer_scale[at, 1:2], gath, sums)
    trade.start()
    tick()
    trade.spread()
    for load in loads[1:4]:
        load.wait()

    refs.up_total[...] = jnp.zeros_like(refs.up_total)

    def down(slot):
        hidden[...] = dot(gath[slot], refs.w_down[...], 1, 1)

        def body(place, carry):
            span = pl.ds(pl.multiple_of(place * CHUNK, CHUNK), CHUNK)
            low = (hidden[span] * refs.slope[slot, span].astype(F32)).astype(BF16)
            d_hidden[slot, span] = low
            return carry + fold(low.astype(F32))

        zero = jnp.zeros((8, hidden.shape[1]), F32)
        refs.up_total[...] += lax.fori_loop(0, rows // CHUNK, body, zero)

    def back(slot, first, count):
        return dot(d_hidden[slot, pl.ds(first, count)], refs.w_up[...], 1, 1)

    down(0)
    tick()
    refs.own[...] = back(0, 0, rows)
    tick()
    down(1)
    part[1] = back(1, 0, rows).astype(BF16)
    trade.sum_near().start()
    tick()
    trade.pass_on(0)
    for stage in range(2):
        slot = trade.slot(stage)
        trade.arrived(stage)
        down(slot)
        tick()

        def one(place, carry):
            first = pl.multiple_of(place * trade.keep + (1 - place) * trade.give, half)
            part[slot, pl.ds(first, half)] = back(slot, first, half).astype(BF16)

            @pl.when(place == 0)
            def _():
                trade.pair(stage).start()

            return carry

        lax.fori_loop(0, 2, one, 0)
        trade.send_sum(stage)
        if stage == 0:
            trade.pass_on(1)
        tick()
    refs.up_sums[at : at + 1] = jnp.sum(refs.up_total[...], 0, keepdims=True)
    for load in loads[4:]:
        load.wait()
    data, inner = refs.data_m.at[at], refs.w_down.shape[0]
    weight_grad(refs.active, gath, data, 0, inner)
    begin(at, 0, 0)
    tick()
    weight_grad(refs.gath_b, d_hidden, data, inner, refs.w_up.shape[0])
    begin(at, 0, 1)
    tick()
    trade.finish()
    leave_back(
        refs.grad,
        refs.own,
        refs.got,
        refs.normal_b,
        refs.inverse_b,
        refs.ln_gain[at, 1:2],
        sums,
    )
    trade.drain_gather()
    trade.drain_sum()
    tick()


def back_attend(refs, group, base, at, head_count, loads, tick, begin, meanwhile):
    rows = refs.grad.shape[0]
    half = rows // 2
    data = refs.data_t.at[at]
    wide = refs.mixture.shape[2]
    gath, part, d_mixed, d_scores = refs.gath_t, refs.part, refs.d_mixed, refs.d_scores
    qkv = refs.qkv
    trade = Exchange(group, base, gath, part, refs.got, refs.summed)
    sums = refs.sums.at[2 * at]
    loads[0].wait()
    enter_back(refs.grad, refs.branch_a, refs.layer_scale[at, 0:1], gath, sums)
    trade.start()
    tick()
    trade.spread()
    if meanwhile is not None:
        meanwhile()
        tick()
    for load in loads[1:5]:
        load.wait()
    spare = jnp.zeros((rows, wide - head_count * HEAD_DIM), BF16)

    def attend(slot):
        d_mix = dot(gath[slot], refs.w_out[...], 1, 1).astype(BF16)
        pieces = ([], [], [])
        for head in range(head_count):
            lanes = slice(head * HEAD_DIM, (head + 1) * HEAD_DIM)
            queries = qkv[slot, :, 0:wide][:, lanes]
            keys = qkv[slot, :, wide : 2 * wide][:, lanes]
            values = qkv[slot, :, 2 * wide : 3 * wide][:, lanes]
            share = refs.weights[slot, head]
            d_head = d_mix[:, lanes]
            wide_share = share.astype(F32)
            d_share = dot(d_head, values, 1, 1)
            middle = jnp.sum(wide_share * d_share, -1, keepdims=True)
            d_score = (wide_share * (d_share - middle)).astype(BF16)
            d_scores[slot, head] = d_score
            pieces[0].append((dot(d_score, keys) * HEAD_DIM**-0.5).astype(BF16))
            pieces[1].append(dot(d_score, queries, 0, 0).astype(BF16))
            pieces[2].append(dot(share, d_head, 0, 0).astype(BF16))
        for place in range(3):
            d_mixed[slot, :, place * wide : (place + 1) * wide] = jnp.concatenate(
                pieces[place] + [spare], -1
            )

    def back(slot, first, count):
        return dot(d_mixed[slot, pl.ds(first, count)], refs.w_qkv[...], 1, 1)

    attend(0)
    tick()
    refs.own[...] = back(0, 0, rows)
    attend(1)
    tick()
    part[1] = back(1, 0, rows).astype(BF16)
    trade.sum_near().start()
    trade.pass_on(0)
    for stage in range(2):
        slot = trade.slot(stage)
        trade.arrived(stage)
        attend(slot)
        tick()

        def one(place, carry):
            first = pl.multiple_of(place * trade.keep + (1 - place) * trade.give, half)
            part[slot, pl.ds(first, half)] = back(slot, first, half).astype(BF16)

            @pl.when(place == 0)
            def _():
                trade.pair(stage).start()

            return carry

        lax.fori_loop(0, 2, one, 0)
        trade.send_sum(stage)
        if stage == 0:
            trade.pass_on(1)
        tick()
    for load in loads[5:]:
        load.wait()

    def add(slot, total):
        def body(span, carry):
            return carry + fold(d_mixed[slot, span].astype(F32))

        step, count = by_chunk(rows, body)
        return lax.fori_loop(0, count, step, total)

    total = jnp.zeros((8, 3 * wide), F32)
    for slot in range(4):
        total = add(slot, total)
    refs.qkv_sums[at : at + 1] = jnp.sum(total, 0, keepdims=True)
    used = 3 * head_count * HEAD_DIM
    weight_grad(d_mixed, refs.gath_a, data, 0, used)
    tick()
    weight_grad(refs.mixture, gath, data, used, used // 3)
    begin(at, 1, 0)
    tick()
    for head in range(head_count):
        total = None
        for slot in range(4):
            placed = dot(refs.spots[slot], d_scores[slot, head]).astype(BF16)
            term = dot(placed, refs.turned[slot])
            total = term if total is None else total + term
        row = at * head_count + head
        refs.table_sums[row : row + 1] = table_row(total)
    trade.finish()
    leave_back(
        refs.grad,
        refs.own,
        refs.got,
        refs.normal_a,
        refs.inverse_a,
        refs.ln_gain[at, 0:1],
        sums,
    )
    trade.drain_gather()
    trade.drain_sum()
    tick()


class BackInputs(NamedTuple):
    grad_in: object
    middle: object
    branch_a_all: object
    branch_b_all: object
    normal_a_all: object
    normal_b_all: object
    inverse_all: object
    mixture_all: object
    qkv_all: object
    weights_all: object
    gath_a_all: object
    active_all: object
    slope_all: object
    gath_b_all: object
    gath_z: object
    w_qkv_all: object
    w_out_all: object
    w_up_all: object
    w_down_all: object
    spots_all: object
    turned_all: object
    up_bias: object
    ln_gain: object
    layer_scale: object
    row_bias: object


class BackOutputs(NamedTuple):
    grad: object
    stream: object
    d_qkv: object
    d_out: object
    d_up: object
    d_down: object
    small_out: object


class BackScratch(NamedTuple):
    spots: object
    turned: object
    branch_a: object
    branch_b: object
    normal_a: object
    normal_b: object
    own: object
    own_f: object
    inverse_a: object
    inverse_b: object
    mixture: object
    qkv: object
    weights: object
    gath_a: object
    active: object
    slope: object
    gath_b: object
    gath_m: object
    gath_t: object
    w_qkv: object
    w_out: object
    w_up: object
    w_down: object
    d_hidden: object
    hidden: object
    hidden_f: object
    d_mixed: object
    d_scores: object
    part: object
    part_f: object
    got: object
    got_f: object
    summed: object
    summed_f: object
    sums: object
    up_total: object
    up_sums: object
    qkv_sums: object
    table_sums: object
    lines: object
    near_got: object
    pair_sum: object
    far_got: object
    data_m: object
    data_t: object
    got_m: object
    got_t: object
    small: object
    got_small: object
    send_sems: object
    recv_sems: object
    load_sems: object
    ring_send_m: object
    ring_recv_m: object
    ring_send_t: object
    ring_recv_t: object
    ring_send_s: object
    ring_recv_s: object
    out_sems: object


def backward_body(layers, head_count, count, *all_refs):
    refs = Names((*BackInputs._fields, *BackOutputs._fields, *BackScratch._fields), all_refs)
    rows, width = refs.grad.shape
    last = layers - 1
    group = Group(refs.send_sems, refs.recv_sems)
    barrier = pltpu.get_barrier_semaphore()
    greeted = group.greet(barrier)
    ring = Ring(count) if count else None
    if ring:
        for other in ring.sides:
            pl.semaphore_signal(barrier, inc=1, device_id={"dp": other}, device_id_type=MESH)
        greeted += 2
    pl.semaphore_wait(barrier, greeted)
    ticker = Ticker(ring)
    used = refs.d_qkv.shape[1]
    leaves = []

    def leave(at, kind, sub):
        pairs = (
            ((refs.data_m, 0, refs.d_down),),
            ((refs.data_m, refs.d_down.shape[1], refs.d_up),),
            ((refs.data_t, 0, refs.d_qkv), (refs.data_t, used, refs.d_out)),
        )[2 * kind + sub]
        for source, first, target in pairs:
            step = pltpu.make_async_copy(
                source.at[at, pl.ds(first, target.shape[1])],
                target.at[at],
                refs.out_sems.at[len(leaves)],
            )
            step.start()
            leaves.append(step)

    def begin(at, kind, sub):
        if not ring:
            leave(at, kind, sub)
            return
        leaf = (
            (refs.data_m, refs.got_m, refs.ring_send_m, refs.ring_recv_m),
            (refs.data_t, refs.got_t, refs.ring_send_t, refs.ring_recv_t),
        )[kind]
        streams = ring.streams(tuple(ref.at[at] for ref in leaf))
        ticker.add(streams[2 * sub : 2 * sub + 2], lambda: leave(at, kind, sub))

    refs.grad[...] = refs.grad_in[...]
    refs.w_out[refs.w_out_all.shape[1] :] = jnp.zeros_like(refs.w_out[refs.w_out_all.shape[1] :])
    end = front(refs, group, last, ticker.tick, begin)
    loads_m = None
    for at in reversed(range(layers)):
        base = (2 + 2 * at) * Exchange.COPIES
        if at < last:
            back_mlp(refs, group, base, at, loads_m, ticker.tick, begin)
        loads_t = attend_loads(refs, at)
        if at:
            loads_m = mlp_loads(refs, at - 1)
        back_attend(
            refs,
            group,
            base + Exchange.COPIES,
            at,
            head_count,
            loads_t,
            ticker.tick,
            begin,
            end if at == last else None,
        )

    shared = 8 * layers
    lines = refs.lines
    lines[...] = jnp.zeros_like(lines)
    for kind in range(4):
        for at in range(2 * layers):
            row = kind * 2 * layers + at
            lines[row : row + 1] = refs.sums[at, kind : kind + 1]
    base = (2 + 2 * layers) * Exchange.COPIES
    first = group.copy(base, base, lines.at[pl.ds(0, shared)], refs.near_got, group.near)
    first.start()
    ticker.tick()
    first.wait_recv()
    refs.pair_sum[...] = lines[0:shared] + refs.near_got[...]
    second = group.copy(base + 1, base + 1, refs.pair_sum, refs.far_got, group.far)
    second.start()
    ticker.tick()
    second.wait_recv()
    first.wait_send()
    lines[0:shared] = refs.pair_sum[...] + refs.far_got[...]
    row = shared
    for leaf, height in (
        (refs.qkv_sums, layers),
        (refs.up_sums, layers),
        (refs.table_sums, layers * head_count),
    ):
        lines[row : row + height] = leaf[0:height]
        row += height
    cuts = [
        (slice(at * SMALL_ROWS, (at + 1) * SMALL_ROWS), slice(at * 128, (at + 1) * 128))
        for at in range(width // 128)
    ]
    if ring:
        small = refs.small
        small[...] = jnp.zeros_like(small)
        for rows_at, lanes in cuts:
            small[rows_at] = lines[:, lanes]
        ticker.add(
            ring.streams((small, refs.got_small, refs.ring_send_s, refs.ring_recv_s)),
            lambda: None,
        )
        ticker.finish()
    second.wait_send()
    if ring:
        for rows_at, lanes in cuts:
            refs.small_out[:, lanes] = small[rows_at]
    else:
        refs.small_out[...] = lines[...]
    for step in leaves:
        step.wait()


def run_backward(count, inputs, head_count):
    grad, w_out, w_up = inputs[0], inputs[16], inputs[17]
    rows, width = grad.shape
    layers, wide = w_out.shape[0], inputs[15].shape[2] // 3
    inner = w_up.shape[2]
    used = head_count * HEAD_DIM
    ring_count = count or 2
    steps = 2 * (ring_count - 1)
    in_vmem = pl.BlockSpec(memory_space=pltpu.VMEM)
    in_hbm = pl.BlockSpec(memory_space=pl.ANY)
    assert inner == width == 3 * wide == 4 * used and layers == 2

    def wide_rows(*shape):
        return pltpu.VMEM(shape, F32)

    def low(*shape):
        return pltpu.VMEM(shape, BF16)

    def sems(*shape):
        return pltpu.SemaphoreType.DMA(shape)

    def ring_got(total, pieces):
        piece = total // (2 * ring_count * pieces)
        return low(layers, 2, pieces, ring_count - 1, piece, width)

    own = wide_rows(rows, width)
    four = low(4, rows, width)
    square = low(4, head_count, rows, rows)
    lines = wide_rows(8 * layers, width)
    small_rows = -(-SMALL_ROWS * (width // 128) // (16 * ring_count)) * 16 * ring_count
    exchanges = (2 + 2 * layers) * Exchange.COPIES + 2
    scratch = (
        [low(4, SPAN, rows), low(4, rows, SPAN)]
        + [own] * 6
        + [wide_rows(rows, 128)] * 2
        + [low(4, rows, wide), four, square, four, four, four, four, four, four]
        + [low(width, 3 * wide), low(wide, width), low(width, inner), low(inner, width)]
        + [four, own, own, four, square, four, four]
        + [low(3, rows, width)] * 2
        + [low(rows, width)] * 2
        + [wide_rows(2 * layers, 8, width)]
        + [wide_rows(8, width)] * 4
        + [wide_rows(SMALL_ROWS, width), lines, lines, lines]
        + [low(layers, 2 * width, width), low(layers, width, width)]
        + [ring_got(2 * width, PIECES), ring_got(width, 1)]
        + [wide_rows(small_rows, 128)]
        + [wide_rows(2, 1, ring_count - 1, small_rows // (2 * ring_count), 128)]
        + [sems(exchanges)] * 2
        + [sems(1 + 2 * layers, 9)]
        + [sems(layers, 2, PIECES, steps)] * 2
        + [sems(layers, 2, 1, steps)] * 2
        + [sems(2, 1, steps)] * 2
        + [sems(4 * layers)]
    )
    return pl.pallas_call(
        functools.partial(backward_body, layers, head_count, count),
        name="backward",
        out_shape=[
            jax.ShapeDtypeStruct((rows, width), F32),
            jax.ShapeDtypeStruct((rows, width), F32),
            jax.ShapeDtypeStruct((layers, 3 * used, width), BF16),
            jax.ShapeDtypeStruct((layers, used, width), BF16),
            jax.ShapeDtypeStruct((layers, width, inner), BF16),
            jax.ShapeDtypeStruct((layers, inner, width), BF16),
            jax.ShapeDtypeStruct((SMALL_ROWS, width), F32),
        ],
        in_specs=[in_vmem] * 2 + [in_hbm] * 19 + [in_vmem] * 4,
        out_specs=[in_vmem] * 2 + [in_hbm] * 4 + [in_vmem],
        scratch_shapes=scratch,
        compiler_params=pltpu.CompilerParams(
            collective_id=1, has_side_effects=True, vmem_limit_bytes=65400 * 1024
        ),
    )(*inputs)


SMALL_ROWS = 32


class Ring:
    def __init__(self, count):
        self.count = count
        self.steps = 2 * (count - 1)
        self.place = self.place_of(lax.axis_index("dp"))
        self.sides = (
            self.number_of((self.place + 1) % count),
            self.number_of((self.place + count - 1) % count),
        )

    def place_of(self, number):
        row, side = number // 2, number % 2
        return row + side * (self.count - 1 - 2 * row)

    def number_of(self, place):
        side = place // (self.count // 2)
        return 2 * (place + side * (self.count - 1 - 2 * place)) + side

    def streams(self, *sets):
        return [
            (leaf, way, sub)
            for leaf in sets
            for sub in range(leaf[1].shape[1])
            for way in range(2)
        ]

    def rows(self, stream, step):
        (data, got, _, _), way, sub = stream
        piece = got.shape[3]
        if way == 0:
            chunk = (self.place + 3 * self.count - step) % self.count
        else:
            chunk = (self.place + step) % self.count
        first = ((sub * 2 + way) * self.count + chunk) * piece
        return pl.ds(pl.multiple_of(first, piece), piece)

    def copy(self, stream, step, gather):
        (data, got, send_sems, recv_sems), way, sub = stream
        rows = self.rows(stream, step)
        return pltpu.make_async_remote_copy(
            src_ref=data.at[rows],
            dst_ref=data.at[rows] if gather else got.at[way, sub, step],
            send_sem=send_sems.at[way, sub, step],
            recv_sem=recv_sems.at[way, sub, step],
            device_id={"dp": self.sides[way]},
            device_id_type=MESH,
        )

    def start(self, streams):
        for stream in streams:
            self.copy(stream, 0, False).start()

    def add(self, stream, step):
        (data, got, _, _), way, sub = stream
        self.copy(stream, step, False).wait_recv()
        rows = self.rows(stream, step + 1)
        data[rows] = data[rows] + got[way, sub, step]

    def drain(self, streams):
        for step in range(self.count - 1, self.steps):
            for stream in streams:
                self.copy(stream, step, True).wait_send()


def ring_fits(count, rows):
    return count == 8 and rows % (2 * count * 16) == 0


def widen_body(
    wide,
    lengths,
    stream,
    gradient,
    out_in,
    up_in,
    down_in,
    small,
    result,
    d_tokens,
    d_out,
    d_up,
    d_down,
    d_bias,
    d_up_bias,
    *kinds,
):
    number = pl.program_id(0)
    rows, width = stream.shape
    layers, _, used = d_bias.shape
    place = lax.axis_index("tensor")
    length = lengths[place, 0] + lengths[place, 1]
    row = number * rows + lax.broadcasted_iota(jnp.int32, (rows, width), 0)
    result[...] = jnp.where(row < length, stream[...], 0.0).astype(BF16)
    d_tokens[...] = gradient[...]
    d_out[...] = out_in[...].astype(F32)
    d_up[...] = up_in[...].astype(F32)
    d_down[...] = down_in[...].astype(F32)

    @pl.when(number == 0)
    def _():
        for kind, leaf in enumerate(kinds):
            for at in range(layers):
                first = 2 * (kind * layers + at)
                leaf[at] = small[first : first + 2]
        first = 8 * layers
        for at in range(layers):
            for half in range(2):
                start = 2 * half * wide
                d_bias[at, half : half + 1] = small[
                    first + at : first + at + 1, start : start + used
                ]
        first += layers
        d_up_bias[...] = small[first : first + layers]


def run_widen(lengths, stream, gradient, d_out, d_up, d_down, small, wide, used):
    rows, width = stream.shape
    layers = d_out.shape[0]
    parts = 4
    steps = layers * parts

    def rows_of(total):
        return pl.BlockSpec((total // steps, width), lambda at: (at, 0))

    def block(leaf):
        return pl.BlockSpec(
            (1, leaf.shape[1] // parts, width), lambda at: (at // parts, at % parts, 0)
        )

    def whole(*shape):
        return pl.BlockSpec(shape, lambda at: (0,) * len(shape))

    def full(*shape):
        return jax.ShapeDtypeStruct(shape, F32)

    return pl.pallas_call(
        functools.partial(widen_body, wide),
        name="widen",
        grid=(steps,),
        out_shape=[
            jax.ShapeDtypeStruct((rows, width), BF16),
            full(rows, width),
            full(*d_out.shape),
            full(*d_up.shape),
            full(*d_down.shape),
            full(layers, 2, used),
            full(layers, width),
            *[full(layers, 2, width)] * 4,
        ],
        in_specs=[
            pl.BlockSpec(memory_space=pltpu.SMEM),
            rows_of(rows),
            rows_of(rows),
            block(d_out),
            block(d_up),
            block(d_down),
            whole(*small.shape),
        ],
        out_specs=[
            rows_of(rows),
            rows_of(rows),
            block(d_out),
            block(d_up),
            block(d_down),
            whole(layers, 2, used),
            whole(layers, width),
            *[whole(layers, 2, width)] * 4,
        ],
    )(lengths, stream, gradient, d_out, d_up, d_down, small)


def per_device(
    tokens,
    cotangent,
    segments,
    lengths,
    rel_index,
    w_qkv,
    qv_bias,
    w_out,
    w_fc1,
    fc1_bias,
    w_fc2,
    rel_table,
    ln_gain,
    ln_bias,
    layer_scale,
    row_bias,
):
    own_rows, width = tokens.shape
    group_rows, bin_rows = rel_index.shape
    layer_count = w_qkv.shape[0]
    head_count = rel_table.shape[2]
    local_width = w_qkv.shape[3]
    wide = -(-local_width // 256) * 256
    bin_total = group_rows // bin_rows
    place = lax.axis_index("tensor")
    assert own_rows == bin_rows and bin_total == 4

    extra = wide - local_width
    qkv_used = jnp.pad(w_qkv, ((0, 0), (0, 0), (0, 0), (0, extra))).reshape(
        layer_count, width, 3 * wide
    )
    norms = (ln_gain, ln_bias, layer_scale, row_bias)

    (
        gath_a,
        qkv,
        shares,
        mixture,
        gath_b,
        slope,
        active,
        normal_a,
        branch_a,
        normal_b,
        branch_b,
        inverse,
        spots,
        turned,
        gath_z,
        gradient,
        middle,
    ) = run_forward(
        lengths,
        rel_index,
        rel_table,
        (tokens, cotangent),
        (qkv_used, qv_bias, w_out, w_fc1, fc1_bias, w_fc2),
        norms,
    )
    dp_count = lax.axis_size("dp")
    with_ring = ring_fits(dp_count, width)
    gradient, stream, *sums = run_backward(
        dp_count if with_ring else None,
        (
            gradient,
            middle,
            branch_a,
            branch_b,
            normal_a,
            normal_b,
            inverse,
            mixture,
            qkv,
            shares,
            gath_a,
            active,
            slope,
            gath_b,
            gath_z,
            qkv_used,
            w_out,
            w_fc1,
            w_fc2,
            spots,
            turned,
            fc1_bias,
            ln_gain,
            layer_scale,
            row_bias,
        ),
        head_count,
    )
    if not with_ring:
        sums = lax.psum(sums, "dp")
    *weight_sums, small = sums
    d_qkv, d_out, d_up, d_down = weight_sums
    result, d_tokens, d_out, d_up, d_down, d_bias, d_up_bias, *kinds = run_widen(
        lengths, stream, gradient, d_out, d_up, d_down, small, wide, local_width
    )
    d_qkv = jnp.transpose(
        d_qkv.astype(F32).reshape(layer_count, 3, local_width, width), (0, 3, 1, 2)
    )
    first = 8 * layer_count + 2 * layer_count
    d_table = small[first : first + layer_count * head_count, : rel_table.shape[1]]
    d_table = jnp.transpose(d_table.reshape(layer_count, head_count, -1), (0, 2, 1))
    return (
        result,
        d_tokens,
        d_qkv,
        d_bias,
        d_out,
        d_up,
        d_up_bias,
        d_down,
        d_table,
        *kinds,
    )


def solution(mesh):
    in_specs = (
        P(("dp", "tensor"), None),
        P(("dp", "tensor"), None),
        P("dp"),
        P("dp", None),
        P("dp", None),
        P(None, None, None, "tensor"),
        P(None, None, "tensor"),
        P(None, "tensor", None),
        P(None, None, "tensor"),
        P(None, "tensor"),
        P(None, "tensor", None),
        P(None, None, "tensor"),
        P(),
        P(),
        P(),
        P(),
    )
    out_specs = (
        P(("dp", "tensor"), None),
        P(("dp", "tensor"), None),
        P(None, None, None, "tensor"),
        P(None, None, "tensor"),
        P(None, "tensor", None),
        P(None, None, "tensor"),
        P(None, "tensor"),
        P(None, "tensor", None),
        P(None, None, "tensor"),
        P(),
        P(),
        P(),
        P(),
    )
    return jax.shard_map(
        per_device, mesh=mesh, in_specs=in_specs, out_specs=out_specs, check_vma=False
    )
```

```python
import functools
from typing import NamedTuple

import jax
import jax.numpy as jnp
from jax import lax
from jax.experimental import pallas as pl
from jax.experimental.pallas import tpu as pltpu
from jax.sharding import PartitionSpec as P

HEAD_DIM = 64
SIDE = 14
STRIDE = 2 * SIDE - 1
CELLS = SIDE * SIDE
CHUNK = 32
MESH = pl.DeviceIdType.MESH
BF16 = jnp.bfloat16
F32 = jnp.float32


def dot(left_side, right_side, left_axis=1, right_axis=0):
    return lax.dot_general(
        left_side,
        right_side,
        (((left_axis,), (right_axis,)), ((), ())),
        preferred_element_type=F32,
    )


class Group:
    def __init__(self, send_sems, recv_sems):
        own = lax.axis_index("tensor")
        self.core = own % 2
        self.near = own + 1 - 2 * self.core
        self.far = (own + 2) % 4
        self.far_chip = 1 - own // 2
        self.sems = (send_sems, recv_sems)

    def greet(self, barrier):
        for other in (self.near, self.far, self.far + 1 - 2 * self.core):
            pl.semaphore_signal(
                barrier, inc=1, device_id={"tensor": other}, device_id_type=MESH
            )
        return 3

    def copy(self, sent, arrived, source, target, other):
        return pltpu.make_async_remote_copy(
            src_ref=source,
            dst_ref=target,
            send_sem=self.sems[0].at[sent],
            recv_sem=self.sems[1].at[arrived],
            device_id={"tensor": other},
            device_id_type=MESH,
        )


class Exchange:
    COPIES = 10

    def __init__(self, group, base, gath, part, got, summed):
        self.group, self.base = group, base
        self.gath, self.part, self.got, self.summed = gath, part, got, summed
        self.rows = (part if gath is None else gath).shape[1] // 2
        self.keep = group.core * self.rows
        self.give = (1 - group.core) * self.rows

    def slot(self, stage):
        core = self.group.core
        return 2 + core + stage * (1 - 2 * core)

    def span(self, first):
        return pl.ds(pl.multiple_of(first, self.rows), self.rows)

    def symmetric(self, number, source, target, other):
        at = self.base + number
        return self.group.copy(at, at, source, target, other)

    def to_near(self):
        return self.symmetric(0, self.gath.at[0], self.gath.at[1], self.group.near)

    def across(self, stage):
        core, rows = self.group.core, self.span(self.keep)
        source = core + stage * (1 - 2 * core)
        return self.symmetric(
            2 + stage,
            self.gath.at[source, rows],
            self.gath.at[self.slot(stage), rows],
            self.group.far,
        )

    def relay(self, stage):
        rows = self.span(self.keep)
        return self.symmetric(
            4 + stage,
            self.gath.at[self.slot(stage), rows],
            self.gath.at[self.slot(1 - stage), rows],
            self.group.near,
        )

    def sum_near(self):
        return self.symmetric(1, self.part.at[1], self.got.at[0], self.group.near)

    def pair(self, stage):
        return self.symmetric(
            6 + stage,
            self.part.at[self.slot(stage), self.span(self.give)],
            self.got.at[1, self.span(stage * self.rows)],
            self.group.near,
        )

    def home(self, stage, sender):
        return self.group.copy(
            self.base + 8 + stage,
            self.base + 8 + sender,
            self.summed.at[self.span(stage * self.rows)],
            self.got.at[2, self.span(sender * self.rows)],
            self.group.far_chip * 2 + stage,
        )

    def start(self):
        self.to_near().start()

        @pl.when(self.group.core == 0)
        def _():
            self.across(0).start()

    def spread(self):
        self.to_near().wait_recv()

        @pl.when(self.group.core == 1)
        def _():
            self.across(0).start()

        self.across(1).start()

    def pass_on(self, stage):
        self.across(stage).wait_recv()
        self.relay(stage).start()

    def arrived(self, stage):
        self.relay(stage).wait_recv()

    def send_sum(self, stage):
        self.pair(stage).wait_recv()
        rows = self.span(stage * self.rows)
        self.summed[rows] = self.part[self.slot(stage), self.span(self.keep)] + self.got[1, rows]
        self.home(stage, self.group.core).start()

    def finish(self):
        self.sum_near().wait_recv()
        for sender in range(2):
            self.home(0, sender).wait_recv()

    def drain_gather(self):
        self.to_near().wait_send()
        for stage in range(2):
            self.across(stage).wait_send()
            self.relay(stage).wait_send()

    def drain_sum(self):
        self.sum_near().wait_send()
        for stage in range(2):
            self.pair(stage).wait_send()
            self.home(stage, self.group.core).wait_send()


def by_chunk(total_rows, body, size=CHUNK):
    def step(at, carry):
        return body(pl.ds(pl.multiple_of(at * size, size), size), carry)

    return step, total_rows // size


def norm_chunk(values, gain, shift):
    center = values - jnp.mean(values, -1, keepdims=True)
    inverse = lax.rsqrt(jnp.mean(center * center, -1, keepdims=True) + 1e-06)
    normal = center * inverse
    return (normal * gain + shift).astype(BF16), normal, inverse


def gelu_parts(values):
    share = 0.5 * (1.0 + lax.erf(values * 0.7071067811865476))
    slope = share + values * (jnp.exp(-0.5 * values * values) * 0.3989422804014327)
    return values * share, slope


SPAN = 384
LAST = (SIDE - 1) * (STRIDE + 1)
CLASS = LAST + 1
TABLE_WIDTH = 2 * SPAN


def prepare(head_count, lengths, index_rows, table, bias, spots, turned, same):
    rows = bias.shape[3]
    own = lax.axis_index("tensor")
    order = (own, own + 1 - 2 * (own % 2), (own + 2) % 4, 3 - own)

    ones = []
    for slot in range(4):
        first = lengths[order[slot], 0]
        both = first + lengths[order[slot], 1]

        def pick(row):
            return index_rows[pl.ds(order[slot] * rows + row, 1), :]

        at = lax.broadcasted_iota(jnp.int32, (1, rows), 1)
        code = LAST - jnp.where(at < first, pick(1), pick(first + 1))
        code = jnp.where((at == 0) | (at == first), CLASS, code)
        code = jnp.where(at < both, code, -1)
        upright = lax.broadcasted_iota(jnp.int32, (SPAN, rows), 0)
        spots[slot] = (upright == code).astype(F32).astype(BF16)
        column = jnp.transpose(jnp.broadcast_to(code.astype(F32), (128, rows)))
        column = jnp.concatenate([column] * (SPAN // 128), -1)
        flat = lax.broadcasted_iota(jnp.int32, (rows, SPAN), 1).astype(F32)
        ones.append((flat == column).astype(F32).astype(BF16))
        mirrored = jnp.where(column < CLASS, LAST - column, column)
        mirrored = jnp.where(column < 0, -1.0, mirrored)
        turned[slot] = (flat == mirrored).astype(F32).astype(BF16)

        def image_of(values):
            return (values >= first).astype(jnp.int32) + (values >= both).astype(jnp.int32)

        by_row = image_of(lax.broadcasted_iota(jnp.int32, (rows, rows), 0))
        by_col = image_of(lax.broadcasted_iota(jnp.int32, (rows, rows), 1))
        same[slot] = (by_row == by_col).astype(F32)

    key_at = lax.broadcasted_iota(jnp.int32, (SPAN, SPAN), 0)
    query_at = lax.broadcasted_iota(jnp.int32, (SPAN, SPAN), 1)
    shift = SPAN - LAST

    def each(at, carry):
        row = table[pl.ds(at, 1), :]
        rolled = pltpu.roll(
            jnp.broadcast_to(row, (SPAN, TABLE_WIDTH)), 0, 1, stride=1, stride_axis=0
        )
        pairs = rolled[:, SPAN:]
        tail = shift + STRIDE * STRIDE
        pairs = jnp.where(query_at == CLASS, row[:, tail : tail + 1], pairs)
        pairs = jnp.where(key_at == CLASS, row[:, tail + 1 : tail + 2], pairs)
        pairs = jnp.where(
            (query_at == CLASS) & (key_at == CLASS), row[:, tail + 2 : tail + 3], pairs
        ).astype(BF16)
        for slot in range(4):
            half = dot(ones[slot], pairs, 1, 1).astype(BF16)
            looked = dot(half, spots[slot])
            bias[at // head_count, slot, at % head_count] = jnp.where(
                same[slot] > 0.5, looked, -1000000000.0
            ).astype(BF16)
        return carry

    lax.fori_loop(0, table.shape[0], each, 0)


def shifted_table(rel_table):
    layers, entries, head_count = rel_table.shape
    shift = SPAN - LAST
    table = jnp.transpose(rel_table, (0, 2, 1)).reshape(layers * head_count, entries).astype(F32)
    return jnp.pad(table, ((0, 0), (shift, TABLE_WIDTH - shift - entries)))


def table_row(pairs):
    query_at = lax.broadcasted_iota(jnp.int32, (SPAN, SPAN), 0)
    key_at = lax.broadcasted_iota(jnp.int32, (SPAN, SPAN), 1)
    zero = jnp.zeros((SPAN, SPAN), F32)
    patches = jnp.where((query_at <= LAST) & (key_at <= LAST), pairs, zero)
    rolled = pltpu.roll(
        jnp.concatenate([patches, zero], -1), 0, 1, stride=1, stride_axis=0
    )
    row = jnp.sum(rolled, 0, keepdims=True)
    at = lax.broadcasted_iota(jnp.int32, (1, TABLE_WIDTH), 1)
    tails = (
        (query_at == CLASS) & (key_at <= LAST),
        (query_at <= LAST) & (key_at == CLASS),
        (query_at == CLASS) & (key_at == CLASS),
    )
    for number, mask in enumerate(tails):
        row = jnp.where(at == STRIDE * STRIDE + number, jnp.sum(jnp.where(mask, pairs, zero)), row)
    return row


class Names:
    def __init__(self, names, refs):
        for name, ref in zip(names, refs, strict=True):
            setattr(self, name, ref)


def load_all(pairs, sems):
    steps = []
    for place, (source, target) in enumerate(pairs):
        step = pltpu.make_async_copy(source, target, sems.at[place])
        step.start()
        steps.append(step)
    return steps


def each_chunk(rows, body):
    def step(at, carry):
        body(pl.ds(pl.multiple_of(at * CHUNK, CHUNK), CHUNK))
        return carry

    lax.fori_loop(0, rows // CHUNK, step, 0)


def attend_rows(refs, at, slot, first, head_count):
    qkv = refs.qkv
    rows = qkv.shape[2] // 2
    wide = qkv.shape[3] // 3
    span = pl.ds(first, rows)
    heads = []
    for head in range(head_count):
        lanes = slice(head * HEAD_DIM, (head + 1) * HEAD_DIM)
        queries = qkv[at, slot, span, 0:wide][:, lanes]
        keys = qkv[at, slot, :, wide : 2 * wide][:, lanes]
        values = qkv[at, slot, :, 2 * wide : 3 * wide][:, lanes]
        scores = dot(queries, keys, 1, 1) + refs.bias[at, slot, head, span].astype(F32)
        powers = jnp.exp(scores - jnp.max(scores, -1, keepdims=True))
        weights = (powers / jnp.sum(powers, -1, keepdims=True)).astype(BF16)
        refs.weights[at, slot, head, span] = weights
        heads.append(dot(weights, values).astype(BF16))
    heads.append(jnp.zeros((rows, wide - head_count * HEAD_DIM), BF16))
    refs.mixture[at, slot, span] = jnp.concatenate(heads, -1)


class ForwardInputs(NamedTuple):
    lengths: object
    tokens: object
    cotangent: object
    qv_bias: object
    fc1_bias: object
    table: object
    ln_gain: object
    ln_bias: object
    layer_scale: object
    row_bias: object
    index_in: object
    w_qkv_in: object
    w_out_in: object
    w_up_in: object
    w_down_in: object


class ForwardKept(NamedTuple):
    gath_a: object
    qkv: object
    weights: object
    mixture: object
    gath_b: object
    slope: object
    active: object
    normal_a: object
    branch_a: object
    normal_b: object
    branch_b: object
    inverse: object
    spots: object
    turned: object


class ForwardOutputs(NamedTuple):
    gath_z_out: object
    grad: object
    stream: object


class ForwardScratch(NamedTuple):
    gath_z: object
    bias: object
    same: object
    index_rows: object
    w_qkv: object
    w_out: object
    w_up: object
    w_down: object
    qkv_bias: object
    up_bias: object
    hidden: object
    part: object
    got: object
    summed: object
    own: object
    send_sems: object
    recv_sems: object
    load_sems: object
    out_sems: object


def forward_body(layers, head_count, *all_refs):
    kept_outs = tuple(name + "_kept" for name in ForwardKept._fields)
    refs = Names(
        (*ForwardInputs._fields, *kept_outs, *ForwardOutputs._fields, *ForwardKept._fields, *ForwardScratch._fields), all_refs
    )
    stream, own, got, part = refs.stream, refs.own, refs.got, refs.part
    rows, width = stream.shape
    half = rows // 2
    last = layers - 1
    used = refs.w_out_in.shape[1]
    wide = refs.w_out.shape[1]
    loads = load_all(
        (
            (refs.index_in, refs.index_rows),
            (refs.w_qkv_in, refs.w_qkv),
            *(
                (refs.w_out_in.at[at], refs.w_out.at[at, pl.ds(0, used)])
                for at in range(layers)
            ),
            (refs.w_up_in, refs.w_up),
            (refs.w_down_in, refs.w_down),
        ),
        refs.load_sems,
    )
    group = Group(refs.send_sems, refs.recv_sems)
    barrier = pltpu.get_barrier_semaphore()
    greeted = group.greet(barrier)
    pl.semaphore_wait(barrier, greeted)
    early = Exchange(group, 2 * Exchange.COPIES, refs.gath_z, None, None, None)

    def load(span):
        stream[span] = refs.tokens[span].astype(F32)

    each_chunk(rows, load)
    refs.qkv_bias[...] = jnp.zeros_like(refs.qkv_bias)
    for at in range(layers):
        refs.w_out[at, used:] = jnp.zeros_like(refs.w_out[at, used:])
        refs.up_bias[at] = refs.fc1_bias[at : at + 1].astype(F32)
        for half_at in range(2):
            first = 2 * half_at * wide
            refs.qkv_bias[at, :, first : first + used] = refs.qv_bias[
                at, half_at : half_at + 1
            ].astype(F32)

    def keep(number, at):
        source = getattr(refs, ForwardKept._fields[number])
        target = getattr(refs, kept_outs[number])
        if number < 12:
            source, target = source.at[at], target.at[at]
        return pltpu.make_async_copy(source, target, refs.out_sems.at[number, at])

    def layer(at, carry):
        trade = Exchange(group, 0, refs.gath_a.at[at], part, got, refs.summed)

        def enter(span):
            low, normal, inv = norm_chunk(
                stream[span], refs.ln_gain[at, 0:1], refs.ln_bias[at, 0:1]
            )
            refs.gath_a[at, 0, span] = low
            refs.normal_a[at, span] = normal
            refs.inverse[at, 0, span] = jnp.broadcast_to(inv, (CHUNK, 128))

        each_chunk(rows, enter)
        trade.start()

        @pl.when(at == 0)
        def _():
            place = lax.axis_index("tensor")
            length = refs.lengths[place, 0] + refs.lengths[place, 1]

            def mask(number, carry):
                span = pl.ds(pl.multiple_of(number * CHUNK, CHUNK), CHUNK)
                row = number * CHUNK + lax.broadcasted_iota(jnp.int32, (CHUNK, width), 0)
                values = jnp.where(row < length, refs.cotangent[span].astype(F32), 0.0)
                refs.grad[span] = values
                refs.gath_z[0, span] = (values * refs.layer_scale[last, 1:2]).astype(BF16)
                return carry

            lax.fori_loop(0, rows // CHUNK, mask, 0)

        trade.spread()

        @pl.when(at == 0)
        def _():
            early.start()
            early.spread()
            loads[0].wait()
            prepare(
                head_count,
                refs.lengths,
                refs.index_rows,
                refs.table,
                refs.bias,
                refs.spots,
                refs.turned,
                refs.same,
            )
            keep(12, 0).start()
            keep(13, 0).start()
            for step in loads[1:]:
                step.wait()

        scale = jnp.concatenate(
            [
                jnp.full((1, refs.qkv.shape[3] // 3), HEAD_DIM**-0.5, F32),
                jnp.full((1, 2 * refs.qkv.shape[3] // 3), 1.0, F32),
            ],
            -1,
        )

        def project(slot):
            mixed = dot(refs.gath_a[at, slot], refs.w_qkv[at])
            mixed = (mixed + refs.qkv_bias[at]).astype(BF16).astype(F32) * scale
            refs.qkv[at, slot] = mixed.astype(BF16)

        def attend(slot, first):
            attend_rows(refs, at, slot, first, head_count)
            return dot(refs.mixture[at, slot, pl.ds(first, half)], refs.w_out[at])

        turn = 2 * (at == 0).astype(jnp.int32)

        @pl.when(at == 0)
        def _():
            trade.pass_on(0)
            trade.pass_on(1)

        def one_slot(number, carry):
            role = (number + turn) % 4
            stage = role % 2
            away = role >= 2
            slot = jnp.where(away, trade.slot(stage), role)

            @pl.when(away)
            def _():
                trade.arrived(stage)

            project(slot)

            def one(place, carry):
                first = pl.multiple_of(
                    place * trade.keep + (1 - place) * trade.give, half
                )
                result = attend(slot, first)

                @pl.when(role == 0)
                def _():
                    own[pl.ds(first, half)] = result

                @pl.when(role > 0)
                def _():
                    part[slot, pl.ds(first, half)] = result.astype(BF16)

                @pl.when(away & (place == 0))
                def _():
                    trade.pair(stage).start()

                return carry

            lax.fori_loop(0, 2, one, 0)

            @pl.when(away)
            def _():
                trade.send_sum(stage)

            @pl.when(role == 1)
            def _():
                trade.sum_near().start()

            @pl.when((at > 0) & (role == 1))
            def _():
                trade.pass_on(0)

            @pl.when((at > 0) & (role == 2))
            def _():
                trade.pass_on(1)

            return carry

        lax.fori_loop(0, 4, one_slot, 0)
        for number in range(4):
            keep(number, at).start()

        @pl.when(at == 0)
        def _():
            for stage in range(2):
                early.pass_on(stage)

        trade.finish()

        def between(span):
            total = own[span] + got[0, span].astype(F32) + got[2, span].astype(F32)
            branch = total + refs.row_bias[at, 0:1]
            refs.branch_a[at, span] = branch
            middle = stream[span] + refs.layer_scale[at, 0:1] * branch
            stream[span] = middle
            low, normal, inv = norm_chunk(middle, refs.ln_gain[at, 1:2], refs.ln_bias[at, 1:2])
            refs.gath_b[at, 0, span] = low
            refs.normal_b[at, span] = normal
            refs.inverse[at, 1, span] = jnp.broadcast_to(inv, (CHUNK, 128))

        each_chunk(rows, between)
        for number in (7, 8, 9, 11):
            keep(number, at).start()

        @pl.when(at < last)
        def _():
            trade_b = Exchange(
                group, Exchange.COPIES, refs.gath_b.at[at], part, got, refs.summed
            )
            trade_b.start()
            trade.drain_gather()
            trade.drain_sum()
            trade_b.spread()

            def raise_rows(slot):
                refs.hidden[...] = dot(refs.gath_b[at, slot], refs.w_up[at]) + refs.up_bias[at]

                def act(place, carry):
                    span = pl.ds(pl.multiple_of(place * 16, 16), 16)
                    high, incline = gelu_parts(refs.hidden[span])
                    refs.active[at, slot, span] = high.astype(BF16)
                    refs.slope[at, slot, span] = incline.astype(BF16)
                    return carry

                lax.fori_loop(0, rows // 16, act, 0)

            def lower(slot, first, count):
                return dot(refs.active[at, slot, pl.ds(first, count)], refs.w_down[at])

            def one_slot(role, carry):
                stage = role % 2
                away = role >= 2
                slot = jnp.where(away, trade_b.slot(stage), role)

                @pl.when(away)
                def _():
                    trade_b.arrived(stage)

                raise_rows(slot)

                def one(place, carry):
                    first = pl.multiple_of(
                        place * trade_b.keep + (1 - place) * trade_b.give, half
                    )
                    result = lower(slot, first, half)

                    @pl.when(role == 0)
                    def _():
                        own[pl.ds(first, half)] = result

                    @pl.when(role > 0)
                    def _():
                        part[slot, pl.ds(first, half)] = result.astype(BF16)

                    @pl.when(away & (place == 0))
                    def _():
                        trade_b.pair(stage).start()

                    return carry

                lax.fori_loop(0, 2, one, 0)

                @pl.when(away)
                def _():
                    trade_b.send_sum(stage)

                @pl.when(role == 1)
                def _():
                    trade_b.sum_near().start()
                    trade_b.pass_on(0)

                @pl.when(role == 2)
                def _():
                    trade_b.pass_on(1)

                return carry

            lax.fori_loop(0, 4, one_slot, 0)
            for number in (4, 5, 6):
                keep(number, at).start()
            trade_b.finish()

            def after(span):
                total = own[span] + got[0, span].astype(F32) + got[2, span].astype(F32)
                branch = total + refs.row_bias[at, 1:2]
                refs.branch_b[at, span] = branch
                stream[span] = stream[span] + refs.layer_scale[at, 1:2] * branch

            each_chunk(rows, after)
            keep(10, at).start()
            trade_b.drain_gather()
            trade_b.drain_sum()

        @pl.when(at == last)
        def _():
            pltpu.make_async_copy(
                refs.gath_b.at[at, 0], refs.gath_b_kept.at[at, 0], refs.out_sems.at[4, at]
            ).start()
            trade.drain_gather()
            trade.drain_sum()

        return carry

    lax.fori_loop(0, layers, layer, 0)
    for stage in range(2):
        early.arrived(stage)
    early.drain_gather()
    leave = pltpu.make_async_copy(refs.gath_z, refs.gath_z_out, refs.load_sems.at[0])
    leave.start()
    pltpu.make_async_copy(
        refs.gath_b.at[last, 0], refs.gath_b_kept.at[last, 0], refs.out_sems.at[4, last]
    ).wait()
    for at in range(layers):
        for number in range(12):
            if at < last or number not in (4, 5, 6, 10):
                keep(number, at).wait()
    keep(12, 0).wait()
    keep(13, 0).wait()
    leave.wait()


def run_forward(lengths, index_rows, rel_table, rows_in, weights, norms):
    tokens, cotangent = rows_in
    rows, width = tokens.shape
    w_qkv, qv_bias, w_out, w_up, fc1_bias, w_down = weights
    layers, _, head_count = rel_table.shape
    wide = w_qkv.shape[2] // 3
    inner = w_up.shape[2]
    in_vmem = pl.BlockSpec(memory_space=pltpu.VMEM)
    in_hbm = pl.BlockSpec(memory_space=pl.ANY)

    def low(*shape):
        return jax.ShapeDtypeStruct(shape, BF16)

    def full(*shape):
        return jax.ShapeDtypeStruct(shape, F32)

    kept = [
        low(layers, 4, *tail)
        for tail in (
            (rows, width),
            (rows, 3 * wide),
            (head_count, rows, rows),
            (rows, wide),
            (rows, width),
            (rows, inner),
            (rows, inner),
        )
    ]
    own = full(rows, width)
    kept += [full(layers, rows, width)] * 4 + [full(layers, 2, rows, 128)]
    kept += [low(4, SPAN, rows), low(4, rows, SPAN)]
    near = [own, own]
    scratch = [
        *kept,
        low(4, rows, width),
        low(layers, 4, head_count, rows, rows),
        full(4, rows, rows),
        jax.ShapeDtypeStruct(index_rows.shape, index_rows.dtype),
        low(*w_qkv.shape),
        low(layers, wide, width),
        low(*w_up.shape),
        low(*w_down.shape),
        full(layers, 1, 3 * wide),
        full(layers, 1, inner),
        full(rows, inner),
        low(4, rows, width),
        low(3, rows, width),
        low(rows, width),
        own,
    ]
    copies = 3 * Exchange.COPIES
    return pl.pallas_call(
        functools.partial(forward_body, layers, head_count),
        name="forward",
        out_shape=[*kept, low(4, rows, width), *near],
        in_specs=[pl.BlockSpec(memory_space=pltpu.SMEM)] + [in_vmem] * 9 + [in_hbm] * 5,
        out_specs=[in_hbm] * (len(kept) + 1) + [in_vmem] * len(near),
        scratch_shapes=[
            *[pltpu.VMEM(leaf.shape, leaf.dtype) for leaf in scratch],
            pltpu.SemaphoreType.DMA((copies,)),
            pltpu.SemaphoreType.DMA((copies,)),
            pltpu.SemaphoreType.DMA((4 + layers,)),
            pltpu.SemaphoreType.DMA((len(kept), layers)),
        ],
        compiler_params=pltpu.CompilerParams(
            collective_id=0, has_side_effects=True, vmem_limit_bytes=65400 * 1024
        ),
    )(
        lengths,
        tokens,
        cotangent,
        qv_bias,
        fc1_bias,
        shifted_table(rel_table),
        *norms,
        index_rows,
        w_qkv,
        w_out,
        w_up,
        w_down,
    )


def fold(values):
    return jnp.sum(values.reshape(-1, 8, values.shape[-1]), 0)


def enter_back(grad, branch, scale, gath, sums):
    rows, width = grad.shape

    def body(span, carry):
        values = grad[span]
        gath[0, span] = (values * scale).astype(BF16)
        return carry[0] + fold(values * branch[span]), carry[1] + fold(values)

    step, count = by_chunk(rows, body)
    zero = jnp.zeros((8, width), F32)
    by_branch, alone = lax.fori_loop(0, count, step, (zero, zero))
    sums[2:3] = jnp.sum(by_branch, 0, keepdims=True)
    sums[3:4] = jnp.sum(alone, 0, keepdims=True) * scale


def leave_back(grad, own, got, normal, inverse, gain, sums):
    rows, width = grad.shape

    def body(span, carry):
        total = own[span] + got[0, span].astype(F32) + got[2, span].astype(F32)
        unit = normal[span]
        scaled = total * gain
        centered = (
            scaled
            - jnp.mean(scaled, -1, keepdims=True)
            - unit * jnp.mean(scaled * unit, -1, keepdims=True)
        )
        grad[span] = grad[span] + inverse[span, 0:1] * centered
        return carry[0] + fold(total * unit), carry[1] + fold(total)

    step, count = by_chunk(rows, body)
    zero = jnp.zeros((8, width), F32)
    by_unit, alone = lax.fori_loop(0, count, step, (zero, zero))
    sums[0:1] = jnp.sum(by_unit, 0, keepdims=True)
    sums[1:2] = jnp.sum(alone, 0, keepdims=True)


def weight_grad(left, right, out, start, count, tick=None):
    block = 256
    used = count * block // left.shape[2]

    def step(place, carry):
        span = pl.ds(pl.multiple_of(place * block, block), block)
        total = None
        for slot in range(4):
            term = dot(left[slot, :, span], right[slot], 0, 0)
            total = term if total is None else total + term
        there = pl.ds(pl.multiple_of(start + place * used, 16), used)
        out[there] = total[:used].astype(out.dtype)
        return carry

    if tick is None:
        lax.fori_loop(0, left.shape[2] // block, step, 0)
    else:
        for place in range(left.shape[2] // block):
            step(place, 0)
            tick()


PIECES = 2


class Ticker:
    def __init__(self, ring):
        self.ring = ring
        self.under_way = []

    def add(self, streams, done):
        self.ring.start(streams)
        self.under_way.append([streams, 0, done])

    def tick(self):
        if self.under_way:
            self.one()

    def one(self):
        ring = self.ring
        streams, step, done = self.under_way.pop(0)
        turn = ring.count - 1
        for stream in streams:
            if step < turn:
                ring.add(stream, step)
                ring.copy(stream, step, False).wait_send()
            else:
                ring.copy(stream, step, True).wait_recv()
            if step + 1 < ring.steps:
                ring.copy(stream, step + 1, step + 1 >= turn).start()
        if step + 1 < ring.steps:
            self.under_way.append([streams, step + 1, done])
        else:
            ring.drain(streams)
            done()

    def alike(self, step):
        turn = self.ring.count - 1
        return turn - 1 - step if step < turn else self.ring.steps - 1 - step

    def finish(self):
        ring = self.ring
        turn = ring.count - 1
        while self.under_way:
            run = min(self.alike(step) for _, step, _ in self.under_way)
            if run < 2:
                for _ in range(len(self.under_way)):
                    self.one()
                continue
            rings = [tuple(leaf) for leaf in self.under_way]

            def body(number, carry):
                for streams, start, _ in rings:
                    step = start + number
                    for stream in streams:
                        if start < turn:
                            ring.add(stream, step)
                            ring.copy(stream, step, False).wait_send()
                        else:
                            ring.copy(stream, step, True).wait_recv()
                        ring.copy(stream, step + 1, start >= turn).start()
                return carry

            lax.fori_loop(0, run, body, 0)
            for leaf in self.under_way:
                leaf[1] += run


def mlp_loads(refs, at):
    return load_all(
        (
            (refs.branch_b_all.at[at], refs.branch_b),
            (refs.w_down_all.at[at], refs.w_down),
            (refs.slope_all.at[at], refs.slope),
            (refs.w_up_all.at[at], refs.w_up),
            (refs.normal_b_all.at[at], refs.normal_b),
            (refs.inverse_all.at[at, 1], refs.inverse_b),
            (refs.active_all.at[at], refs.active),
            (refs.gath_b_all.at[at], refs.gath_b),
        ),
        refs.load_sems.at[1 + 2 * at],
    )


def attend_loads(refs, at):
    return load_all(
        (
            (refs.branch_a_all.at[at], refs.branch_a),
            (refs.w_out_all.at[at], refs.w_out.at[pl.ds(0, refs.w_out_all.shape[1])]),
            (refs.qkv_all.at[at], refs.qkv),
            (refs.weights_all.at[at], refs.weights),
            (refs.w_qkv_all.at[at], refs.w_qkv),
            (refs.normal_a_all.at[at], refs.normal_a),
            (refs.inverse_all.at[at, 0], refs.inverse_a),
            (refs.mixture_all.at[at], refs.mixture),
            (refs.gath_a_all.at[at], refs.gath_a),
        ),
        refs.load_sems.at[2 + 2 * at],
    )


def front(refs, group, at, tick, begin):
    rows = refs.grad.shape[0]
    half = rows // 2
    ahead = Exchange(
        group, Exchange.COPIES, refs.gath_b, refs.part_f, refs.got_f, refs.summed_f
    )
    trade = Exchange(group, 0, None, refs.part, refs.got, refs.summed)
    loads = load_all(
        (
            (refs.gath_b_all.at[at, 0], refs.gath_b.at[0]),
            (refs.w_up_all.at[at], refs.w_up),
            (refs.w_down_all.at[at], refs.w_down),
            (refs.gath_z, refs.gath_m),
            (refs.normal_b_all.at[at], refs.normal_b),
            (refs.inverse_all.at[at, 1], refs.inverse_b),
            (refs.spots_all, refs.spots),
            (refs.turned_all, refs.turned),
        ),
        refs.load_sems.at[0],
    )
    loads[0].wait()
    ahead.start()
    ahead.spread()
    for load in loads[1:4]:
        load.wait()

    def work(slot):
        refs.hidden[...] = dot(refs.gath_b[slot], refs.w_up[...]) + refs.up_bias[at : at + 1].astype(F32)
        refs.hidden_f[...] = dot(refs.gath_m[slot], refs.w_down[...], 1, 1)

        def act(place, carry):
            span = pl.ds(pl.multiple_of(place * 16, 16), 16)
            high, incline = gelu_parts(refs.hidden[span])
            refs.active[slot, span] = high.astype(BF16)
            back = (refs.hidden_f[span] * incline).astype(BF16)
            refs.d_hidden[slot, span] = back
            refs.up_total[...] += fold(back.astype(F32))
            return carry

        lax.fori_loop(0, rows // 16, act, 0)

    refs.up_total[...] = jnp.zeros_like(refs.up_total)

    def chip_slot(slot, carry):
        work(slot)
        result = dot(refs.d_hidden[slot], refs.w_up[...], 1, 1)
        result_f = dot(refs.active[slot], refs.w_down[...])

        @pl.when(slot == 0)
        def _():
            refs.own[...] = result
            refs.own_f[...] = result_f

        @pl.when(slot == 1)
        def _():
            refs.part[1] = result.astype(BF16)
            refs.part_f[1] = result_f.astype(BF16)

        return carry

    lax.fori_loop(0, 2, chip_slot, 0)
    trade.sum_near().start()
    ahead.sum_near().start()
    ahead.pass_on(0)

    def far_slot(stage, carry):
        slot = ahead.slot(stage)
        ahead.arrived(stage)
        work(slot)

        def one(place, carry):
            first = pl.multiple_of(place * ahead.keep + (1 - place) * ahead.give, half)
            span = pl.ds(first, half)
            refs.part[slot, span] = dot(
                refs.d_hidden[slot, span], refs.w_up[...], 1, 1
            ).astype(BF16)

            @pl.when(place == 0)
            def _():
                trade.pair(stage).start()

            refs.part_f[slot, span] = dot(refs.active[slot, span], refs.w_down[...]).astype(BF16)

            @pl.when(place == 0)
            def _():
                ahead.pair(stage).start()

            return carry

        lax.fori_loop(0, 2, one, 0)
        trade.send_sum(stage)
        ahead.send_sum(stage)

        @pl.when(stage == 0)
        def _():
            ahead.pass_on(1)

        return carry

    lax.fori_loop(0, 2, far_slot, 0)
    data, inner = refs.data_m.at[at], refs.w_down.shape[0]
    weight_grad(refs.active, refs.gath_m, data, 0, inner)
    begin(at, 0, 0)
    weight_grad(refs.gath_b, refs.d_hidden, data, inner, refs.w_up.shape[0])
    begin(at, 0, 1)
    refs.up_sums[at : at + 1] = jnp.sum(refs.up_total[...], 0, keepdims=True)
    for load in loads[4:]:
        load.wait()
    trade.finish()
    tick()
    leave_back(
        refs.grad,
        refs.own,
        refs.got,
        refs.normal_b,
        refs.inverse_b,
        refs.ln_gain[at, 1:2],
        refs.sums.at[2 * at + 1],
    )
    ahead.drain_gather()
    trade.drain_sum()

    def end():
        ahead.finish()
        sums = refs.sums.at[2 * at + 1]
        scale = refs.layer_scale[at, 1:2]
        width = refs.grad.shape[1]

        def body(span, carry):
            branch = (
                refs.own_f[span]
                + refs.got_f[0, span].astype(F32)
                + refs.got_f[2, span].astype(F32)
                + refs.row_bias[at, 1:2]
            )
            refs.stream[span] = refs.middle[span] + scale * branch
            values = refs.grad_in[span]
            return carry[0] + fold(values * branch), carry[1] + fold(values)

        step, count = by_chunk(rows, body)
        zero = jnp.zeros((8, width), F32)
        by_branch, alone = lax.fori_loop(0, count, step, (zero, zero))
        sums[2:3] = jnp.sum(by_branch, 0, keepdims=True)
        sums[3:4] = jnp.sum(alone, 0, keepdims=True) * scale
        ahead.drain_sum()

    return end


def back_mlp(refs, group, base, at, loads, tick, begin):
    rows = refs.grad.shape[0]
    half = rows // 2
    gath, part, hidden, d_hidden = refs.gath_m, refs.part, refs.hidden, refs.d_hidden
    trade = Exchange(group, base, gath, part, refs.got, refs.summed)
    sums = refs.sums.at[2 * at + 1]
    loads[0].wait()
    enter_back(refs.grad, refs.branch_b, refs.layer_scale[at, 1:2], gath, sums)
    trade.start()
    tick()
    trade.spread()
    for load in loads[1:4]:
        load.wait()

    refs.up_total[...] = jnp.zeros_like(refs.up_total)

    def down(slot):
        hidden[...] = dot(gath[slot], refs.w_down[...], 1, 1)

        def body(place, carry):
            span = pl.ds(pl.multiple_of(place * CHUNK, CHUNK), CHUNK)
            low = (hidden[span] * refs.slope[slot, span].astype(F32)).astype(BF16)
            d_hidden[slot, span] = low
            return carry + fold(low.astype(F32))

        zero = jnp.zeros((8, hidden.shape[1]), F32)
        refs.up_total[...] += lax.fori_loop(0, rows // CHUNK, body, zero)

    def back(slot, first, count):
        return dot(d_hidden[slot, pl.ds(first, count)], refs.w_up[...], 1, 1)

    down(0)
    tick()
    refs.own[...] = back(0, 0, rows)
    tick()
    down(1)
    part[1] = back(1, 0, rows).astype(BF16)
    trade.sum_near().start()
    tick()
    trade.pass_on(0)
    for stage in range(2):
        slot = trade.slot(stage)
        trade.arrived(stage)
        down(slot)
        tick()

        def one(place, carry):
            first = pl.multiple_of(place * trade.keep + (1 - place) * trade.give, half)
            part[slot, pl.ds(first, half)] = back(slot, first, half).astype(BF16)

            @pl.when(place == 0)
            def _():
                trade.pair(stage).start()

            return carry

        lax.fori_loop(0, 2, one, 0)
        trade.send_sum(stage)
        if stage == 0:
            trade.pass_on(1)
        tick()
    refs.up_sums[at : at + 1] = jnp.sum(refs.up_total[...], 0, keepdims=True)
    for load in loads[4:]:
        load.wait()
    data, inner = refs.data_m.at[at], refs.w_down.shape[0]
    weight_grad(refs.active, gath, data, 0, inner)
    begin(at, 0, 0)
    tick()
    weight_grad(refs.gath_b, d_hidden, data, inner, refs.w_up.shape[0])
    begin(at, 0, 1)
    tick()
    trade.finish()
    leave_back(
        refs.grad,
        refs.own,
        refs.got,
        refs.normal_b,
        refs.inverse_b,
        refs.ln_gain[at, 1:2],
        sums,
    )
    trade.drain_gather()
    trade.drain_sum()
    tick()


def back_attend(refs, group, base, at, head_count, loads, tick, begin, meanwhile):
    rows = refs.grad.shape[0]
    half = rows // 2
    data = refs.data_t.at[at]
    wide = refs.mixture.shape[2]
    gath, part, d_mixed, d_scores = refs.gath_t, refs.part, refs.d_mixed, refs.d_scores
    qkv = refs.qkv
    trade = Exchange(group, base, gath, part, refs.got, refs.summed)
    sums = refs.sums.at[2 * at]
    loads[0].wait()
    enter_back(refs.grad, refs.branch_a, refs.layer_scale[at, 0:1], gath, sums)
    trade.start()
    tick()
    trade.spread()
    if meanwhile is not None:
        meanwhile()
        tick()
    for load in loads[1:5]:
        load.wait()
    spare = jnp.zeros((rows, wide - head_count * HEAD_DIM), BF16)

    def attend(slot):
        d_mix = dot(gath[slot], refs.w_out[...], 1, 1).astype(BF16)
        pieces = ([], [], [])
        for head in range(head_count):
            lanes = slice(head * HEAD_DIM, (head + 1) * HEAD_DIM)
            queries = qkv[slot, :, 0:wide][:, lanes]
            keys = qkv[slot, :, wide : 2 * wide][:, lanes]
            values = qkv[slot, :, 2 * wide : 3 * wide][:, lanes]
            share = refs.weights[slot, head]
            d_head = d_mix[:, lanes]
            wide_share = share.astype(F32)
            d_share = dot(d_head, values, 1, 1)
            middle = jnp.sum(wide_share * d_share, -1, keepdims=True)
            d_score = (wide_share * (d_share - middle)).astype(BF16)
            d_scores[slot, head] = d_score
            pieces[0].append((dot(d_score, keys) * HEAD_DIM**-0.5).astype(BF16))
            pieces[1].append(dot(d_score, queries, 0, 0).astype(BF16))
            pieces[2].append(dot(share, d_head, 0, 0).astype(BF16))
        for place in range(3):
            d_mixed[slot, :, place * wide : (place + 1) * wide] = jnp.concatenate(
                pieces[place] + [spare], -1
            )

    def back(slot, first, count):
        return dot(d_mixed[slot, pl.ds(first, count)], refs.w_qkv[...], 1, 1)

    attend(0)
    tick()
    refs.own[...] = back(0, 0, rows)
    attend(1)
    tick()
    part[1] = back(1, 0, rows).astype(BF16)
    trade.sum_near().start()
    trade.pass_on(0)
    for stage in range(2):
        slot = trade.slot(stage)
        trade.arrived(stage)
        attend(slot)
        tick()

        def one(place, carry):
            first = pl.multiple_of(place * trade.keep + (1 - place) * trade.give, half)
            part[slot, pl.ds(first, half)] = back(slot, first, half).astype(BF16)

            @pl.when(place == 0)
            def _():
                trade.pair(stage).start()

            return carry

        lax.fori_loop(0, 2, one, 0)
        trade.send_sum(stage)
        if stage == 0:
            trade.pass_on(1)
        tick()
    for load in loads[5:]:
        load.wait()

    def add(slot, total):
        def body(span, carry):
            return carry + fold(d_mixed[slot, span].astype(F32))

        step, count = by_chunk(rows, body)
        return lax.fori_loop(0, count, step, total)

    total = jnp.zeros((8, 3 * wide), F32)
    for slot in range(4):
        total = add(slot, total)
    refs.qkv_sums[at : at + 1] = jnp.sum(total, 0, keepdims=True)
    used = 3 * head_count * HEAD_DIM
    weight_grad(d_mixed, refs.gath_a, data, 0, used)
    tick()
    weight_grad(refs.mixture, gath, data, used, used // 3)
    begin(at, 1, 0)
    tick()
    for head in range(head_count):
        total = None
        for slot in range(4):
            placed = dot(refs.spots[slot], d_scores[slot, head]).astype(BF16)
            term = dot(placed, refs.turned[slot])
            total = term if total is None else total + term
        row = at * head_count + head
        refs.table_sums[row : row + 1] = table_row(total)
    trade.finish()
    leave_back(
        refs.grad,
        refs.own,
        refs.got,
        refs.normal_a,
        refs.inverse_a,
        refs.ln_gain[at, 0:1],
        sums,
    )
    trade.drain_gather()
    trade.drain_sum()
    tick()


class BackInputs(NamedTuple):
    grad_in: object
    middle: object
    branch_a_all: object
    branch_b_all: object
    normal_a_all: object
    normal_b_all: object
    inverse_all: object
    mixture_all: object
    qkv_all: object
    weights_all: object
    gath_a_all: object
    active_all: object
    slope_all: object
    gath_b_all: object
    gath_z: object
    w_qkv_all: object
    w_out_all: object
    w_up_all: object
    w_down_all: object
    spots_all: object
    turned_all: object
    up_bias: object
    ln_gain: object
    layer_scale: object
    row_bias: object


class BackOutputs(NamedTuple):
    grad: object
    stream: object
    d_qkv: object
    d_out: object
    d_up: object
    d_down: object
    small_out: object


class BackScratch(NamedTuple):
    spots: object
    turned: object
    branch_a: object
    branch_b: object
    normal_a: object
    normal_b: object
    own: object
    own_f: object
    inverse_a: object
    inverse_b: object
    mixture: object
    qkv: object
    weights: object
    gath_a: object
    active: object
    slope: object
    gath_b: object
    gath_m: object
    gath_t: object
    w_qkv: object
    w_out: object
    w_up: object
    w_down: object
    d_hidden: object
    hidden: object
    hidden_f: object
    d_mixed: object
    d_scores: object
    part: object
    part_f: object
    got: object
    got_f: object
    summed: object
    summed_f: object
    sums: object
    up_total: object
    up_sums: object
    qkv_sums: object
    table_sums: object
    lines: object
    near_got: object
    pair_sum: object
    far_got: object
    data_m: object
    data_t: object
    got_m: object
    got_t: object
    small: object
    got_small: object
    send_sems: object
    recv_sems: object
    load_sems: object
    ring_send_m: object
    ring_recv_m: object
    ring_send_t: object
    ring_recv_t: object
    ring_send_s: object
    ring_recv_s: object
    out_sems: object


def backward_body(layers, head_count, count, *all_refs):
    refs = Names((*BackInputs._fields, *BackOutputs._fields, *BackScratch._fields), all_refs)
    rows, width = refs.grad.shape
    last = layers - 1
    group = Group(refs.send_sems, refs.recv_sems)
    barrier = pltpu.get_barrier_semaphore()
    greeted = group.greet(barrier)
    ring = Ring(count) if count else None
    if ring:
        for other in ring.sides:
            pl.semaphore_signal(barrier, inc=1, device_id={"dp": other}, device_id_type=MESH)
        greeted += 2
    pl.semaphore_wait(barrier, greeted)
    ticker = Ticker(ring)
    used = refs.d_qkv.shape[1]
    leaves = []

    def leave(at, kind, sub):
        pairs = (
            ((refs.data_m, 0, refs.d_down),),
            ((refs.data_m, refs.d_down.shape[1], refs.d_up),),
            ((refs.data_t, 0, refs.d_qkv), (refs.data_t, used, refs.d_out)),
        )[2 * kind + sub]
        for source, first, target in pairs:
            step = pltpu.make_async_copy(
                source.at[at, pl.ds(first, target.shape[1])],
                target.at[at],
                refs.out_sems.at[len(leaves)],
            )
            step.start()
            leaves.append(step)

    def begin(at, kind, sub):
        if not ring:
            leave(at, kind, sub)
            return
        leaf = (
            (refs.data_m, refs.got_m, refs.ring_send_m, refs.ring_recv_m),
            (refs.data_t, refs.got_t, refs.ring_send_t, refs.ring_recv_t),
        )[kind]
        streams = ring.streams(tuple(ref.at[at] for ref in leaf))
        ticker.add(streams[2 * sub : 2 * sub + 2], lambda: leave(at, kind, sub))

    refs.grad[...] = refs.grad_in[...]
    refs.w_out[refs.w_out_all.shape[1] :] = jnp.zeros_like(refs.w_out[refs.w_out_all.shape[1] :])
    end = front(refs, group, last, ticker.tick, begin)
    loads_m = None
    for at in reversed(range(layers)):
        base = (2 + 2 * at) * Exchange.COPIES
        if at < last:
            back_mlp(refs, group, base, at, loads_m, ticker.tick, begin)
        loads_t = attend_loads(refs, at)
        if at:
            loads_m = mlp_loads(refs, at - 1)
        back_attend(
            refs,
            group,
            base + Exchange.COPIES,
            at,
            head_count,
            loads_t,
            ticker.tick,
            begin,
            end if at == last else None,
        )

    shared = 8 * layers
    lines = refs.lines
    lines[...] = jnp.zeros_like(lines)
    for kind in range(4):
        for at in range(2 * layers):
            row = kind * 2 * layers + at
            lines[row : row + 1] = refs.sums[at, kind : kind + 1]
    base = (2 + 2 * layers) * Exchange.COPIES
    first = group.copy(base, base, lines.at[pl.ds(0, shared)], refs.near_got, group.near)
    first.start()
    ticker.tick()
    first.wait_recv()
    refs.pair_sum[...] = lines[0:shared] + refs.near_got[...]
    second = group.copy(base + 1, base + 1, refs.pair_sum, refs.far_got, group.far)
    second.start()
    ticker.tick()
    second.wait_recv()
    first.wait_send()
    lines[0:shared] = refs.pair_sum[...] + refs.far_got[...]
    row = shared
    for leaf, height in (
        (refs.qkv_sums, layers),
        (refs.up_sums, layers),
        (refs.table_sums, layers * head_count),
    ):
        lines[row : row + height] = leaf[0:height]
        row += height
    cuts = [
        (slice(at * SMALL_ROWS, (at + 1) * SMALL_ROWS), slice(at * 128, (at + 1) * 128))
        for at in range(width // 128)
    ]
    if ring:
        small = refs.small
        small[...] = jnp.zeros_like(small)
        for rows_at, lanes in cuts:
            small[rows_at] = lines[:, lanes]
        ticker.add(
            ring.streams((small, refs.got_small, refs.ring_send_s, refs.ring_recv_s)),
            lambda: None,
        )
        ticker.finish()
    second.wait_send()
    if ring:
        for rows_at, lanes in cuts:
            refs.small_out[:, lanes] = small[rows_at]
    else:
        refs.small_out[...] = lines[...]
    for step in leaves:
        step.wait()


def run_backward(count, inputs, head_count):
    grad, w_out, w_up = inputs[0], inputs[16], inputs[17]
    rows, width = grad.shape
    layers, wide = w_out.shape[0], inputs[15].shape[2] // 3
    inner = w_up.shape[2]
    used = head_count * HEAD_DIM
    ring_count = count or 2
    steps = 2 * (ring_count - 1)
    in_vmem = pl.BlockSpec(memory_space=pltpu.VMEM)
    in_hbm = pl.BlockSpec(memory_space=pl.ANY)
    assert inner == width == 3 * wide == 4 * used and layers == 2

    def wide_rows(*shape):
        return pltpu.VMEM(shape, F32)

    def low(*shape):
        return pltpu.VMEM(shape, BF16)

    def sems(*shape):
        return pltpu.SemaphoreType.DMA(shape)

    def ring_got(total, pieces):
        piece = total // (2 * ring_count * pieces)
        return low(layers, 2, pieces, ring_count - 1, piece, width)

    own = wide_rows(rows, width)
    four = low(4, rows, width)
    square = low(4, head_count, rows, rows)
    lines = wide_rows(8 * layers, width)
    small_rows = -(-SMALL_ROWS * (width // 128) // (16 * ring_count)) * 16 * ring_count
    exchanges = (2 + 2 * layers) * Exchange.COPIES + 2
    scratch = (
        [low(4, SPAN, rows), low(4, rows, SPAN)]
        + [own] * 6
        + [wide_rows(rows, 128)] * 2
        + [low(4, rows, wide), four, square, four, four, four, four, four, four]
        + [low(width, 3 * wide), low(wide, width), low(width, inner), low(inner, width)]
        + [four, own, own, four, square, four, four]
        + [low(3, rows, width)] * 2
        + [low(rows, width)] * 2
        + [wide_rows(2 * layers, 8, width)]
        + [wide_rows(8, width)] * 4
        + [wide_rows(SMALL_ROWS, width), lines, lines, lines]
        + [low(layers, 2 * width, width), low(layers, width, width)]
        + [ring_got(2 * width, PIECES), ring_got(width, 1)]
        + [wide_rows(small_rows, 128)]
        + [wide_rows(2, 1, ring_count - 1, small_rows // (2 * ring_count), 128)]
        + [sems(exchanges)] * 2
        + [sems(1 + 2 * layers, 9)]
        + [sems(layers, 2, PIECES, steps)] * 2
        + [sems(layers, 2, 1, steps)] * 2
        + [sems(2, 1, steps)] * 2
        + [sems(4 * layers)]
    )
    return pl.pallas_call(
        functools.partial(backward_body, layers, head_count, count),
        name="backward",
        out_shape=[
            jax.ShapeDtypeStruct((rows, width), F32),
            jax.ShapeDtypeStruct((rows, width), F32),
            jax.ShapeDtypeStruct((layers, 3 * used, width), BF16),
            jax.ShapeDtypeStruct((layers, used, width), BF16),
            jax.ShapeDtypeStruct((layers, width, inner), BF16),
            jax.ShapeDtypeStruct((layers, inner, width), BF16),
            jax.ShapeDtypeStruct((SMALL_ROWS, width), F32),
        ],
        in_specs=[in_vmem] * 2 + [in_hbm] * 19 + [in_vmem] * 4,
        out_specs=[in_vmem] * 2 + [in_hbm] * 4 + [in_vmem],
        scratch_shapes=scratch,
        compiler_params=pltpu.CompilerParams(
            collective_id=1, has_side_effects=True, vmem_limit_bytes=65400 * 1024
        ),
    )(*inputs)


SMALL_ROWS = 32


class Ring:
    def __init__(self, count):
        self.count = count
        self.steps = 2 * (count - 1)
        self.place = self.place_of(lax.axis_index("dp"))
        self.sides = (
            self.number_of((self.place + 1) % count),
            self.number_of((self.place + count - 1) % count),
        )

    def place_of(self, number):
        row, side = number // 2, number % 2
        return row + side * (self.count - 1 - 2 * row)

    def number_of(self, place):
        side = place // (self.count // 2)
        return 2 * (place + side * (self.count - 1 - 2 * place)) + side

    def streams(self, *sets):
        return [
            (leaf, way, sub)
            for leaf in sets
            for sub in range(leaf[1].shape[1])
            for way in range(2)
        ]

    def rows(self, stream, step):
        (data, got, _, _), way, sub = stream
        piece = got.shape[3]
        if way == 0:
            chunk = (self.place + 3 * self.count - step) % self.count
        else:
            chunk = (self.place + step) % self.count
        first = ((sub * 2 + way) * self.count + chunk) * piece
        return pl.ds(pl.multiple_of(first, piece), piece)

    def copy(self, stream, step, gather):
        (data, got, send_sems, recv_sems), way, sub = stream
        rows = self.rows(stream, step)
        return pltpu.make_async_remote_copy(
            src_ref=data.at[rows],
            dst_ref=data.at[rows] if gather else got.at[way, sub, step],
            send_sem=send_sems.at[way, sub, step],
            recv_sem=recv_sems.at[way, sub, step],
            device_id={"dp": self.sides[way]},
            device_id_type=MESH,
        )

    def start(self, streams):
        for stream in streams:
            self.copy(stream, 0, False).start()

    def add(self, stream, step):
        (data, got, _, _), way, sub = stream
        self.copy(stream, step, False).wait_recv()
        rows = self.rows(stream, step + 1)
        data[rows] = data[rows] + got[way, sub, step]

    def drain(self, streams):
        for step in range(self.count - 1, self.steps):
            for stream in streams:
                self.copy(stream, step, True).wait_send()


def ring_fits(count, rows):
    return count == 8 and rows % (2 * count * 16) == 0


def widen_body(
    wide,
    lengths,
    stream,
    gradient,
    out_in,
    up_in,
    down_in,
    small,
    result,
    d_tokens,
    d_out,
    d_up,
    d_down,
    d_bias,
    d_up_bias,
    *kinds,
):
    number = pl.program_id(0)
    rows, width = stream.shape
    layers, _, used = d_bias.shape
    place = lax.axis_index("tensor")
    length = lengths[place, 0] + lengths[place, 1]
    row = number * rows + lax.broadcasted_iota(jnp.int32, (rows, width), 0)
    result[...] = jnp.where(row < length, stream[...], 0.0).astype(BF16)
    d_tokens[...] = gradient[...]
    d_out[...] = out_in[...].astype(F32)
    d_up[...] = up_in[...].astype(F32)
    d_down[...] = down_in[...].astype(F32)

    @pl.when(number == 0)
    def _():
        for kind, leaf in enumerate(kinds):
            for at in range(layers):
                first = 2 * (kind * layers + at)
                leaf[at] = small[first : first + 2]
        first = 8 * layers
        for at in range(layers):
            for half in range(2):
                start = 2 * half * wide
                d_bias[at, half : half + 1] = small[
                    first + at : first + at + 1, start : start + used
                ]
        first += layers
        d_up_bias[...] = small[first : first + layers]


def run_widen(lengths, stream, gradient, d_out, d_up, d_down, small, wide, used):
    rows, width = stream.shape
    layers = d_out.shape[0]
    parts = 2
    steps = layers * parts

    def rows_of(total):
        return pl.BlockSpec((total // steps, width), lambda at: (at, 0))

    def block(leaf):
        return pl.BlockSpec(
            (1, leaf.shape[1] // parts, width), lambda at: (at // parts, at % parts, 0)
        )

    def whole(*shape):
        return pl.BlockSpec(shape, lambda at: (0,) * len(shape))

    def full(*shape):
        return jax.ShapeDtypeStruct(shape, F32)

    return pl.pallas_call(
        functools.partial(widen_body, wide),
        name="widen",
        grid=(steps,),
        out_shape=[
            jax.ShapeDtypeStruct((rows, width), BF16),
            full(rows, width),
            full(*d_out.shape),
            full(*d_up.shape),
            full(*d_down.shape),
            full(layers, 2, used),
            full(layers, width),
            *[full(layers, 2, width)] * 4,
        ],
        in_specs=[
            pl.BlockSpec(memory_space=pltpu.SMEM),
            rows_of(rows),
            rows_of(rows),
            block(d_out),
            block(d_up),
            block(d_down),
            whole(*small.shape),
        ],
        out_specs=[
            rows_of(rows),
            rows_of(rows),
            block(d_out),
            block(d_up),
            block(d_down),
            whole(layers, 2, used),
            whole(layers, width),
            *[whole(layers, 2, width)] * 4,
        ],
    )(lengths, stream, gradient, d_out, d_up, d_down, small)


def per_device(
    tokens,
    cotangent,
    segments,
    lengths,
    rel_index,
    w_qkv,
    qv_bias,
    w_out,
    w_fc1,
    fc1_bias,
    w_fc2,
    rel_table,
    ln_gain,
    ln_bias,
    layer_scale,
    row_bias,
):
    own_rows, width = tokens.shape
    group_rows, bin_rows = rel_index.shape
    layer_count = w_qkv.shape[0]
    head_count = rel_table.shape[2]
    local_width = w_qkv.shape[3]
    wide = -(-local_width // 256) * 256
    bin_total = group_rows // bin_rows
    place = lax.axis_index("tensor")
    assert own_rows == bin_rows and bin_total == 4

    extra = wide - local_width
    qkv_used = jnp.pad(w_qkv, ((0, 0), (0, 0), (0, 0), (0, extra))).reshape(
        layer_count, width, 3 * wide
    )
    norms = (ln_gain, ln_bias, layer_scale, row_bias)

    (
        gath_a,
        qkv,
        shares,
        mixture,
        gath_b,
        slope,
        active,
        normal_a,
        branch_a,
        normal_b,
        branch_b,
        inverse,
        spots,
        turned,
        gath_z,
        gradient,
        middle,
    ) = run_forward(
        lengths,
        rel_index,
        rel_table,
        (tokens, cotangent),
        (qkv_used, qv_bias, w_out, w_fc1, fc1_bias, w_fc2),
        norms,
    )
    dp_count = lax.axis_size("dp")
    with_ring = ring_fits(dp_count, width)
    gradient, stream, *sums = run_backward(
        dp_count if with_ring else None,
        (
            gradient,
            middle,
            branch_a,
            branch_b,
            normal_a,
            normal_b,
            inverse,
            mixture,
            qkv,
            shares,
            gath_a,
            active,
            slope,
            gath_b,
            gath_z,
            qkv_used,
            w_out,
            w_fc1,
            w_fc2,
            spots,
            turned,
            fc1_bias,
            ln_gain,
            layer_scale,
            row_bias,
        ),
        head_count,
    )
    if not with_ring:
        sums = lax.psum(sums, "dp")
    *weight_sums, small = sums
    d_qkv, d_out, d_up, d_down = weight_sums
    result, d_tokens, d_out, d_up, d_down, d_bias, d_up_bias, *kinds = run_widen(
        lengths, stream, gradient, d_out, d_up, d_down, small, wide, local_width
    )
    d_qkv = jnp.transpose(
        d_qkv.astype(F32).reshape(layer_count, 3, local_width, width), (0, 3, 1, 2)
    )
    first = 8 * layer_count + 2 * layer_count
    d_table = small[first : first + layer_count * head_count, : rel_table.shape[1]]
    d_table = jnp.transpose(d_table.reshape(layer_count, head_count, -1), (0, 2, 1))
    return (
        result,
        d_tokens,
        d_qkv,
        d_bias,
        d_out,
        d_up,
        d_up_bias,
        d_down,
        d_table,
        *kinds,
    )


def solution(mesh):
    in_specs = (
        P(("dp", "tensor"), None),
        P(("dp", "tensor"), None),
        P("dp"),
        P("dp", None),
        P("dp", None),
        P(None, None, None, "tensor"),
        P(None, None, "tensor"),
        P(None, "tensor", None),
        P(None, None, "tensor"),
        P(None, "tensor"),
        P(None, "tensor", None),
        P(None, None, "tensor"),
        P(),
        P(),
        P(),
        P(),
    )
    out_specs = (
        P(("dp", "tensor"), None),
        P(("dp", "tensor"), None),
        P(None, None, None, "tensor"),
        P(None, None, "tensor"),
        P(None, "tensor", None),
        P(None, None, "tensor"),
        P(None, "tensor"),
        P(None, "tensor", None),
        P(None, None, "tensor"),
        P(),
        P(),
        P(),
        P(),
    )
    return jax.shard_map(
        per_device, mesh=mesh, in_specs=in_specs, out_specs=out_specs, check_vma=False
    )
```

```python
import functools
from typing import NamedTuple

import jax
import jax.numpy as jnp
from jax import lax
from jax.experimental import pallas as pl
from jax.experimental.pallas import tpu as pltpu
from jax.sharding import PartitionSpec as P

HEAD_DIM = 64
SIDE = 14
STRIDE = 2 * SIDE - 1
CELLS = SIDE * SIDE
CHUNK = 32
MESH = pl.DeviceIdType.MESH
BF16 = jnp.bfloat16
F32 = jnp.float32


def dot(left_side, right_side, left_axis=1, right_axis=0):
    return lax.dot_general(
        left_side,
        right_side,
        (((left_axis,), (right_axis,)), ((), ())),
        preferred_element_type=F32,
    )


class Group:
    def __init__(self, send_sems, recv_sems):
        own = lax.axis_index("tensor")
        self.core = own % 2
        self.near = own + 1 - 2 * self.core
        self.far = (own + 2) % 4
        self.far_chip = 1 - own // 2
        self.sems = (send_sems, recv_sems)

    def greet(self, barrier):
        for other in (self.near, self.far, self.far + 1 - 2 * self.core):
            pl.semaphore_signal(
                barrier, inc=1, device_id={"tensor": other}, device_id_type=MESH
            )
        return 3

    def copy(self, sent, arrived, source, target, other):
        return pltpu.make_async_remote_copy(
            src_ref=source,
            dst_ref=target,
            send_sem=self.sems[0].at[sent],
            recv_sem=self.sems[1].at[arrived],
            device_id={"tensor": other},
            device_id_type=MESH,
        )


class Exchange:
    COPIES = 10

    def __init__(self, group, base, gath, part, got, summed):
        self.group, self.base = group, base
        self.gath, self.part, self.got, self.summed = gath, part, got, summed
        self.rows = (part if gath is None else gath).shape[1] // 2
        self.keep = group.core * self.rows
        self.give = (1 - group.core) * self.rows

    def slot(self, stage):
        core = self.group.core
        return 2 + core + stage * (1 - 2 * core)

    def span(self, first):
        return pl.ds(pl.multiple_of(first, self.rows), self.rows)

    def symmetric(self, number, source, target, other):
        at = self.base + number
        return self.group.copy(at, at, source, target, other)

    def to_near(self):
        return self.symmetric(0, self.gath.at[0], self.gath.at[1], self.group.near)

    def across(self, stage):
        core, rows = self.group.core, self.span(self.keep)
        source = core + stage * (1 - 2 * core)
        return self.symmetric(
            2 + stage,
            self.gath.at[source, rows],
            self.gath.at[self.slot(stage), rows],
            self.group.far,
        )

    def relay(self, stage):
        rows = self.span(self.keep)
        return self.symmetric(
            4 + stage,
            self.gath.at[self.slot(stage), rows],
            self.gath.at[self.slot(1 - stage), rows],
            self.group.near,
        )

    def sum_near(self):
        return self.symmetric(1, self.part.at[1], self.got.at[0], self.group.near)

    def pair(self, stage):
        return self.symmetric(
            6 + stage,
            self.part.at[self.slot(stage), self.span(self.give)],
            self.got.at[1, self.span(stage * self.rows)],
            self.group.near,
        )

    def home(self, stage, sender):
        return self.group.copy(
            self.base + 8 + stage,
            self.base + 8 + sender,
            self.summed.at[self.span(stage * self.rows)],
            self.got.at[2, self.span(sender * self.rows)],
            self.group.far_chip * 2 + stage,
        )

    def start(self):
        self.to_near().start()

        @pl.when(self.group.core == 0)
        def _():
            self.across(0).start()

    def spread(self):
        self.to_near().wait_recv()

        @pl.when(self.group.core == 1)
        def _():
            self.across(0).start()

        self.across(1).start()

    def pass_on(self, stage):
        self.across(stage).wait_recv()
        self.relay(stage).start()

    def arrived(self, stage):
        self.relay(stage).wait_recv()

    def send_sum(self, stage):
        self.pair(stage).wait_recv()
        rows = self.span(stage * self.rows)
        self.summed[rows] = self.part[self.slot(stage), self.span(self.keep)] + self.got[1, rows]
        self.home(stage, self.group.core).start()

    def finish(self):
        self.sum_near().wait_recv()
        for sender in range(2):
            self.home(0, sender).wait_recv()

    def drain_gather(self):
        self.to_near().wait_send()
        for stage in range(2):
            self.across(stage).wait_send()
            self.relay(stage).wait_send()

    def drain_sum(self):
        self.sum_near().wait_send()
        for stage in range(2):
            self.pair(stage).wait_send()
            self.home(stage, self.group.core).wait_send()


def by_chunk(total_rows, body, size=CHUNK):
    def step(at, carry):
        return body(pl.ds(pl.multiple_of(at * size, size), size), carry)

    return step, total_rows // size


def norm_chunk(values, gain, shift):
    center = values - jnp.mean(values, -1, keepdims=True)
    inverse = lax.rsqrt(jnp.mean(center * center, -1, keepdims=True) + 1e-06)
    normal = center * inverse
    return (normal * gain + shift).astype(BF16), normal, inverse


def gelu_parts(values):
    share = 0.5 * (1.0 + lax.erf(values * 0.7071067811865476))
    slope = share + values * (jnp.exp(-0.5 * values * values) * 0.3989422804014327)
    return values * share, slope


SPAN = 384
LAST = (SIDE - 1) * (STRIDE + 1)
CLASS = LAST + 1
TABLE_WIDTH = 2 * SPAN


def prepare(head_count, lengths, index_rows, table, bias, spots, turned, same):
    rows = bias.shape[3]
    own = lax.axis_index("tensor")
    order = (own, own + 1 - 2 * (own % 2), (own + 2) % 4, 3 - own)

    ones = []
    for slot in range(4):
        first = lengths[order[slot], 0]
        both = first + lengths[order[slot], 1]

        def pick(row):
            return index_rows[pl.ds(order[slot] * rows + row, 1), :]

        at = lax.broadcasted_iota(jnp.int32, (1, rows), 1)
        code = LAST - jnp.where(at < first, pick(1), pick(first + 1))
        code = jnp.where((at == 0) | (at == first), CLASS, code)
        code = jnp.where(at < both, code, -1)
        upright = lax.broadcasted_iota(jnp.int32, (SPAN, rows), 0)
        spots[slot] = (upright == code).astype(F32).astype(BF16)
        column = jnp.transpose(jnp.broadcast_to(code.astype(F32), (128, rows)))
        column = jnp.concatenate([column] * (SPAN // 128), -1)
        flat = lax.broadcasted_iota(jnp.int32, (rows, SPAN), 1).astype(F32)
        ones.append((flat == column).astype(F32).astype(BF16))
        mirrored = jnp.where(column < CLASS, LAST - column, column)
        mirrored = jnp.where(column < 0, -1.0, mirrored)
        turned[slot] = (flat == mirrored).astype(F32).astype(BF16)

        def image_of(values):
            return (values >= first).astype(jnp.int32) + (values >= both).astype(jnp.int32)

        by_row = image_of(lax.broadcasted_iota(jnp.int32, (rows, rows), 0))
        by_col = image_of(lax.broadcasted_iota(jnp.int32, (rows, rows), 1))
        same[slot] = (by_row == by_col).astype(F32)

    key_at = lax.broadcasted_iota(jnp.int32, (SPAN, SPAN), 0)
    query_at = lax.broadcasted_iota(jnp.int32, (SPAN, SPAN), 1)
    shift = SPAN - LAST

    def each(at, carry):
        row = table[pl.ds(at, 1), :]
        rolled = pltpu.roll(
            jnp.broadcast_to(row, (SPAN, TABLE_WIDTH)), 0, 1, stride=1, stride_axis=0
        )
        pairs = rolled[:, SPAN:]
        tail = shift + STRIDE * STRIDE
        pairs = jnp.where(query_at == CLASS, row[:, tail : tail + 1], pairs)
        pairs = jnp.where(key_at == CLASS, row[:, tail + 1 : tail + 2], pairs)
        pairs = jnp.where(
            (query_at == CLASS) & (key_at == CLASS), row[:, tail + 2 : tail + 3], pairs
        ).astype(BF16)
        for slot in range(4):
            half = dot(ones[slot], pairs, 1, 1).astype(BF16)
            looked = dot(half, spots[slot])
            bias[at // head_count, slot, at % head_count] = jnp.where(
                same[slot] > 0.5, looked, -1000000000.0
            ).astype(BF16)
        return carry

    lax.fori_loop(0, table.shape[0], each, 0)


def shifted_table(rel_table):
    layers, entries, head_count = rel_table.shape
    shift = SPAN - LAST
    table = jnp.transpose(rel_table, (0, 2, 1)).reshape(layers * head_count, entries).astype(F32)
    return jnp.pad(table, ((0, 0), (shift, TABLE_WIDTH - shift - entries)))


def table_row(pairs):
    query_at = lax.broadcasted_iota(jnp.int32, (SPAN, SPAN), 0)
    key_at = lax.broadcasted_iota(jnp.int32, (SPAN, SPAN), 1)
    zero = jnp.zeros((SPAN, SPAN), F32)
    patches = jnp.where((query_at <= LAST) & (key_at <= LAST), pairs, zero)
    rolled = pltpu.roll(
        jnp.concatenate([patches, zero], -1), 0, 1, stride=1, stride_axis=0
    )
    row = jnp.sum(rolled, 0, keepdims=True)
    at = lax.broadcasted_iota(jnp.int32, (1, TABLE_WIDTH), 1)
    tails = (
        (query_at == CLASS) & (key_at <= LAST),
        (query_at <= LAST) & (key_at == CLASS),
        (query_at == CLASS) & (key_at == CLASS),
    )
    for number, mask in enumerate(tails):
        row = jnp.where(at == STRIDE * STRIDE + number, jnp.sum(jnp.where(mask, pairs, zero)), row)
    return row


class Names:
    def __init__(self, names, refs):
        for name, ref in zip(names, refs, strict=True):
            setattr(self, name, ref)


def load_all(pairs, sems):
    steps = []
    for place, (source, target) in enumerate(pairs):
        step = pltpu.make_async_copy(source, target, sems.at[place])
        step.start()
        steps.append(step)
    return steps


def each_chunk(rows, body):
    def step(at, carry):
        body(pl.ds(pl.multiple_of(at * CHUNK, CHUNK), CHUNK))
        return carry

    lax.fori_loop(0, rows // CHUNK, step, 0)


def attend_rows(refs, at, slot, first, head_count):
    qkv = refs.qkv
    rows = qkv.shape[2] // 2
    wide = qkv.shape[3] // 3
    span = pl.ds(first, rows)
    heads = []
    for head in range(head_count):
        lanes = slice(head * HEAD_DIM, (head + 1) * HEAD_DIM)
        queries = qkv[at, slot, span, 0:wide][:, lanes]
        keys = qkv[at, slot, :, wide : 2 * wide][:, lanes]
        values = qkv[at, slot, :, 2 * wide : 3 * wide][:, lanes]
        scores = dot(queries, keys, 1, 1) + refs.bias[at, slot, head, span].astype(F32)
        powers = jnp.exp(scores - jnp.max(scores, -1, keepdims=True))
        weights = (powers / jnp.sum(powers, -1, keepdims=True)).astype(BF16)
        refs.weights[at, slot, head, span] = weights
        heads.append(dot(weights, values).astype(BF16))
    heads.append(jnp.zeros((rows, wide - head_count * HEAD_DIM), BF16))
    refs.mixture[at, slot, span] = jnp.concatenate(heads, -1)


class ForwardInputs(NamedTuple):
    lengths: object
    tokens: object
    cotangent: object
    qv_bias: object
    fc1_bias: object
    table: object
    ln_gain: object
    ln_bias: object
    layer_scale: object
    row_bias: object
    index_in: object
    w_qkv_in: object
    w_out_in: object
    w_up_in: object
    w_down_in: object


class ForwardKept(NamedTuple):
    gath_a: object
    qkv: object
    weights: object
    mixture: object
    gath_b: object
    slope: object
    active: object
    normal_a: object
    branch_a: object
    normal_b: object
    branch_b: object
    inverse: object
    spots: object
    turned: object


class ForwardOutputs(NamedTuple):
    gath_z_out: object
    grad: object
    stream: object


class ForwardScratch(NamedTuple):
    gath_z: object
    bias: object
    same: object
    index_rows: object
    w_qkv: object
    w_out: object
    w_up: object
    w_down: object
    qkv_bias: object
    up_bias: object
    hidden: object
    part: object
    got: object
    summed: object
    own: object
    send_sems: object
    recv_sems: object
    load_sems: object
    out_sems: object


def forward_body(layers, head_count, *all_refs):
    kept_outs = tuple(name + "_kept" for name in ForwardKept._fields)
    refs = Names(
        (*ForwardInputs._fields, *kept_outs, *ForwardOutputs._fields, *ForwardKept._fields, *ForwardScratch._fields), all_refs
    )
    stream, own, got, part = refs.stream, refs.own, refs.got, refs.part
    rows, width = stream.shape
    half = rows // 2
    last = layers - 1
    used = refs.w_out_in.shape[1]
    wide = refs.w_out.shape[1]
    loads = load_all(
        (
            (refs.index_in, refs.index_rows),
            (refs.w_qkv_in, refs.w_qkv),
            *(
                (refs.w_out_in.at[at], refs.w_out.at[at, pl.ds(0, used)])
                for at in range(layers)
            ),
            (refs.w_up_in, refs.w_up),
            (refs.w_down_in, refs.w_down),
        ),
        refs.load_sems,
    )
    group = Group(refs.send_sems, refs.recv_sems)
    barrier = pltpu.get_barrier_semaphore()
    greeted = group.greet(barrier)
    pl.semaphore_wait(barrier, greeted)
    early = Exchange(group, 2 * Exchange.COPIES, refs.gath_z, None, None, None)

    def load(span):
        stream[span] = refs.tokens[span].astype(F32)

    each_chunk(rows, load)
    refs.qkv_bias[...] = jnp.zeros_like(refs.qkv_bias)
    for at in range(layers):
        refs.w_out[at, used:] = jnp.zeros_like(refs.w_out[at, used:])
        refs.up_bias[at] = refs.fc1_bias[at : at + 1].astype(F32)
        for half_at in range(2):
            first = 2 * half_at * wide
            refs.qkv_bias[at, :, first : first + used] = refs.qv_bias[
                at, half_at : half_at + 1
            ].astype(F32)

    def keep(number, at):
        source = getattr(refs, ForwardKept._fields[number])
        target = getattr(refs, kept_outs[number])
        if number < 12:
            source, target = source.at[at], target.at[at]
        return pltpu.make_async_copy(source, target, refs.out_sems.at[number, at])

    def layer(at, carry):
        trade = Exchange(group, 0, refs.gath_a.at[at], part, got, refs.summed)

        def enter(span):
            low, normal, inv = norm_chunk(
                stream[span], refs.ln_gain[at, 0:1], refs.ln_bias[at, 0:1]
            )
            refs.gath_a[at, 0, span] = low
            refs.normal_a[at, span] = normal
            refs.inverse[at, 0, span] = jnp.broadcast_to(inv, (CHUNK, 128))

        each_chunk(rows, enter)
        trade.start()

        @pl.when(at == 0)
        def _():
            place = lax.axis_index("tensor")
            length = refs.lengths[place, 0] + refs.lengths[place, 1]

            def mask(number, carry):
                span = pl.ds(pl.multiple_of(number * CHUNK, CHUNK), CHUNK)
                row = number * CHUNK + lax.broadcasted_iota(jnp.int32, (CHUNK, width), 0)
                values = jnp.where(row < length, refs.cotangent[span].astype(F32), 0.0)
                refs.grad[span] = values
                refs.gath_z[0, span] = (values * refs.layer_scale[last, 1:2]).astype(BF16)
                return carry

            lax.fori_loop(0, rows // CHUNK, mask, 0)

        trade.spread()

        @pl.when(at == 0)
        def _():
            early.start()
            early.spread()
            loads[0].wait()
            prepare(
                head_count,
                refs.lengths,
                refs.index_rows,
                refs.table,
                refs.bias,
                refs.spots,
                refs.turned,
                refs.same,
            )
            keep(12, 0).start()
            keep(13, 0).start()
            for step in loads[1:]:
                step.wait()

        scale = jnp.concatenate(
            [
                jnp.full((1, refs.qkv.shape[3] // 3), HEAD_DIM**-0.5, F32),
                jnp.full((1, 2 * refs.qkv.shape[3] // 3), 1.0, F32),
            ],
            -1,
        )

        def project(slot):
            mixed = dot(refs.gath_a[at, slot], refs.w_qkv[at])
            mixed = (mixed + refs.qkv_bias[at]).astype(BF16).astype(F32) * scale
            refs.qkv[at, slot] = mixed.astype(BF16)

        def attend(slot, first):
            attend_rows(refs, at, slot, first, head_count)
            return dot(refs.mixture[at, slot, pl.ds(first, half)], refs.w_out[at])

        turn = 2 * (at == 0).astype(jnp.int32)

        @pl.when(at == 0)
        def _():
            trade.pass_on(0)
            trade.pass_on(1)

        def one_slot(number, carry):
            role = (number + turn) % 4
            stage = role % 2
            away = role >= 2
            slot = jnp.where(away, trade.slot(stage), role)

            @pl.when(away)
            def _():
                trade.arrived(stage)

            project(slot)

            def one(place, carry):
                first = pl.multiple_of(
                    place * trade.keep + (1 - place) * trade.give, half
                )
                result = attend(slot, first)

                @pl.when(role == 0)
                def _():
                    own[pl.ds(first, half)] = result

                @pl.when(role > 0)
                def _():
                    part[slot, pl.ds(first, half)] = result.astype(BF16)

                @pl.when(away & (place == 0))
                def _():
                    trade.pair(stage).start()

                return carry

            lax.fori_loop(0, 2, one, 0)

            @pl.when(away)
            def _():
                trade.send_sum(stage)

            @pl.when(role == 1)
            def _():
                trade.sum_near().start()

            @pl.when((at > 0) & (role == 1))
            def _():
                trade.pass_on(0)

            @pl.when((at > 0) & (role == 2))
            def _():
                trade.pass_on(1)

            return carry

        lax.fori_loop(0, 4, one_slot, 0)
        for number in range(4):
            keep(number, at).start()

        @pl.when(at == 0)
        def _():
            for stage in range(2):
                early.pass_on(stage)

        trade.finish()

        def between(span):
            total = own[span] + got[0, span].astype(F32) + got[2, span].astype(F32)
            branch = total + refs.row_bias[at, 0:1]
            refs.branch_a[at, span] = branch
            middle = stream[span] + refs.layer_scale[at, 0:1] * branch
            stream[span] = middle
            low, normal, inv = norm_chunk(middle, refs.ln_gain[at, 1:2], refs.ln_bias[at, 1:2])
            refs.gath_b[at, 0, span] = low
            refs.normal_b[at, span] = normal
            refs.inverse[at, 1, span] = jnp.broadcast_to(inv, (CHUNK, 128))

        each_chunk(rows, between)
        for number in (7, 8, 9, 11):
            keep(number, at).start()

        @pl.when(at < last)
        def _():
            trade_b = Exchange(
                group, Exchange.COPIES, refs.gath_b.at[at], part, got, refs.summed
            )
            trade_b.start()
            trade.drain_gather()
            trade.drain_sum()
            trade_b.spread()

            def raise_rows(slot):
                refs.hidden[...] = dot(refs.gath_b[at, slot], refs.w_up[at]) + refs.up_bias[at]

                def act(place, carry):
                    span = pl.ds(pl.multiple_of(place * CHUNK, CHUNK), CHUNK)
                    high, incline = gelu_parts(refs.hidden[span])
                    refs.active[at, slot, span] = high.astype(BF16)
                    refs.slope[at, slot, span] = incline.astype(BF16)
                    return carry

                lax.fori_loop(0, rows // CHUNK, act, 0)

            def lower(slot, first, count):
                return dot(refs.active[at, slot, pl.ds(first, count)], refs.w_down[at])

            def one_slot(role, carry):
                stage = role % 2
                away = role >= 2
                slot = jnp.where(away, trade_b.slot(stage), role)

                @pl.when(away)
                def _():
                    trade_b.arrived(stage)

                raise_rows(slot)

                def one(place, carry):
                    first = pl.multiple_of(
                        place * trade_b.keep + (1 - place) * trade_b.give, half
                    )
                    result = lower(slot, first, half)

                    @pl.when(role == 0)
                    def _():
                        own[pl.ds(first, half)] = result

                    @pl.when(role > 0)
                    def _():
                        part[slot, pl.ds(first, half)] = result.astype(BF16)

                    @pl.when(away & (place == 0))
                    def _():
                        trade_b.pair(stage).start()

                    return carry

                lax.fori_loop(0, 2, one, 0)

                @pl.when(away)
                def _():
                    trade_b.send_sum(stage)

                @pl.when(role == 1)
                def _():
                    trade_b.sum_near().start()
                    trade_b.pass_on(0)

                @pl.when(role == 2)
                def _():
                    trade_b.pass_on(1)

                return carry

            lax.fori_loop(0, 4, one_slot, 0)
            for number in (4, 5, 6):
                keep(number, at).start()
            trade_b.finish()

            def after(span):
                total = own[span] + got[0, span].astype(F32) + got[2, span].astype(F32)
                branch = total + refs.row_bias[at, 1:2]
                refs.branch_b[at, span] = branch
                stream[span] = stream[span] + refs.layer_scale[at, 1:2] * branch

            each_chunk(rows, after)
            keep(10, at).start()
            trade_b.drain_gather()
            trade_b.drain_sum()

        @pl.when(at == last)
        def _():
            pltpu.make_async_copy(
                refs.gath_b.at[at, 0], refs.gath_b_kept.at[at, 0], refs.out_sems.at[4, at]
            ).start()
            trade.drain_gather()
            trade.drain_sum()

        return carry

    lax.fori_loop(0, layers, layer, 0)
    for stage in range(2):
        early.arrived(stage)
    early.drain_gather()
    leave = pltpu.make_async_copy(refs.gath_z, refs.gath_z_out, refs.load_sems.at[0])
    leave.start()
    pltpu.make_async_copy(
        refs.gath_b.at[last, 0], refs.gath_b_kept.at[last, 0], refs.out_sems.at[4, last]
    ).wait()
    for at in range(layers):
        for number in range(12):
            if at < last or number not in (4, 5, 6, 10):
                keep(number, at).wait()
    keep(12, 0).wait()
    keep(13, 0).wait()
    leave.wait()


def run_forward(lengths, index_rows, rel_table, rows_in, weights, norms):
    tokens, cotangent = rows_in
    rows, width = tokens.shape
    w_qkv, qv_bias, w_out, w_up, fc1_bias, w_down = weights
    layers, _, head_count = rel_table.shape
    wide = w_qkv.shape[2] // 3
    inner = w_up.shape[2]
    in_vmem = pl.BlockSpec(memory_space=pltpu.VMEM)
    in_hbm = pl.BlockSpec(memory_space=pl.ANY)

    def low(*shape):
        return jax.ShapeDtypeStruct(shape, BF16)

    def full(*shape):
        return jax.ShapeDtypeStruct(shape, F32)

    kept = [
        low(layers, 4, *tail)
        for tail in (
            (rows, width),
            (rows, 3 * wide),
            (head_count, rows, rows),
            (rows, wide),
            (rows, width),
            (rows, inner),
            (rows, inner),
        )
    ]
    own = full(rows, width)
    kept += [full(layers, rows, width)] * 4 + [full(layers, 2, rows, 128)]
    kept += [low(4, SPAN, rows), low(4, rows, SPAN)]
    near = [own, own]
    scratch = [
        *kept,
        low(4, rows, width),
        low(layers, 4, head_count, rows, rows),
        full(4, rows, rows),
        jax.ShapeDtypeStruct(index_rows.shape, index_rows.dtype),
        low(*w_qkv.shape),
        low(layers, wide, width),
        low(*w_up.shape),
        low(*w_down.shape),
        full(layers, 1, 3 * wide),
        full(layers, 1, inner),
        full(rows, inner),
        low(4, rows, width),
        low(3, rows, width),
        low(rows, width),
        own,
    ]
    copies = 3 * Exchange.COPIES
    return pl.pallas_call(
        functools.partial(forward_body, layers, head_count),
        name="forward",
        out_shape=[*kept, low(4, rows, width), *near],
        in_specs=[pl.BlockSpec(memory_space=pltpu.SMEM)] + [in_vmem] * 9 + [in_hbm] * 5,
        out_specs=[in_hbm] * (len(kept) + 1) + [in_vmem] * len(near),
        scratch_shapes=[
            *[pltpu.VMEM(leaf.shape, leaf.dtype) for leaf in scratch],
            pltpu.SemaphoreType.DMA((copies,)),
            pltpu.SemaphoreType.DMA((copies,)),
            pltpu.SemaphoreType.DMA((4 + layers,)),
            pltpu.SemaphoreType.DMA((len(kept), layers)),
        ],
        compiler_params=pltpu.CompilerParams(
            collective_id=0, has_side_effects=True, vmem_limit_bytes=65400 * 1024
        ),
    )(
        lengths,
        tokens,
        cotangent,
        qv_bias,
        fc1_bias,
        shifted_table(rel_table),
        *norms,
        index_rows,
        w_qkv,
        w_out,
        w_up,
        w_down,
    )


def fold(values):
    return jnp.sum(values.reshape(-1, 8, values.shape[-1]), 0)


def enter_back(grad, branch, scale, gath, sums):
    rows, width = grad.shape

    def body(span, carry):
        values = grad[span]
        gath[0, span] = (values * scale).astype(BF16)
        return carry[0] + fold(values * branch[span]), carry[1] + fold(values)

    step, count = by_chunk(rows, body)
    zero = jnp.zeros((8, width), F32)
    by_branch, alone = lax.fori_loop(0, count, step, (zero, zero))
    sums[2:3] = jnp.sum(by_branch, 0, keepdims=True)
    sums[3:4] = jnp.sum(alone, 0, keepdims=True) * scale


def leave_back(grad, own, got, normal, inverse, gain, sums):
    rows, width = grad.shape

    def body(span, carry):
        total = own[span] + got[0, span].astype(F32) + got[2, span].astype(F32)
        unit = normal[span]
        scaled = total * gain
        centered = (
            scaled
            - jnp.mean(scaled, -1, keepdims=True)
            - unit * jnp.mean(scaled * unit, -1, keepdims=True)
        )
        grad[span] = grad[span] + inverse[span, 0:1] * centered
        return carry[0] + fold(total * unit), carry[1] + fold(total)

    step, count = by_chunk(rows, body)
    zero = jnp.zeros((8, width), F32)
    by_unit, alone = lax.fori_loop(0, count, step, (zero, zero))
    sums[0:1] = jnp.sum(by_unit, 0, keepdims=True)
    sums[1:2] = jnp.sum(alone, 0, keepdims=True)


def weight_grad(left, right, out, start, count, tick=None):
    block = 256
    used = count * block // left.shape[2]

    def step(place, carry):
        span = pl.ds(pl.multiple_of(place * block, block), block)
        total = None
        for slot in range(4):
            term = dot(left[slot, :, span], right[slot], 0, 0)
            total = term if total is None else total + term
        there = pl.ds(pl.multiple_of(start + place * used, 16), used)
        out[there] = total[:used].astype(out.dtype)
        return carry

    if tick is None:
        lax.fori_loop(0, left.shape[2] // block, step, 0)
    else:
        for place in range(left.shape[2] // block):
            step(place, 0)
            tick()


PIECES = 2


class Ticker:
    def __init__(self, ring):
        self.ring = ring
        self.under_way = []

    def add(self, streams, done):
        self.ring.start(streams)
        self.under_way.append([streams, 0, done])

    def tick(self):
        if self.under_way:
            self.one()

    def one(self):
        ring = self.ring
        streams, step, done = self.under_way.pop(0)
        turn = ring.count - 1
        for stream in streams:
            if step < turn:
                ring.add(stream, step)
                ring.copy(stream, step, False).wait_send()
            else:
                ring.copy(stream, step, True).wait_recv()
            if step + 1 < ring.steps:
                ring.copy(stream, step + 1, step + 1 >= turn).start()
        if step + 1 < ring.steps:
            self.under_way.append([streams, step + 1, done])
        else:
            ring.drain(streams)
            done()

    def alike(self, step):
        turn = self.ring.count - 1
        return turn - 1 - step if step < turn else self.ring.steps - 1 - step

    def finish(self):
        ring = self.ring
        turn = ring.count - 1
        while self.under_way:
            run = min(self.alike(step) for _, step, _ in self.under_way)
            if run < 2:
                for _ in range(len(self.under_way)):
                    self.one()
                continue
            rings = [tuple(leaf) for leaf in self.under_way]

            def body(number, carry):
                for streams, start, _ in rings:
                    step = start + number
                    for stream in streams:
                        if start < turn:
                            ring.add(stream, step)
                            ring.copy(stream, step, False).wait_send()
                        else:
                            ring.copy(stream, step, True).wait_recv()
                        ring.copy(stream, step + 1, start >= turn).start()
                return carry

            lax.fori_loop(0, run, body, 0)
            for leaf in self.under_way:
                leaf[1] += run


def mlp_loads(refs, at):
    return load_all(
        (
            (refs.branch_b_all.at[at], refs.branch_b),
            (refs.w_down_all.at[at], refs.w_down),
            (refs.slope_all.at[at], refs.slope),
            (refs.w_up_all.at[at], refs.w_up),
            (refs.normal_b_all.at[at], refs.normal_b),
            (refs.inverse_all.at[at, 1], refs.inverse_b),
            (refs.active_all.at[at], refs.active),
            (refs.gath_b_all.at[at], refs.gath_b),
        ),
        refs.load_sems.at[1 + 2 * at],
    )


def attend_loads(refs, at):
    return load_all(
        (
            (refs.branch_a_all.at[at], refs.branch_a),
            (refs.w_out_all.at[at], refs.w_out.at[pl.ds(0, refs.w_out_all.shape[1])]),
            (refs.qkv_all.at[at], refs.qkv),
            (refs.weights_all.at[at], refs.weights),
            (refs.w_qkv_all.at[at], refs.w_qkv),
            (refs.normal_a_all.at[at], refs.normal_a),
            (refs.inverse_all.at[at, 0], refs.inverse_a),
            (refs.mixture_all.at[at], refs.mixture),
            (refs.gath_a_all.at[at], refs.gath_a),
        ),
        refs.load_sems.at[2 + 2 * at],
    )


def front(refs, group, at, tick, begin):
    rows = refs.grad.shape[0]
    half = rows // 2
    ahead = Exchange(
        group, Exchange.COPIES, refs.gath_b, refs.part_f, refs.got_f, refs.summed_f
    )
    trade = Exchange(group, 0, None, refs.part, refs.got, refs.summed)
    loads = load_all(
        (
            (refs.gath_b_all.at[at, 0], refs.gath_b.at[0]),
            (refs.w_up_all.at[at], refs.w_up),
            (refs.w_down_all.at[at], refs.w_down),
            (refs.gath_z, refs.gath_m),
            (refs.normal_b_all.at[at], refs.normal_b),
            (refs.inverse_all.at[at, 1], refs.inverse_b),
            (refs.spots_all, refs.spots),
            (refs.turned_all, refs.turned),
        ),
        refs.load_sems.at[0],
    )
    loads[0].wait()
    ahead.start()
    ahead.spread()
    for load in loads[1:4]:
        load.wait()

    def work(slot):
        refs.hidden[...] = dot(refs.gath_b[slot], refs.w_up[...]) + refs.up_bias[at : at + 1].astype(F32)
        refs.hidden_f[...] = dot(refs.gath_m[slot], refs.w_down[...], 1, 1)

        def act(place, carry):
            span = pl.ds(pl.multiple_of(place * CHUNK, CHUNK), CHUNK)
            high, incline = gelu_parts(refs.hidden[span])
            refs.active[slot, span] = high.astype(BF16)
            back = (refs.hidden_f[span] * incline).astype(BF16)
            refs.d_hidden[slot, span] = back
            refs.up_total[...] += fold(back.astype(F32))
            return carry

        lax.fori_loop(0, rows // CHUNK, act, 0)

    refs.up_total[...] = jnp.zeros_like(refs.up_total)

    def chip_slot(slot, carry):
        work(slot)
        result = dot(refs.d_hidden[slot], refs.w_up[...], 1, 1)
        result_f = dot(refs.active[slot], refs.w_down[...])

        @pl.when(slot == 0)
        def _():
            refs.own[...] = result
            refs.own_f[...] = result_f

        @pl.when(slot == 1)
        def _():
            refs.part[1] = result.astype(BF16)
            refs.part_f[1] = result_f.astype(BF16)

        return carry

    lax.fori_loop(0, 2, chip_slot, 0)
    trade.sum_near().start()
    ahead.sum_near().start()
    ahead.pass_on(0)

    def far_slot(stage, carry):
        slot = ahead.slot(stage)
        ahead.arrived(stage)
        work(slot)

        def one(place, carry):
            first = pl.multiple_of(place * ahead.keep + (1 - place) * ahead.give, half)
            span = pl.ds(first, half)
            refs.part[slot, span] = dot(
                refs.d_hidden[slot, span], refs.w_up[...], 1, 1
            ).astype(BF16)

            @pl.when(place == 0)
            def _():
                trade.pair(stage).start()

            refs.part_f[slot, span] = dot(refs.active[slot, span], refs.w_down[...]).astype(BF16)

            @pl.when(place == 0)
            def _():
                ahead.pair(stage).start()

            return carry

        lax.fori_loop(0, 2, one, 0)
        trade.send_sum(stage)
        ahead.send_sum(stage)

        @pl.when(stage == 0)
        def _():
            ahead.pass_on(1)

        return carry

    lax.fori_loop(0, 2, far_slot, 0)
    data, inner = refs.data_m.at[at], refs.w_down.shape[0]
    weight_grad(refs.active, refs.gath_m, data, 0, inner)
    begin(at, 0, 0)
    weight_grad(refs.gath_b, refs.d_hidden, data, inner, refs.w_up.shape[0])
    begin(at, 0, 1)
    refs.up_sums[at : at + 1] = jnp.sum(refs.up_total[...], 0, keepdims=True)
    for load in loads[4:]:
        load.wait()
    trade.finish()
    tick()
    leave_back(
        refs.grad,
        refs.own,
        refs.got,
        refs.normal_b,
        refs.inverse_b,
        refs.ln_gain[at, 1:2],
        refs.sums.at[2 * at + 1],
    )
    ahead.drain_gather()
    trade.drain_sum()

    def end():
        ahead.finish()
        sums = refs.sums.at[2 * at + 1]
        scale = refs.layer_scale[at, 1:2]
        width = refs.grad.shape[1]

        def body(span, carry):
            branch = (
                refs.own_f[span]
                + refs.got_f[0, span].astype(F32)
                + refs.got_f[2, span].astype(F32)
                + refs.row_bias[at, 1:2]
            )
            refs.stream[span] = refs.middle[span] + scale * branch
            values = refs.grad_in[span]
            return carry[0] + fold(values * branch), carry[1] + fold(values)

        step, count = by_chunk(rows, body)
        zero = jnp.zeros((8, width), F32)
        by_branch, alone = lax.fori_loop(0, count, step, (zero, zero))
        sums[2:3] = jnp.sum(by_branch, 0, keepdims=True)
        sums[3:4] = jnp.sum(alone, 0, keepdims=True) * scale
        ahead.drain_sum()

    return end


def back_mlp(refs, group, base, at, loads, tick, begin):
    rows = refs.grad.shape[0]
    half = rows // 2
    gath, part, hidden, d_hidden = refs.gath_m, refs.part, refs.hidden, refs.d_hidden
    trade = Exchange(group, base, gath, part, refs.got, refs.summed)
    sums = refs.sums.at[2 * at + 1]
    loads[0].wait()
    enter_back(refs.grad, refs.branch_b, refs.layer_scale[at, 1:2], gath, sums)
    trade.start()
    tick()
    trade.spread()
    for load in loads[1:4]:
        load.wait()

    refs.up_total[...] = jnp.zeros_like(refs.up_total)

    def down(slot):
        hidden[...] = dot(gath[slot], refs.w_down[...], 1, 1)

        def body(place, carry):
            span = pl.ds(pl.multiple_of(place * CHUNK, CHUNK), CHUNK)
            low = (hidden[span] * refs.slope[slot, span].astype(F32)).astype(BF16)
            d_hidden[slot, span] = low
            return carry + fold(low.astype(F32))

        zero = jnp.zeros((8, hidden.shape[1]), F32)
        refs.up_total[...] += lax.fori_loop(0, rows // CHUNK, body, zero)

    def back(slot, first, count):
        return dot(d_hidden[slot, pl.ds(first, count)], refs.w_up[...], 1, 1)

    down(0)
    tick()
    refs.own[...] = back(0, 0, rows)
    tick()
    down(1)
    part[1] = back(1, 0, rows).astype(BF16)
    trade.sum_near().start()
    tick()
    trade.pass_on(0)
    for stage in range(2):
        slot = trade.slot(stage)
        trade.arrived(stage)
        down(slot)
        tick()

        def one(place, carry):
            first = pl.multiple_of(place * trade.keep + (1 - place) * trade.give, half)
            part[slot, pl.ds(first, half)] = back(slot, first, half).astype(BF16)

            @pl.when(place == 0)
            def _():
                trade.pair(stage).start()

            return carry

        lax.fori_loop(0, 2, one, 0)
        trade.send_sum(stage)
        if stage == 0:
            trade.pass_on(1)
        tick()
    refs.up_sums[at : at + 1] = jnp.sum(refs.up_total[...], 0, keepdims=True)
    for load in loads[4:]:
        load.wait()
    data, inner = refs.data_m.at[at], refs.w_down.shape[0]
    weight_grad(refs.active, gath, data, 0, inner)
    begin(at, 0, 0)
    tick()
    weight_grad(refs.gath_b, d_hidden, data, inner, refs.w_up.shape[0])
    begin(at, 0, 1)
    tick()
    trade.finish()
    leave_back(
        refs.grad,
        refs.own,
        refs.got,
        refs.normal_b,
        refs.inverse_b,
        refs.ln_gain[at, 1:2],
        sums,
    )
    trade.drain_gather()
    trade.drain_sum()
    tick()


def back_attend(refs, group, base, at, head_count, loads, tick, begin, meanwhile):
    rows = refs.grad.shape[0]
    half = rows // 2
    data = refs.data_t.at[at]
    wide = refs.mixture.shape[2]
    gath, part, d_mixed, d_scores = refs.gath_t, refs.part, refs.d_mixed, refs.d_scores
    qkv = refs.qkv
    trade = Exchange(group, base, gath, part, refs.got, refs.summed)
    sums = refs.sums.at[2 * at]
    loads[0].wait()
    enter_back(refs.grad, refs.branch_a, refs.layer_scale[at, 0:1], gath, sums)
    trade.start()
    tick()
    trade.spread()
    if meanwhile is not None:
        meanwhile()
        tick()
    for load in loads[1:5]:
        load.wait()
    spare = jnp.zeros((rows, wide - head_count * HEAD_DIM), BF16)

    def attend(slot):
        d_mix = dot(gath[slot], refs.w_out[...], 1, 1).astype(BF16)
        pieces = ([], [], [])
        for head in range(head_count):
            lanes = slice(head * HEAD_DIM, (head + 1) * HEAD_DIM)
            queries = qkv[slot, :, 0:wide][:, lanes]
            keys = qkv[slot, :, wide : 2 * wide][:, lanes]
            values = qkv[slot, :, 2 * wide : 3 * wide][:, lanes]
            share = refs.weights[slot, head]
            d_head = d_mix[:, lanes]
            wide_share = share.astype(F32)
            d_share = dot(d_head, values, 1, 1)
            middle = jnp.sum(wide_share * d_share, -1, keepdims=True)
            d_score = (wide_share * (d_share - middle)).astype(BF16)
            d_scores[slot, head] = d_score
            pieces[0].append((dot(d_score, keys) * HEAD_DIM**-0.5).astype(BF16))
            pieces[1].append(dot(d_score, queries, 0, 0).astype(BF16))
            pieces[2].append(dot(share, d_head, 0, 0).astype(BF16))
        for place in range(3):
            d_mixed[slot, :, place * wide : (place + 1) * wide] = jnp.concatenate(
                pieces[place] + [spare], -1
            )

    def back(slot, first, count):
        return dot(d_mixed[slot, pl.ds(first, count)], refs.w_qkv[...], 1, 1)

    attend(0)
    tick()
    refs.own[...] = back(0, 0, rows)
    attend(1)
    tick()
    part[1] = back(1, 0, rows).astype(BF16)
    trade.sum_near().start()
    trade.pass_on(0)
    for stage in range(2):
        slot = trade.slot(stage)
        trade.arrived(stage)
        attend(slot)
        tick()

        def one(place, carry):
            first = pl.multiple_of(place * trade.keep + (1 - place) * trade.give, half)
            part[slot, pl.ds(first, half)] = back(slot, first, half).astype(BF16)

            @pl.when(place == 0)
            def _():
                trade.pair(stage).start()

            return carry

        lax.fori_loop(0, 2, one, 0)
        trade.send_sum(stage)
        if stage == 0:
            trade.pass_on(1)
        tick()
    for load in loads[5:]:
        load.wait()

    def add(slot, total):
        def body(span, carry):
            return carry + fold(d_mixed[slot, span].astype(F32))

        step, count = by_chunk(rows, body)
        return lax.fori_loop(0, count, step, total)

    total = jnp.zeros((8, 3 * wide), F32)
    for slot in range(4):
        total = add(slot, total)
    refs.qkv_sums[at : at + 1] = jnp.sum(total, 0, keepdims=True)
    used = 3 * head_count * HEAD_DIM
    weight_grad(d_mixed, refs.gath_a, data, 0, used)
    tick()
    weight_grad(refs.mixture, gath, data, used, used // 3)
    begin(at, 1, 0)
    tick()
    for head in range(head_count):
        total = None
        for slot in range(4):
            placed = dot(refs.spots[slot], d_scores[slot, head]).astype(BF16)
            term = dot(placed, refs.turned[slot])
            total = term if total is None else total + term
        row = at * head_count + head
        refs.table_sums[row : row + 1] = table_row(total)
    trade.finish()
    leave_back(
        refs.grad,
        refs.own,
        refs.got,
        refs.normal_a,
        refs.inverse_a,
        refs.ln_gain[at, 0:1],
        sums,
    )
    trade.drain_gather()
    trade.drain_sum()
    tick()


class BackInputs(NamedTuple):
    grad_in: object
    middle: object
    branch_a_all: object
    branch_b_all: object
    normal_a_all: object
    normal_b_all: object
    inverse_all: object
    mixture_all: object
    qkv_all: object
    weights_all: object
    gath_a_all: object
    active_all: object
    slope_all: object
    gath_b_all: object
    gath_z: object
    w_qkv_all: object
    w_out_all: object
    w_up_all: object
    w_down_all: object
    spots_all: object
    turned_all: object
    up_bias: object
    ln_gain: object
    layer_scale: object
    row_bias: object


class BackOutputs(NamedTuple):
    grad: object
    stream: object
    d_qkv: object
    d_out: object
    d_up: object
    d_down: object
    small_out: object


class BackScratch(NamedTuple):
    spots: object
    turned: object
    branch_a: object
    branch_b: object
    normal_a: object
    normal_b: object
    own: object
    own_f: object
    inverse_a: object
    inverse_b: object
    mixture: object
    qkv: object
    weights: object
    gath_a: object
    active: object
    slope: object
    gath_b: object
    gath_m: object
    gath_t: object
    w_qkv: object
    w_out: object
    w_up: object
    w_down: object
    d_hidden: object
    hidden: object
    hidden_f: object
    d_mixed: object
    d_scores: object
    part: object
    part_f: object
    got: object
    got_f: object
    summed: object
    summed_f: object
    sums: object
    up_total: object
    up_sums: object
    qkv_sums: object
    table_sums: object
    lines: object
    near_got: object
    pair_sum: object
    far_got: object
    data_m: object
    data_t: object
    got_m: object
    got_t: object
    small: object
    got_small: object
    send_sems: object
    recv_sems: object
    load_sems: object
    ring_send_m: object
    ring_recv_m: object
    ring_send_t: object
    ring_recv_t: object
    ring_send_s: object
    ring_recv_s: object
    out_sems: object


def backward_body(layers, head_count, count, *all_refs):
    refs = Names((*BackInputs._fields, *BackOutputs._fields, *BackScratch._fields), all_refs)
    rows, width = refs.grad.shape
    last = layers - 1
    group = Group(refs.send_sems, refs.recv_sems)
    barrier = pltpu.get_barrier_semaphore()
    greeted = group.greet(barrier)
    ring = Ring(count) if count else None
    if ring:
        for other in ring.sides:
            pl.semaphore_signal(barrier, inc=1, device_id={"dp": other}, device_id_type=MESH)
        greeted += 2
    pl.semaphore_wait(barrier, greeted)
    ticker = Ticker(ring)
    used = refs.d_qkv.shape[1]
    leaves = []

    def leave(at, kind, sub):
        pairs = (
            ((refs.data_m, 0, refs.d_down),),
            ((refs.data_m, refs.d_down.shape[1], refs.d_up),),
            ((refs.data_t, 0, refs.d_qkv), (refs.data_t, used, refs.d_out)),
        )[2 * kind + sub]
        for source, first, target in pairs:
            step = pltpu.make_async_copy(
                source.at[at, pl.ds(first, target.shape[1])],
                target.at[at],
                refs.out_sems.at[len(leaves)],
            )
            step.start()
            leaves.append(step)

    def begin(at, kind, sub):
        if not ring:
            leave(at, kind, sub)
            return
        leaf = (
            (refs.data_m, refs.got_m, refs.ring_send_m, refs.ring_recv_m),
            (refs.data_t, refs.got_t, refs.ring_send_t, refs.ring_recv_t),
        )[kind]
        streams = ring.streams(tuple(ref.at[at] for ref in leaf))
        ticker.add(streams[2 * sub : 2 * sub + 2], lambda: leave(at, kind, sub))

    refs.grad[...] = refs.grad_in[...]
    refs.w_out[refs.w_out_all.shape[1] :] = jnp.zeros_like(refs.w_out[refs.w_out_all.shape[1] :])
    end = front(refs, group, last, ticker.tick, begin)
    loads_m = None
    for at in reversed(range(layers)):
        base = (2 + 2 * at) * Exchange.COPIES
        if at < last:
            back_mlp(refs, group, base, at, loads_m, ticker.tick, begin)
        loads_t = attend_loads(refs, at)
        if at:
            loads_m = mlp_loads(refs, at - 1)
        back_attend(
            refs,
            group,
            base + Exchange.COPIES,
            at,
            head_count,
            loads_t,
            ticker.tick,
            begin,
            end if at == last else None,
        )

    shared = 8 * layers
    lines = refs.lines
    lines[...] = jnp.zeros_like(lines)
    for kind in range(4):
        for at in range(2 * layers):
            row = kind * 2 * layers + at
            lines[row : row + 1] = refs.sums[at, kind : kind + 1]
    base = (2 + 2 * layers) * Exchange.COPIES
    first = group.copy(base, base, lines.at[pl.ds(0, shared)], refs.near_got, group.near)
    first.start()
    ticker.tick()
    first.wait_recv()
    refs.pair_sum[...] = lines[0:shared] + refs.near_got[...]
    second = group.copy(base + 1, base + 1, refs.pair_sum, refs.far_got, group.far)
    second.start()
    ticker.tick()
    second.wait_recv()
    first.wait_send()
    lines[0:shared] = refs.pair_sum[...] + refs.far_got[...]
    row = shared
    for leaf, height in (
        (refs.qkv_sums, layers),
        (refs.up_sums, layers),
        (refs.table_sums, layers * head_count),
    ):
        lines[row : row + height] = leaf[0:height]
        row += height
    cuts = [
        (slice(at * SMALL_ROWS, (at + 1) * SMALL_ROWS), slice(at * 128, (at + 1) * 128))
        for at in range(width // 128)
    ]
    if ring:
        small = refs.small
        small[...] = jnp.zeros_like(small)
        for rows_at, lanes in cuts:
            small[rows_at] = lines[:, lanes]
        ticker.add(
            ring.streams((small, refs.got_small, refs.ring_send_s, refs.ring_recv_s)),
            lambda: None,
        )
        ticker.finish()
    second.wait_send()
    if ring:
        for rows_at, lanes in cuts:
            refs.small_out[:, lanes] = small[rows_at]
    else:
        refs.small_out[...] = lines[...]
    for step in leaves:
        step.wait()


def run_backward(count, inputs, head_count):
    grad, w_out, w_up = inputs[0], inputs[16], inputs[17]
    rows, width = grad.shape
    layers, wide = w_out.shape[0], inputs[15].shape[2] // 3
    inner = w_up.shape[2]
    used = head_count * HEAD_DIM
    ring_count = count or 2
    steps = 2 * (ring_count - 1)
    in_vmem = pl.BlockSpec(memory_space=pltpu.VMEM)
    in_hbm = pl.BlockSpec(memory_space=pl.ANY)
    assert inner == width == 3 * wide == 4 * used and layers == 2

    def wide_rows(*shape):
        return pltpu.VMEM(shape, F32)

    def low(*shape):
        return pltpu.VMEM(shape, BF16)

    def sems(*shape):
        return pltpu.SemaphoreType.DMA(shape)

    def ring_got(total, pieces):
        piece = total // (2 * ring_count * pieces)
        return low(layers, 2, pieces, ring_count - 1, piece, width)

    own = wide_rows(rows, width)
    four = low(4, rows, width)
    square = low(4, head_count, rows, rows)
    lines = wide_rows(8 * layers, width)
    small_rows = -(-SMALL_ROWS * (width // 128) // (16 * ring_count)) * 16 * ring_count
    exchanges = (2 + 2 * layers) * Exchange.COPIES + 2
    scratch = (
        [low(4, SPAN, rows), low(4, rows, SPAN)]
        + [own] * 6
        + [wide_rows(rows, 128)] * 2
        + [low(4, rows, wide), four, square, four, four, four, four, four, four]
        + [low(width, 3 * wide), low(wide, width), low(width, inner), low(inner, width)]
        + [four, own, own, four, square, four, four]
        + [low(3, rows, width)] * 2
        + [low(rows, width)] * 2
        + [wide_rows(2 * layers, 8, width)]
        + [wide_rows(8, width)] * 4
        + [wide_rows(SMALL_ROWS, width), lines, lines, lines]
        + [low(layers, 2 * width, width), low(layers, width, width)]
        + [ring_got(2 * width, PIECES), ring_got(width, 1)]
        + [wide_rows(small_rows, 128)]
        + [wide_rows(2, 1, ring_count - 1, small_rows // (2 * ring_count), 128)]
        + [sems(exchanges)] * 2
        + [sems(1 + 2 * layers, 9)]
        + [sems(layers, 2, PIECES, steps)] * 2
        + [sems(layers, 2, 1, steps)] * 2
        + [sems(2, 1, steps)] * 2
        + [sems(4 * layers)]
    )
    return pl.pallas_call(
        functools.partial(backward_body, layers, head_count, count),
        name="backward",
        out_shape=[
            jax.ShapeDtypeStruct((rows, width), F32),
            jax.ShapeDtypeStruct((rows, width), F32),
            jax.ShapeDtypeStruct((layers, 3 * used, width), BF16),
            jax.ShapeDtypeStruct((layers, used, width), BF16),
            jax.ShapeDtypeStruct((layers, width, inner), BF16),
            jax.ShapeDtypeStruct((layers, inner, width), BF16),
            jax.ShapeDtypeStruct((SMALL_ROWS, width), F32),
        ],
        in_specs=[in_vmem] * 2 + [in_hbm] * 19 + [in_vmem] * 4,
        out_specs=[in_vmem] * 2 + [in_hbm] * 4 + [in_vmem],
        scratch_shapes=scratch,
        compiler_params=pltpu.CompilerParams(
            collective_id=1, has_side_effects=True, vmem_limit_bytes=65400 * 1024
        ),
    )(*inputs)


SMALL_ROWS = 32


class Ring:
    def __init__(self, count):
        self.count = count
        self.steps = 2 * (count - 1)
        self.place = self.place_of(lax.axis_index("dp"))
        self.sides = (
            self.number_of((self.place + 1) % count),
            self.number_of((self.place + count - 1) % count),
        )

    def place_of(self, number):
        row, side = number // 2, number % 2
        return row + side * (self.count - 1 - 2 * row)

    def number_of(self, place):
        side = place // (self.count // 2)
        return 2 * (place + side * (self.count - 1 - 2 * place)) + side

    def streams(self, *sets):
        return [
            (leaf, way, sub)
            for leaf in sets
            for sub in range(leaf[1].shape[1])
            for way in range(2)
        ]

    def rows(self, stream, step):
        (data, got, _, _), way, sub = stream
        piece = got.shape[3]
        if way == 0:
            chunk = (self.place + 3 * self.count - step) % self.count
        else:
            chunk = (self.place + step) % self.count
        first = ((sub * 2 + way) * self.count + chunk) * piece
        return pl.ds(pl.multiple_of(first, piece), piece)

    def copy(self, stream, step, gather):
        (data, got, send_sems, recv_sems), way, sub = stream
        rows = self.rows(stream, step)
        return pltpu.make_async_remote_copy(
            src_ref=data.at[rows],
            dst_ref=data.at[rows] if gather else got.at[way, sub, step],
            send_sem=send_sems.at[way, sub, step],
            recv_sem=recv_sems.at[way, sub, step],
            device_id={"dp": self.sides[way]},
            device_id_type=MESH,
        )

    def start(self, streams):
        for stream in streams:
            self.copy(stream, 0, False).start()

    def add(self, stream, step):
        (data, got, _, _), way, sub = stream
        self.copy(stream, step, False).wait_recv()
        rows = self.rows(stream, step + 1)
        data[rows] = data[rows] + got[way, sub, step]

    def drain(self, streams):
        for step in range(self.count - 1, self.steps):
            for stream in streams:
                self.copy(stream, step, True).wait_send()


def ring_fits(count, rows):
    return count == 8 and rows % (2 * count * 16) == 0


def widen_body(
    wide,
    lengths,
    stream,
    gradient,
    out_in,
    up_in,
    down_in,
    small,
    result,
    d_tokens,
    d_out,
    d_up,
    d_down,
    d_bias,
    d_up_bias,
    *kinds,
):
    number = pl.program_id(0)
    rows, width = stream.shape
    layers, _, used = d_bias.shape
    place = lax.axis_index("tensor")
    length = lengths[place, 0] + lengths[place, 1]
    row = number * rows + lax.broadcasted_iota(jnp.int32, (rows, width), 0)
    result[...] = jnp.where(row < length, stream[...], 0.0).astype(BF16)
    d_tokens[...] = gradient[...]
    d_out[...] = out_in[...].astype(F32)
    d_up[...] = up_in[...].astype(F32)
    d_down[...] = down_in[...].astype(F32)

    @pl.when(number == 0)
    def _():
        for kind, leaf in enumerate(kinds):
            for at in range(layers):
                first = 2 * (kind * layers + at)
                leaf[at] = small[first : first + 2]
        first = 8 * layers
        for at in range(layers):
            for half in range(2):
                start = 2 * half * wide
                d_bias[at, half : half + 1] = small[
                    first + at : first + at + 1, start : start + used
                ]
        first += layers
        d_up_bias[...] = small[first : first + layers]


def run_widen(lengths, stream, gradient, d_out, d_up, d_down, small, wide, used):
    rows, width = stream.shape
    layers = d_out.shape[0]
    parts = 2
    steps = layers * parts

    def rows_of(total):
        return pl.BlockSpec((total // steps, width), lambda at: (at, 0))

    def block(leaf):
        return pl.BlockSpec(
            (1, leaf.shape[1] // parts, width), lambda at: (at // parts, at % parts, 0)
        )

    def whole(*shape):
        return pl.BlockSpec(shape, lambda at: (0,) * len(shape))

    def full(*shape):
        return jax.ShapeDtypeStruct(shape, F32)

    return pl.pallas_call(
        functools.partial(widen_body, wide),
        name="widen",
        grid=(steps,),
        out_shape=[
            jax.ShapeDtypeStruct((rows, width), BF16),
            full(rows, width),
            full(*d_out.shape),
            full(*d_up.shape),
            full(*d_down.shape),
            full(layers, 2, used),
            full(layers, width),
            *[full(layers, 2, width)] * 4,
        ],
        in_specs=[
            pl.BlockSpec(memory_space=pltpu.SMEM),
            rows_of(rows),
            rows_of(rows),
            block(d_out),
            block(d_up),
            block(d_down),
            whole(*small.shape),
        ],
        out_specs=[
            rows_of(rows),
            rows_of(rows),
            block(d_out),
            block(d_up),
            block(d_down),
            whole(layers, 2, used),
            whole(layers, width),
            *[whole(layers, 2, width)] * 4,
        ],
    )(lengths, stream, gradient, d_out, d_up, d_down, small)


def per_device(
    tokens,
    cotangent,
    segments,
    lengths,
    rel_index,
    w_qkv,
    qv_bias,
    w_out,
    w_fc1,
    fc1_bias,
    w_fc2,
    rel_table,
    ln_gain,
    ln_bias,
    layer_scale,
    row_bias,
):
    own_rows, width = tokens.shape
    group_rows, bin_rows = rel_index.shape
    layer_count = w_qkv.shape[0]
    head_count = rel_table.shape[2]
    local_width = w_qkv.shape[3]
    wide = -(-local_width // 256) * 256
    bin_total = group_rows // bin_rows
    place = lax.axis_index("tensor")
    assert own_rows == bin_rows and bin_total == 4

    extra = wide - local_width
    qkv_used = jnp.pad(w_qkv, ((0, 0), (0, 0), (0, 0), (0, extra))).reshape(
        layer_count, width, 3 * wide
    )
    norms = (ln_gain, ln_bias, layer_scale, row_bias)

    (
        gath_a,
        qkv,
        shares,
        mixture,
        gath_b,
        slope,
        active,
        normal_a,
        branch_a,
        normal_b,
        branch_b,
        inverse,
        spots,
        turned,
        gath_z,
        gradient,
        middle,
    ) = run_forward(
        lengths,
        rel_index,
        rel_table,
        (tokens, cotangent),
        (qkv_used, qv_bias, w_out, w_fc1, fc1_bias, w_fc2),
        norms,
    )
    dp_count = lax.axis_size("dp")
    with_ring = ring_fits(dp_count, width)
    gradient, stream, *sums = run_backward(
        dp_count if with_ring else None,
        (
            gradient,
            middle,
            branch_a,
            branch_b,
            normal_a,
            normal_b,
            inverse,
            mixture,
            qkv,
            shares,
            gath_a,
            active,
            slope,
            gath_b,
            gath_z,
            qkv_used,
            w_out,
            w_fc1,
            w_fc2,
            spots,
            turned,
            fc1_bias,
            ln_gain,
            layer_scale,
            row_bias,
        ),
        head_count,
    )
    if not with_ring:
        sums = lax.psum(sums, "dp")
    *weight_sums, small = sums
    d_qkv, d_out, d_up, d_down = weight_sums
    result, d_tokens, d_out, d_up, d_down, d_bias, d_up_bias, *kinds = run_widen(
        lengths, stream, gradient, d_out, d_up, d_down, small, wide, local_width
    )
    d_qkv = jnp.transpose(
        d_qkv.astype(F32).reshape(layer_count, 3, local_width, width), (0, 3, 1, 2)
    )
    first = 8 * layer_count + 2 * layer_count
    d_table = small[first : first + layer_count * head_count, : rel_table.shape[1]]
    d_table = jnp.transpose(d_table.reshape(layer_count, head_count, -1), (0, 2, 1))
    return (
        result,
        d_tokens,
        d_qkv,
        d_bias,
        d_out,
        d_up,
        d_up_bias,
        d_down,
        d_table,
        *kinds,
    )


def solution(mesh):
    in_specs = (
        P(("dp", "tensor"), None),
        P(("dp", "tensor"), None),
        P("dp"),
        P("dp", None),
        P("dp", None),
        P(None, None, None, "tensor"),
        P(None, None, "tensor"),
        P(None, "tensor", None),
        P(None, None, "tensor"),
        P(None, "tensor"),
        P(None, "tensor", None),
        P(None, None, "tensor"),
        P(),
        P(),
        P(),
        P(),
    )
    out_specs = (
        P(("dp", "tensor"), None),
        P(("dp", "tensor"), None),
        P(None, None, None, "tensor"),
        P(None, None, "tensor"),
        P(None, "tensor", None),
        P(None, None, "tensor"),
        P(None, "tensor"),
        P(None, "tensor", None),
        P(None, None, "tensor"),
        P(),
        P(),
        P(),
        P(),
    )
    return jax.shard_map(
        per_device, mesh=mesh, in_specs=in_specs, out_specs=out_specs, check_vma=False
    )
```
